32 devices in a mesh: ctx: 16 (over z, x, core), wa: 2 (over y).
Axes of the slice: x: 2, y: 2, z: 4, core: 2. Of those that a mesh axis runs over, the one named last changes fastest.
Arguments:
- layer_input: bfloat16 [16, 2, 64, 1280], P('ctx'), may hold values from -6 to 6
- w_query: bfloat16 [1280, 1280], P(None, 'wa'), may hold values from -0.15625 to 0.15625
- w_key: bfloat16 [1280, 1280], P(None, 'wa'), may hold values from -0.15625 to 0.15625
- w_value: bfloat16 [1280, 1280], P(None, 'wa'), may hold values from -0.15625 to 0.15625
- w_out: bfloat16 [1280, 1280], P('wa'), may hold values from -0.15625 to 0.15625
- w_up: bfloat16 [1280, 5120], P(None, 'wa'), may hold values from -0.15625 to 0.15625
- w_gate: bfloat16 [1280, 5120], P(None, 'wa'), may hold values from -0.15625 to 0.15625
- w_down: bfloat16 [5120, 1280], P('wa'), may hold values from -0.078125 to 0.078125
- qk_scale: float32 [1280], P('wa'), may hold values from 0.9 to 1.6
- up_scale: float32 [5120], P('wa'), may hold values from 0.5 to 2
- gate_scale: float32 [5120], P('wa'), may hold values from 0.5 to 2
- attention_step: float32 [1280], replicated, may hold values from 0.2 to 0.8
- feedforward_step: float32 [1280], replicated, may hold values from 0.2 to 0.8
- cotangent: bfloat16 [16, 2, 64, 1280], P('ctx'), may hold values from -6 to 6
Outputs:
- layer_output: bfloat16 [16, 2, 64, 1280], P('ctx')
- input_grad: float32 [16, 2, 64, 1280], P('ctx')
- grad_query: float32 [1280, 1280], P('ctx', 'wa')
- grad_key: float32 [1280, 1280], P('ctx', 'wa')
- grad_value: float32 [1280, 1280], P('ctx', 'wa')
- grad_out: float32 [1280, 1280], P(('wa', 'ctx'))
- grad_up: float32 [1280, 5120], P('ctx', 'wa')
- grad_gate: float32 [1280, 5120], P('ctx', 'wa')
- grad_down: float32 [5120, 1280], P(('wa', 'ctx'))
- grad_qk_scale: float32 [1280], P(('wa', 'ctx'))
- grad_up_scale: float32 [5120], P(('wa', 'ctx'))
- grad_gate_scale: float32 [5120], P(('wa', 'ctx'))
- grad_attention_step: float32 [1280], P('ctx')
- grad_feedforward_step: float32 [1280], P('ctx')
The draws below stay inside these ranges and needn't reach their ends.
All inputs are finite; a program needn't handle non-finite values.
Results may differ from the reference program's by a relative error of at most 0.02.
Values may be sent and summed in bfloat16 or wider, within the bound.
A program may use at most 256 MiB of HBM per device.

```python
import math
import jax
import jax.numpy as jnp
from jax import lax

D = 1280
H = 20
HD = 64
FF = 5120
HC = 1280
BLK = 64
N_CTX = 16


def raised(drawn, rng, source, target, blocks, factor):
    owner, partner = [(jnp.arange(drawn.shape[axis_at]) // (drawn.shape[axis_at] // blocks)).reshape([-1 if axis == axis_at else 1 for axis in range(drawn.ndim)]) for axis_at in (source, target)]
    chosen = jax.random.permutation(rng, blocks)[partner]
    strong = (owner == chosen) | (owner == (partner + blocks // 2) % blocks)
    return jnp.where(strong, factor * drawn, drawn)


def levels(rng, extent, cuts, low, high):
    loudness, own = 1.0, jax.random.fold_in(rng, 6)
    for position, shards_of in cuts:
        heights = jnp.exp(jax.random.uniform(jax.random.fold_in(own, position), (shards_of,), jnp.float32, low / len(cuts), high / len(cuts)))
        loudness = loudness * jnp.repeat(heights, extent[position] // shards_of).reshape([-1 if axis == position else 1 for axis in range(len(extent))])
    return loudness


def scatter_about(own_key, extent, scale, limit, pieces=(), held_as=jnp.bfloat16):
    entries = scale * jax.random.normal(own_key, extent, jnp.float32)
    if pieces:
        entries = entries * levels(own_key, extent, pieces, -0.22, 0.18)
    return jnp.clip(entries, -limit, limit).astype(held_as)


def gaussian_with(stream_key, shape, deviation, bound, split, heavy, kind=jnp.bfloat16):
    entries = deviation * jax.random.normal(stream_key, shape, jnp.float32)
    if split:
        entries = entries * levels(stream_key, shape, split, -0.22, 0.18)
    return jnp.clip(raised(entries, jax.random.fold_in(stream_key, 3), *heavy), -bound, bound).astype(kind)


def setup_inputs(seed: int = 0) -> dict:
    arg_keys = jax.random.split(jax.random.key(seed), 15)
    layer_input = gaussian_with(arg_keys[0], (N_CTX, 2, BLK, D), 1.0, 6.0, ((0, 16),), (0, 3, 16, 2.0))
    w_query = scatter_about(arg_keys[1], (D, HC), D ** -0.5, 0.15625, ((1, 2),))
    w_key = scatter_about(arg_keys[2], (D, HC), D ** -0.5, 0.15625, ((1, 2),))
    w_value = scatter_about(arg_keys[3], (D, HC), D ** -0.5, 0.15625, ((1, 2),))
    w_out = scatter_about(arg_keys[4], (HC, D), HC ** -0.5, 0.15625, ((0, 2),))
    w_up = scatter_about(arg_keys[5], (D, FF), D ** -0.5, 0.15625, ((1, 2),))
    w_gate = scatter_about(arg_keys[6], (D, FF), D ** -0.5, 0.15625, ((1, 2),))
    w_down = scatter_about(arg_keys[7], (FF, D), FF ** -0.5, 0.078125, ((0, 2),))
    qk_scale = jnp.clip(jnp.exp(math.log(1.6) - 0.5753642 * jax.random.uniform(arg_keys[8], (HC,), jnp.float32) ** levels(arg_keys[8], (HC,), ((0, 2),), -0.2, 0.2)), 0.9, 1.6)
    up_scale = jnp.clip(jnp.exp(math.log(2.0) - 1.3862944 * jax.random.uniform(arg_keys[9], (FF,), jnp.float32) ** levels(arg_keys[9], (FF,), ((0, 2),), -0.2, 0.2)), 0.5, 2.0)
    gate_scale = jnp.clip(jnp.exp(math.log(2.0) - 1.3862944 * jax.random.uniform(arg_keys[10], (FF,), jnp.float32) ** levels(arg_keys[10], (FF,), ((0, 2),), -0.2, 0.2)), 0.5, 2.0)
    attention_step = jnp.clip(jax.random.uniform(arg_keys[11], (D,), jnp.float32, 0.2, 0.8), 0.2, 0.8)
    feedforward_step = jnp.clip(jax.random.uniform(arg_keys[12], (D,), jnp.float32, 0.2, 0.8), 0.2, 0.8)
    cotangent = gaussian_with(arg_keys[13], (N_CTX, 2, BLK, D), 1.0, 6.0, ((0, 16),), (0, 3, 16, 2.0))
    return dict(layer_input=layer_input, w_query=w_query, w_key=w_key, w_value=w_value, w_out=w_out, w_up=w_up, w_gate=w_gate, w_down=w_down, qk_scale=qk_scale, up_scale=up_scale, gate_scale=gate_scale, attention_step=attention_step, feedforward_step=feedforward_step, cotangent=cotangent)


NORM_EPS = 1e-06
MASK_FILL = -1e+30
HIGHEST_PREC = lax.Precision.HIGHEST

@jax.custom_vjp
def low(v):
    return lax.optimization_barrier(v.astype(jnp.bfloat16)).astype(jnp.float32)

@jax.custom_vjp
def low_back(v):
    return v

def low_keep(v):
    return (low(v), None)

def low_pass(kept, grad):
    return (grad,)

def back_keep(v):
    return (v, None)

def back_low(kept, grad):
    return (low(grad),)
low.defvjp(low_keep, low_pass)
low_back.defvjp(back_keep, back_low)

def unit_rms(vector):
    return vector * lax.rsqrt(lax.optimization_barrier(jnp.mean(vector * vector, axis=-1, keepdims=True)) + NORM_EPS)

def head_norm(projected, scales):
    row_count = projected.shape[0]
    shaped = unit_rms(projected.reshape(row_count, H, HD))
    return (shaped * scales.reshape(H, HD)).reshape(row_count, H * HD)

def mix_step(base, branch, step_size):
    return unit_rms(base + step_size * (unit_rms(branch) - base))

def gate_unit(up_raw, gate_raw, up_scale, gate_scale):
    scaled_up = up_raw * up_scale
    scaled_gate = gate_raw * gate_scale
    return scaled_up * (scaled_gate * lax.logistic(scaled_gate))

def token_positions(row_count):
    row_ids = jnp.arange(row_count, dtype=jnp.int32)
    owner_idx = row_ids // (2 * BLK)
    late_half = row_ids // BLK % 2
    offset_in = row_ids % BLK
    block_idx = jnp.where(late_half == 0, owner_idx, 2 * N_CTX - 1 - owner_idx)
    return (block_idx * BLK + offset_in).astype(jnp.int32)

def layer(input_rows, query_w, key_w, value_w, out_w, up_w, gate_w, down_w, qk_scale, up_scale, gate_scale, attention_step, feedforward_step):
    token_rows = input_rows.reshape(-1, D)
    total_rows = token_rows.shape[0]
    score_scale = 1.0 / math.sqrt(HD)
    q_raw = low_back(jnp.dot(token_rows, query_w, precision=HIGHEST_PREC))
    k_raw = low_back(jnp.dot(token_rows, key_w, precision=HIGHEST_PREC))
    v_raw = low_back(jnp.dot(token_rows, value_w, precision=HIGHEST_PREC))
    queries = low(head_norm(q_raw, qk_scale)).reshape(total_rows, H, HD)
    keys = low(head_norm(k_raw, qk_scale)).reshape(total_rows, H, HD)
    values = low(v_raw).reshape(total_rows, H, HD)
    positions = token_positions(total_rows)
    q_span = math.gcd(total_rows, 256)

    def attend(packed):
        block_queries, block_pos = packed
        raw_scores = low_back(jnp.einsum('qhd,khd->hqk', block_queries, keys, precision=HIGHEST_PREC))
        allowed = positions[None, :] <= block_pos[:, None]
        logits = jnp.where(allowed[None], raw_scores * score_scale, MASK_FILL)
        row_top = lax.optimization_barrier(jnp.max(logits, axis=-1, keepdims=True))
        weights = jnp.exp(logits - row_top)
        probabilities = low(weights / lax.optimization_barrier(jnp.sum(weights, axis=-1, keepdims=True)))
        return jnp.einsum('hqk,khd->qhd', probabilities, values, precision=HIGHEST_PREC)
    attended = lax.map(jax.checkpoint(attend), (queries.reshape(total_rows // q_span, q_span, H, HD), positions.reshape(total_rows // q_span, q_span)))
    attended = low(low_back(attended.reshape(total_rows, H * HD)))
    branch_attn = low_back(jnp.dot(attended, out_w, precision=HIGHEST_PREC))
    hidden_one = mix_step(token_rows, branch_attn, attention_step)
    hidden_low = low(hidden_one)
    up_raw = low_back(jnp.dot(hidden_low, up_w, precision=HIGHEST_PREC))
    gate_raw = low_back(jnp.dot(hidden_low, gate_w, precision=HIGHEST_PREC))
    gated = low(gate_unit(up_raw, gate_raw, up_scale, gate_scale))
    branch_mlp = low_back(jnp.dot(gated, down_w, precision=HIGHEST_PREC))
    return mix_step(hidden_one, branch_mlp, feedforward_step).reshape(input_rows.shape)

def reference(layer_input, w_query, w_key, w_value, w_out, w_up, w_gate, w_down, qk_scale, up_scale, gate_scale, attention_step, feedforward_step, cotangent):
    floats = (layer_input.astype(jnp.float32), w_query.astype(jnp.float32), w_key.astype(jnp.float32), w_value.astype(jnp.float32), w_out.astype(jnp.float32), w_up.astype(jnp.float32), w_gate.astype(jnp.float32), w_down.astype(jnp.float32), qk_scale.astype(jnp.float32), up_scale.astype(jnp.float32), gate_scale.astype(jnp.float32), attention_step.astype(jnp.float32), feedforward_step.astype(jnp.float32))
    result, pull = jax.vjp(layer, *floats)
    grads = pull(cotangent.astype(jnp.float32))
    return (result.astype(jnp.bfloat16), grads[0], grads[1], grads[2], grads[3], grads[4], grads[5], grads[6], grads[7], grads[8], grads[9], grads[10], grads[11], grads[12])
```

```python
import functools
from functools import partial
import math

import jax
import jax.numpy as jnp
from jax import lax
from jax.experimental import pallas as pl
from jax.experimental.pallas import tpu as pltpu
from jax.sharding import PartitionSpec as P

HD = 64
MESH = pl.DeviceIdType.MESH


def layout_of(n_ctx):
    chips = n_ctx // 2
    across = 2 if chips <= 8 else 4
    return chips // across, across


class Gather:
    def __init__(self, n_ctx, out, sems, z_rows, x_rows):
        self.line, self.across = layout_of(n_ctx)
        self.out = out
        self.rows = out.shape[1]
        self.sems = sems
        self.z_rows, self.x_rows = z_rows, x_rows
        ctx = lax.axis_index("ctx")
        self.ctx = ctx
        self.wa = lax.axis_index("wa")
        self.core = lax.rem(ctx, 2)
        chip = lax.div(ctx, 2)
        self.x = lax.rem(chip, self.across)
        self.z = lax.div(chip, self.across)
        self.count = 0
        self.sends = []

    @staticmethod
    def sem_count(n_ctx):
        line, across = layout_of(n_ctx)
        slots = 2 * line - 1
        return slots * (2 + 3 * (across - 1) + 1)

    def index(self, z, x, core):
        return (z * self.across + x) * 2 + core

    def sem(self, kind, slot, dx=0):
        line, across = self.line, self.across
        slots = 2 * line - 1
        base = {"z": 0, "y": 1, "c": 2, "x": 3, "yx": 3 + (across - 1), "cx": 3 + 2 * (across - 1)}[kind]
        return (base + dx) * slots + slot

    def slots_of(self, k):
        if k == 0:
            return [(0, 0)]
        return [(2 * k - 1, -k), (2 * k, k)]

    def exists(self, dz):
        z = self.z + dz
        return (z >= 0) & (z < self.line)

    def copy(self, sem, block, rows, device):
        start, size = rows
        view = self.out.at[block, pl.ds(start, size)]
        return pltpu.make_async_remote_copy(
            src_ref=view, dst_ref=view, send_sem=self.sems.at[0, sem], recv_sem=self.sems.at[1, sem],
            device_id=device, device_id_type=MESH)

    def part(self, size):
        return (pl.multiple_of(self.wa * (self.rows - size), 16), size)

    def lacking(self, size):
        return (pl.multiple_of(self.wa * size, 16), self.rows - size)

    def wanted(self, size):
        return (pl.multiple_of((1 - self.wa) * size, 16), self.rows - size)

    def full(self):
        return (0, self.rows)

    def peers(self):
        res = [(None, (self.ctx, 1 - self.wa)), (None, (self.index(self.z, self.x, 1 - self.core), self.wa))]
        for d in (-1, 1):
            res.append((self.exists(d), (self.index(self.z + d, self.x, self.core), self.wa)))
        for dx in range(1, self.across):
            res.append((None, (self.index(self.z, lax.rem(self.x + dx, self.across), self.core), self.wa)))
        return res

    def barrier(self):
        sem = pltpu.get_barrier_semaphore()
        total = 0
        for pred, dev in self.peers():
            def sig(dev=dev):
                pl.semaphore_signal(sem, inc=1, device_id=dev, device_id_type=MESH)
            if pred is None:
                sig()
                total = total + 1
            else:
                pl.when(pred)(sig)
                total = total + pred.astype(jnp.int32)
        pl.semaphore_wait(sem, total)

    def guard(self, dz, fn):
        if dz == 0:
            fn()
        else:
            pl.when(self.exists(dz))(fn)

    def send(self, dz, sem, block, rows, device, pred=None):
        desc = self.copy(sem, block, rows, device)
        self.sends.append((dz, pred, desc))
        desc.start()

    def z_next(self, k, dz, slot):
        if k + 1 >= self.line:
            return
        steps = (-1, 1) if dz == 0 else ((1,) if dz < 0 else (-1,))
        for d in steps:
            rslot = 2 * (k + 1) - 1 if d > 0 else 2 * (k + 1)
            block = self.index(self.z + dz, self.x, self.core)
            desc = self.copy(self.sem("z", rslot), block, self.part(self.z_rows), (self.index(self.z + d, self.x, self.core), self.wa))
            ok = self.exists(d) if dz == 0 else (self.exists(d) & self.exists(dz))
            pl.when(ok)(desc.start)
            self.sends.append((ok, desc))

    def x_send(self, dz, slot):
        block = self.index(self.z + dz, self.x, self.core)
        for dx in range(1, self.across):
            dev = (self.index(self.z, lax.rem(self.x + dx, self.across), self.core), self.wa)
            desc = self.copy(self.sem("x", slot, dx - 1), block, self.part(self.x_rows), dev)
            self.emit(dz, desc)

    def emit(self, dz, desc):
        if dz == 0:
            desc.start()
            self.sends.append((None, desc))
        else:
            ok = self.exists(dz)
            pl.when(ok)(desc.start)
            self.sends.append((ok, desc))

    def wait_recv(self, dz, desc):
        self.guard(dz, desc.wait_recv)

    def col(self, dx):
        return lax.rem(self.x + self.across - dx, self.across)

    def step_z(self, k):
        for slot, dz in self.slots_of(k):
            block = self.index(self.z + dz, self.x, self.core)
            if k > 0:
                self.wait_recv(dz, self.copy(self.sem("z", slot), block, self.part(self.z_rows), (self.ctx, self.wa)))
            self.z_next(k, dz, slot)
            self.x_send(dz, slot)
            if k > 0 and self.z_rows < self.rows:
                self.emit(dz, self.copy(self.sem("y", slot), block, self.lacking(self.z_rows), (self.ctx, 1 - self.wa)))
            if k == 0:
                self.emit(0, self.copy(self.sem("c", slot), block, self.full(), (self.index(self.z, self.x, 1 - self.core), self.wa)))

    def step_y(self, k):
        if k == 0:
            return
        for slot, dz in self.slots_of(k):
            block = self.index(self.z + dz, self.x, self.core)
            if self.z_rows < self.rows:
                self.wait_recv(dz, self.copy(self.sem("y", slot), block, self.wanted(self.z_rows), (self.ctx, self.wa)))
            self.emit(dz, self.copy(self.sem("c", slot), block, self.full(), (self.index(self.z, self.x, 1 - self.core), self.wa)))

    def step_x(self, k):
        for slot, dz in self.slots_of(k):
            for dx in range(1, self.across):
                block = self.index(self.z + dz, self.col(dx), self.core)
                self.wait_recv(dz, self.copy(self.sem("x", slot, dx - 1), block, self.part(self.x_rows), (self.ctx, self.wa)))
                if self.x_rows < self.rows:
                    self.emit(dz, self.copy(self.sem("yx", slot, dx - 1), block, self.lacking(self.x_rows), (self.ctx, 1 - self.wa)))

    def step_yx(self, k):
        for slot, dz in self.slots_of(k):
            for dx in range(1, self.across):
                block = self.index(self.z + dz, self.col(dx), self.core)
                if self.x_rows < self.rows:
                    self.wait_recv(dz, self.copy(self.sem("yx", slot, dx - 1), block, self.wanted(self.x_rows), (self.ctx, self.wa)))
                self.emit(dz, self.copy(self.sem("cx", slot, dx - 1), block, self.full(), (self.index(self.z, self.x, 1 - self.core), self.wa)))

    def step_c(self, k):
        for slot, dz in self.slots_of(k):
            block = self.index(self.z + dz, self.x, 1 - self.core)
            self.wait_recv(dz, self.copy(self.sem("c", slot), block, self.full(), (self.ctx, self.wa)))
            for dx in range(1, self.across):
                block = self.index(self.z + dz, self.col(dx), 1 - self.core)
                self.wait_recv(dz, self.copy(self.sem("cx", slot, dx - 1), block, self.full(), (self.ctx, self.wa)))

    def steps(self):
        line = self.line
        res = []
        for t in range(line + 3):
            if t < line:
                res.append(functools.partial(self.step_z, t))
            if 0 <= t - 1 < line:
                res.append(functools.partial(self.step_x, t - 1))
                res.append(functools.partial(self.step_y, t - 1))
            if 0 <= t - 2 < line:
                res.append(functools.partial(self.step_yx, t - 2))
            if 0 <= t - 3 < line:
                res.append(functools.partial(self.step_c, t - 3))
        return res

    def finish(self):
        for ok, desc in self.sends:
            if ok is None:
                desc.wait_send()
            else:
                pl.when(ok)(desc.wait_send)


def gather_kernel(n_ctx, z_rows, x_rows, x_ref, out_ref, sems, lsem):
    g = Gather(n_ctx, out_ref, sems, z_rows, x_rows)
    own = pltpu.make_async_copy(x_ref, out_ref.at[g.ctx], lsem)
    own.start()
    g.barrier()
    own.wait()
    for s in g.steps():
        s()
    g.finish()


def all_gather(x, n_ctx, collective_id, z_rows=96, x_rows=80):
    rows, width = x.shape
    n = Gather.sem_count(n_ctx)
    return pl.pallas_call(
        functools.partial(gather_kernel, n_ctx, z_rows, x_rows),
        out_shape=jax.ShapeDtypeStruct((n_ctx, rows, width), x.dtype),
        in_specs=[pl.BlockSpec(memory_space=pl.ANY)],
        out_specs=pl.BlockSpec(memory_space=pl.ANY),
        scratch_shapes=[pltpu.SemaphoreType.DMA((2, n)), pltpu.SemaphoreType.DMA],
        compiler_params=pltpu.CompilerParams(collective_id=collective_id, has_side_effects=True),
        name="gather_rows",
    )(x)


NORM_EPS = 1e-06


def unit_rms(vector):
    return vector * lax.rsqrt(jnp.mean(vector * vector, axis=-1, keepdims=True) + NORM_EPS)


def head_norm(projected, scales, head_count):
    row_count = projected.shape[0]
    shaped = unit_rms(projected.reshape(row_count, head_count, -1))
    return (shaped * scales.reshape(head_count, -1)).reshape(row_count, -1)


def mix_step(base, branch, step_size):
    return unit_rms(base + step_size * (unit_rms(branch) - base))


def gate_unit(up_raw, gate_raw, up_scale, gate_scale):
    scaled_up = up_raw * up_scale
    scaled_gate = gate_raw * gate_scale
    return scaled_up * (scaled_gate * lax.logistic(scaled_gate))


def token_positions(start, count, pair_count, block_len):
    row_ids = start + jnp.arange(count, dtype=jnp.int32)
    owner_idx = row_ids // (2 * block_len)
    late_half = row_ids // block_len % 2
    offset_in = row_ids % block_len
    block_idx = jnp.where(late_half == 0, owner_idx, 2 * pair_count - 1 - owner_idx)
    return block_idx * block_len + offset_in


def dot32(a, b):
    return jnp.dot(a, b, preferred_element_type=jnp.float32)


def dot_tn(a, b):
    return lax.dot_general(a, b, (((0,), (0,)), ((), ())), preferred_element_type=jnp.float32)


def dot_nt(a, b):
    return lax.dot_general(a, b, (((1,), (1,)), ((), ())), preferred_element_type=jnp.float32)


def shards(layer_input, w_query, w_key, w_value, w_out, w_up, w_gate, w_down, qk_scale, up_scale,
           gate_scale, attention_step, feedforward_step, cotangent):
    n_ctx = lax.axis_size("ctx")
    ctx = lax.axis_index("ctx")
    block_len = layer_input.shape[2]
    width = layer_input.shape[3]
    rows = 2 * block_len
    channels = w_query.shape[1]
    heads = channels // HD
    scale = 1.0 / math.sqrt(HD)
    total = rows * n_ctx
    own_pos = token_positions(ctx * rows, rows, n_ctx, block_len)
    all_pos = token_positions(0, total, n_ctx, block_len)
    allowed = all_pos[None, :] <= own_pos[:, None]
    bf = jnp.bfloat16

    x = layer_input.reshape(rows, width)
    xf = x.astype(jnp.float32)
    x_all = all_gather(x, n_ctx, 0).reshape(total, width)
    norm_heads = partial(head_norm, head_count=heads)
    q_all = norm_heads(dot32(x_all, w_query), qk_scale).astype(bf)
    k_all = norm_heads(dot32(x_all, w_key), qk_scale).astype(bf)
    v_all = dot32(x_all, w_value).astype(bf)
    q_raw = dot32(x, w_query)
    k_raw = dot32(x, w_key)
    q_norm, pull_query = jax.vjp(norm_heads, q_raw, qk_scale)
    k_norm, pull_key = jax.vjp(norm_heads, k_raw, qk_scale)
    split = lambda a: a.reshape(-1, heads, HD)
    qh, kh_all, vh_all, qh_all = split(q_norm.astype(bf)), split(k_all), split(v_all), split(q_all)
    s = jnp.einsum("qhd,khd->hqk", qh, kh_all, preferred_element_type=jnp.float32) * scale
    e = jnp.where(allowed[None], jnp.exp(s), 0.0)
    lse = jnp.log(jnp.sum(e, axis=-1))
    p = e * jnp.exp(-lse)[..., None]
    attended = jnp.einsum("hqk,khd->qhd", p.astype(bf), vh_all, preferred_element_type=jnp.float32)
    ob = attended.reshape(rows, channels).astype(bf)
    branch_attn = lax.psum(dot32(ob, w_out).astype(bf), "wa").astype(jnp.float32)
    hidden_one, pull_attn = jax.vjp(mix_step, xf, branch_attn, attention_step)
    hb = hidden_one.astype(bf)
    up_raw = dot32(hb, w_up)
    gate_raw = dot32(hb, w_gate)
    gated, pull_gate = jax.vjp(gate_unit, up_raw, gate_raw, up_scale, gate_scale)
    gated_low = gated.astype(bf)
    branch_mlp = lax.psum(dot32(gated_low, w_down).astype(bf), "wa").astype(jnp.float32)
    result, pull_mlp = jax.vjp(mix_step, hidden_one, branch_mlp, feedforward_step)
    layer_output = result.astype(bf).reshape(layer_input.shape)
    upstream = cotangent.reshape(rows, width).astype(jnp.float32)
    hidden_res, grad_branch_mlp, grad_ff_step = pull_mlp(upstream)
    dmb = grad_branch_mlp.astype(bf)
    hb_all = all_gather(hb, n_ctx, 1).reshape(total, width)
    dmb_all = all_gather(dmb, n_ctx, 2).reshape(total, width)
    dgated = dot_nt(dmb, w_down)
    dup, dgate, _, _ = pull_gate(dgated)
    dub, dgb = dup.astype(bf), dgate.astype(bf)
    terms = dot_nt(dub, w_up) + dot_nt(dgb, w_gate)
    hidden_grad = hidden_res + lax.psum(terms.astype(bf), "wa").astype(jnp.float32)
    input_res, grad_branch_attn, grad_attn_step = pull_attn(hidden_grad)
    dab = grad_branch_attn.astype(bf)
    dab_all = all_gather(dab, n_ctx, 3).reshape(total, width)

    mine = w_up.shape[1] // n_ctx
    cut = lambda a, axis: lax.dynamic_slice_in_dim(a, ctx * mine, mine, axis)
    wu, wg, wd = cut(w_up, 1), cut(w_gate, 1), cut(w_down, 0)
    us, gs = cut(up_scale, 0), cut(gate_scale, 0)
    gated_my, pull_my = jax.vjp(gate_unit, dot32(hb_all, wu), dot32(hb_all, wg), us, gs)
    du_my, dg_my, grad_up_scale, grad_gate_scale = pull_my(dot_nt(dmb_all, wd))
    grad_down = dot_tn(gated_my.astype(bf), dmb_all)
    swap = lambda a: lax.all_to_all(a, "ctx", 0, 1, tiled=True)
    grad_up = swap(dot_tn(hb_all, du_my.astype(bf)))
    grad_gate = swap(dot_tn(hb_all, dg_my.astype(bf)))

    doh = dot_nt(dab, w_out).astype(bf).reshape(rows, heads, HD)
    delta = jnp.sum(doh.astype(jnp.float32) * attended, axis=-1).T
    stats = lax.all_gather(jnp.concatenate([lse, delta], 0), "ctx", axis=0)
    stats = stats.transpose(1, 0, 2).reshape(2 * heads, total)
    doh_all = dot_nt(dab_all, w_out).astype(bf).reshape(total, heads, HD)
    dp = jnp.einsum("qhd,khd->hqk", doh, vh_all, preferred_element_type=jnp.float32)
    ds = (p * (dp - delta[..., None]) * scale).astype(bf)
    dq = jnp.einsum("hqk,khd->qhd", ds, kh_all, preferred_element_type=jnp.float32).reshape(rows, channels)
    kh, vh = split(k_norm.astype(bf)), split(dot32(x, w_value).astype(bf))
    allowed_t = own_pos[:, None] <= all_pos[None, :]
    st = jnp.einsum("khd,qhd->hkq", kh, qh_all, preferred_element_type=jnp.float32) * scale
    pt = jnp.where(allowed_t[None], jnp.exp(st - stats[:heads, None, :]), 0.0)
    dpt = jnp.einsum("khd,qhd->hkq", vh, doh_all, preferred_element_type=jnp.float32)
    dst = (pt * (dpt - stats[heads:, None, :]) * scale).astype(bf)
    dk = jnp.einsum("hkq,qhd->khd", dst, qh_all, preferred_element_type=jnp.float32).reshape(rows, channels)
    dv = jnp.einsum("hkq,qhd->khd", pt.astype(bf), doh_all, preferred_element_type=jnp.float32).reshape(rows, channels)
    grad_q_raw, scale_q = pull_query(dq)
    grad_k_raw, scale_k = pull_key(dk)
    dqb, dkb, dvb = grad_q_raw.astype(bf), grad_k_raw.astype(bf), dv.astype(bf)
    terms = dot_nt(dqb, w_query) + dot_nt(dkb, w_key) + dot_nt(dvb, w_value)
    input_grad = (input_res + lax.psum(terms.astype(bf), "wa").astype(jnp.float32)).reshape(layer_input.shape)
    cols = jnp.concatenate([dqb, dkb, dvb, ob], axis=1).reshape(rows, 4, n_ctx, -1).transpose(0, 2, 1, 3).reshape(rows, -1)
    got = lax.all_to_all(cols, "ctx", 1, 0, tiled=True).reshape(total, 4, -1)
    part = got.shape[2]
    grad_out = dot_tn(got[:, 3], dab_all)
    gqkv = dot_tn(x_all, got[:, :3].reshape(total, 3 * part))
    gqkv = lax.all_to_all(gqkv, "ctx", 0, 1, tiled=True).reshape(width // n_ctx, n_ctx, 3, part)
    gqkv = gqkv.transpose(2, 0, 1, 3).reshape(3, width // n_ctx, channels)
    sums = jnp.concatenate([grad_ff_step.reshape(n_ctx, -1), grad_attn_step.reshape(n_ctx, -1), (scale_q + scale_k).reshape(n_ctx, -1)], axis=1)
    sums = jnp.sum(lax.all_to_all(sums, "ctx", 0, 0, tiled=True), axis=0)
    step_part = width // n_ctx
    return (layer_output, input_grad, gqkv[0], gqkv[1], gqkv[2], grad_out, grad_up, grad_gate, grad_down,
            sums[2 * step_part:], grad_up_scale, grad_gate_scale, sums[step_part:2 * step_part], sums[:step_part])


def solution(mesh):
    placed = (
        P("ctx", None, None, None),
        P(None, "wa"),
        P(None, "wa"),
        P(None, "wa"),
        P("wa", None),
        P(None, "wa"),
        P(None, "wa"),
        P("wa", None),
        P("wa"),
        P("wa"),
        P("wa"),
        P(),
        P(),
        P("ctx", None, None, None),
    )
    return jax.shard_map(
        shards,
        mesh=mesh,
        in_specs=placed,
        out_specs=(
            P("ctx", None, None, None),
            P("ctx", None, None, None),
            P("ctx", "wa"),
            P("ctx", "wa"),
            P("ctx", "wa"),
            P(("wa", "ctx"), None),
            P("ctx", "wa"),
            P("ctx", "wa"),
            P(("wa", "ctx"), None),
            P(("wa", "ctx")),
            P(("wa", "ctx")),
            P(("wa", "ctx")),
            P("ctx"),
            P("ctx"),
        ),
        check_vma=False,
    )
```

```python
import functools
from functools import partial
import math

import jax
import jax.numpy as jnp
from jax import lax
from jax.experimental import pallas as pl
from jax.experimental.pallas import tpu as pltpu
from jax.sharding import PartitionSpec as P

HD = 64
MESH = pl.DeviceIdType.MESH


def layout_of(n_ctx):
    chips = n_ctx // 2
    across = 2 if chips <= 8 else 4
    return chips // across, across


class Place:
    def __init__(self, n_ctx):
        self.n_ctx = n_ctx
        self.line, self.across = layout_of(n_ctx)
        self.ctx = lax.axis_index("ctx")
        self.wa = lax.axis_index("wa")
        self.core = lax.rem(self.ctx, 2)
        chip = lax.div(self.ctx, 2)
        self.x = lax.rem(chip, self.across)
        self.z = lax.div(chip, self.across)

    def index(self, z, x, core):
        return (z * self.across + x) * 2 + core

    def at(self, z, x, core):
        return (self.index(z, x, core), self.wa)

    def sibling(self):
        return self.at(self.z, self.x, 1 - self.core)

    def partner(self):
        return (self.ctx, 1 - self.wa)

    def inside(self, z):
        return (z >= 0) & (z < self.line)

    def column(self, shift):
        return lax.rem(self.x + shift, self.across)

    def barrier(self):
        sem = pltpu.get_barrier_semaphore()

        def signal(device):
            pl.semaphore_signal(sem, inc=1, device_id=device, device_id_type=MESH)

        signal(self.sibling())
        signal(self.partner())
        for shift in range(1, self.across):
            signal(self.at(self.z, self.column(shift), self.core))
        count = jnp.int32(self.across + 1)
        for step in (-1, 1):
            near = self.inside(self.z + step)
            pl.when(near)(functools.partial(signal, self.at(self.z + step, self.x, self.core)))
            count = count + near.astype(jnp.int32)
        pl.semaphore_wait(sem, count)

    def barrier_all(self):
        sem = pltpu.get_barrier_semaphore()
        pl.semaphore_signal(sem, inc=1, device_id=self.partner(), device_id_type=MESH)

        @pl.loop(1, self.n_ctx)
        def _(shift):
            other = lax.rem(self.ctx + shift, self.n_ctx)
            pl.semaphore_signal(sem, inc=1, device_id=(other, self.wa), device_id_type=MESH)

        pl.semaphore_wait(sem, self.n_ctx)


class Gather:
    def __init__(self, place, out, sems, base, first, rows, z_rows, x_rows):
        self.p = place
        self.out = out
        self.sems = sems
        self.base = base
        self.first, self.rows = first, rows
        self.z_rows, self.x_rows = z_rows, x_rows
        self.slots = 2 * place.line

    @staticmethod
    def sem_count(n_ctx):
        line, across = layout_of(n_ctx)
        return 2 * line * 3 * across

    def sem(self, kind, s, k, shift=0):
        kinds = self.p.across - 1
        order = {"z": 0, "y": 1, "c": 2, "x": 3, "yx": 3 + kinds, "cx": 3 + 2 * kinds}[kind]
        return self.base + (order + shift) * self.slots + (0 if s > 0 else self.p.line) + k

    def copy(self, sem, block, start, size, device):
        view = self.out.at[block, pl.ds(pl.multiple_of(self.first + start, 16), size)]
        return pltpu.make_async_remote_copy(
            src_ref=view, dst_ref=view, send_sem=self.sems.at[0, sem], recv_sem=self.sems.at[1, sem],
            device_id=device, device_id_type=MESH)

    def exists(self, s, k):
        ok = self.p.inside(self.p.z - s * k) & (k >= 0) & (k < self.p.line)
        return ok if s > 0 else ok & (k > 0)

    def d_z(self, s, k, block, device):
        return self.copy(self.sem("z", s, k), block, self.p.wa * (self.rows - self.z_rows), self.z_rows, device)

    def d_x(self, s, k, shift, block, device):
        return self.copy(self.sem("x", s, k, shift - 1), block, self.p.wa * (self.rows - self.x_rows), self.x_rows, device)

    def d_y(self, kind, s, k, shift, block, size, sending):
        side = self.p.wa if sending else 1 - self.p.wa
        return self.copy(self.sem(kind, s, k, shift), block, side * size, self.rows - size, self.p.partner())

    def d_c(self, kind, s, k, shift, block):
        return self.copy(self.sem(kind, s, k, shift), block, 0, self.rows, self.p.sibling())

    def ok_forward(self, s, k):
        p = self.p
        return p.inside(p.z - s * k) & p.inside(p.z + s) & (k >= 0) & (k + 1 < p.line)

    def step_z(self, k):
        p = self.p
        me = (p.ctx, p.wa)
        for s in (1, -1):
            block = p.index(p.z - s * k, p.x, p.core)

            @pl.when(self.exists(s, k) & (k > 0))
            def _():
                self.d_z(s, k, block, me).wait_recv()

            @pl.when(self.ok_forward(s, k))
            def _():
                self.d_z(s, k + 1, block, p.at(p.z + s, p.x, p.core)).start()

            @pl.when(self.exists(s, k))
            def _():
                for shift in range(1, p.across):
                    self.d_x(s, k, shift, block, p.at(p.z, p.column(shift), p.core)).start()
                if s > 0:
                    @pl.when(k == 0)
                    def _():
                        self.d_c("c", s, k, 0, block).start()

                if self.z_rows < self.rows:
                    @pl.when(k > 0)
                    def _():
                        self.d_y("y", s, k, 0, block, self.z_rows, True).start()

    def step_y(self, k):
        p = self.p
        for s in (1, -1):
            @pl.when(self.exists(s, k) & (k > 0))
            def _():
                block = p.index(p.z - s * k, p.x, p.core)
                if self.z_rows < self.rows:
                    self.d_y("y", s, k, 0, block, self.z_rows, False).wait_recv()
                self.d_c("c", s, k, 0, block).start()

    def step_x(self, k):
        p = self.p
        for s in (1, -1):
            @pl.when(self.exists(s, k))
            def _():
                for shift in range(1, p.across):
                    block = p.index(p.z - s * k, p.column(p.across - shift), p.core)
                    self.d_x(s, k, shift, block, (p.ctx, p.wa)).wait_recv()
                    if self.x_rows < self.rows:
                        self.d_y("yx", s, k, shift - 1, block, self.x_rows, True).start()

    def step_yx(self, k):
        p = self.p
        for s in (1, -1):
            @pl.when(self.exists(s, k))
            def _():
                for shift in range(1, p.across):
                    block = p.index(p.z - s * k, p.column(p.across - shift), p.core)
                    if self.x_rows < self.rows:
                        self.d_y("yx", s, k, shift - 1, block, self.x_rows, False).wait_recv()
                    self.d_c("cx", s, k, shift - 1, block).start()

    def step_c(self, k):
        p = self.p
        for s in (1, -1):
            @pl.when(self.exists(s, k))
            def _():
                self.d_c("c", s, k, 0, p.index(p.z - s * k, p.x, 1 - p.core)).wait_recv()
                for shift in range(1, p.across):
                    block = p.index(p.z - s * k, p.column(p.across - shift), 1 - p.core)
                    self.d_c("cx", s, k, shift - 1, block).wait_recv()

    def finish(self):
        p = self.p

        @pl.loop(0, p.line)
        def _(k):
            for s in (1, -1):
                block = p.index(p.z - s * k, p.x, p.core)

                @pl.when(self.ok_forward(s, k))
                def _():
                    self.d_z(s, k + 1, block, p.at(p.z + s, p.x, p.core)).wait_send()

                @pl.when(self.exists(s, k))
                def _():
                    self.d_c("c", s, k, 0, block).wait_send()
                    if self.z_rows < self.rows:
                        @pl.when(k > 0)
                        def _():
                            self.d_y("y", s, k, 0, block, self.z_rows, True).wait_send()
                    for shift in range(1, p.across):
                        self.d_x(s, k, shift, block, p.at(p.z, p.column(shift), p.core)).wait_send()
                        other = p.index(p.z - s * k, p.column(p.across - shift), p.core)
                        if self.x_rows < self.rows:
                            self.d_y("yx", s, k, shift - 1, other, self.x_rows, True).wait_send()
                        self.d_c("cx", s, k, shift - 1, other).wait_send()


class Pieces:
    def __init__(self, place, out, sems, cut):
        n = Gather.sem_count(place.n_ctx)
        self.p = place
        self.parts = []
        first = 0
        for number, (rows, z_rows, x_rows) in enumerate(cut):
            self.parts.append(Gather(place, out, sems, number * n, first, rows, z_rows, x_rows))
            first += rows

    def each(self, name, k):
        for part in self.parts:
            getattr(part, name)(k)

    def step(self, t):
        self.each("step_z", t)
        for part in self.parts:
            part.step_x(t - 1)
            part.step_y(t - 1)
        self.each("step_yx", t - 2)
        self.each("step_c", t - 3)

    def step_count(self):
        return self.p.line + 3

    def finish(self):
        for part in self.parts:
            part.finish()


def gather_sems(n_ctx, cut):
    return pltpu.SemaphoreType.DMA((2, len(cut) * Gather.sem_count(n_ctx)))


def gather_kernel(n_ctx, cut, x_ref, out_ref, sems, lsem):
    place = Place(n_ctx)
    g = Pieces(place, out_ref, sems, cut)
    own = pltpu.make_async_copy(x_ref, out_ref.at[place.ctx], lsem)
    own.start()
    place.barrier()
    own.wait()

    @pl.loop(0, g.step_count())
    def _(t):
        g.step(t)

    g.finish()


def all_gather(x, n_ctx, collective_id, cut):
    rows, width = x.shape
    return pl.pallas_call(
        functools.partial(gather_kernel, n_ctx, cut),
        out_shape=jax.ShapeDtypeStruct((n_ctx, rows, width), x.dtype),
        in_specs=[pl.BlockSpec(memory_space=pltpu.VMEM)],
        out_specs=pl.BlockSpec(memory_space=pl.ANY),
        scratch_shapes=[gather_sems(n_ctx, cut), pltpu.SemaphoreType.DMA],
        compiler_params=pltpu.CompilerParams(collective_id=collective_id, has_side_effects=True),
        name="gather_rows",
    )(x)


NORM_EPS = 1e-06
BF = jnp.bfloat16
F32 = jnp.float32


def dot32(a, b):
    return jnp.dot(a, b, preferred_element_type=F32)


def dot_tn(a, b):
    return lax.dot_general(a, b, (((0,), (0,)), ((), ())), preferred_element_type=F32)


def dot_nt(a, b):
    return lax.dot_general(a, b, (((1,), (1,)), ((), ())), preferred_element_type=F32)


def row_mean(v):
    return jnp.mean(v, axis=-1, keepdims=True)


def inv_rms(v):
    return lax.rsqrt(row_mean(v * v) + NORM_EPS)


def rms_back(v, inv, grad):
    n = v * inv
    return (grad - n * row_mean(n * grad)) * inv


def pair_mean(v):
    row = lax.broadcasted_iota(jnp.int32, (128, 128), 0)
    col = lax.broadcasted_iota(jnp.int32, (128, 128), 1)
    ones = jnp.where((row < HD) == (col < HD), 1.0 / HD, 0.0).astype(BF)
    high = v.astype(BF)
    lowp = (v - high.astype(F32)).astype(BF)
    return dot32(high, ones) + dot32(lowp, ones)


def head_rms(v):
    return lax.rsqrt(pair_mean(v * v) + NORM_EPS)


def position_of(shard, index, block_len, n_ctx):
    late = index >= block_len
    block = jnp.where(late, 2 * n_ctx - 1 - shard, shard)
    return block * block_len + jnp.where(late, index - block_len, index)


def stack_heads(v):
    first = lax.broadcasted_iota(jnp.int32, v.shape, 1) < HD
    zero = jnp.zeros_like(v)
    return jnp.concatenate([jnp.where(first, v, zero), jnp.where(first, zero, v)], axis=0)


def join_heads(v):
    rows = v.shape[0] // 2
    first = lax.broadcasted_iota(jnp.int32, (rows, 128), 1) < HD
    return jnp.where(first, v[:rows], v[rows:])


def load_rows(src, dst, sem):
    return pltpu.make_async_copy(src, dst, sem)


LOG2E = 1.4426950408889634
EXCHANGE = 256
TOGETHER = 4


def fwd_kernel(n_ctx, cut, x_ref, wq_ref, wk_ref, wv_ref, qs_ref, wo_ref, step_ref,
               xall_ref, qall_ref, kall_ref, vall_ref, qraw_ref, kraw_ref, o_ref, lse_ref, h1_ref, ha_ref,
               gsems, lsems, wsems, esems, xbuf, qbuf, kbuf, vbuf, q2, acc, lpart, sbuf, rbuf):
    place = Place(n_ctx)
    rows, width = x_ref.shape
    block_len = rows // 2
    channels = wq_ref.shape[1]
    tiles = channels // 128
    group = 2 * place.across
    plane = group * rows
    gather = Pieces(place, xall_ref, gsems, cut)
    own = load_rows(x_ref, xall_ref.at[place.ctx], lsems.at[0])
    own.start()
    place.barrier()
    own.wait()
    gather.each("step_z", 0)

    xv = x_ref[...]
    kraw_ref[...] = dot32(xv, wk_ref[...])
    qraw_ref[...] = dot32(xv, wq_ref[...])
    for t in range(tiles):
        cols = slice(t * 128, (t + 1) * 128)
        raw = qraw_ref[:, cols]
        q2[t] = stack_heads((raw * head_rms(raw) * qs_ref[:, cols]).astype(BF))
    acc[...] = jnp.zeros_like(acc)
    lpart[...] = jnp.zeros_like(lpart)

    def plane_of(s, k):
        return place.z - s * k

    def hbm(ref, zp):
        return ref.at[pl.ds(zp * group, group)]

    def x_load(s, k):
        side = 0 if s > 0 else 1
        return load_rows(hbm(xall_ref, plane_of(s, k)), xbuf.at[side], lsems.at[1 + side])

    def stores(s, k):
        side = 0 if s > 0 else 1
        zp = plane_of(s, k)
        return [load_rows(buf.at[side], hbm(ref, zp), wsems.at[side, i])
                for i, (buf, ref) in enumerate(((qbuf, qall_ref), (kbuf, kall_ref), (vbuf, vall_ref)))]

    def project(s, k):
        side = 0 if s > 0 else 1
        x_load(s, k).wait()

        @pl.loop(0, group // TOGETHER)
        def _(r):
            some = pl.ds(r * TOGETHER, TOGETHER)
            xr = xbuf[side, some].reshape(TOGETHER * rows, width)
            for w_ref, buf in ((wq_ref, qbuf), (wk_ref, kbuf)):
                raw = dot32(xr, w_ref[...])
                for t in range(tiles):
                    cols = slice(t * 128, (t + 1) * 128)
                    part = raw[:, cols]
                    normed = (part * head_rms(part) * qs_ref[:, cols]).astype(BF)
                    buf[side, some, :, cols] = normed.reshape(TOGETHER, rows, 128)
            vbuf[side, some] = dot32(xr, wv_ref[...]).astype(BF).reshape(TOGETHER, rows, channels)

        for copy in stores(s, k):
            copy.start()

    def attend(s, k):
        side = 0 if s > 0 else 1
        zp = plane_of(s, k)
        qi = lax.broadcasted_iota(jnp.int32, (2 * rows, 1), 0)
        qi = jnp.where(qi >= rows, qi - rows, qi)
        qpos = position_of(place.ctx, qi, block_len, n_ctx)
        ki = lax.broadcasted_iota(jnp.int32, (1, plane), 1)
        kpos = position_of(zp * group + lax.div(ki, rows), lax.rem(ki, rows), block_len, n_ctx)
        allowed = kpos <= qpos

        @pl.loop(0, tiles)
        def _(t):
            cols = pl.ds(pl.multiple_of(t * 128, 128), 128)
            kt = kbuf[side, :, :, cols].reshape(plane, 128)
            vt = vbuf[side, :, :, cols].reshape(plane, 128)
            score = dot_nt(q2[t], kt)
            e = jnp.where(allowed, jnp.exp2(score * (LOG2E / math.sqrt(HD))), 0.0)
            total = e[:, :128]
            for j in range(1, plane // 128):
                total = total + e[:, j * 128:(j + 1) * 128]
            lpart[t] += total
            acc[t] += dot32(e.astype(BF), vt)

        for copy in stores(s, k):
            copy.wait()

    def both(k, fn):
        for s in (1, -1):
            pl.when(gather.parts[0].exists(s, k))(functools.partial(fn, s, k))

    @pl.loop(1, place.line + 2)
    def _(t):
        gather.each("step_z", t)
        gather.each("step_x", t - 1)
        gather.each("step_y", t - 1)
        both(t - 2, attend)
        gather.each("step_yx", t - 1)
        gather.each("step_c", t - 1)
        both(t - 1, lambda s, k: x_load(s, k).start())
        both(t - 1, project)

    for t in range(tiles):
        mass = jnp.sum(lpart[t], axis=1, keepdims=True)
        o_ref[:, t * 128:(t + 1) * 128] = join_heads(acc[t] / mass)
        lse_ref[t] = jnp.broadcast_to(jnp.log(mass) * LOG2E, (2 * rows, 128))

    exchange(place, lambda cols: dot32(o_ref[...].astype(BF), wo_ref[:, cols]), ha_ref, sbuf, rbuf, esems)
    ha = ha_ref[...]
    xf = x_ref[...].astype(F32)
    w = xf + step_ref[...] * (ha * inv_rms(ha) - xf)
    h1_ref[...] = w * inv_rms(w)
    gather.finish()


def exchange(place, term, sum_ref, sbuf, rbuf, esems):
    width = sum_ref.shape[1]

    def copy(n):
        return pltpu.make_async_remote_copy(
            src_ref=sbuf.at[n], dst_ref=rbuf.at[n], send_sem=esems.at[0, n], recv_sem=esems.at[1, n],
            device_id=place.partner(), device_id_type=MESH)

    count = width // EXCHANGE
    for n in range(count):
        sbuf[n] = term(slice(n * EXCHANGE, (n + 1) * EXCHANGE)).astype(BF)
        copy(n).start()
    for n in range(count):
        copy(n).wait()
        sum_ref[:, n * EXCHANGE:(n + 1) * EXCHANGE] = sbuf[n].astype(F32) + rbuf[n].astype(F32)


def vmem_spec():
    return pl.BlockSpec(memory_space=pltpu.VMEM)


def any_spec():
    return pl.BlockSpec(memory_space=pl.ANY)


def forward_attention(x, w_query, w_key, w_value, qk_scale, w_out, step, n_ctx, collective_id, cut):
    rows, width = x.shape
    channels = w_query.shape[1]
    tiles = channels // 128
    line, across = layout_of(n_ctx)
    group = 2 * across
    count = width // EXCHANGE
    shape = jax.ShapeDtypeStruct
    return pl.pallas_call(
        functools.partial(fwd_kernel, n_ctx, cut),
        out_shape=(shape((n_ctx, rows, width), BF),) + (shape((n_ctx, rows, channels), BF),) * 3
        + (shape((rows, channels), F32),) * 3 + (shape((tiles, 2 * rows, 128), F32),) + (shape((rows, width), F32),) * 2,
        in_specs=[vmem_spec()] * 7,
        out_specs=(any_spec(),) * 4 + (vmem_spec(),) * 6,
        scratch_shapes=[
            gather_sems(n_ctx, cut), pltpu.SemaphoreType.DMA((3,)), pltpu.SemaphoreType.DMA((2, 3)),
            pltpu.SemaphoreType.DMA((2, count)),
            pltpu.VMEM((2, group, rows, width), BF),
            pltpu.VMEM((2, group, rows, channels), BF), pltpu.VMEM((2, group, rows, channels), BF),
            pltpu.VMEM((2, group, rows, channels), BF),
            pltpu.VMEM((tiles, 2 * rows, 128), BF), pltpu.VMEM((tiles, 2 * rows, 128), F32),
            pltpu.VMEM((tiles, 2 * rows, 128), F32),
            pltpu.VMEM((count, rows, EXCHANGE), BF), pltpu.VMEM((count, rows, EXCHANGE), BF)],
        compiler_params=pltpu.CompilerParams(collective_id=collective_id, has_side_effects=True,
                                             vmem_limit_bytes=48 << 20),
        cost_estimate=pl.CostEstimate(flops=12 * 10 ** 9, bytes_accessed=40 * 10 ** 6, transcendentals=3 * 10 ** 6),
        name="forward_attention",
    )(x, w_query, w_key, w_value, qk_scale, w_out, step)


BLOCK = 4
STATS = 128


def split_parts(v, count):
    parts = []
    rest = v
    for _ in range(count):
        part = rest.astype(BF)
        parts.append(part)
        rest = rest - part.astype(F32)
    return parts


def transposed(src, dst, dtype):
    for n in range(src.shape[1] // 128):
        dst[n * 128:(n + 1) * 128, :] = src[:, n * 128:(n + 1) * 128].T.astype(dtype)


class UnitScatter:
    def __init__(self, place, source, target, send_sems, recv_sems, senders, per_sender, per_owner):
        self.p, self.source, self.target = place, source, target
        self.send_sems, self.recv_sems = send_sems, recv_sems
        self.senders, self.per_sender, self.per_owner = senders, per_sender, per_owner

    def rows(self, unit):
        return pl.ds(pl.multiple_of(unit * 8, 8), 8)

    def copy(self, unit, slot, owner):
        return pltpu.make_async_remote_copy(
            src_ref=self.source.at[self.rows(unit)], dst_ref=self.target.at[self.rows(slot)],
            send_sem=self.send_sems.at[unit], recv_sem=self.recv_sems.at[slot],
            device_id=(owner, self.p.wa), device_id_type=MESH)

    def local(self, unit, slot):
        return pltpu.make_async_copy(self.source.at[self.rows(unit)], self.target.at[self.rows(slot)],
                                     self.recv_sems.at[slot])

    def outgoing(self, remote, near):
        p = self.p

        @pl.when(p.ctx < self.senders)
        def _():
            @pl.loop(0, self.per_sender)
            def _(unit):
                place_of = p.ctx * self.per_sender + unit
                owner, slot = lax.div(place_of, self.per_owner), lax.rem(place_of, self.per_owner)

                @pl.when(owner != p.ctx)
                def _():
                    remote(self.copy(unit, slot, owner))

                if near is not None:
                    @pl.when(owner == p.ctx)
                    def _():
                        near(self.local(unit, slot))

    def start(self):
        self.outgoing(lambda c: c.start(), lambda c: c.start())

    def wait(self):
        p = self.p

        @pl.loop(0, self.per_owner)
        def _(slot):
            place_of = p.ctx * self.per_owner + slot
            sender, unit = lax.div(place_of, self.per_sender), lax.rem(place_of, self.per_sender)

            @pl.when(sender != p.ctx)
            def _():
                self.copy(unit, slot, p.ctx).wait_recv()

            @pl.when(sender == p.ctx)
            def _():
                self.local(unit, slot).wait()

    def sent(self):
        self.outgoing(lambda c: c.wait_send(), None)


class Scatter:
    def __init__(self, place, source, target, sems, count, senders):
        self.p, self.source, self.target, self.sems = place, source, target, sems
        self.count, self.senders = count, senders

    def copy(self, dest, sender):
        return pltpu.make_async_remote_copy(
            src_ref=self.source(dest), dst_ref=self.target(sender),
            send_sem=self.sems.at[0, dest], recv_sem=self.sems.at[1, sender],
            device_id=(dest, self.p.wa), device_id_type=MESH)

    def each(self, fn):
        p = self.p

        @pl.loop(1, p.n_ctx)
        def _(shift):
            fn(lax.rem(p.ctx + shift, p.n_ctx))

    def start(self):
        p = self.p

        @pl.when(p.ctx < self.senders)
        def _():
            def go(dest):
                @pl.when(dest < self.count)
                def _():
                    self.copy(dest, p.ctx).start()
            self.each(go)

            @pl.when(p.ctx < self.count)
            def _():
                self.local().start()

    def local(self):
        return pltpu.make_async_copy(self.source(self.p.ctx), self.target(self.p.ctx), self.sems.at[1, self.p.ctx])

    def wait(self):
        p = self.p

        @pl.when(p.ctx < self.count)
        def _():
            def got(sender):
                @pl.when(sender < self.senders)
                def _():
                    self.copy(p.ctx, sender).wait_recv()
            self.each(got)

            @pl.when(p.ctx < self.senders)
            def _():
                self.local().wait()

    def sent(self):
        p = self.p

        @pl.when(p.ctx < self.senders)
        def _():
            def left(dest):
                @pl.when(dest < self.count)
                def _():
                    self.copy(dest, p.ctx).wait_send()
            self.each(left)


def bwd_kernel(n_ctx, cut, aligned, out_aligned, *refs):
    (dab_ref, dmb_ref, qraw_ref, kraw_ref, lse_ref, o_ref, dxr_ref, qs_ref, us_ref, gs_ref,
     wo_ref, wq_ref, wk_ref, wv_ref, xall_ref, qall_ref, kall_ref, vall_ref, hball_ref, wu_ref, wg_ref, wd_ref,
     dx_ref, gq_ref, gk_ref, gv_ref, gout_ref, gup_ref, ggate_ref, gdown_ref, gqs_ref, gus_ref, ggs_ref,
     daball_ref, dmball_ref, statall_ref, turned, turned_qkv, gocc,
     asems, msems, ssts, lsems, csems, esems, usems, tsems, osems, rsems, vsems, ssems,
     hbbuf, dmbuf, dabbuf, stbuf, qbuf, kvbuf, dobuf, rowstats, stats, delta, q2, k2, v2, do2, dq2, dk2, dv2,
     wuw, wgw, wdw, gu, gg, gd, colu, colg, comb, got_u, dqkv, got_t, got_o, obs, accq, got_q, sbuf, rbuf) = refs
    place = Place(n_ctx)
    rows, width = dxr_ref.shape
    block_len = rows // 2
    channels = qraw_ref.shape[1]
    tiles = channels // 128
    hidden = us_ref.shape[1]
    mine = hidden // n_ctx
    group = 2 * place.across
    subs = group // BLOCK
    many = BLOCK * rows
    window = gu.shape[0]
    scale = 1.0 / math.sqrt(HD)
    a_gather = Pieces(place, daball_ref, asems, cut)
    m_gather = Pieces(place, dmball_ref, msems, cut)
    s_gather = Pieces(place, statall_ref, ssts, ((rows, rows, rows),))
    start = jnp.minimum(lax.div(place.ctx * mine, 128) * 128, hidden - window)
    start = pl.multiple_of(start, 128)
    offset = pl.multiple_of(place.ctx * mine - start, 8)
    win = pl.ds(start, window)
    own = [load_rows(dab_ref, daball_ref.at[place.ctx], lsems.at[0]),
           load_rows(dmb_ref, dmball_ref.at[place.ctx], lsems.at[1]),
           load_rows(wu_ref.at[:, win], wuw, lsems.at[2]), load_rows(wg_ref.at[:, win], wgw, lsems.at[3]),
           load_rows(wd_ref.at[win, :], wdw, lsems.at[4])]
    for copy in own:
        copy.start()
    for t in range(tiles):
        obs[t] = o_ref[:, t * 128:(t + 1) * 128].astype(BF)
    place.barrier_all()
    own[0].wait()
    own[1].wait()
    a_gather.each("step_z", 0)
    d_out = dot_nt(dab_ref[...], wo_ref[...]).astype(BF)
    lane = lax.broadcasted_iota(jnp.int32, (rows, 128), 1)
    packed = jnp.zeros((rows, 128), F32)
    for t in range(tiles):
        cols = slice(t * 128, (t + 1) * 128)
        do2[t] = stack_heads(d_out[:, cols])
        both_heads = stack_heads(d_out[:, cols].astype(F32) * o_ref[:, cols])
        delta[t] = jnp.broadcast_to(jnp.sum(both_heads, axis=1, keepdims=True), (2 * rows, 128))
        for h in range(2):
            part_rows = slice(h * rows, (h + 1) * rows)
            values = split_parts(lse_ref[t, part_rows], 3) + split_parts(delta[t, part_rows], 2)
            for i, value in enumerate(values):
                packed = jnp.where(lane == i * 2 * tiles + 2 * t + h, value.astype(F32), packed)
    stats[...] = packed.astype(BF)
    own_stats = load_rows(stats, statall_ref.at[place.ctx], lsems.at[0])
    own_stats.start()
    own_stats.wait()
    s_gather.each("step_z", 0)
    m_gather.each("step_z", 0)
    o_scatter = Scatter(place, lambda dest: obs.at[dest], lambda sender: got_o.at[sender], osems, tiles, n_ctx)
    o_scatter.start()

    for t in range(tiles):
        cols = slice(t * 128, (t + 1) * 128)
        for raw_ref, dest in ((qraw_ref, q2), (kraw_ref, k2)):
            raw = raw_ref[:, cols]
            dest[t] = stack_heads((raw * head_rms(raw) * qs_ref[:, cols]).astype(BF))
    dq2[...] = jnp.zeros_like(dq2)
    dk2[...] = jnp.zeros_like(dk2)
    dv2[...] = jnp.zeros_like(dv2)
    gu[...] = jnp.zeros_like(gu)
    gg[...] = jnp.zeros_like(gg)
    gd[...] = jnp.zeros_like(gd)
    colu[...] = jnp.zeros_like(colu)
    colg[...] = jnp.zeros_like(colg)
    gocc[...] = jnp.zeros_like(gocc)

    def row_positions(shape, axis, first):
        i = lax.broadcasted_iota(jnp.int32, shape, axis)
        return position_of(first + lax.div(i, rows), lax.rem(i, rows), block_len, n_ctx)

    def own_positions(shape, axis):
        i = lax.broadcasted_iota(jnp.int32, shape, axis)
        return position_of(place.ctx, lax.rem(i, rows), block_len, n_ctx)

    total_blocks = n_ctx // BLOCK

    def kv_loads(b):
        side = lax.rem(b, 2)
        return [load_rows(ref.at[pl.ds(b * BLOCK, BLOCK)], kvbuf.at[side, i], csems.at[side, i])
                for i, ref in enumerate((kall_ref, vall_ref))]

    def wide(v):
        return jnp.concatenate([v] * (many // 128), axis=1)

    for copy in kv_loads(0):
        copy.start()

    @pl.loop(0, total_blocks)
    def _(b):
        side = lax.rem(b, 2)

        @pl.when(b + 1 < total_blocks)
        def _():
            for copy in kv_loads(b + 1):
                copy.start()

        for copy in kv_loads(b):
            copy.wait()
        allowed = row_positions((1, many), 1, b * BLOCK) <= own_positions((2 * rows, 1), 0)

        @pl.loop(0, tiles)
        def _(t):
            cols = pl.ds(pl.multiple_of(t * 128, 128), 128)
            kt = kvbuf[side, 0, :, :, cols].reshape(many, 128)
            vt = kvbuf[side, 1, :, :, cols].reshape(many, 128)
            score = dot_nt(q2[t], kt)
            p = jnp.where(allowed, jnp.exp2(score * (LOG2E * scale) - wide(lse_ref[t])), 0.0)
            dp = dot_nt(do2[t], vt)
            ds = (p * (dp - wide(delta[t])) * scale).astype(BF)
            dq2[t] += dot32(ds, kt)

    own_v = load_rows(vall_ref.at[place.ctx], dobuf.at[0], lsems.at[0])
    own_v.start()
    own_v.wait()
    for t in range(tiles):
        v2[t] = stack_heads(dobuf[0, :, t * 128:(t + 1) * 128])
    for copy in own[2:]:
        copy.wait()
    o_scatter.wait()

    def block_of(s, k, sub):
        return ((place.z - s * k) * subs + sub) * BLOCK

    def a_loads(first):
        return [load_rows(daball_ref.at[pl.ds(first, BLOCK)], dabbuf, rsems.at[0]),
                load_rows(qall_ref.at[pl.ds(first, BLOCK)], qbuf, rsems.at[1]),
                load_rows(statall_ref.at[pl.ds(first, BLOCK)], stbuf, rsems.at[4])]

    def m_loads(first):
        return [load_rows(dmball_ref.at[pl.ds(first, BLOCK)], dmbuf, rsems.at[2]),
                load_rows(hball_ref.at[pl.ds(first, BLOCK)], hbbuf, rsems.at[3])]

    def keys_part(first):
        for copy in a_loads(first):
            copy.wait()
        dab = dabbuf[...].reshape(many, width)
        dobuf[...] = dot_nt(dab, wo_ref[...]).astype(BF).reshape(BLOCK, rows, channels)
        for j in range(BLOCK):
            rowstats[:, j * rows:(j + 1) * rows] = stbuf[j].astype(F32).T

        @pl.when(place.ctx < tiles)
        def _():
            gocc[...] += dot_tn(got_o[pl.ds(first, BLOCK)].reshape(many, 128), dab)

        allowed = own_positions((2 * rows, 1), 0) <= row_positions((1, many), 1, first)
        heads = 2 * tiles

        @pl.loop(0, tiles)
        def _(t):
            cols = pl.ds(pl.multiple_of(t * 128, 128), 128)
            qt = qbuf[:, :, cols].reshape(many, 128)
            dot_ = dobuf[:, :, cols].reshape(many, 128)

            def both_rows(parts, at):
                def one(h):
                    row = rowstats[pl.ds(at * heads + h, 1), :]
                    for i in range(1, parts):
                        row = row + rowstats[pl.ds((at + i) * heads + h, 1), :]
                    return jnp.broadcast_to(row, (rows, many))
                return jnp.concatenate([one(2 * t), one(2 * t + 1)], axis=0)

            score = dot_nt(k2[t], qt)
            p = jnp.where(allowed, jnp.exp2(score * (LOG2E * scale) - both_rows(3, 0)), 0.0)
            dp = dot_nt(v2[t], dot_)
            ds = (p * (dp - both_rows(2, 3)) * scale).astype(BF)
            dv2[t] += dot32(p.astype(BF), dot_)
            dk2[t] += dot32(ds, qt)

    def hidden_part(first):
        for copy in m_loads(first):
            copy.wait()
        hb = hbbuf[...].reshape(many, width)
        dm = dmbuf[...].reshape(many, width)
        us, gs = us_ref[:, win], gs_ref[:, win]
        u = dot32(hb, wuw[...])
        g = dot32(hb, wgw[...])
        dgated = dot_nt(dm, wdw[...])
        a, c = u * us, g * gs
        s = lax.logistic(c)
        cs = c * s
        r = s * (1.0 + c * (1.0 - s))
        da = dgated * cs
        dc = dgated * a * r
        colu[...] += jnp.sum((da * u).reshape(many // 8, 8, window), axis=0)
        colg[...] += jnp.sum((dc * g).reshape(many // 8, 8, window), axis=0)
        gu[...] += dot_tn((da * us).astype(BF), hb)
        gg[...] += dot_tn((dc * gs).astype(BF), hb)
        gd[...] += dot_tn((a * cs).astype(BF), dm)

    def both(k, fn):
        for s in (1, -1):
            @pl.when(a_gather.parts[0].exists(s, k))
            def _():
                @pl.loop(0, subs)
                def _(sub):
                    fn(block_of(s, k, sub))

    def begin(loads):
        def go(first):
            for copy in loads(first):
                copy.start()
        return go

    def keys_full(first):
        begin(a_loads)(first)
        keys_part(first)

    def hidden_full(first):
        begin(m_loads)(first)
        hidden_part(first)

    @pl.loop(1, place.line + 1)
    def _(t):
        a_gather.each("step_z", t)
        s_gather.each("step_z", t)
        m_gather.each("step_z", t)
        for name in ("step_x", "step_y", "step_yx", "step_c"):
            a_gather.each(name, t - 1)
            s_gather.each(name, t - 1)
        both(t - 1, keys_full)
        for name in ("step_x", "step_y", "step_yx", "step_c"):
            m_gather.each(name, t - 1)
        both(t - 1, hidden_full)

    gdown_ref[...] = gd[pl.ds(offset, mine), :]
    comb[0:mine] = gu[pl.ds(offset, mine), :]
    comb[mine:2 * mine] = gg[pl.ds(offset, mine), :]
    comb[2 * mine:] = jnp.zeros((comb.shape[0] - 2 * mine, width), F32)
    transposed(comb, turned, BF)
    part = width // n_ctx

    def row_block(ref, size):
        return lambda dest: ref.at[pl.ds(pl.multiple_of(dest * size, 8), size)]

    if aligned:
        u_scatter = Scatter(place, row_block(turned, part), lambda sender: got_u.at[sender], usems, n_ctx, n_ctx)
        u_scatter.start()
    shift = lax.rem(window - offset, window)
    gus_ref[...] = pltpu.roll(jnp.broadcast_to(jnp.sum(colu[...], axis=0, keepdims=True), (8, window)), shift, 1)
    ggs_ref[...] = pltpu.roll(jnp.broadcast_to(jnp.sum(colg[...], axis=0, keepdims=True), (8, window)), shift, 1)

    if out_aligned:
        g_scatter = UnitScatter(place, gocc, gout_ref, ssems.at[0], ssems.at[1], tiles, 16, channels // n_ctx // 8)
        g_scatter.start()

    for t in range(tiles):
        cols = slice(t * 128, (t + 1) * 128)
        scales = qs_ref[:, cols]
        grad_scale = jnp.zeros((1, 128), F32)
        for n, (raw_ref, grads) in enumerate(((qraw_ref, dq2), (kraw_ref, dk2))):
            raw = raw_ref[:, cols]
            inv = head_rms(raw)
            normed = raw * inv
            grad = join_heads(grads[t])
            grad_scale = grad_scale + jnp.sum(grad * normed, axis=0, keepdims=True)
            e = grad * scales
            dqkv[n * tiles + t] = ((e - normed * pair_mean(normed * e)) * inv).astype(BF)
        gqs_ref[:, cols] = grad_scale
        dqkv[2 * tiles + t] = join_heads(dv2[t]).astype(BF)
    t_scatter = Scatter(place, lambda dest: dqkv.at[dest], lambda sender: got_t.at[sender], tsems, 3 * tiles, n_ctx)
    t_scatter.start()

    def input_terms(cols):
        total = None
        for n, w_ref in enumerate((wq_ref, wk_ref, wv_ref)):
            grad = jnp.concatenate([dqkv[n * tiles + t] for t in range(tiles)], axis=1)
            term = dot_nt(grad, w_ref[cols, :])
            total = term if total is None else total + term
        return total

    exchange(place, input_terms, dx_ref, sbuf, rbuf, esems)
    dx_ref[...] += dxr_ref[...]

    t_scatter.wait()

    @pl.when(place.ctx < 3 * tiles)
    def _():
        accq[...] = jnp.zeros_like(accq)

        @pl.loop(0, total_blocks)
        def _(b):
            load = load_rows(xall_ref.at[pl.ds(b * BLOCK, BLOCK)], hbbuf, rsems.at[0])
            load.start()
            load.wait()
            accq[...] += dot_tn(got_t[pl.ds(b * BLOCK, BLOCK)].reshape(many, 128), hbbuf[...].reshape(many, width))

        transposed(accq, turned_qkv, F32)

    if aligned:
        q_scatter = Scatter(place, row_block(turned_qkv, part), lambda sender: got_q.at[sender], vsems, n_ctx, 3 * tiles)
        q_scatter.start()
        u_scatter.wait()
        for j in range(n_ctx):
            gup_ref[:, j * mine:(j + 1) * mine] = got_u[j, :, 0:mine].astype(F32)
            ggate_ref[:, j * mine:(j + 1) * mine] = got_u[j, :, mine:2 * mine].astype(F32)
        q_scatter.wait()
        for n, ref in enumerate((gq_ref, gk_ref, gv_ref)):
            for t in range(tiles):
                ref[:, t * 128:(t + 1) * 128] = got_q[n * tiles + t]
        u_scatter.sent()
        q_scatter.sent()
    if out_aligned:
        g_scatter.wait()
        g_scatter.sent()
    a_gather.finish()
    m_gather.finish()
    s_gather.finish()
    o_scatter.sent()
    t_scatter.sent()


def backward_attention(dab, dmb, q_raw, k_raw, lse, attended, dxr, qk_scale, up_scale, gate_scale,
                       w_out, w_query, w_key, w_value, x_all, q_all, k_all, v_all, hb_all, w_up, w_gate, w_down,
                       n_ctx, collective_id, cut):
    rows, width = dxr.shape
    channels = q_raw.shape[1]
    tiles = channels // 128
    hidden = up_scale.shape[1]
    mine = hidden // n_ctx
    part = width // n_ctx
    aligned = part % 16 == 0
    out_rows = channels // n_ctx
    out_aligned = out_rows % 8 == 0
    window = 256
    pair = -(-2 * mine // 128) * 128
    count = width // EXCHANGE
    many = BLOCK * rows
    n_blocks = n_ctx
    shape = jax.ShapeDtypeStruct
    dma = pltpu.SemaphoreType.DMA
    V = pltpu.VMEM
    stack = lambda dtype: V((tiles, 2 * rows, 128), dtype)
    outs = (
        shape((rows, width), F32),
        shape((part, channels), F32), shape((part, channels), F32), shape((part, channels), F32),
        shape((out_rows, width), F32),
        shape((part, hidden), F32), shape((part, hidden), F32), shape((mine, width), F32),
        shape((1, channels), F32), shape((8, window), F32), shape((8, window), F32),
        shape((n_ctx, rows, width), BF), shape((n_ctx, rows, width), BF), shape((n_ctx, rows, STATS), BF),
        shape((width, pair), BF), shape((width, 128), F32), shape((128, width), F32))
    return pl.pallas_call(
        functools.partial(bwd_kernel, n_ctx, cut, aligned, out_aligned),
        out_shape=outs,
        in_specs=[vmem_spec()] * 14 + [any_spec()] * 8,
        out_specs=(vmem_spec(),) * 11 + (any_spec(),) * 3 + (vmem_spec(),) * 3,
        scratch_shapes=[
            gather_sems(n_ctx, cut), gather_sems(n_ctx, cut), gather_sems(n_ctx, ((rows, rows, rows),)), dma((5,)), dma((2, 2)), dma((2, count)),
            dma((2, n_ctx)), dma((2, n_ctx)), dma((2, n_ctx)), dma((5,)), dma((2, n_ctx)), dma((2, 16)),
            V((BLOCK, rows, width), BF), V((BLOCK, rows, width), BF), V((BLOCK, rows, width), BF), V((BLOCK, rows, STATS), BF),
            V((BLOCK, rows, channels), BF), V((2, 2, BLOCK, rows, channels), BF), V((BLOCK, rows, channels), BF),
            V((STATS, many), F32), V((rows, STATS), BF), stack(F32), stack(BF), stack(BF), stack(BF), stack(BF), stack(F32), stack(F32), stack(F32),
            V((width, window), BF), V((width, window), BF), V((window, width), BF),
            V((window, width), F32), V((window, width), F32), V((window, width), F32),
            V((8, window), F32), V((8, window), F32), V((pair, width), F32), V((n_ctx, part, pair), BF),
            V((3 * tiles, rows, 128), BF), V((n_ctx, rows, 128), BF), V((n_ctx, rows, 128), BF), V((tiles, rows, 128), BF),
            V((128, width), F32), V((3 * tiles, part, 128), F32),
            V((count, rows, EXCHANGE), BF), V((count, rows, EXCHANGE), BF)],
        compiler_params=pltpu.CompilerParams(collective_id=collective_id, has_side_effects=True,
                                             vmem_limit_bytes=60 << 20),
        cost_estimate=pl.CostEstimate(flops=20 * 10 ** 9, bytes_accessed=60 * 10 ** 6, transcendentals=6 * 10 ** 6),
        name="backward_attention",
    )(dab, dmb, q_raw, k_raw, lse, attended, dxr, qk_scale, up_scale, gate_scale,
      w_out, w_query, w_key, w_value, x_all, q_all, k_all, v_all, hb_all, w_up, w_gate, w_down)


def unit_rms(vector):
    return vector * lax.rsqrt(jnp.mean(vector * vector, axis=-1, keepdims=True) + NORM_EPS)


def mix_step(base, branch, step_size):
    return unit_rms(base + step_size * (unit_rms(branch) - base))


def gate_unit(up_raw, gate_raw, up_scale, gate_scale):
    scaled_up = up_raw * up_scale
    scaled_gate = gate_raw * gate_scale
    return scaled_up * (scaled_gate * lax.logistic(scaled_gate))


CUT = ((64, 48, 32), (64, 48, 48))


def shards(layer_input, w_query, w_key, w_value, w_out, w_up, w_gate, w_down, qk_scale, up_scale,
           gate_scale, attention_step, feedforward_step, cotangent):
    n_ctx = lax.axis_size("ctx")
    ctx = lax.axis_index("ctx")
    rows = 2 * layer_input.shape[2]
    width = layer_input.shape[3]
    channels = w_query.shape[1]
    hidden = w_up.shape[1]
    tiles = channels // 128
    x = layer_input.reshape(rows, width)
    xf = x.astype(F32)
    flat = lambda v: v.reshape(1, -1)
    x_all, q_all, k_all, v_all, q_raw, k_raw, attended, lse, hidden_one, branch_attn = forward_attention(
        x, w_query, w_key, w_value, flat(qk_scale), w_out, flat(attention_step), n_ctx, 0, CUT)
    _, pull_attn = jax.vjp(mix_step, xf, branch_attn, attention_step)
    hb = hidden_one.astype(BF)
    hb_all = all_gather(hb, n_ctx, 1, CUT)
    up_raw = dot32(hb, w_up)
    gate_raw = dot32(hb, w_gate)
    gated, pull_gate = jax.vjp(gate_unit, up_raw, gate_raw, up_scale, gate_scale)
    branch_mlp = lax.psum(dot32(gated.astype(BF), w_down).astype(BF), "wa").astype(F32)
    result, pull_mlp = jax.vjp(mix_step, hidden_one, branch_mlp, feedforward_step)
    layer_output = result.astype(BF).reshape(layer_input.shape)
    hidden_res, grad_branch_mlp, grad_ff_step = pull_mlp(cotangent.reshape(rows, width).astype(F32))
    dmb = grad_branch_mlp.astype(BF)
    dup, dgate, _, _ = pull_gate(dot_nt(dmb, w_down))
    terms = dot_nt(dup.astype(BF), w_up) + dot_nt(dgate.astype(BF), w_gate)
    hidden_grad = hidden_res + lax.psum(terms.astype(BF), "wa").astype(F32)
    input_res, grad_branch_attn, grad_attn_step = pull_attn(hidden_grad)
    dab = grad_branch_attn.astype(BF)
    (input_grad, gq, gk, gv, grad_out, grad_up, grad_gate, grad_down, gqs, gus, ggs,
     _, _, _, turned, turned_qkv, gocc) = backward_attention(
        dab, dmb, q_raw, k_raw, lse, attended, input_res, flat(qk_scale), flat(up_scale), flat(gate_scale),
        w_out, w_query, w_key, w_value, x_all, q_all, k_all, v_all, hb_all, w_up, w_gate, w_down, n_ctx, 2, CUT)
    mine = hidden // n_ctx
    part = width // n_ctx
    turned, turned_qkv, gocc = lax.optimization_barrier((turned, turned_qkv, gocc))
    if part % 16:
        got = lax.all_to_all(turned, "ctx", 0, 0, tiled=True).reshape(n_ctx, part, -1).transpose(1, 0, 2).astype(F32)
        grad_up = got[:, :, :mine].reshape(part, hidden)
        grad_gate = got[:, :, mine:2 * mine].reshape(part, hidden)
        got = lax.all_to_all(turned_qkv, "ctx", 0, 0, tiled=True).reshape(n_ctx, part, 128)[:3 * tiles]
        gq, gk, gv = got.reshape(3, tiles, part, 128).transpose(0, 2, 1, 3).reshape(3, part, channels)
    if (channels // n_ctx) % 8:
        whole = jnp.zeros((n_ctx, 128, width), F32)
        whole = lax.dynamic_update_slice_in_dim(whole, gocc[None], ctx, 0)[:tiles]
        grad_out = lax.psum_scatter(whole.reshape(channels, width), "ctx", scatter_dimension=0, tiled=True)
    sums = jnp.concatenate([v.reshape(n_ctx, -1) for v in (grad_ff_step, grad_attn_step, gqs)], axis=1)
    sums = jnp.sum(lax.all_to_all(sums, "ctx", 0, 0, tiled=True), axis=0)
    return (layer_output, input_grad.reshape(layer_input.shape), gq, gk, gv, grad_out, grad_up, grad_gate, grad_down,
            sums[2 * part:], gus[0, :mine], ggs[0, :mine], sums[part:2 * part], sums[:part])


def solution(mesh):
    placed = (
        P("ctx", None, None, None),
        P(None, "wa"),
        P(None, "wa"),
        P(None, "wa"),
        P("wa", None),
        P(None, "wa"),
        P(None, "wa"),
        P("wa", None),
        P("wa"),
        P("wa"),
        P("wa"),
        P(),
        P(),
        P("ctx", None, None, None),
    )
    return jax.shard_map(
        shards,
        mesh=mesh,
        in_specs=placed,
        out_specs=(
            P("ctx", None, None, None),
            P("ctx", None, None, None),
            P("ctx", "wa"),
            P("ctx", "wa"),
            P("ctx", "wa"),
            P(("wa", "ctx"), None),
            P("ctx", "wa"),
            P("ctx", "wa"),
            P(("wa", "ctx"), None),
            P(("wa", "ctx")),
            P(("wa", "ctx")),
            P(("wa", "ctx")),
            P("ctx"),
            P("ctx"),
        ),
        check_vma=False,
    )
```

```python
import functools
from functools import partial
import math

import jax
import jax.numpy as jnp
from jax import lax
from jax.experimental import pallas as pl
from jax.experimental.pallas import tpu as pltpu
from jax.sharding import PartitionSpec as P

HD = 64
MESH = pl.DeviceIdType.MESH


def layout_of(n_ctx):
    chips = n_ctx // 2
    across = 2 if chips <= 8 else 4
    return chips // across, across


class Place:
    def __init__(self, n_ctx):
        self.n_ctx = n_ctx
        self.line, self.across = layout_of(n_ctx)
        self.ctx = lax.axis_index("ctx")
        self.wa = lax.axis_index("wa")
        self.core = lax.rem(self.ctx, 2)
        chip = lax.div(self.ctx, 2)
        self.x = lax.rem(chip, self.across)
        self.z = lax.div(chip, self.across)

    def index(self, z, x, core):
        return (z * self.across + x) * 2 + core

    def at(self, z, x, core):
        return (self.index(z, x, core), self.wa)

    def sibling(self):
        return self.at(self.z, self.x, 1 - self.core)

    def partner(self):
        return (self.ctx, 1 - self.wa)

    def inside(self, z):
        return (z >= 0) & (z < self.line)

    def column(self, shift):
        return lax.rem(self.x + shift, self.across)

    def barrier(self):
        sem = pltpu.get_barrier_semaphore()

        def signal(device):
            pl.semaphore_signal(sem, inc=1, device_id=device, device_id_type=MESH)

        signal(self.sibling())
        signal(self.partner())
        for shift in range(1, self.across):
            signal(self.at(self.z, self.column(shift), self.core))
        count = jnp.int32(self.across + 1)
        for step in (-1, 1):
            near = self.inside(self.z + step)
            pl.when(near)(functools.partial(signal, self.at(self.z + step, self.x, self.core)))
            count = count + near.astype(jnp.int32)
        pl.semaphore_wait(sem, count)

    def barrier_all(self):
        sem = pltpu.get_barrier_semaphore()
        pl.semaphore_signal(sem, inc=1, device_id=self.partner(), device_id_type=MESH)

        @pl.loop(1, self.n_ctx)
        def _(shift):
            other = lax.rem(self.ctx + shift, self.n_ctx)
            pl.semaphore_signal(sem, inc=1, device_id=(other, self.wa), device_id_type=MESH)

        pl.semaphore_wait(sem, self.n_ctx)


class Gather:
    def __init__(self, place, out, sems, base, first, rows, z_rows, x_rows):
        self.p = place
        self.out = out
        self.sems = sems
        self.base = base
        self.first, self.rows = first, rows
        self.z_rows, self.x_rows = z_rows, x_rows
        self.slots = 2 * place.line

    @staticmethod
    def sem_count(n_ctx):
        line, across = layout_of(n_ctx)
        return 2 * line * 3 * across

    def sem(self, kind, s, k, shift=0):
        kinds = self.p.across - 1
        order = {"z": 0, "y": 1, "c": 2, "x": 3, "yx": 3 + kinds, "cx": 3 + 2 * kinds}[kind]
        return self.base + (order + shift) * self.slots + (0 if s > 0 else self.p.line) + k

    def copy(self, sem, block, start, size, device):
        view = self.out.at[block, pl.ds(pl.multiple_of(self.first + start, 16), size)]
        return pltpu.make_async_remote_copy(
            src_ref=view, dst_ref=view, send_sem=self.sems.at[0, sem], recv_sem=self.sems.at[1, sem],
            device_id=device, device_id_type=MESH)

    def exists(self, s, k):
        ok = self.p.inside(self.p.z - s * k) & (k >= 0) & (k < self.p.line)
        return ok if s > 0 else ok & (k > 0)

    def d_z(self, s, k, block, device):
        return self.copy(self.sem("z", s, k), block, self.p.wa * (self.rows - self.z_rows), self.z_rows, device)

    def d_x(self, s, k, shift, block, device):
        return self.copy(self.sem("x", s, k, shift - 1), block, self.p.wa * (self.rows - self.x_rows), self.x_rows, device)

    def d_y(self, kind, s, k, shift, block, size, sending):
        side = self.p.wa if sending else 1 - self.p.wa
        return self.copy(self.sem(kind, s, k, shift), block, side * size, self.rows - size, self.p.partner())

    def d_c(self, kind, s, k, shift, block):
        return self.copy(self.sem(kind, s, k, shift), block, 0, self.rows, self.p.sibling())

    def ok_forward(self, s, k):
        p = self.p
        return p.inside(p.z - s * k) & p.inside(p.z + s) & (k >= 0) & (k + 1 < p.line)

    def step_z(self, k):
        p = self.p
        me = (p.ctx, p.wa)
        for s in (1, -1):
            block = p.index(p.z - s * k, p.x, p.core)

            @pl.when(self.exists(s, k) & (k > 0))
            def _():
                self.d_z(s, k, block, me).wait_recv()

            @pl.when(self.ok_forward(s, k))
            def _():
                self.d_z(s, k + 1, block, p.at(p.z + s, p.x, p.core)).start()

            @pl.when(self.exists(s, k))
            def _():
                for shift in range(1, p.across):
                    self.d_x(s, k, shift, block, p.at(p.z, p.column(shift), p.core)).start()
                if s > 0:
                    @pl.when(k == 0)
                    def _():
                        self.d_c("c", s, k, 0, block).start()

                if self.z_rows < self.rows:
                    @pl.when(k > 0)
                    def _():
                        self.d_y("y", s, k, 0, block, self.z_rows, True).start()

    def step_y(self, k):
        p = self.p
        for s in (1, -1):
            @pl.when(self.exists(s, k) & (k > 0))
            def _():
                block = p.index(p.z - s * k, p.x, p.core)
                if self.z_rows < self.rows:
                    self.d_y("y", s, k, 0, block, self.z_rows, False).wait_recv()
                self.d_c("c", s, k, 0, block).start()

    def step_x(self, k):
        p = self.p
        for s in (1, -1):
            @pl.when(self.exists(s, k))
            def _():
                for shift in range(1, p.across):
                    block = p.index(p.z - s * k, p.column(p.across - shift), p.core)
                    self.d_x(s, k, shift, block, (p.ctx, p.wa)).wait_recv()
                    if self.x_rows < self.rows:
                        self.d_y("yx", s, k, shift - 1, block, self.x_rows, True).start()

    def step_yx(self, k):
        p = self.p
        for s in (1, -1):
            @pl.when(self.exists(s, k))
            def _():
                for shift in range(1, p.across):
                    block = p.index(p.z - s * k, p.column(p.across - shift), p.core)
                    if self.x_rows < self.rows:
                        self.d_y("yx", s, k, shift - 1, block, self.x_rows, False).wait_recv()
                    self.d_c("cx", s, k, shift - 1, block).start()

    def step_c(self, k):
        p = self.p
        for s in (1, -1):
            @pl.when(self.exists(s, k))
            def _():
                self.d_c("c", s, k, 0, p.index(p.z - s * k, p.x, 1 - p.core)).wait_recv()
                for shift in range(1, p.across):
                    block = p.index(p.z - s * k, p.column(p.across - shift), 1 - p.core)
                    self.d_c("cx", s, k, shift - 1, block).wait_recv()

    def finish(self):
        p = self.p

        @pl.loop(0, p.line)
        def _(k):
            for s in (1, -1):
                block = p.index(p.z - s * k, p.x, p.core)

                @pl.when(self.ok_forward(s, k))
                def _():
                    self.d_z(s, k + 1, block, p.at(p.z + s, p.x, p.core)).wait_send()

                @pl.when(self.exists(s, k))
                def _():
                    self.d_c("c", s, k, 0, block).wait_send()
                    if self.z_rows < self.rows:
                        @pl.when(k > 0)
                        def _():
                            self.d_y("y", s, k, 0, block, self.z_rows, True).wait_send()
                    for shift in range(1, p.across):
                        self.d_x(s, k, shift, block, p.at(p.z, p.column(shift), p.core)).wait_send()
                        other = p.index(p.z - s * k, p.column(p.across - shift), p.core)
                        if self.x_rows < self.rows:
                            self.d_y("yx", s, k, shift - 1, other, self.x_rows, True).wait_send()
                        self.d_c("cx", s, k, shift - 1, other).wait_send()


class Pieces:
    def __init__(self, place, out, sems, cut):
        n = Gather.sem_count(place.n_ctx)
        self.p = place
        self.parts = []
        first = 0
        for number, (rows, z_rows, x_rows) in enumerate(cut):
            self.parts.append(Gather(place, out, sems, number * n, first, rows, z_rows, x_rows))
            first += rows

    def each(self, name, k):
        for part in self.parts:
            getattr(part, name)(k)

    def step(self, t):
        self.each("step_z", t)
        for part in self.parts:
            part.step_x(t - 1)
            part.step_y(t - 1)
        self.each("step_yx", t - 2)
        self.each("step_c", t - 3)

    def step_count(self):
        return self.p.line + 3

    def finish(self):
        for part in self.parts:
            part.finish()


def gather_sems(n_ctx, cut):
    return pltpu.SemaphoreType.DMA((2, len(cut) * Gather.sem_count(n_ctx)))


NORM_EPS = 1e-06
BF = jnp.bfloat16
F32 = jnp.float32


def dot32(a, b):
    return jnp.dot(a, b, preferred_element_type=F32)


def dot_tn(a, b):
    return lax.dot_general(a, b, (((0,), (0,)), ((), ())), preferred_element_type=F32)


def dot_nt(a, b):
    return lax.dot_general(a, b, (((1,), (1,)), ((), ())), preferred_element_type=F32)


def row_mean(v):
    return jnp.mean(v, axis=-1, keepdims=True)


def inv_rms(v):
    return lax.rsqrt(row_mean(v * v) + NORM_EPS)


def rms_back(v, inv, grad):
    n = v * inv
    return (grad - n * row_mean(n * grad)) * inv


def pair_mean(v):
    row = lax.broadcasted_iota(jnp.int32, (128, 128), 0)
    col = lax.broadcasted_iota(jnp.int32, (128, 128), 1)
    ones = jnp.where((row < HD) == (col < HD), 1.0 / HD, 0.0).astype(BF)
    high = v.astype(BF)
    lowp = (v - high.astype(F32)).astype(BF)
    return dot32(high, ones) + dot32(lowp, ones)


def head_rms(v):
    return lax.rsqrt(pair_mean(v * v) + NORM_EPS)


def position_of(shard, index, block_len, n_ctx):
    late = index >= block_len
    block = jnp.where(late, 2 * n_ctx - 1 - shard, shard)
    return block * block_len + jnp.where(late, index - block_len, index)


def stack_heads(v):
    first = lax.broadcasted_iota(jnp.int32, v.shape, 1) < HD
    zero = jnp.zeros_like(v)
    return jnp.concatenate([jnp.where(first, v, zero), jnp.where(first, zero, v)], axis=0)


def join_heads(v):
    rows = v.shape[0] // 2
    first = lax.broadcasted_iota(jnp.int32, (rows, 128), 1) < HD
    return jnp.where(first, v[:rows], v[rows:])


def load_rows(src, dst, sem):
    return pltpu.make_async_copy(src, dst, sem)


LOG2E = 1.4426950408889634
EXCHANGE = 256
TOGETHER = 4


def fwd_kernel(n_ctx, cut, x_ref, wq_ref, wk_ref, wv_ref, qs_ref, wo_ref, step_ref,
               xall_ref, qall_ref, kall_ref, vall_ref, qraw_ref, kraw_ref, o_ref, lse_ref, h1_ref, ha_ref,
               gsems, lsems, wsems, esems, xbuf, qbuf, kbuf, vbuf, q2, acc, lpart, sbuf, rbuf):
    place = Place(n_ctx)
    rows, width = x_ref.shape
    block_len = rows // 2
    channels = wq_ref.shape[1]
    tiles = channels // 128
    group = 2 * place.across
    plane = group * rows
    gather = Pieces(place, xall_ref, gsems, cut)
    own = load_rows(x_ref, xall_ref.at[place.ctx], lsems.at[0])
    own.start()
    place.barrier()
    own.wait()
    gather.each("step_z", 0)

    xv = x_ref[...]
    kraw_ref[...] = dot32(xv, wk_ref[...])
    qraw_ref[...] = dot32(xv, wq_ref[...])
    for t in range(tiles):
        cols = slice(t * 128, (t + 1) * 128)
        raw = qraw_ref[:, cols]
        q2[t] = stack_heads((raw * head_rms(raw) * qs_ref[:, cols]).astype(BF))
    acc[...] = jnp.zeros_like(acc)
    lpart[...] = jnp.zeros_like(lpart)

    def plane_of(s, k):
        return place.z - s * k

    def hbm(ref, zp):
        return ref.at[pl.ds(zp * group, group)]

    def x_load(s, k):
        side = 0 if s > 0 else 1
        return load_rows(hbm(xall_ref, plane_of(s, k)), xbuf.at[side], lsems.at[1 + side])

    def stores(s, k):
        side = 0 if s > 0 else 1
        zp = plane_of(s, k)
        return [load_rows(buf.at[side], hbm(ref, zp), wsems.at[side, i])
                for i, (buf, ref) in enumerate(((qbuf, qall_ref), (kbuf, kall_ref), (vbuf, vall_ref)))]

    def project(s, k):
        side = 0 if s > 0 else 1
        x_load(s, k).wait()

        @pl.loop(0, group // TOGETHER)
        def _(r):
            some = pl.ds(r * TOGETHER, TOGETHER)
            xr = xbuf[side, some].reshape(TOGETHER * rows, width)
            for w_ref, buf in ((wq_ref, qbuf), (wk_ref, kbuf)):
                raw = dot32(xr, w_ref[...])
                for t in range(tiles):
                    cols = slice(t * 128, (t + 1) * 128)
                    part = raw[:, cols]
                    normed = (part * head_rms(part) * qs_ref[:, cols]).astype(BF)
                    buf[side, some, :, cols] = normed.reshape(TOGETHER, rows, 128)
            vbuf[side, some] = dot32(xr, wv_ref[...]).astype(BF).reshape(TOGETHER, rows, channels)

        for copy in stores(s, k):
            copy.start()

    def attend(s, k):
        side = 0 if s > 0 else 1
        zp = plane_of(s, k)
        qi = lax.broadcasted_iota(jnp.int32, (2 * rows, 1), 0)
        qi = jnp.where(qi >= rows, qi - rows, qi)
        qpos = position_of(place.ctx, qi, block_len, n_ctx)
        ki = lax.broadcasted_iota(jnp.int32, (1, plane), 1)
        kpos = position_of(zp * group + lax.div(ki, rows), lax.rem(ki, rows), block_len, n_ctx)
        allowed = kpos <= qpos

        @pl.loop(0, tiles)
        def _(t):
            cols = pl.ds(pl.multiple_of(t * 128, 128), 128)
            kt = kbuf[side, :, :, cols].reshape(plane, 128)
            vt = vbuf[side, :, :, cols].reshape(plane, 128)
            score = dot_nt(q2[t], kt)
            e = jnp.where(allowed, jnp.exp2(score * (LOG2E / math.sqrt(HD))), 0.0)
            total = e[:, :128]
            for j in range(1, plane // 128):
                total = total + e[:, j * 128:(j + 1) * 128]
            lpart[t] += total
            acc[t] += dot32(e.astype(BF), vt)

        for copy in stores(s, k):
            copy.wait()

    def both(k, fn):
        for s in (1, -1):
            pl.when(gather.parts[0].exists(s, k))(functools.partial(fn, s, k))

    @pl.loop(1, place.line + 2)
    def _(t):
        gather.each("step_z", t)
        gather.each("step_x", t - 1)
        gather.each("step_y", t - 1)
        both(t - 2, attend)
        gather.each("step_yx", t - 1)
        gather.each("step_c", t - 1)
        both(t - 1, lambda s, k: x_load(s, k).start())
        both(t - 1, project)

    for t in range(tiles):
        mass = jnp.sum(lpart[t], axis=1, keepdims=True)
        o_ref[:, t * 128:(t + 1) * 128] = join_heads(acc[t] / mass)
        lse_ref[t] = jnp.broadcast_to(jnp.log(mass) * LOG2E, (2 * rows, 128))

    exchange(place, lambda cols: dot32(o_ref[...].astype(BF), wo_ref[:, cols]), ha_ref, sbuf, rbuf, esems)
    ha = ha_ref[...]
    xf = x_ref[...].astype(F32)
    w = xf + step_ref[...] * (ha * inv_rms(ha) - xf)
    h1_ref[...] = w * inv_rms(w)
    gather.finish()


def exchange(place, term, sum_ref, sbuf, rbuf, esems, between=None):
    width = sum_ref.shape[1]

    def copy(n):
        return pltpu.make_async_remote_copy(
            src_ref=sbuf.at[n], dst_ref=rbuf.at[n], send_sem=esems.at[0, n], recv_sem=esems.at[1, n],
            device_id=place.partner(), device_id_type=MESH)

    count = width // EXCHANGE
    for n in range(count):
        sbuf[n] = term(slice(n * EXCHANGE, (n + 1) * EXCHANGE)).astype(BF)
        copy(n).start()
    if between is not None:
        between()
    for n in range(count):
        copy(n).wait()
        sum_ref[:, n * EXCHANGE:(n + 1) * EXCHANGE] = sbuf[n].astype(F32) + rbuf[n].astype(F32)


def vmem_spec():
    return pl.BlockSpec(memory_space=pltpu.VMEM)


def any_spec():
    return pl.BlockSpec(memory_space=pl.ANY)


def forward_attention(x, w_query, w_key, w_value, qk_scale, w_out, step, n_ctx, collective_id, cut):
    rows, width = x.shape
    channels = w_query.shape[1]
    tiles = channels // 128
    line, across = layout_of(n_ctx)
    group = 2 * across
    count = width // EXCHANGE
    shape = jax.ShapeDtypeStruct
    return pl.pallas_call(
        functools.partial(fwd_kernel, n_ctx, cut),
        out_shape=(shape((n_ctx, rows, width), BF),) + (shape((n_ctx, rows, channels), BF),) * 3
        + (shape((rows, channels), F32),) * 3 + (shape((tiles, 2 * rows, 128), F32),) + (shape((rows, width), F32),) * 2,
        in_specs=[vmem_spec()] * 7,
        out_specs=(any_spec(),) * 4 + (vmem_spec(),) * 6,
        scratch_shapes=[
            gather_sems(n_ctx, cut), pltpu.SemaphoreType.DMA((3,)), pltpu.SemaphoreType.DMA((2, 3)),
            pltpu.SemaphoreType.DMA((2, count)),
            pltpu.VMEM((2, group, rows, width), BF),
            pltpu.VMEM((2, group, rows, channels), BF), pltpu.VMEM((2, group, rows, channels), BF),
            pltpu.VMEM((2, group, rows, channels), BF),
            pltpu.VMEM((tiles, 2 * rows, 128), BF), pltpu.VMEM((tiles, 2 * rows, 128), F32),
            pltpu.VMEM((tiles, 2 * rows, 128), F32),
            pltpu.VMEM((count, rows, EXCHANGE), BF), pltpu.VMEM((count, rows, EXCHANGE), BF)],
        compiler_params=pltpu.CompilerParams(collective_id=collective_id, has_side_effects=True,
                                             vmem_limit_bytes=48 << 20),
        cost_estimate=pl.CostEstimate(flops=12 * 10 ** 9, bytes_accessed=40 * 10 ** 6, transcendentals=3 * 10 ** 6),
        name="forward_attention",
    )(x, w_query, w_key, w_value, qk_scale, w_out, step)


HIDDEN_CUT = 256


def mid_kernel(n_ctx, cut, h1_ref, ha_ref, x_ref, cot_ref, fs_ref, as_ref, us_ref, gs_ref, wu_ref, wg_ref, wd_ref,
               hball_ref, dmball_ref, out_ref, dab_ref, dxr_ref, gfs_ref, gas_ref,
               hsems, msems, lsems, wsems, e1sems, e2sems, wu, wg, wd, hbv, dmv, u_buf, g_buf, low_a, low_b, total,
               s1, r1, s2, r2):
    place = Place(n_ctx)
    rows, width = h1_ref.shape
    hidden = us_ref.shape[1]
    cuts = hidden // HIDDEN_CUT
    h_gather = Pieces(place, hball_ref, hsems, cut)
    m_gather = Pieces(place, dmball_ref, msems, cut)

    def part(n):
        return slice(n * HIDDEN_CUT, (n + 1) * HIDDEN_CUT)

    loads = [[load_rows(wu_ref.at[:, part(n)], wu.at[:, part(n)], wsems.at[0, n]),
              load_rows(wg_ref.at[:, part(n)], wg.at[:, part(n)], wsems.at[1, n])] for n in range(cuts)]
    down = [load_rows(wd_ref.at[part(n)], wd.at[part(n)], wsems.at[2, n]) for n in range(cuts)]
    for pair in loads:
        for copy in pair:
            copy.start()
    for copy in down:
        copy.start()
    hbv[...] = h1_ref[...].astype(BF)
    own = load_rows(hbv, hball_ref.at[place.ctx], lsems.at[0])
    own.start()
    place.barrier()
    own.wait()
    h_gather.each("step_z", 0)

    hb = hbv[...]
    for n in range(cuts):
        for copy in loads[n]:
            copy.wait()
        u = dot32(hb, wu[:, part(n)])
        g = dot32(hb, wg[:, part(n)])
        u_buf[:, part(n)] = u
        g_buf[:, part(n)] = g
        c = g * gs_ref[:, part(n)]
        low_a[:, part(n)] = (u * us_ref[:, part(n)] * (c * lax.logistic(c))).astype(BF)
    for copy in down:
        copy.wait()

    def serve_first():
        h_gather.each("step_z", 1)
        h_gather.each("step_x", 0)

    exchange(place, lambda cols: dot32(low_a[...], wd[:, cols]), total, s1, r1, e1sems, serve_first)
    h1 = h1_ref[...]
    fs = fs_ref[...]
    hm = total[...]
    m_inv = inv_rms(hm)
    step = hm * m_inv - h1
    z = h1 + fs * step
    z_inv = inv_rms(z)
    out_ref[...] = (z * z_inv).astype(BF)
    dz = rms_back(z, z_inv, cot_ref[...].astype(F32))
    gfs_ref[...] = jnp.sum(dz * step, axis=0, keepdims=True)
    dxr_ref[...] = (1.0 - fs) * dz
    dmv[...] = rms_back(hm, m_inv, fs * dz).astype(BF)
    own = load_rows(dmv, dmball_ref.at[place.ctx], lsems.at[1])
    own.start()
    h_gather.each("step_z", 2)
    own.wait()
    m_gather.each("step_z", 0)
    h_gather.each("step_yx", 0)
    h_gather.each("step_x", 1)
    h_gather.each("step_y", 1)

    dm = dmv[...]
    for n in range(cuts):
        dgated = dot_nt(dm, wd[part(n), :])
        u, g = u_buf[:, part(n)], g_buf[:, part(n)]
        us, gs = us_ref[:, part(n)], gs_ref[:, part(n)]
        c = g * gs
        s = lax.logistic(c)
        low_a[:, part(n)] = (dgated * (c * s) * us).astype(BF)
        low_b[:, part(n)] = (dgated * (u * us) * (s * (1.0 + c * (1.0 - s))) * gs).astype(BF)
        if n == cuts // 2:
            h_gather.each("step_z", 3)

    def serve_second():
        h_gather.each("step_yx", 1)
        h_gather.each("step_x", 2)
        h_gather.each("step_y", 2)
        m_gather.each("step_z", 1)
        m_gather.each("step_x", 0)

    exchange(place, lambda cols: dot_nt(low_a[...], wu[cols, :]) + dot_nt(low_b[...], wg[cols, :]), total, s2, r2,
             e2sems, serve_second)
    m_gather.each("step_z", 2)
    h_gather.each("step_x", 3)
    h_gather.each("step_y", 3)
    dh1 = dxr_ref[...] + total[...]
    xf = x_ref[...].astype(F32)
    step_size = as_ref[...]
    ha = ha_ref[...]
    a_inv = inv_rms(ha)
    step = ha * a_inv - xf
    w = xf + step_size * step
    dw = rms_back(w, inv_rms(w), dh1)
    gas_ref[...] = jnp.sum(dw * step, axis=0, keepdims=True)
    dxr_ref[...] = (1.0 - step_size) * dw
    dab_ref[...] = rms_back(ha, a_inv, step_size * dw).astype(BF)

    @pl.loop(4, place.line)
    def _(k):
        h_gather.each("step_z", k)
        h_gather.each("step_x", k)
        h_gather.each("step_y", k)

    @pl.loop(1, place.line + 1)
    def _(t):
        @pl.when(t > 1)
        def _():
            h_gather.each("step_yx", t)
        h_gather.each("step_c", t - 1)

        @pl.when(t > 1)
        def _():
            m_gather.each("step_x", t - 1)

            @pl.when(t + 1 > 2)
            def _():
                m_gather.each("step_z", t + 1)
        m_gather.each("step_y", t - 1)
        m_gather.each("step_yx", t - 1)
        m_gather.each("step_c", t - 1)

    h_gather.finish()
    m_gather.finish()


def feed_forward(hidden_one, branch_attn, x, cotangent, ff_step, attn_step, up_scale, gate_scale, w_up, w_gate, w_down,
                 n_ctx, collective_id, cut):
    rows, width = x.shape
    hidden = w_up.shape[1]
    cuts = hidden // HIDDEN_CUT
    count = width // EXCHANGE
    shape = jax.ShapeDtypeStruct
    dma = pltpu.SemaphoreType.DMA
    V = pltpu.VMEM
    box = V((count, rows, EXCHANGE), BF)
    return pl.pallas_call(
        functools.partial(mid_kernel, n_ctx, cut),
        out_shape=(shape((n_ctx, rows, width), BF), shape((n_ctx, rows, width), BF), shape((rows, width), BF),
                   shape((rows, width), BF), shape((rows, width), F32), shape((1, width), F32), shape((1, width), F32)),
        in_specs=[vmem_spec()] * 8 + [any_spec()] * 3,
        out_specs=(any_spec(),) * 2 + (vmem_spec(),) * 5,
        scratch_shapes=[
            gather_sems(n_ctx, cut), gather_sems(n_ctx, cut), dma((2,)), dma((3, cuts)), dma((2, count)), dma((2, count)),
            V((width, hidden), BF), V((width, hidden), BF), V((hidden, width), BF), V((rows, width), BF),
            V((rows, width), BF), V((rows, hidden), F32), V((rows, hidden), F32), V((rows, hidden), BF),
            V((rows, hidden), BF), V((rows, width), F32), box, box, box, box],
        compiler_params=pltpu.CompilerParams(collective_id=collective_id, has_side_effects=True,
                                             vmem_limit_bytes=52 << 20),
        cost_estimate=pl.CostEstimate(flops=5 * 10 ** 9, bytes_accessed=30 * 10 ** 6, transcendentals=10 ** 6),
        name="feed_forward",
    )(hidden_one, branch_attn, x, cotangent, ff_step, attn_step, up_scale, gate_scale, w_up, w_gate, w_down)


BLOCK = 4
STATS = 128


def split_parts(v, count):
    parts = []
    rest = v
    for _ in range(count):
        part = rest.astype(BF)
        parts.append(part)
        rest = rest - part.astype(F32)
    return parts


def transposed(src, dst, dtype):
    for n in range(src.shape[1] // 128):
        dst[n * 128:(n + 1) * 128, :] = src[:, n * 128:(n + 1) * 128].T.astype(dtype)


class UnitScatter:
    def __init__(self, place, source, target, send_sems, recv_sems, senders, per_sender, per_owner):
        self.p, self.source, self.target = place, source, target
        self.send_sems, self.recv_sems = send_sems, recv_sems
        self.senders, self.per_sender, self.per_owner = senders, per_sender, per_owner

    def rows(self, unit):
        return pl.ds(pl.multiple_of(unit * 8, 8), 8)

    def copy(self, unit, slot, owner):
        return pltpu.make_async_remote_copy(
            src_ref=self.source.at[self.rows(unit)], dst_ref=self.target.at[self.rows(slot)],
            send_sem=self.send_sems.at[unit], recv_sem=self.recv_sems.at[slot],
            device_id=(owner, self.p.wa), device_id_type=MESH)

    def local(self, unit, slot):
        return pltpu.make_async_copy(self.source.at[self.rows(unit)], self.target.at[self.rows(slot)],
                                     self.recv_sems.at[slot])

    def outgoing(self, remote, near):
        p = self.p

        @pl.when(p.ctx < self.senders)
        def _():
            @pl.loop(0, self.per_sender)
            def _(unit):
                place_of = p.ctx * self.per_sender + unit
                owner, slot = lax.div(place_of, self.per_owner), lax.rem(place_of, self.per_owner)

                @pl.when(owner != p.ctx)
                def _():
                    remote(self.copy(unit, slot, owner))

                if near is not None:
                    @pl.when(owner == p.ctx)
                    def _():
                        near(self.local(unit, slot))

    def start(self):
        self.outgoing(lambda c: c.start(), lambda c: c.start())

    def wait(self):
        p = self.p

        @pl.loop(0, self.per_owner)
        def _(slot):
            place_of = p.ctx * self.per_owner + slot
            sender, unit = lax.div(place_of, self.per_sender), lax.rem(place_of, self.per_sender)

            @pl.when(sender != p.ctx)
            def _():
                self.copy(unit, slot, p.ctx).wait_recv()

            @pl.when(sender == p.ctx)
            def _():
                self.local(unit, slot).wait()

    def sent(self):
        self.outgoing(lambda c: c.wait_send(), None)


class Scatter:
    def __init__(self, place, source, target, sems, count, senders):
        self.p, self.source, self.target, self.sems = place, source, target, sems
        self.count, self.senders = count, senders

    def copy(self, dest, sender):
        return pltpu.make_async_remote_copy(
            src_ref=self.source(dest), dst_ref=self.target(sender),
            send_sem=self.sems.at[0, dest], recv_sem=self.sems.at[1, sender],
            device_id=(dest, self.p.wa), device_id_type=MESH)

    def each(self, fn):
        p = self.p

        @pl.loop(1, p.n_ctx)
        def _(shift):
            fn(lax.rem(p.ctx + shift, p.n_ctx))

    def start(self):
        p = self.p

        @pl.when(p.ctx < self.senders)
        def _():
            def go(dest):
                @pl.when(dest < self.count)
                def _():
                    self.copy(dest, p.ctx).start()
            self.each(go)

            @pl.when(p.ctx < self.count)
            def _():
                self.local().start()

    def local(self):
        return pltpu.make_async_copy(self.source(self.p.ctx), self.target(self.p.ctx), self.sems.at[1, self.p.ctx])

    def wait(self):
        p = self.p

        @pl.when(p.ctx < self.count)
        def _():
            def got(sender):
                @pl.when(sender < self.senders)
                def _():
                    self.copy(p.ctx, sender).wait_recv()
            self.each(got)

            @pl.when(p.ctx < self.senders)
            def _():
                self.local().wait()

    def sent(self):
        p = self.p

        @pl.when(p.ctx < self.senders)
        def _():
            def left(dest):
                @pl.when(dest < self.count)
                def _():
                    self.copy(dest, p.ctx).wait_send()
            self.each(left)


def bwd_kernel(n_ctx, cut, aligned, out_aligned, *refs):
    (dab_ref, qraw_ref, kraw_ref, lse_ref, o_ref, dxr_ref, qs_ref, us_ref, gs_ref,
     wo_ref, wq_ref, wk_ref, wv_ref, xall_ref, qall_ref, kall_ref, vall_ref, hball_ref, dmball_ref, wu_ref, wg_ref, wd_ref,
     dx_ref, gq_ref, gk_ref, gv_ref, gout_ref, gup_ref, ggate_ref, gdown_ref, gqs_ref, gus_ref, ggs_ref,
     daball_ref, statall_ref, turned, turned_qkv, gocc,
     asems, ssts, lsems, csems, esems, usems, tsems, osems, rsems, vsems, ssems, xsems,
     hbbuf, dmbuf, dabbuf, stbuf, qbuf, kvbuf, dobuf, rowstats, stats, delta, q2, k2, v2, do2, dq2, dk2, dv2,
     wuw, wgw, wdw, gu, gg, gd, colu, colg, comb, got_u, dqkv, got_t, got_o, obs, accq, got_q, sbuf, rbuf) = refs
    place = Place(n_ctx)
    rows, width = dxr_ref.shape
    block_len = rows // 2
    channels = qraw_ref.shape[1]
    tiles = channels // 128
    hidden = us_ref.shape[1]
    mine = hidden // n_ctx
    group = 2 * place.across
    subs = group // BLOCK
    many = BLOCK * rows
    window = gu.shape[0]
    scale = 1.0 / math.sqrt(HD)
    a_gather = Pieces(place, daball_ref, asems, cut)
    s_gather = Pieces(place, statall_ref, ssts, ((rows, rows, rows),))
    start = jnp.minimum(lax.div(place.ctx * mine, 128) * 128, hidden - window)
    start = pl.multiple_of(start, 128)
    offset = pl.multiple_of(place.ctx * mine - start, 8)
    win = pl.ds(start, window)
    own = [load_rows(dab_ref, daball_ref.at[place.ctx], lsems.at[0]),
           load_rows(wu_ref.at[:, win], wuw, lsems.at[2]), load_rows(wg_ref.at[:, win], wgw, lsems.at[3]),
           load_rows(wd_ref.at[win, :], wdw, lsems.at[4])]
    for copy in own:
        copy.start()
    for t in range(tiles):
        obs[t] = o_ref[:, t * 128:(t + 1) * 128].astype(BF)
    place.barrier_all()
    own[0].wait()
    a_gather.each("step_z", 0)
    d_out = dot_nt(dab_ref[...], wo_ref[...]).astype(BF)
    lane = lax.broadcasted_iota(jnp.int32, (rows, 128), 1)
    packed = jnp.zeros((rows, 128), F32)
    for t in range(tiles):
        cols = slice(t * 128, (t + 1) * 128)
        do2[t] = stack_heads(d_out[:, cols])
        both_heads = stack_heads(d_out[:, cols].astype(F32) * o_ref[:, cols])
        delta[t] = jnp.broadcast_to(jnp.sum(both_heads, axis=1, keepdims=True), (2 * rows, 128))
        for h in range(2):
            part_rows = slice(h * rows, (h + 1) * rows)
            values = split_parts(lse_ref[t, part_rows], 3) + split_parts(delta[t, part_rows], 2)
            for i, value in enumerate(values):
                packed = jnp.where(lane == i * 2 * tiles + 2 * t + h, value.astype(F32), packed)
    stats[...] = packed.astype(BF)
    own_stats = load_rows(stats, statall_ref.at[place.ctx], lsems.at[0])
    own_stats.start()
    own_stats.wait()
    s_gather.each("step_z", 0)
    o_scatter = Scatter(place, lambda dest: obs.at[dest], lambda sender: got_o.at[sender], osems, tiles, n_ctx)
    o_scatter.start()

    for t in range(tiles):
        cols = slice(t * 128, (t + 1) * 128)
        for raw_ref, dest in ((qraw_ref, q2), (kraw_ref, k2)):
            raw = raw_ref[:, cols]
            dest[t] = stack_heads((raw * head_rms(raw) * qs_ref[:, cols]).astype(BF))
    dq2[...] = jnp.zeros_like(dq2)
    dk2[...] = jnp.zeros_like(dk2)
    dv2[...] = jnp.zeros_like(dv2)
    gu[...] = jnp.zeros_like(gu)
    gg[...] = jnp.zeros_like(gg)
    gd[...] = jnp.zeros_like(gd)
    colu[...] = jnp.zeros_like(colu)
    colg[...] = jnp.zeros_like(colg)
    gocc[...] = jnp.zeros_like(gocc)

    def row_positions(shape, axis, first):
        i = lax.broadcasted_iota(jnp.int32, shape, axis)
        return position_of(first + lax.div(i, rows), lax.rem(i, rows), block_len, n_ctx)

    def own_positions(shape, axis):
        i = lax.broadcasted_iota(jnp.int32, shape, axis)
        return position_of(place.ctx, lax.rem(i, rows), block_len, n_ctx)

    total_blocks = n_ctx // BLOCK

    def kv_loads(b):
        side = lax.rem(b, 2)
        return [load_rows(ref.at[pl.ds(b * BLOCK, BLOCK)], kvbuf.at[side, i], csems.at[side, i])
                for i, ref in enumerate((kall_ref, vall_ref))]

    def wide(v):
        return jnp.concatenate([v] * (many // 128), axis=1)

    for copy in kv_loads(0):
        copy.start()

    @pl.loop(0, total_blocks)
    def _(b):
        side = lax.rem(b, 2)

        @pl.when(b + 1 < total_blocks)
        def _():
            for copy in kv_loads(b + 1):
                copy.start()

        for copy in kv_loads(b):
            copy.wait()
        allowed = row_positions((1, many), 1, b * BLOCK) <= own_positions((2 * rows, 1), 0)

        @pl.loop(0, tiles)
        def _(t):
            cols = pl.ds(pl.multiple_of(t * 128, 128), 128)
            kt = kvbuf[side, 0, :, :, cols].reshape(many, 128)
            vt = kvbuf[side, 1, :, :, cols].reshape(many, 128)
            score = dot_nt(q2[t], kt)
            p = jnp.where(allowed, jnp.exp2(score * (LOG2E * scale) - wide(lse_ref[t])), 0.0)
            dp = dot_nt(do2[t], vt)
            ds = (p * (dp - wide(delta[t])) * scale).astype(BF)
            dq2[t] += dot32(ds, kt)

    own_v = load_rows(vall_ref.at[place.ctx], dobuf.at[0], lsems.at[0])
    own_v.start()
    own_v.wait()
    for t in range(tiles):
        v2[t] = stack_heads(dobuf[0, :, t * 128:(t + 1) * 128])
    for copy in own[1:]:
        copy.wait()
    o_scatter.wait()

    def block_of(s, k, sub):
        return ((place.z - s * k) * subs + sub) * BLOCK

    def a_loads(first):
        return [load_rows(daball_ref.at[pl.ds(first, BLOCK)], dabbuf, rsems.at[0]),
                load_rows(qall_ref.at[pl.ds(first, BLOCK)], qbuf, rsems.at[1]),
                load_rows(statall_ref.at[pl.ds(first, BLOCK)], stbuf, rsems.at[4])]

    def m_loads(b):
        side = lax.rem(b, 2)
        return [load_rows(dmball_ref.at[pl.ds(b * BLOCK, BLOCK)], dmbuf.at[side], xsems.at[side, 0]),
                load_rows(hball_ref.at[pl.ds(b * BLOCK, BLOCK)], hbbuf.at[side], xsems.at[side, 1])]

    def keys_part(first):
        for copy in a_loads(first):
            copy.wait()
        dab = dabbuf[...].reshape(many, width)
        dobuf[...] = dot_nt(dab, wo_ref[...]).astype(BF).reshape(BLOCK, rows, channels)
        for j in range(BLOCK):
            rowstats[:, j * rows:(j + 1) * rows] = stbuf[j].astype(F32).T

        @pl.when(place.ctx < tiles)
        def _():
            gocc[...] += dot_tn(got_o[pl.ds(first, BLOCK)].reshape(many, 128), dab)

        allowed = own_positions((2 * rows, 1), 0) <= row_positions((1, many), 1, first)
        heads = 2 * tiles

        @pl.loop(0, tiles)
        def _(t):
            cols = pl.ds(pl.multiple_of(t * 128, 128), 128)
            qt = qbuf[:, :, cols].reshape(many, 128)
            dot_ = dobuf[:, :, cols].reshape(many, 128)

            def both_rows(parts, at):
                def one(h):
                    row = rowstats[pl.ds(at * heads + h, 1), :]
                    for i in range(1, parts):
                        row = row + rowstats[pl.ds((at + i) * heads + h, 1), :]
                    return jnp.broadcast_to(row, (rows, many))
                return jnp.concatenate([one(2 * t), one(2 * t + 1)], axis=0)

            score = dot_nt(k2[t], qt)
            p = jnp.where(allowed, jnp.exp2(score * (LOG2E * scale) - both_rows(3, 0)), 0.0)
            dp = dot_nt(v2[t], dot_)
            ds = (p * (dp - both_rows(2, 3)) * scale).astype(BF)
            dv2[t] += dot32(p.astype(BF), dot_)
            dk2[t] += dot32(ds, qt)

    def hidden_part(side):
        hb = hbbuf[side].reshape(many, width)
        dm = dmbuf[side].reshape(many, width)
        us, gs = us_ref[:, win], gs_ref[:, win]
        u = dot32(hb, wuw[...])
        g = dot32(hb, wgw[...])
        dgated = dot_nt(dm, wdw[...])
        a, c = u * us, g * gs
        s = lax.logistic(c)
        cs = c * s
        r = s * (1.0 + c * (1.0 - s))
        da = dgated * cs
        dc = dgated * a * r
        colu[...] += jnp.sum((da * u).reshape(many // 8, 8, window), axis=0)
        colg[...] += jnp.sum((dc * g).reshape(many // 8, 8, window), axis=0)
        gu[...] += dot_tn((da * us).astype(BF), hb)
        gg[...] += dot_tn((dc * gs).astype(BF), hb)
        gd[...] += dot_tn((a * cs).astype(BF), dm)

    def hidden_all():
        for copy in m_loads(0):
            copy.start()

        @pl.loop(0, total_blocks)
        def _(b):
            @pl.when(b + 1 < total_blocks)
            def _():
                for copy in m_loads(b + 1):
                    copy.start()

            for copy in m_loads(b):
                copy.wait()
            hidden_part(lax.rem(b, 2))

            for gather in (a_gather, s_gather):
                gather.each("step_z", b + 1)
                gather.each("step_x", b)
                gather.each("step_y", b)
                gather.each("step_yx", b - 1)
                gather.each("step_c", b - 2)

    def both(k, fn):
        for s in (1, -1):
            @pl.when(a_gather.parts[0].exists(s, k))
            def _():
                @pl.loop(0, subs)
                def _(sub):
                    fn(block_of(s, k, sub))

    def begin(loads):
        def go(first):
            for copy in loads(first):
                copy.start()
        return go

    def keys_full(first):
        begin(a_loads)(first)
        keys_part(first)

    hidden_all()

    gdown_ref[...] = gd[pl.ds(offset, mine), :]
    comb[0:mine] = gu[pl.ds(offset, mine), :]
    comb[mine:2 * mine] = gg[pl.ds(offset, mine), :]
    comb[2 * mine:] = jnp.zeros((comb.shape[0] - 2 * mine, width), F32)
    transposed(comb, turned, BF)
    part = width // n_ctx

    def row_block(ref, size):
        return lambda dest: ref.at[pl.ds(pl.multiple_of(dest * size, 8), size)]

    if aligned:
        u_scatter = Scatter(place, row_block(turned, part), lambda sender: got_u.at[sender], usems, n_ctx, n_ctx)
        u_scatter.start()
    shift = lax.rem(window - offset, window)
    gus_ref[...] = pltpu.roll(jnp.broadcast_to(jnp.sum(colu[...], axis=0, keepdims=True), (8, window)), shift, 1)
    ggs_ref[...] = pltpu.roll(jnp.broadcast_to(jnp.sum(colg[...], axis=0, keepdims=True), (8, window)), shift, 1)

    @pl.loop(0, place.line)
    def _(k):
        for gather in (a_gather, s_gather):
            gather.each("step_yx", total_blocks - 1 + k)
            gather.each("step_c", total_blocks - 2 + k)
        both(k, keys_full)

    for gather in (a_gather, s_gather):
        gather.each("step_c", total_blocks - 2 + place.line)

    if out_aligned:
        g_scatter = UnitScatter(place, gocc, gout_ref, ssems.at[0], ssems.at[1], tiles, 16, channels // n_ctx // 8)
        g_scatter.start()

    for t in range(tiles):
        cols = slice(t * 128, (t + 1) * 128)
        scales = qs_ref[:, cols]
        grad_scale = jnp.zeros((1, 128), F32)
        for n, (raw_ref, grads) in enumerate(((qraw_ref, dq2), (kraw_ref, dk2))):
            raw = raw_ref[:, cols]
            inv = head_rms(raw)
            normed = raw * inv
            grad = join_heads(grads[t])
            grad_scale = grad_scale + jnp.sum(grad * normed, axis=0, keepdims=True)
            e = grad * scales
            dqkv[n * tiles + t] = ((e - normed * pair_mean(normed * e)) * inv).astype(BF)
        gqs_ref[:, cols] = grad_scale
        dqkv[2 * tiles + t] = join_heads(dv2[t]).astype(BF)
    t_scatter = Scatter(place, lambda dest: dqkv.at[dest], lambda sender: got_t.at[sender], tsems, 3 * tiles, n_ctx)
    t_scatter.start()

    def input_terms(cols):
        total = None
        for n, w_ref in enumerate((wq_ref, wk_ref, wv_ref)):
            grad = jnp.concatenate([dqkv[n * tiles + t] for t in range(tiles)], axis=1)
            term = dot_nt(grad, w_ref[cols, :])
            total = term if total is None else total + term
        return total

    pl.when(place.ctx < 3 * tiles)(load_rows(xall_ref.at[pl.ds(0, BLOCK)], hbbuf.at[0], xsems.at[0, 0]).start)
    exchange(place, input_terms, dx_ref, sbuf, rbuf, esems)
    dx_ref[...] += dxr_ref[...]

    t_scatter.wait()

    @pl.when(place.ctx < 3 * tiles)
    def _():
        accq[...] = jnp.zeros_like(accq)

        def x_load(b):
            side = lax.rem(b, 2)
            return load_rows(xall_ref.at[pl.ds(b * BLOCK, BLOCK)], hbbuf.at[side], xsems.at[side, 0])

        @pl.loop(0, total_blocks)
        def _(b):
            @pl.when(b + 1 < total_blocks)
            def _():
                x_load(b + 1).start()

            x_load(b).wait()
            accq[...] += dot_tn(got_t[pl.ds(b * BLOCK, BLOCK)].reshape(many, 128),
                                hbbuf[lax.rem(b, 2)].reshape(many, width))

        transposed(accq, turned_qkv, F32)

    if aligned:
        q_scatter = Scatter(place, row_block(turned_qkv, part), lambda sender: got_q.at[sender], vsems, n_ctx, 3 * tiles)
        q_scatter.start()
        u_scatter.wait()
        for j in range(n_ctx):
            gup_ref[:, j * mine:(j + 1) * mine] = got_u[j, :, 0:mine].astype(F32)
            ggate_ref[:, j * mine:(j + 1) * mine] = got_u[j, :, mine:2 * mine].astype(F32)
        q_scatter.wait()
        for n, ref in enumerate((gq_ref, gk_ref, gv_ref)):
            for t in range(tiles):
                ref[:, t * 128:(t + 1) * 128] = got_q[n * tiles + t]
        u_scatter.sent()
        q_scatter.sent()
    if out_aligned:
        g_scatter.wait()
        g_scatter.sent()
    a_gather.finish()
    s_gather.finish()
    o_scatter.sent()
    t_scatter.sent()


def backward_attention(dab, q_raw, k_raw, lse, attended, dxr, qk_scale, up_scale, gate_scale,
                       w_out, w_query, w_key, w_value, x_all, q_all, k_all, v_all, hb_all, dmb_all, w_up, w_gate, w_down,
                       n_ctx, collective_id, cut):
    rows, width = dxr.shape
    channels = q_raw.shape[1]
    tiles = channels // 128
    hidden = up_scale.shape[1]
    mine = hidden // n_ctx
    part = width // n_ctx
    aligned = part % 16 == 0
    out_rows = channels // n_ctx
    out_aligned = out_rows % 8 == 0
    window = 256
    pair = -(-2 * mine // 128) * 128
    count = width // EXCHANGE
    many = BLOCK * rows
    n_blocks = n_ctx
    shape = jax.ShapeDtypeStruct
    dma = pltpu.SemaphoreType.DMA
    V = pltpu.VMEM
    stack = lambda dtype: V((tiles, 2 * rows, 128), dtype)
    outs = (
        shape((rows, width), F32),
        shape((part, channels), F32), shape((part, channels), F32), shape((part, channels), F32),
        shape((out_rows, width), F32),
        shape((part, hidden), F32), shape((part, hidden), F32), shape((mine, width), F32),
        shape((1, channels), F32), shape((8, window), F32), shape((8, window), F32),
        shape((n_ctx, rows, width), BF), shape((n_ctx, rows, STATS), BF),
        shape((width, pair), BF), shape((width, 128), F32), shape((128, width), F32))
    return pl.pallas_call(
        functools.partial(bwd_kernel, n_ctx, cut, aligned, out_aligned),
        out_shape=outs,
        in_specs=[vmem_spec()] * 13 + [any_spec()] * 9,
        out_specs=(vmem_spec(),) * 11 + (any_spec(),) * 2 + (vmem_spec(),) * 3,
        scratch_shapes=[
            gather_sems(n_ctx, cut), gather_sems(n_ctx, ((rows, rows, rows),)), dma((5,)), dma((2, 2)), dma((2, count)),
            dma((2, n_ctx)), dma((2, n_ctx)), dma((2, n_ctx)), dma((5,)), dma((2, n_ctx)), dma((2, 16)), dma((2, 2)),
            V((2, BLOCK, rows, width), BF), V((2, BLOCK, rows, width), BF), V((BLOCK, rows, width), BF), V((BLOCK, rows, STATS), BF),
            V((BLOCK, rows, channels), BF), V((2, 2, BLOCK, rows, channels), BF), V((BLOCK, rows, channels), BF),
            V((STATS, many), F32), V((rows, STATS), BF), stack(F32), stack(BF), stack(BF), stack(BF), stack(BF), stack(F32), stack(F32), stack(F32),
            V((width, window), BF), V((width, window), BF), V((window, width), BF),
            V((window, width), F32), V((window, width), F32), V((window, width), F32),
            V((8, window), F32), V((8, window), F32), V((pair, width), F32), V((n_ctx, part, pair), BF),
            V((3 * tiles, rows, 128), BF), V((n_ctx, rows, 128), BF), V((n_ctx, rows, 128), BF), V((tiles, rows, 128), BF),
            V((128, width), F32), V((3 * tiles, part, 128), F32),
            V((count, rows, EXCHANGE), BF), V((count, rows, EXCHANGE), BF)],
        compiler_params=pltpu.CompilerParams(collective_id=collective_id, has_side_effects=True,
                                             vmem_limit_bytes=60 << 20),
        cost_estimate=pl.CostEstimate(flops=20 * 10 ** 9, bytes_accessed=60 * 10 ** 6, transcendentals=6 * 10 ** 6),
        name="backward_attention",
    )(dab, q_raw, k_raw, lse, attended, dxr, qk_scale, up_scale, gate_scale,
      w_out, w_query, w_key, w_value, x_all, q_all, k_all, v_all, hb_all, dmb_all, w_up, w_gate, w_down)


CUT = ((64, 48, 32), (64, 48, 48))


def shards(layer_input, w_query, w_key, w_value, w_out, w_up, w_gate, w_down, qk_scale, up_scale,
           gate_scale, attention_step, feedforward_step, cotangent):
    n_ctx = lax.axis_size("ctx")
    ctx = lax.axis_index("ctx")
    rows = 2 * layer_input.shape[2]
    width = layer_input.shape[3]
    channels = w_query.shape[1]
    hidden = w_up.shape[1]
    tiles = channels // 128
    x = layer_input.reshape(rows, width)
    flat = lambda v: v.reshape(1, -1)
    x_all, q_all, k_all, v_all, q_raw, k_raw, attended, lse, hidden_one, branch_attn = forward_attention(
        x, w_query, w_key, w_value, flat(qk_scale), w_out, flat(attention_step), n_ctx, 0, CUT)
    hb_all, dmb_all, result, dab, input_res, grad_ff_step, grad_attn_step = feed_forward(
        hidden_one, branch_attn, x, cotangent.reshape(rows, width), flat(feedforward_step), flat(attention_step),
        flat(up_scale), flat(gate_scale), w_up, w_gate, w_down, n_ctx, 1, CUT)
    layer_output = result.reshape(layer_input.shape)
    (input_grad, gq, gk, gv, grad_out, grad_up, grad_gate, grad_down, gqs, gus, ggs,
     _, _, turned, turned_qkv, gocc) = backward_attention(
        dab, q_raw, k_raw, lse, attended, input_res, flat(qk_scale), flat(up_scale), flat(gate_scale),
        w_out, w_query, w_key, w_value, x_all, q_all, k_all, v_all, hb_all, dmb_all, w_up, w_gate, w_down, n_ctx, 2, CUT)
    mine = hidden // n_ctx
    part = width // n_ctx
    turned, turned_qkv, gocc = lax.optimization_barrier((turned, turned_qkv, gocc))
    if part % 16:
        got = lax.all_to_all(turned, "ctx", 0, 0, tiled=True).reshape(n_ctx, part, -1).transpose(1, 0, 2).astype(F32)
        grad_up = got[:, :, :mine].reshape(part, hidden)
        grad_gate = got[:, :, mine:2 * mine].reshape(part, hidden)
        got = lax.all_to_all(turned_qkv, "ctx", 0, 0, tiled=True).reshape(n_ctx, part, 128)[:3 * tiles]
        gq, gk, gv = got.reshape(3, tiles, part, 128).transpose(0, 2, 1, 3).reshape(3, part, channels)
    if (channels // n_ctx) % 8:
        whole = jnp.zeros((n_ctx, 128, width), F32)
        whole = lax.dynamic_update_slice_in_dim(whole, gocc[None], ctx, 0)[:tiles]
        grad_out = lax.psum_scatter(whole.reshape(channels, width), "ctx", scatter_dimension=0, tiled=True)
    sums = jnp.concatenate([v.reshape(n_ctx, -1) for v in (grad_ff_step, grad_attn_step, gqs)], axis=1)
    sums = jnp.sum(lax.all_to_all(sums, "ctx", 0, 0, tiled=True), axis=0)
    return (layer_output, input_grad.reshape(layer_input.shape), gq, gk, gv, grad_out, grad_up, grad_gate, grad_down,
            sums[2 * part:], gus[0, :mine], ggs[0, :mine], sums[part:2 * part], sums[:part])


def solution(mesh):
    placed = (
        P("ctx", None, None, None),
        P(None, "wa"),
        P(None, "wa"),
        P(None, "wa"),
        P("wa", None),
        P(None, "wa"),
        P(None, "wa"),
        P("wa", None),
        P("wa"),
        P("wa"),
        P("wa"),
        P(),
        P(),
        P("ctx", None, None, None),
    )
    return jax.shard_map(
        shards,
        mesh=mesh,
        in_specs=placed,
        out_specs=(
            P("ctx", None, None, None),
            P("ctx", None, None, None),
            P("ctx", "wa"),
            P("ctx", "wa"),
            P("ctx", "wa"),
            P(("wa", "ctx"), None),
            P("ctx", "wa"),
            P("ctx", "wa"),
            P(("wa", "ctx"), None),
            P(("wa", "ctx")),
            P(("wa", "ctx")),
            P(("wa", "ctx")),
            P("ctx"),
            P("ctx"),
        ),
        check_vma=False,
    )
```

```python
import functools
from functools import partial
import math

import jax
import jax.numpy as jnp
from jax import lax
from jax.experimental import pallas as pl
from jax.experimental.pallas import tpu as pltpu
from jax.sharding import PartitionSpec as P

HD = 64
MESH = pl.DeviceIdType.MESH


def layout_of(n_ctx):
    chips = n_ctx // 2
    across = 2 if chips <= 8 else 4
    return chips // across, across


class Place:
    def __init__(self, n_ctx):
        self.n_ctx = n_ctx
        self.line, self.across = layout_of(n_ctx)
        self.ctx = lax.axis_index("ctx")
        self.wa = lax.axis_index("wa")
        self.core = lax.rem(self.ctx, 2)
        chip = lax.div(self.ctx, 2)
        self.x = lax.rem(chip, self.across)
        self.z = lax.div(chip, self.across)

    def index(self, z, x, core):
        return (z * self.across + x) * 2 + core

    def at(self, z, x, core):
        return (self.index(z, x, core), self.wa)

    def sibling(self):
        return self.at(self.z, self.x, 1 - self.core)

    def partner(self):
        return (self.ctx, 1 - self.wa)

    def inside(self, z):
        return (z >= 0) & (z < self.line)

    def column(self, shift):
        return lax.rem(self.x + shift, self.across)

    def barrier(self):
        sem = pltpu.get_barrier_semaphore()

        def signal(device):
            pl.semaphore_signal(sem, inc=1, device_id=device, device_id_type=MESH)

        signal(self.sibling())
        signal(self.partner())
        for shift in range(1, self.across):
            signal(self.at(self.z, self.column(shift), self.core))
        count = jnp.int32(self.across + 1)
        for step in (-1, 1):
            near = self.inside(self.z + step)
            pl.when(near)(functools.partial(signal, self.at(self.z + step, self.x, self.core)))
            count = count + near.astype(jnp.int32)
        pl.semaphore_wait(sem, count)

    def barrier_all(self):
        sem = pltpu.get_barrier_semaphore()
        pl.semaphore_signal(sem, inc=1, device_id=self.partner(), device_id_type=MESH)

        @pl.loop(1, self.n_ctx)
        def _(shift):
            other = lax.rem(self.ctx + shift, self.n_ctx)
            pl.semaphore_signal(sem, inc=1, device_id=(other, self.wa), device_id_type=MESH)

        pl.semaphore_wait(sem, self.n_ctx)


class Gather:
    def __init__(self, place, out, sems, base, first, rows, z_rows, x_rows):
        self.p = place
        self.out = out
        self.sems = sems
        self.base = base
        self.first, self.rows = first, rows
        self.z_rows, self.x_rows = z_rows, x_rows
        self.slots = 2 * place.line

    @staticmethod
    def sem_count(n_ctx):
        line, across = layout_of(n_ctx)
        return 2 * line * 3 * across

    def sem(self, kind, s, k, shift=0):
        kinds = self.p.across - 1
        order = {"z": 0, "y": 1, "c": 2, "x": 3, "yx": 3 + kinds, "cx": 3 + 2 * kinds}[kind]
        return self.base + (order + shift) * self.slots + (0 if s > 0 else self.p.line) + k

    def copy(self, sem, block, start, size, device):
        view = self.out.at[block, pl.ds(pl.multiple_of(self.first + start, 16), size)]
        return pltpu.make_async_remote_copy(
            src_ref=view, dst_ref=view, send_sem=self.sems.at[0, sem], recv_sem=self.sems.at[1, sem],
            device_id=device, device_id_type=MESH)

    def exists(self, s, k):
        ok = self.p.inside(self.p.z - s * k) & (k >= 0) & (k < self.p.line)
        return ok if s > 0 else ok & (k > 0)

    def d_z(self, s, k, block, device):
        return self.copy(self.sem("z", s, k), block, self.p.wa * (self.rows - self.z_rows), self.z_rows, device)

    def d_x(self, s, k, shift, block, device):
        return self.copy(self.sem("x", s, k, shift - 1), block, self.p.wa * (self.rows - self.x_rows), self.x_rows, device)

    def d_y(self, kind, s, k, shift, block, size, sending):
        side = self.p.wa if sending else 1 - self.p.wa
        return self.copy(self.sem(kind, s, k, shift), block, side * size, self.rows - size, self.p.partner())

    def d_c(self, kind, s, k, shift, block):
        return self.copy(self.sem(kind, s, k, shift), block, 0, self.rows, self.p.sibling())

    def ok_forward(self, s, k):
        p = self.p
        return p.inside(p.z - s * k) & p.inside(p.z + s) & (k >= 0) & (k + 1 < p.line)

    def step_z(self, k):
        p = self.p
        me = (p.ctx, p.wa)
        for s in (1, -1):
            block = p.index(p.z - s * k, p.x, p.core)

            @pl.when(self.exists(s, k) & (k > 0))
            def _():
                self.d_z(s, k, block, me).wait_recv()

            @pl.when(self.ok_forward(s, k))
            def _():
                self.d_z(s, k + 1, block, p.at(p.z + s, p.x, p.core)).start()

            @pl.when(self.exists(s, k))
            def _():
                for shift in range(1, p.across):
                    self.d_x(s, k, shift, block, p.at(p.z, p.column(shift), p.core)).start()
                if s > 0:
                    @pl.when(k == 0)
                    def _():
                        self.d_c("c", s, k, 0, block).start()

                if self.z_rows < self.rows:
                    @pl.when(k > 0)
                    def _():
                        self.d_y("y", s, k, 0, block, self.z_rows, True).start()

    def step_y(self, k):
        p = self.p
        for s in (1, -1):
            @pl.when(self.exists(s, k) & (k > 0))
            def _():
                block = p.index(p.z - s * k, p.x, p.core)
                if self.z_rows < self.rows:
                    self.d_y("y", s, k, 0, block, self.z_rows, False).wait_recv()
                self.d_c("c", s, k, 0, block).start()

    def step_x(self, k):
        p = self.p
        for s in (1, -1):
            @pl.when(self.exists(s, k))
            def _():
                for shift in range(1, p.across):
                    block = p.index(p.z - s * k, p.column(p.across - shift), p.core)
                    self.d_x(s, k, shift, block, (p.ctx, p.wa)).wait_recv()
                    if self.x_rows < self.rows:
                        self.d_y("yx", s, k, shift - 1, block, self.x_rows, True).start()

    def step_yx(self, k):
        p = self.p
        for s in (1, -1):
            @pl.when(self.exists(s, k))
            def _():
                for shift in range(1, p.across):
                    block = p.index(p.z - s * k, p.column(p.across - shift), p.core)
                    if self.x_rows < self.rows:
                        self.d_y("yx", s, k, shift - 1, block, self.x_rows, False).wait_recv()
                    self.d_c("cx", s, k, shift - 1, block).start()

    def step_c(self, k):
        p = self.p
        for s in (1, -1):
            @pl.when(self.exists(s, k))
            def _():
                self.d_c("c", s, k, 0, p.index(p.z - s * k, p.x, 1 - p.core)).wait_recv()
                for shift in range(1, p.across):
                    block = p.index(p.z - s * k, p.column(p.across - shift), 1 - p.core)
                    self.d_c("cx", s, k, shift - 1, block).wait_recv()

    def finish(self):
        p = self.p

        @pl.loop(0, p.line)
        def _(k):
            for s in (1, -1):
                block = p.index(p.z - s * k, p.x, p.core)

                @pl.when(self.ok_forward(s, k))
                def _():
                    self.d_z(s, k + 1, block, p.at(p.z + s, p.x, p.core)).wait_send()

                @pl.when(self.exists(s, k))
                def _():
                    self.d_c("c", s, k, 0, block).wait_send()
                    if self.z_rows < self.rows:
                        @pl.when(k > 0)
                        def _():
                            self.d_y("y", s, k, 0, block, self.z_rows, True).wait_send()
                    for shift in range(1, p.across):
                        self.d_x(s, k, shift, block, p.at(p.z, p.column(shift), p.core)).wait_send()
                        other = p.index(p.z - s * k, p.column(p.across - shift), p.core)
                        if self.x_rows < self.rows:
                            self.d_y("yx", s, k, shift - 1, other, self.x_rows, True).wait_send()
                        self.d_c("cx", s, k, shift - 1, other).wait_send()


class Pieces:
    def __init__(self, place, out, sems, cut):
        n = Gather.sem_count(place.n_ctx)
        self.p = place
        self.parts = []
        first = 0
        for number, (rows, z_rows, x_rows) in enumerate(cut):
            self.parts.append(Gather(place, out, sems, number * n, first, rows, z_rows, x_rows))
            first += rows

    def each(self, name, k):
        for part in self.parts:
            getattr(part, name)(k)

    def step(self, t):
        self.each("step_z", t)
        for part in self.parts:
            part.step_x(t - 1)
            part.step_y(t - 1)
        self.each("step_yx", t - 2)
        self.each("step_c", t - 3)

    def step_count(self):
        return self.p.line + 3

    def finish(self):
        for part in self.parts:
            part.finish()


def gather_sems(n_ctx, cut):
    return pltpu.SemaphoreType.DMA((2, len(cut) * Gather.sem_count(n_ctx)))


NORM_EPS = 1e-06
BF = jnp.bfloat16
F32 = jnp.float32


def dot32(a, b):
    return jnp.dot(a, b, preferred_element_type=F32)


def dot_tn(a, b):
    return lax.dot_general(a, b, (((0,), (0,)), ((), ())), preferred_element_type=F32)


def dot_nt(a, b):
    return lax.dot_general(a, b, (((1,), (1,)), ((), ())), preferred_element_type=F32)


def row_mean(v):
    return jnp.mean(v, axis=-1, keepdims=True)


def inv_rms(v):
    return lax.rsqrt(row_mean(v * v) + NORM_EPS)


def rms_back(v, inv, grad):
    n = v * inv
    return (grad - n * row_mean(n * grad)) * inv


def pair_mean(v):
    row = lax.broadcasted_iota(jnp.int32, (128, 128), 0)
    col = lax.broadcasted_iota(jnp.int32, (128, 128), 1)
    ones = jnp.where((row < HD) == (col < HD), 1.0 / HD, 0.0).astype(BF)
    high = v.astype(BF)
    lowp = (v - high.astype(F32)).astype(BF)
    return dot32(high, ones) + dot32(lowp, ones)


def head_rms(v):
    return lax.rsqrt(pair_mean(v * v) + NORM_EPS)


def position_of(shard, index, block_len, n_ctx):
    late = index >= block_len
    block = jnp.where(late, 2 * n_ctx - 1 - shard, shard)
    return block * block_len + jnp.where(late, index - block_len, index)


def stack_heads(v):
    first = lax.broadcasted_iota(jnp.int32, v.shape, 1) < HD
    zero = jnp.zeros_like(v)
    return jnp.concatenate([jnp.where(first, v, zero), jnp.where(first, zero, v)], axis=0)


def join_heads(v):
    rows = v.shape[0] // 2
    first = lax.broadcasted_iota(jnp.int32, (rows, 128), 1) < HD
    return jnp.where(first, v[:rows], v[rows:])


def load_rows(src, dst, sem):
    return pltpu.make_async_copy(src, dst, sem)


LOG2E = 1.4426950408889634
EXCHANGE = 256
TOGETHER = 4


def fwd_kernel(n_ctx, cut, x_ref, wq_ref, wk_ref, wv_ref, qs_ref, wo_ref, step_ref,
               xall_ref, qall_ref, kall_ref, vall_ref, qraw_ref, kraw_ref, o_ref, lse_ref, h1_ref, ha_ref,
               gsems, lsems, wsems, esems, xbuf, qbuf, kbuf, vbuf, q2, acc, lpart, sbuf, rbuf):
    place = Place(n_ctx)
    rows, width = x_ref.shape
    block_len = rows // 2
    channels = wq_ref.shape[1]
    tiles = channels // 128
    group = 2 * place.across
    plane = group * rows
    gather = Pieces(place, xall_ref, gsems, cut)
    own = load_rows(x_ref, xall_ref.at[place.ctx], lsems.at[0])
    own.start()
    place.barrier()
    own.wait()
    gather.each("step_z", 0)

    xv = x_ref[...]
    kraw_ref[...] = dot32(xv, wk_ref[...])
    qraw_ref[...] = dot32(xv, wq_ref[...])
    for t in range(tiles):
        cols = slice(t * 128, (t + 1) * 128)
        raw = qraw_ref[:, cols]
        q2[t] = stack_heads((raw * head_rms(raw) * qs_ref[:, cols]).astype(BF))
    acc[...] = jnp.zeros_like(acc)
    lpart[...] = jnp.zeros_like(lpart)

    def plane_of(s, k):
        return place.z - s * k

    def hbm(ref, zp):
        return ref.at[pl.ds(zp * group, group)]

    def x_load(s, k):
        side = 0 if s > 0 else 1
        return load_rows(hbm(xall_ref, plane_of(s, k)), xbuf.at[side], lsems.at[1 + side])

    def stores(s, k):
        side = 0 if s > 0 else 1
        zp = plane_of(s, k)
        return [load_rows(buf.at[side], hbm(ref, zp), wsems.at[side, i])
                for i, (buf, ref) in enumerate(((qbuf, qall_ref), (kbuf, kall_ref), (vbuf, vall_ref)))]

    def project(s, k):
        side = 0 if s > 0 else 1
        x_load(s, k).wait()

        @pl.loop(0, group // TOGETHER)
        def _(r):
            some = pl.ds(r * TOGETHER, TOGETHER)
            xr = xbuf[side, some].reshape(TOGETHER * rows, width)
            for w_ref, buf in ((wq_ref, qbuf), (wk_ref, kbuf)):
                raw = dot32(xr, w_ref[...])
                for t in range(tiles):
                    cols = slice(t * 128, (t + 1) * 128)
                    part = raw[:, cols]
                    normed = (part * head_rms(part) * qs_ref[:, cols]).astype(BF)
                    buf[side, some, :, cols] = normed.reshape(TOGETHER, rows, 128)
            vbuf[side, some] = dot32(xr, wv_ref[...]).astype(BF).reshape(TOGETHER, rows, channels)

        for copy in stores(s, k):
            copy.start()

    def attend(s, k):
        side = 0 if s > 0 else 1
        zp = plane_of(s, k)
        qi = lax.broadcasted_iota(jnp.int32, (2 * rows, 1), 0)
        qi = jnp.where(qi >= rows, qi - rows, qi)
        qpos = position_of(place.ctx, qi, block_len, n_ctx)
        ki = lax.broadcasted_iota(jnp.int32, (1, plane), 1)
        kpos = position_of(zp * group + lax.div(ki, rows), lax.rem(ki, rows), block_len, n_ctx)
        allowed = kpos <= qpos

        @pl.loop(0, tiles)
        def _(t):
            cols = pl.ds(pl.multiple_of(t * 128, 128), 128)
            kt = kbuf[side, :, :, cols].reshape(plane, 128)
            vt = vbuf[side, :, :, cols].reshape(plane, 128)
            score = dot_nt(q2[t], kt)
            e = jnp.where(allowed, jnp.exp2(score * (LOG2E / math.sqrt(HD))), 0.0)
            total = e[:, :128]
            for j in range(1, plane // 128):
                total = total + e[:, j * 128:(j + 1) * 128]
            lpart[t] += total
            acc[t] += dot32(e.astype(BF), vt)

        for copy in stores(s, k):
            copy.wait()

    def both(k, fn):
        for s in (1, -1):
            pl.when(gather.parts[0].exists(s, k))(functools.partial(fn, s, k))

    @pl.loop(1, place.line + 2)
    def _(t):
        gather.each("step_z", t)
        gather.each("step_x", t - 1)
        gather.each("step_y", t - 1)
        both(t - 2, attend)
        gather.each("step_yx", t - 1)
        gather.each("step_c", t - 1)
        both(t - 1, lambda s, k: x_load(s, k).start())
        both(t - 1, project)

    for t in range(tiles):
        mass = jnp.sum(lpart[t], axis=1, keepdims=True)
        o_ref[:, t * 128:(t + 1) * 128] = join_heads(acc[t] / mass)
        lse_ref[t] = jnp.broadcast_to(jnp.log(mass) * LOG2E, (2 * rows, 128))

    exchange(place, lambda cols: dot32(o_ref[...].astype(BF), wo_ref[:, cols]), ha_ref, sbuf, rbuf, esems)
    ha = ha_ref[...]
    xf = x_ref[...].astype(F32)
    w = xf + step_ref[...] * (ha * inv_rms(ha) - xf)
    h1_ref[...] = w * inv_rms(w)
    gather.finish()


def exchange(place, term, sum_ref, sbuf, rbuf, esems, between=None):
    width = sum_ref.shape[1]

    def copy(n):
        return pltpu.make_async_remote_copy(
            src_ref=sbuf.at[n], dst_ref=rbuf.at[n], send_sem=esems.at[0, n], recv_sem=esems.at[1, n],
            device_id=place.partner(), device_id_type=MESH)

    count = width // EXCHANGE
    for n in range(count):
        sbuf[n] = term(slice(n * EXCHANGE, (n + 1) * EXCHANGE)).astype(BF)
        copy(n).start()
    if between is not None:
        between()
    for n in range(count):
        copy(n).wait()
        sum_ref[:, n * EXCHANGE:(n + 1) * EXCHANGE] = sbuf[n].astype(F32) + rbuf[n].astype(F32)


def vmem_spec():
    return pl.BlockSpec(memory_space=pltpu.VMEM)


def any_spec():
    return pl.BlockSpec(memory_space=pl.ANY)


def forward_attention(x, w_query, w_key, w_value, qk_scale, w_out, step, n_ctx, collective_id, cut):
    rows, width = x.shape
    channels = w_query.shape[1]
    tiles = channels // 128
    line, across = layout_of(n_ctx)
    group = 2 * across
    count = width // EXCHANGE
    shape = jax.ShapeDtypeStruct
    return pl.pallas_call(
        functools.partial(fwd_kernel, n_ctx, cut),
        out_shape=(shape((n_ctx, rows, width), BF),) + (shape((n_ctx, rows, channels), BF),) * 3
        + (shape((rows, channels), F32),) * 3 + (shape((tiles, 2 * rows, 128), F32),) + (shape((rows, width), F32),) * 2,
        in_specs=[vmem_spec()] * 7,
        out_specs=(any_spec(),) * 4 + (vmem_spec(),) * 6,
        scratch_shapes=[
            gather_sems(n_ctx, cut), pltpu.SemaphoreType.DMA((3,)), pltpu.SemaphoreType.DMA((2, 3)),
            pltpu.SemaphoreType.DMA((2, count)),
            pltpu.VMEM((2, group, rows, width), BF),
            pltpu.VMEM((2, group, rows, channels), BF), pltpu.VMEM((2, group, rows, channels), BF),
            pltpu.VMEM((2, group, rows, channels), BF),
            pltpu.VMEM((tiles, 2 * rows, 128), BF), pltpu.VMEM((tiles, 2 * rows, 128), F32),
            pltpu.VMEM((tiles, 2 * rows, 128), F32),
            pltpu.VMEM((count, rows, EXCHANGE), BF), pltpu.VMEM((count, rows, EXCHANGE), BF)],
        compiler_params=pltpu.CompilerParams(collective_id=collective_id, has_side_effects=True,
                                             vmem_limit_bytes=24 << 20),
        cost_estimate=pl.CostEstimate(flops=12 * 10 ** 9, bytes_accessed=40 * 10 ** 6, transcendentals=3 * 10 ** 6),
        name="forward_attention",
    )(x, w_query, w_key, w_value, qk_scale, w_out, step)


HIDDEN_CUT = 256


def mid_kernel(n_ctx, cut, h1_ref, ha_ref, x_ref, cot_ref, fs_ref, as_ref, us_ref, gs_ref, wu_ref, wg_ref, wd_ref,
               hball_ref, dmball_ref, out_ref, dab_ref, dxr_ref, gfs_ref, gas_ref,
               hsems, msems, lsems, wsems, e1sems, e2sems, wu, wg, wd, hbv, dmv, u_buf, g_buf, low_a, low_b, total,
               s1, r1, s2, r2):
    place = Place(n_ctx)
    rows, width = h1_ref.shape
    hidden = us_ref.shape[1]
    cuts = hidden // HIDDEN_CUT
    h_gather = Pieces(place, hball_ref, hsems, cut)
    m_gather = Pieces(place, dmball_ref, msems, cut)

    def part(n):
        return slice(n * HIDDEN_CUT, (n + 1) * HIDDEN_CUT)

    loads = [[load_rows(wu_ref.at[:, part(n)], wu.at[:, part(n)], wsems.at[0, n]),
              load_rows(wg_ref.at[:, part(n)], wg.at[:, part(n)], wsems.at[1, n])] for n in range(cuts)]
    down = [load_rows(wd_ref.at[part(n)], wd.at[part(n)], wsems.at[2, n]) for n in range(cuts)]
    for pair in loads:
        for copy in pair:
            copy.start()
    for copy in down:
        copy.start()
    hbv[...] = h1_ref[...].astype(BF)
    own = load_rows(hbv, hball_ref.at[place.ctx], lsems.at[0])
    own.start()
    place.barrier()
    own.wait()
    h_gather.each("step_z", 0)

    hb = hbv[...]
    for n in range(cuts):
        for copy in loads[n]:
            copy.wait()
        u = dot32(hb, wu[:, part(n)])
        g = dot32(hb, wg[:, part(n)])
        u_buf[:, part(n)] = u
        g_buf[:, part(n)] = g
        c = g * gs_ref[:, part(n)]
        low_a[:, part(n)] = (u * us_ref[:, part(n)] * (c * lax.logistic(c))).astype(BF)
    for copy in down:
        copy.wait()

    def serve_first():
        h_gather.each("step_z", 1)
        h_gather.each("step_x", 0)

    exchange(place, lambda cols: dot32(low_a[...], wd[:, cols]), total, s1, r1, e1sems, serve_first)
    h1 = h1_ref[...]
    fs = fs_ref[...]
    hm = total[...]
    m_inv = inv_rms(hm)
    step = hm * m_inv - h1
    z = h1 + fs * step
    z_inv = inv_rms(z)
    out_ref[...] = (z * z_inv).astype(BF)
    dz = rms_back(z, z_inv, cot_ref[...].astype(F32))
    gfs_ref[...] = jnp.sum(dz * step, axis=0, keepdims=True)
    dxr_ref[...] = (1.0 - fs) * dz
    dmv[...] = rms_back(hm, m_inv, fs * dz).astype(BF)
    own = load_rows(dmv, dmball_ref.at[place.ctx], lsems.at[1])
    own.start()
    h_gather.each("step_z", 2)
    own.wait()
    m_gather.each("step_z", 0)
    h_gather.each("step_yx", 0)
    h_gather.each("step_x", 1)
    h_gather.each("step_y", 1)

    dm = dmv[...]
    for n in range(cuts):
        dgated = dot_nt(dm, wd[part(n), :])
        u, g = u_buf[:, part(n)], g_buf[:, part(n)]
        us, gs = us_ref[:, part(n)], gs_ref[:, part(n)]
        c = g * gs
        s = lax.logistic(c)
        low_a[:, part(n)] = (dgated * (c * s) * us).astype(BF)
        low_b[:, part(n)] = (dgated * (u * us) * (s * (1.0 + c * (1.0 - s))) * gs).astype(BF)
        if n == cuts // 2:
            h_gather.each("step_z", 3)

    def serve_second():
        h_gather.each("step_yx", 1)
        h_gather.each("step_x", 2)
        h_gather.each("step_y", 2)
        m_gather.each("step_z", 1)
        m_gather.each("step_x", 0)

    exchange(place, lambda cols: dot_nt(low_a[...], wu[cols, :]) + dot_nt(low_b[...], wg[cols, :]), total, s2, r2,
             e2sems, serve_second)
    m_gather.each("step_z", 2)
    h_gather.each("step_x", 3)
    h_gather.each("step_y", 3)
    dh1 = dxr_ref[...] + total[...]
    xf = x_ref[...].astype(F32)
    step_size = as_ref[...]
    ha = ha_ref[...]
    a_inv = inv_rms(ha)
    step = ha * a_inv - xf
    w = xf + step_size * step
    dw = rms_back(w, inv_rms(w), dh1)
    gas_ref[...] = jnp.sum(dw * step, axis=0, keepdims=True)
    dxr_ref[...] = (1.0 - step_size) * dw
    dab_ref[...] = rms_back(ha, a_inv, step_size * dw).astype(BF)

    @pl.loop(4, place.line)
    def _(k):
        h_gather.each("step_z", k)
        h_gather.each("step_x", k)
        h_gather.each("step_y", k)

    @pl.loop(1, place.line + 1)
    def _(t):
        @pl.when(t > 1)
        def _():
            h_gather.each("step_yx", t)
        h_gather.each("step_c", t - 1)

        @pl.when(t > 1)
        def _():
            m_gather.each("step_x", t - 1)

            @pl.when(t + 1 > 2)
            def _():
                m_gather.each("step_z", t + 1)
        m_gather.each("step_y", t - 1)
        m_gather.each("step_yx", t - 1)
        m_gather.each("step_c", t - 1)

    h_gather.finish()
    m_gather.finish()


def feed_forward(hidden_one, branch_attn, x, cotangent, ff_step, attn_step, up_scale, gate_scale, w_up, w_gate, w_down,
                 n_ctx, collective_id, cut):
    rows, width = x.shape
    hidden = w_up.shape[1]
    cuts = hidden // HIDDEN_CUT
    count = width // EXCHANGE
    shape = jax.ShapeDtypeStruct
    dma = pltpu.SemaphoreType.DMA
    V = pltpu.VMEM
    box = V((count, rows, EXCHANGE), BF)
    return pl.pallas_call(
        functools.partial(mid_kernel, n_ctx, cut),
        out_shape=(shape((n_ctx, rows, width), BF), shape((n_ctx, rows, width), BF), shape((rows, width), BF),
                   shape((rows, width), BF), shape((rows, width), F32), shape((1, width), F32), shape((1, width), F32)),
        in_specs=[vmem_spec()] * 8 + [any_spec()] * 3,
        out_specs=(any_spec(),) * 2 + (vmem_spec(),) * 5,
        scratch_shapes=[
            gather_sems(n_ctx, cut), gather_sems(n_ctx, cut), dma((2,)), dma((3, cuts)), dma((2, count)), dma((2, count)),
            V((width, hidden), BF), V((width, hidden), BF), V((hidden, width), BF), V((rows, width), BF),
            V((rows, width), BF), V((rows, hidden), F32), V((rows, hidden), F32), V((rows, hidden), BF),
            V((rows, hidden), BF), V((rows, width), F32), box, box, box, box],
        compiler_params=pltpu.CompilerParams(collective_id=collective_id, has_side_effects=True,
                                             vmem_limit_bytes=30 << 20),
        cost_estimate=pl.CostEstimate(flops=5 * 10 ** 9, bytes_accessed=30 * 10 ** 6, transcendentals=10 ** 6),
        name="feed_forward",
    )(hidden_one, branch_attn, x, cotangent, ff_step, attn_step, up_scale, gate_scale, w_up, w_gate, w_down)


BLOCK = 4
STATS = 128


def split_parts(v, count):
    parts = []
    rest = v
    for _ in range(count):
        part = rest.astype(BF)
        parts.append(part)
        rest = rest - part.astype(F32)
    return parts


def transposed(src, dst, dtype):
    for n in range(src.shape[1] // 128):
        dst[n * 128:(n + 1) * 128, :] = src[:, n * 128:(n + 1) * 128].T.astype(dtype)


class UnitScatter:
    def __init__(self, place, source, target, send_sems, recv_sems, senders, per_sender, per_owner):
        self.p, self.source, self.target = place, source, target
        self.send_sems, self.recv_sems = send_sems, recv_sems
        self.senders, self.per_sender, self.per_owner = senders, per_sender, per_owner

    def rows(self, unit):
        return pl.ds(pl.multiple_of(unit * 8, 8), 8)

    def copy(self, unit, slot, owner):
        return pltpu.make_async_remote_copy(
            src_ref=self.source.at[self.rows(unit)], dst_ref=self.target.at[self.rows(slot)],
            send_sem=self.send_sems.at[unit], recv_sem=self.recv_sems.at[slot],
            device_id=(owner, self.p.wa), device_id_type=MESH)

    def local(self, unit, slot):
        return pltpu.make_async_copy(self.source.at[self.rows(unit)], self.target.at[self.rows(slot)],
                                     self.recv_sems.at[slot])

    def outgoing(self, remote, near):
        p = self.p

        @pl.when(p.ctx < self.senders)
        def _():
            @pl.loop(0, self.per_sender)
            def _(unit):
                place_of = p.ctx * self.per_sender + unit
                owner, slot = lax.div(place_of, self.per_owner), lax.rem(place_of, self.per_owner)

                @pl.when(owner != p.ctx)
                def _():
                    remote(self.copy(unit, slot, owner))

                if near is not None:
                    @pl.when(owner == p.ctx)
                    def _():
                        near(self.local(unit, slot))

    def start(self):
        self.outgoing(lambda c: c.start(), lambda c: c.start())

    def wait(self):
        p = self.p

        @pl.loop(0, self.per_owner)
        def _(slot):
            place_of = p.ctx * self.per_owner + slot
            sender, unit = lax.div(place_of, self.per_sender), lax.rem(place_of, self.per_sender)

            @pl.when(sender != p.ctx)
            def _():
                self.copy(unit, slot, p.ctx).wait_recv()

            @pl.when(sender == p.ctx)
            def _():
                self.local(unit, slot).wait()

    def sent(self):
        self.outgoing(lambda c: c.wait_send(), None)


class Scatter:
    def __init__(self, place, source, target, sems, count, senders):
        self.p, self.source, self.target, self.sems = place, source, target, sems
        self.count, self.senders = count, senders

    def copy(self, dest, sender):
        return pltpu.make_async_remote_copy(
            src_ref=self.source(dest), dst_ref=self.target(sender),
            send_sem=self.sems.at[0, dest], recv_sem=self.sems.at[1, sender],
            device_id=(dest, self.p.wa), device_id_type=MESH)

    def each(self, fn):
        p = self.p

        @pl.loop(1, p.n_ctx)
        def _(shift):
            fn(lax.rem(p.ctx + shift, p.n_ctx))

    def start(self):
        p = self.p

        @pl.when(p.ctx < self.senders)
        def _():
            def go(dest):
                @pl.when(dest < self.count)
                def _():
                    self.copy(dest, p.ctx).start()
            self.each(go)

            @pl.when(p.ctx < self.count)
            def _():
                self.local().start()

    def local(self):
        return pltpu.make_async_copy(self.source(self.p.ctx), self.target(self.p.ctx), self.sems.at[1, self.p.ctx])

    def wait(self):
        p = self.p

        @pl.when(p.ctx < self.count)
        def _():
            def got(sender):
                @pl.when(sender < self.senders)
                def _():
                    self.copy(p.ctx, sender).wait_recv()
            self.each(got)

            @pl.when(p.ctx < self.senders)
            def _():
                self.local().wait()

    def sent(self):
        p = self.p

        @pl.when(p.ctx < self.senders)
        def _():
            def left(dest):
                @pl.when(dest < self.count)
                def _():
                    self.copy(dest, p.ctx).wait_send()
            self.each(left)


def bwd_kernel(n_ctx, cut, aligned, out_aligned, *refs):
    (dab_ref, gfs_ref, gas_ref, qraw_ref, kraw_ref, lse_ref, o_ref, dxr_ref, qs_ref, us_ref, gs_ref,
     wo_ref, wq_ref, wk_ref, wv_ref, xall_ref, qall_ref, kall_ref, vall_ref, hball_ref, dmball_ref, wu_ref, wg_ref, wd_ref,
     dx_ref, got_q, gout_ref, got_u, gdown_ref, got_s, gus_ref, ggs_ref,
     daball_ref, statall_ref, turned, turned_qkv, gocc,
     asems, ssts, lsems, csems, esems, usems, tsems, osems, rsems, vsems, ssems, xsems, nsems,
     hbbuf, dmbuf, dabbuf, stbuf, qbuf, kvbuf, dobuf, rowstats, stats, delta, q2, k2, v2, do2, dq2, dk2, dv2,
     wuw, wgw, wdw, gu, gg, gd, colu, colg, comb, small, small_row, dqkv, got_t, got_o, obs, accq, sbuf, rbuf) = refs
    place = Place(n_ctx)
    rows, width = dxr_ref.shape
    block_len = rows // 2
    channels = qraw_ref.shape[1]
    tiles = channels // 128
    hidden = us_ref.shape[1]
    mine = hidden // n_ctx
    group = 2 * place.across
    subs = group // BLOCK
    many = BLOCK * rows
    window = gu.shape[0]
    scale = 1.0 / math.sqrt(HD)
    a_gather = Pieces(place, daball_ref, asems, cut)
    s_gather = Pieces(place, statall_ref, ssts, ((rows, rows, rows),))
    start = jnp.minimum(lax.div(place.ctx * mine, 128) * 128, hidden - window)
    start = pl.multiple_of(start, 128)
    offset = pl.multiple_of(place.ctx * mine - start, 8)
    win = pl.ds(start, window)
    own = [load_rows(dab_ref, daball_ref.at[place.ctx], lsems.at[0]),
           load_rows(wu_ref.at[:, win], wuw, lsems.at[2]), load_rows(wg_ref.at[:, win], wgw, lsems.at[3]),
           load_rows(wd_ref.at[win, :], wdw, lsems.at[4])]
    for copy in own:
        copy.start()
    for t in range(tiles):
        obs[t] = o_ref[:, t * 128:(t + 1) * 128].astype(BF)
    place.barrier_all()
    own[0].wait()
    a_gather.each("step_z", 0)
    d_out = dot_nt(dab_ref[...], wo_ref[...]).astype(BF)
    lane = lax.broadcasted_iota(jnp.int32, (rows, 128), 1)
    packed = jnp.zeros((rows, 128), F32)
    for t in range(tiles):
        cols = slice(t * 128, (t + 1) * 128)
        do2[t] = stack_heads(d_out[:, cols])
        both_heads = stack_heads(d_out[:, cols].astype(F32) * o_ref[:, cols])
        delta[t] = jnp.broadcast_to(jnp.sum(both_heads, axis=1, keepdims=True), (2 * rows, 128))
        for h in range(2):
            part_rows = slice(h * rows, (h + 1) * rows)
            values = split_parts(lse_ref[t, part_rows], 3) + split_parts(delta[t, part_rows], 2)
            for i, value in enumerate(values):
                packed = jnp.where(lane == i * 2 * tiles + 2 * t + h, value.astype(F32), packed)
    stats[...] = packed.astype(BF)
    own_stats = load_rows(stats, statall_ref.at[place.ctx], lsems.at[0])
    own_stats.start()
    own_stats.wait()
    s_gather.each("step_z", 0)
    o_scatter = Scatter(place, lambda dest: obs.at[dest], lambda sender: got_o.at[sender], osems, tiles, n_ctx)
    o_scatter.start()

    for t in range(tiles):
        cols = slice(t * 128, (t + 1) * 128)
        for raw_ref, dest in ((qraw_ref, q2), (kraw_ref, k2)):
            raw = raw_ref[:, cols]
            dest[t] = stack_heads((raw * head_rms(raw) * qs_ref[:, cols]).astype(BF))
    dq2[...] = jnp.zeros_like(dq2)
    dk2[...] = jnp.zeros_like(dk2)
    dv2[...] = jnp.zeros_like(dv2)
    gu[...] = jnp.zeros_like(gu)
    gg[...] = jnp.zeros_like(gg)
    gd[...] = jnp.zeros_like(gd)
    colu[...] = jnp.zeros_like(colu)
    colg[...] = jnp.zeros_like(colg)
    gocc[...] = jnp.zeros_like(gocc)

    def row_positions(shape, axis, first):
        i = lax.broadcasted_iota(jnp.int32, shape, axis)
        return position_of(first + lax.div(i, rows), lax.rem(i, rows), block_len, n_ctx)

    def own_positions(shape, axis):
        i = lax.broadcasted_iota(jnp.int32, shape, axis)
        return position_of(place.ctx, lax.rem(i, rows), block_len, n_ctx)

    total_blocks = n_ctx // BLOCK

    def kv_loads(b):
        side = lax.rem(b, 2)
        return [load_rows(ref.at[pl.ds(b * BLOCK, BLOCK)], kvbuf.at[side, i], csems.at[side, i])
                for i, ref in enumerate((kall_ref, vall_ref))]

    def wide(v):
        return jnp.concatenate([v] * (many // 128), axis=1)

    for copy in kv_loads(0):
        copy.start()

    @pl.loop(0, total_blocks)
    def _(b):
        side = lax.rem(b, 2)

        @pl.when(b + 1 < total_blocks)
        def _():
            for copy in kv_loads(b + 1):
                copy.start()

        for copy in kv_loads(b):
            copy.wait()
        allowed = row_positions((1, many), 1, b * BLOCK) <= own_positions((2 * rows, 1), 0)

        @pl.loop(0, tiles)
        def _(t):
            cols = pl.ds(pl.multiple_of(t * 128, 128), 128)
            kt = kvbuf[side, 0, :, :, cols].reshape(many, 128)
            vt = kvbuf[side, 1, :, :, cols].reshape(many, 128)
            score = dot_nt(q2[t], kt)
            p = jnp.where(allowed, jnp.exp2(score * (LOG2E * scale) - wide(lse_ref[t])), 0.0)
            dp = dot_nt(do2[t], vt)
            ds = (p * (dp - wide(delta[t])) * scale).astype(BF)
            dq2[t] += dot32(ds, kt)

    own_v = load_rows(vall_ref.at[place.ctx], dobuf.at[0], lsems.at[0])
    own_v.start()
    own_v.wait()
    for t in range(tiles):
        v2[t] = stack_heads(dobuf[0, :, t * 128:(t + 1) * 128])
    for copy in own[1:]:
        copy.wait()
    o_scatter.wait()

    def block_of(s, k, sub):
        return ((place.z - s * k) * subs + sub) * BLOCK

    def a_loads(first):
        return [load_rows(daball_ref.at[pl.ds(first, BLOCK)], dabbuf, rsems.at[0]),
                load_rows(qall_ref.at[pl.ds(first, BLOCK)], qbuf, rsems.at[1]),
                load_rows(statall_ref.at[pl.ds(first, BLOCK)], stbuf, rsems.at[4])]

    def m_loads(b):
        side = lax.rem(b, 2)
        return [load_rows(dmball_ref.at[pl.ds(b * BLOCK, BLOCK)], dmbuf.at[side], xsems.at[side, 0]),
                load_rows(hball_ref.at[pl.ds(b * BLOCK, BLOCK)], hbbuf.at[side], xsems.at[side, 1])]

    def keys_part(first):
        for copy in a_loads(first):
            copy.wait()
        dab = dabbuf[...].reshape(many, width)
        dobuf[...] = dot_nt(dab, wo_ref[...]).astype(BF).reshape(BLOCK, rows, channels)
        for j in range(BLOCK):
            rowstats[:, j * rows:(j + 1) * rows] = stbuf[j].astype(F32).T

        @pl.when(place.ctx < tiles)
        def _():
            gocc[...] += dot_tn(got_o[pl.ds(first, BLOCK)].reshape(many, 128), dab)

        allowed = own_positions((2 * rows, 1), 0) <= row_positions((1, many), 1, first)
        heads = 2 * tiles

        @pl.loop(0, tiles)
        def _(t):
            cols = pl.ds(pl.multiple_of(t * 128, 128), 128)
            qt = qbuf[:, :, cols].reshape(many, 128)
            dot_ = dobuf[:, :, cols].reshape(many, 128)

            def both_rows(parts, at):
                def one(h):
                    row = rowstats[pl.ds(at * heads + h, 1), :]
                    for i in range(1, parts):
                        row = row + rowstats[pl.ds((at + i) * heads + h, 1), :]
                    return jnp.broadcast_to(row, (rows, many))
                return jnp.concatenate([one(2 * t), one(2 * t + 1)], axis=0)

            score = dot_nt(k2[t], qt)
            p = jnp.where(allowed, jnp.exp2(score * (LOG2E * scale) - both_rows(3, 0)), 0.0)
            dp = dot_nt(v2[t], dot_)
            ds = (p * (dp - both_rows(2, 3)) * scale).astype(BF)
            dv2[t] += dot32(p.astype(BF), dot_)
            dk2[t] += dot32(ds, qt)

    def hidden_part(side):
        hb = hbbuf[side].reshape(many, width)
        dm = dmbuf[side].reshape(many, width)
        us, gs = us_ref[:, win], gs_ref[:, win]
        u = dot32(hb, wuw[...])
        g = dot32(hb, wgw[...])
        dgated = dot_nt(dm, wdw[...])
        a, c = u * us, g * gs
        s = lax.logistic(c)
        cs = c * s
        r = s * (1.0 + c * (1.0 - s))
        da = dgated * cs
        dc = dgated * a * r
        colu[...] += jnp.sum((da * u).reshape(many // 8, 8, window), axis=0)
        colg[...] += jnp.sum((dc * g).reshape(many // 8, 8, window), axis=0)
        gu[...] += dot_tn((da * us).astype(BF), hb)
        gg[...] += dot_tn((dc * gs).astype(BF), hb)
        gd[...] += dot_tn((a * cs).astype(BF), dm)

    def hidden_all():
        for copy in m_loads(0):
            copy.start()

        @pl.loop(0, total_blocks)
        def _(b):
            @pl.when(b + 1 < total_blocks)
            def _():
                for copy in m_loads(b + 1):
                    copy.start()

            for copy in m_loads(b):
                copy.wait()
            hidden_part(lax.rem(b, 2))

            for gather in (a_gather, s_gather):
                gather.each("step_z", b + 1)
                gather.each("step_x", b)
                gather.each("step_y", b)
                gather.each("step_yx", b - 1)
                gather.each("step_c", b - 2)

    def both(k, fn):
        for s in (1, -1):
            @pl.when(a_gather.parts[0].exists(s, k))
            def _():
                @pl.loop(0, subs)
                def _(sub):
                    fn(block_of(s, k, sub))

    def begin(loads):
        def go(first):
            for copy in loads(first):
                copy.start()
        return go

    def keys_full(first):
        begin(a_loads)(first)
        keys_part(first)

    hidden_all()

    gdown_ref[...] = gd[pl.ds(offset, mine), :]
    comb[0:mine] = gu[pl.ds(offset, mine), :]
    comb[mine:2 * mine] = gg[pl.ds(offset, mine), :]
    comb[2 * mine:] = jnp.zeros((comb.shape[0] - 2 * mine, width), F32)
    transposed(comb, turned, BF)
    part = width // n_ctx

    def row_block(ref, size):
        return lambda dest: ref.at[pl.ds(pl.multiple_of(dest * size, 8), size)]

    if aligned:
        u_scatter = Scatter(place, row_block(turned, part), lambda sender: got_u.at[sender], usems, n_ctx, n_ctx)
        u_scatter.start()
    shift = lax.rem(window - offset, window)
    gus_ref[...] = pltpu.roll(jnp.broadcast_to(jnp.sum(colu[...], axis=0, keepdims=True), (8, window)), shift, 1)
    ggs_ref[...] = pltpu.roll(jnp.broadcast_to(jnp.sum(colg[...], axis=0, keepdims=True), (8, window)), shift, 1)

    @pl.loop(0, place.line)
    def _(k):
        for gather in (a_gather, s_gather):
            gather.each("step_yx", total_blocks - 1 + k)
            gather.each("step_c", total_blocks - 2 + k)
        both(k, keys_full)

    for gather in (a_gather, s_gather):
        gather.each("step_c", total_blocks - 2 + place.line)

    if out_aligned:
        g_scatter = UnitScatter(place, gocc, gout_ref, ssems.at[0], ssems.at[1], tiles, 16, channels // n_ctx // 8)
        g_scatter.start()

    for t in range(tiles):
        cols = slice(t * 128, (t + 1) * 128)
        scales = qs_ref[:, cols]
        grad_scale = jnp.zeros((1, 128), F32)
        for n, (raw_ref, grads) in enumerate(((qraw_ref, dq2), (kraw_ref, dk2))):
            raw = raw_ref[:, cols]
            inv = head_rms(raw)
            normed = raw * inv
            grad = join_heads(grads[t])
            grad_scale = grad_scale + jnp.sum(grad * normed, axis=0, keepdims=True)
            e = grad * scales
            dqkv[n * tiles + t] = ((e - normed * pair_mean(normed * e)) * inv).astype(BF)
        small_row[:, cols] = grad_scale
        dqkv[2 * tiles + t] = join_heads(dv2[t]).astype(BF)
    t_scatter = Scatter(place, lambda dest: dqkv.at[dest], lambda sender: got_t.at[sender], tsems, 3 * tiles, n_ctx)
    t_scatter.start()
    head_part = channels // n_ctx
    for i in range(n_ctx):
        small[i, 0:1, 0:part] = gfs_ref[:, i * part:(i + 1) * part]
        small[i, 1:2, 0:part] = gas_ref[:, i * part:(i + 1) * part]
        small[i, 2:3, 0:head_part] = small_row[:, i * head_part:(i + 1) * head_part]
    n_scatter = Scatter(place, lambda dest: small.at[dest], lambda sender: got_s.at[sender], nsems, n_ctx, n_ctx)
    n_scatter.start()

    def input_terms(cols):
        total = None
        for n, w_ref in enumerate((wq_ref, wk_ref, wv_ref)):
            grad = jnp.concatenate([dqkv[n * tiles + t] for t in range(tiles)], axis=1)
            term = dot_nt(grad, w_ref[cols, :])
            total = term if total is None else total + term
        return total

    pl.when(place.ctx < 3 * tiles)(load_rows(xall_ref.at[pl.ds(0, BLOCK)], hbbuf.at[0], xsems.at[0, 0]).start)
    exchange(place, input_terms, dx_ref, sbuf, rbuf, esems)
    dx_ref[...] += dxr_ref[...]

    t_scatter.wait()

    @pl.when(place.ctx < 3 * tiles)
    def _():
        accq[...] = jnp.zeros_like(accq)

        def x_load(b):
            side = lax.rem(b, 2)
            return load_rows(xall_ref.at[pl.ds(b * BLOCK, BLOCK)], hbbuf.at[side], xsems.at[side, 0])

        @pl.loop(0, total_blocks)
        def _(b):
            @pl.when(b + 1 < total_blocks)
            def _():
                x_load(b + 1).start()

            x_load(b).wait()
            accq[...] += dot_tn(got_t[pl.ds(b * BLOCK, BLOCK)].reshape(many, 128),
                                hbbuf[lax.rem(b, 2)].reshape(many, width))

        transposed(accq, turned_qkv, BF)

    if aligned:
        q_scatter = Scatter(place, row_block(turned_qkv, part), lambda sender: got_q.at[sender], vsems, n_ctx, 3 * tiles)
        q_scatter.start()
        u_scatter.wait()
        q_scatter.wait()
        u_scatter.sent()
        q_scatter.sent()
    if out_aligned:
        g_scatter.wait()
        g_scatter.sent()
    a_gather.finish()
    s_gather.finish()
    o_scatter.sent()
    t_scatter.sent()
    n_scatter.wait()
    n_scatter.sent()


def backward_attention(dab, grad_ff_step, grad_attn_step, q_raw, k_raw, lse, attended, dxr, qk_scale, up_scale, gate_scale,
                       w_out, w_query, w_key, w_value, x_all, q_all, k_all, v_all, hb_all, dmb_all, w_up, w_gate, w_down,
                       n_ctx, collective_id, cut):
    rows, width = dxr.shape
    channels = q_raw.shape[1]
    tiles = channels // 128
    hidden = up_scale.shape[1]
    mine = hidden // n_ctx
    part = width // n_ctx
    aligned = part % 16 == 0
    out_rows = channels // n_ctx
    out_aligned = out_rows % 8 == 0
    window = 256
    pair = -(-2 * mine // 128) * 128
    count = width // EXCHANGE
    many = BLOCK * rows
    n_blocks = n_ctx
    shape = jax.ShapeDtypeStruct
    dma = pltpu.SemaphoreType.DMA
    V = pltpu.VMEM
    stack = lambda dtype: V((tiles, 2 * rows, 128), dtype)
    outs = (
        shape((rows, width), F32),
        shape((3 * tiles, part, 128), BF), shape((out_rows, width), F32), shape((n_ctx, part, pair), BF),
        shape((mine, width), F32), shape((n_ctx, 8, 128), F32), shape((8, window), F32), shape((8, window), F32),
        shape((n_ctx, rows, width), BF), shape((n_ctx, rows, STATS), BF),
        shape((width, pair), BF), shape((width, 128), BF), shape((128, width), F32))
    return pl.pallas_call(
        functools.partial(bwd_kernel, n_ctx, cut, aligned, out_aligned),
        out_shape=outs,
        in_specs=[vmem_spec()] * 15 + [any_spec()] * 9,
        out_specs=(vmem_spec(),) * 8 + (any_spec(),) * 2 + (vmem_spec(),) * 3,
        scratch_shapes=[
            gather_sems(n_ctx, cut), gather_sems(n_ctx, ((rows, rows, rows),)), dma((5,)), dma((2, 2)), dma((2, count)),
            dma((2, n_ctx)), dma((2, n_ctx)), dma((2, n_ctx)), dma((5,)), dma((2, n_ctx)), dma((2, 16)), dma((2, 2)), dma((2, n_ctx)),
            V((2, BLOCK, rows, width), BF), V((2, BLOCK, rows, width), BF), V((BLOCK, rows, width), BF), V((BLOCK, rows, STATS), BF),
            V((BLOCK, rows, channels), BF), V((2, 2, BLOCK, rows, channels), BF), V((BLOCK, rows, channels), BF),
            V((STATS, many), F32), V((rows, STATS), BF), stack(F32), stack(BF), stack(BF), stack(BF), stack(BF), stack(F32), stack(F32), stack(F32),
            V((width, window), BF), V((width, window), BF), V((window, width), BF),
            V((window, width), F32), V((window, width), F32), V((window, width), F32),
            V((8, window), F32), V((8, window), F32), V((pair, width), F32), V((n_ctx, 8, 128), F32), V((1, channels), F32),
            V((3 * tiles, rows, 128), BF), V((n_ctx, rows, 128), BF), V((n_ctx, rows, 128), BF), V((tiles, rows, 128), BF),
            V((128, width), F32),
            V((count, rows, EXCHANGE), BF), V((count, rows, EXCHANGE), BF)],
        compiler_params=pltpu.CompilerParams(collective_id=collective_id, has_side_effects=True,
                                             vmem_limit_bytes=40 << 20),
        cost_estimate=pl.CostEstimate(flops=20 * 10 ** 9, bytes_accessed=60 * 10 ** 6, transcendentals=6 * 10 ** 6),
        name="backward_attention",
    )(dab, grad_ff_step, grad_attn_step, q_raw, k_raw, lse, attended, dxr, qk_scale, up_scale, gate_scale,
      w_out, w_query, w_key, w_value, x_all, q_all, k_all, v_all, hb_all, dmb_all, w_up, w_gate, w_down)


def last_kernel(result_ref, dx_ref, gotq_ref, gout_ref, gotu_ref, gdown_ref, gots_ref, gus_ref, ggs_ref,
                o_result, o_dx, o_gq, o_gk, o_gv, o_gout, o_gup, o_ggate, o_gdown, o_gqs, o_gus, o_ggs, o_gas, o_gfs):
    o_result[...] = result_ref[...]
    o_dx[...] = dx_ref[...]
    o_gout[...] = gout_ref[...]
    o_gdown[...] = gdown_ref[...]
    mine = o_gus.shape[1]
    tiles = o_gq.shape[1] // 128
    for j in range(gotu_ref.shape[0]):
        o_gup[:, j * mine:(j + 1) * mine] = gotu_ref[j, :, 0:mine].astype(F32)
        o_ggate[:, j * mine:(j + 1) * mine] = gotu_ref[j, :, mine:2 * mine].astype(F32)
    for n, ref in enumerate((o_gq, o_gk, o_gv)):
        for t in range(tiles):
            ref[:, t * 128:(t + 1) * 128] = gotq_ref[n * tiles + t].astype(F32)
    total = jnp.sum(gots_ref[...], axis=0)
    for row, ref in enumerate((o_gfs, o_gas, o_gqs)):
        ref[...] = total[row:row + 1, 0:ref.shape[1]]
    o_gus[...] = gus_ref[0:1, 0:mine]
    o_ggs[...] = ggs_ref[0:1, 0:mine]


def last_step(parts, n_ctx, channels, hidden):
    width = parts[1].shape[1]
    part, mine = width // n_ctx, hidden // n_ctx
    shape = jax.ShapeDtypeStruct
    outs = [shape(parts[0].shape, BF), shape(parts[1].shape, F32)] + [shape((part, channels), F32)] * 3
    outs += [shape(parts[3].shape, F32)] + [shape((part, hidden), F32)] * 2 + [shape((mine, width), F32)]
    outs += [shape((1, channels // n_ctx), F32)] + [shape((1, mine), F32)] * 2 + [shape((1, part), F32)] * 2
    return pl.pallas_call(
        last_kernel, out_shape=tuple(outs), in_specs=[vmem_spec()] * len(parts), out_specs=(vmem_spec(),) * len(outs),
        compiler_params=pltpu.CompilerParams(vmem_limit_bytes=32 << 20), name="last_step")(*parts)


CUT = ((64, 48, 32), (64, 48, 48))


def shards(layer_input, w_query, w_key, w_value, w_out, w_up, w_gate, w_down, qk_scale, up_scale,
           gate_scale, attention_step, feedforward_step, cotangent):
    n_ctx = lax.axis_size("ctx")
    ctx = lax.axis_index("ctx")
    rows = 2 * layer_input.shape[2]
    width = layer_input.shape[3]
    channels = w_query.shape[1]
    hidden = w_up.shape[1]
    tiles = channels // 128
    x = layer_input.reshape(rows, width)
    flat = lambda v: v.reshape(1, -1)
    x_all, q_all, k_all, v_all, q_raw, k_raw, attended, lse, hidden_one, branch_attn = forward_attention(
        x, w_query, w_key, w_value, flat(qk_scale), w_out, flat(attention_step), n_ctx, 0, CUT)
    hb_all, dmb_all, result, dab, input_res, grad_ff_step, grad_attn_step = feed_forward(
        hidden_one, branch_attn, x, cotangent.reshape(rows, width), flat(feedforward_step), flat(attention_step),
        flat(up_scale), flat(gate_scale), w_up, w_gate, w_down, n_ctx, 1, CUT)
    (input_grad, got_q, grad_out, got_u, grad_down, got_s, gus, ggs,
     _, _, turned, turned_qkv, gocc) = backward_attention(
        dab, grad_ff_step, grad_attn_step, q_raw, k_raw, lse, attended, input_res, flat(qk_scale), flat(up_scale),
        flat(gate_scale), w_out, w_query, w_key, w_value, x_all, q_all, k_all, v_all, hb_all, dmb_all,
        w_up, w_gate, w_down, n_ctx, 2, CUT)
    part = width // n_ctx
    if part % 16:
        turned, turned_qkv = lax.optimization_barrier((turned, turned_qkv))
        got_u = lax.all_to_all(turned, "ctx", 0, 0, tiled=True).reshape(n_ctx, part, -1)
        got_q = lax.all_to_all(turned_qkv, "ctx", 0, 0, tiled=True).reshape(n_ctx, part, 128)[:3 * tiles]
    if (channels // n_ctx) % 8:
        gocc = lax.optimization_barrier(gocc)
        whole = jnp.zeros((n_ctx, 128, width), F32)
        whole = lax.dynamic_update_slice_in_dim(whole, gocc[None], ctx, 0)[:tiles]
        grad_out = lax.psum_scatter(whole.reshape(channels, width), "ctx", scatter_dimension=0, tiled=True)
    outs = last_step((result, input_grad, got_q, grad_out, got_u, grad_down, got_s, gus, ggs), n_ctx, channels, hidden)
    tokens = tuple(v.reshape(layer_input.shape) for v in outs[:2])
    return tokens + tuple(outs[2:9]) + tuple(v.reshape(-1) for v in outs[9:])


def solution(mesh):
    placed = (
        P("ctx", None, None, None),
        P(None, "wa"),
        P(None, "wa"),
        P(None, "wa"),
        P("wa", None),
        P(None, "wa"),
        P(None, "wa"),
        P("wa", None),
        P("wa"),
        P("wa"),
        P("wa"),
        P(),
        P(),
        P("ctx", None, None, None),
    )
    return jax.shard_map(
        shards,
        mesh=mesh,
        in_specs=placed,
        out_specs=(
            P("ctx", None, None, None),
            P("ctx", None, None, None),
            P("ctx", "wa"),
            P("ctx", "wa"),
            P("ctx", "wa"),
            P(("wa", "ctx"), None),
            P("ctx", "wa"),
            P("ctx", "wa"),
            P(("wa", "ctx"), None),
            P(("wa", "ctx")),
            P(("wa", "ctx")),
            P(("wa", "ctx")),
            P("ctx"),
            P("ctx"),
        ),
        check_vma=False,
    )
```

```python
import functools
from functools import partial
import math

import jax
import jax.numpy as jnp
from jax import lax
from jax.experimental import pallas as pl
from jax.experimental.pallas import tpu as pltpu
from jax.sharding import PartitionSpec as P

HD = 64
MESH = pl.DeviceIdType.MESH


def layout_of(n_ctx):
    chips = n_ctx // 2
    across = 2 if chips <= 8 else 4
    return chips // across, across


class Place:
    def __init__(self, n_ctx):
        self.n_ctx = n_ctx
        self.line, self.across = layout_of(n_ctx)
        self.ctx = lax.axis_index("ctx")
        self.wa = lax.axis_index("wa")
        self.core = lax.rem(self.ctx, 2)
        chip = lax.div(self.ctx, 2)
        self.x = lax.rem(chip, self.across)
        self.z = lax.div(chip, self.across)

    def index(self, z, x, core):
        return (z * self.across + x) * 2 + core

    def at(self, z, x, core):
        return (self.index(z, x, core), self.wa)

    def sibling(self):
        return self.at(self.z, self.x, 1 - self.core)

    def partner(self):
        return (self.ctx, 1 - self.wa)

    def inside(self, z):
        return (z >= 0) & (z < self.line)

    def column(self, shift):
        return lax.rem(self.x + shift, self.across)

    def barrier(self):
        sem = pltpu.get_barrier_semaphore()

        def signal(device):
            pl.semaphore_signal(sem, inc=1, device_id=device, device_id_type=MESH)

        signal(self.sibling())
        signal(self.partner())
        for shift in range(1, self.across):
            signal(self.at(self.z, self.column(shift), self.core))
        count = jnp.int32(self.across + 1)
        for step in (-1, 1):
            near = self.inside(self.z + step)
            pl.when(near)(functools.partial(signal, self.at(self.z + step, self.x, self.core)))
            count = count + near.astype(jnp.int32)
        pl.semaphore_wait(sem, count)

    def barrier_all(self):
        sem = pltpu.get_barrier_semaphore()
        pl.semaphore_signal(sem, inc=1, device_id=self.partner(), device_id_type=MESH)

        @pl.loop(1, self.n_ctx)
        def _(shift):
            other = lax.rem(self.ctx + shift, self.n_ctx)
            pl.semaphore_signal(sem, inc=1, device_id=(other, self.wa), device_id_type=MESH)

        pl.semaphore_wait(sem, self.n_ctx)


class Gather:
    def __init__(self, place, out, sems, base, first, rows, z_rows, x_rows):
        self.p = place
        self.out = out
        self.sems = sems
        self.base = base
        self.first, self.rows = first, rows
        self.z_rows, self.x_rows = z_rows, x_rows
        self.slots = 2 * place.line

    @staticmethod
    def sem_count(n_ctx):
        line, across = layout_of(n_ctx)
        return 2 * line * 3 * across

    def sem(self, kind, s, k, shift=0):
        kinds = self.p.across - 1
        order = {"z": 0, "y": 1, "c": 2, "x": 3, "yx": 3 + kinds, "cx": 3 + 2 * kinds}[kind]
        return self.base + (order + shift) * self.slots + (0 if s > 0 else self.p.line) + k

    def copy(self, sem, block, start, size, device):
        view = self.out.at[block, pl.ds(pl.multiple_of(self.first + start, 16), size)]
        return pltpu.make_async_remote_copy(
            src_ref=view, dst_ref=view, send_sem=self.sems.at[0, sem], recv_sem=self.sems.at[1, sem],
            device_id=device, device_id_type=MESH)

    def exists(self, s, k):
        ok = self.p.inside(self.p.z - s * k) & (k >= 0) & (k < self.p.line)
        return ok if s > 0 else ok & (k > 0)

    def d_z(self, s, k, block, device):
        return self.copy(self.sem("z", s, k), block, self.p.wa * (self.rows - self.z_rows), self.z_rows, device)

    def d_x(self, s, k, shift, block, device):
        return self.copy(self.sem("x", s, k, shift - 1), block, self.p.wa * (self.rows - self.x_rows), self.x_rows, device)

    def d_y(self, kind, s, k, shift, block, size, sending):
        side = self.p.wa if sending else 1 - self.p.wa
        return self.copy(self.sem(kind, s, k, shift), block, side * size, self.rows - size, self.p.partner())

    def d_c(self, kind, s, k, shift, block):
        return self.copy(self.sem(kind, s, k, shift), block, 0, self.rows, self.p.sibling())

    def ok_forward(self, s, k):
        p = self.p
        return p.inside(p.z - s * k) & p.inside(p.z + s) & (k >= 0) & (k + 1 < p.line)

    def step_z(self, k):
        p = self.p
        me = (p.ctx, p.wa)
        for s in (1, -1):
            block = p.index(p.z - s * k, p.x, p.core)

            @pl.when(self.exists(s, k) & (k > 0))
            def _():
                self.d_z(s, k, block, me).wait_recv()

            @pl.when(self.ok_forward(s, k))
            def _():
                self.d_z(s, k + 1, block, p.at(p.z + s, p.x, p.core)).start()

            @pl.when(self.exists(s, k))
            def _():
                for shift in range(1, p.across):
                    self.d_x(s, k, shift, block, p.at(p.z, p.column(shift), p.core)).start()
                if s > 0:
                    @pl.when(k == 0)
                    def _():
                        self.d_c("c", s, k, 0, block).start()

                if self.z_rows < self.rows:
                    @pl.when(k > 0)
                    def _():
                        self.d_y("y", s, k, 0, block, self.z_rows, True).start()

    def step_y(self, k):
        p = self.p
        for s in (1, -1):
            @pl.when(self.exists(s, k) & (k > 0))
            def _():
                block = p.index(p.z - s * k, p.x, p.core)
                if self.z_rows < self.rows:
                    self.d_y("y", s, k, 0, block, self.z_rows, False).wait_recv()
                self.d_c("c", s, k, 0, block).start()

    def step_x(self, k):
        p = self.p
        for s in (1, -1):
            @pl.when(self.exists(s, k))
            def _():
                for shift in range(1, p.across):
                    block = p.index(p.z - s * k, p.column(p.across - shift), p.core)
                    self.d_x(s, k, shift, block, (p.ctx, p.wa)).wait_recv()
                    if self.x_rows < self.rows:
                        self.d_y("yx", s, k, shift - 1, block, self.x_rows, True).start()

    def step_yx(self, k):
        p = self.p
        for s in (1, -1):
            @pl.when(self.exists(s, k))
            def _():
                for shift in range(1, p.across):
                    block = p.index(p.z - s * k, p.column(p.across - shift), p.core)
                    if self.x_rows < self.rows:
                        self.d_y("yx", s, k, shift - 1, block, self.x_rows, False).wait_recv()
                    self.d_c("cx", s, k, shift - 1, block).start()

    def step_c(self, k):
        p = self.p
        for s in (1, -1):
            @pl.when(self.exists(s, k))
            def _():
                self.d_c("c", s, k, 0, p.index(p.z - s * k, p.x, 1 - p.core)).wait_recv()
                for shift in range(1, p.across):
                    block = p.index(p.z - s * k, p.column(p.across - shift), 1 - p.core)
                    self.d_c("cx", s, k, shift - 1, block).wait_recv()

    def finish(self):
        p = self.p

        @pl.loop(0, p.line)
        def _(k):
            for s in (1, -1):
                block = p.index(p.z - s * k, p.x, p.core)

                @pl.when(self.ok_forward(s, k))
                def _():
                    self.d_z(s, k + 1, block, p.at(p.z + s, p.x, p.core)).wait_send()

                @pl.when(self.exists(s, k))
                def _():
                    self.d_c("c", s, k, 0, block).wait_send()
                    if self.z_rows < self.rows:
                        @pl.when(k > 0)
                        def _():
                            self.d_y("y", s, k, 0, block, self.z_rows, True).wait_send()
                    for shift in range(1, p.across):
                        self.d_x(s, k, shift, block, p.at(p.z, p.column(shift), p.core)).wait_send()
                        other = p.index(p.z - s * k, p.column(p.across - shift), p.core)
                        if self.x_rows < self.rows:
                            self.d_y("yx", s, k, shift - 1, other, self.x_rows, True).wait_send()
                        self.d_c("cx", s, k, shift - 1, other).wait_send()


class Pieces:
    def __init__(self, place, out, sems, cut):
        n = Gather.sem_count(place.n_ctx)
        self.p = place
        self.parts = []
        first = 0
        for number, (rows, z_rows, x_rows) in enumerate(cut):
            self.parts.append(Gather(place, out, sems, number * n, first, rows, z_rows, x_rows))
            first += rows

    def each(self, name, k):
        for part in self.parts:
            getattr(part, name)(k)

    def step(self, t):
        self.each("step_z", t)
        for part in self.parts:
            part.step_x(t - 1)
            part.step_y(t - 1)
        self.each("step_yx", t - 2)
        self.each("step_c", t - 3)

    def step_count(self):
        return self.p.line + 3

    def finish(self):
        for part in self.parts:
            part.finish()


def gather_sems(n_ctx, cut):
    return pltpu.SemaphoreType.DMA((2, len(cut) * Gather.sem_count(n_ctx)))


NORM_EPS = 1e-06
BF = jnp.bfloat16
F32 = jnp.float32


def dot32(a, b):
    return jnp.dot(a, b, preferred_element_type=F32)


def dot_tn(a, b):
    return lax.dot_general(a, b, (((0,), (0,)), ((), ())), preferred_element_type=F32)


def dot_nt(a, b):
    return lax.dot_general(a, b, (((1,), (1,)), ((), ())), preferred_element_type=F32)


def row_mean(v):
    return jnp.mean(v, axis=-1, keepdims=True)


def inv_rms(v):
    return lax.rsqrt(row_mean(v * v) + NORM_EPS)


def rms_back(v, inv, grad):
    n = v * inv
    return (grad - n * row_mean(n * grad)) * inv


def pair_mean(v):
    row = lax.broadcasted_iota(jnp.int32, (128, 128), 0)
    col = lax.broadcasted_iota(jnp.int32, (128, 128), 1)
    ones = jnp.where((row < HD) == (col < HD), 1.0 / HD, 0.0).astype(BF)
    high = v.astype(BF)
    lowp = (v - high.astype(F32)).astype(BF)
    return dot32(high, ones) + dot32(lowp, ones)


def head_rms(v):
    return lax.rsqrt(pair_mean(v * v) + NORM_EPS)


def position_of(shard, index, block_len, n_ctx):
    late = index >= block_len
    block = jnp.where(late, 2 * n_ctx - 1 - shard, shard)
    return block * block_len + jnp.where(late, index - block_len, index)


def stack_heads(v):
    first = lax.broadcasted_iota(jnp.int32, v.shape, 1) < HD
    zero = jnp.zeros_like(v)
    return jnp.concatenate([jnp.where(first, v, zero), jnp.where(first, zero, v)], axis=0)


def join_heads(v):
    rows = v.shape[0] // 2
    first = lax.broadcasted_iota(jnp.int32, (rows, 128), 1) < HD
    return jnp.where(first, v[:rows], v[rows:])


def load_rows(src, dst, sem):
    return pltpu.make_async_copy(src, dst, sem)


LOG2E = 1.4426950408889634
EXCHANGE = 256
TOGETHER = 4


def fwd_kernel(n_ctx, cut, x_ref, qs_ref, step_ref, wq_hbm, wk_hbm, wv_hbm, wo_hbm,
               xall_ref, qall_ref, kall_ref, vall_ref, qraw_ref, kraw_ref, o_ref, lse_ref, h1_ref, ha_ref,
               gsems, lsems, wsems, esems, psems, wq_ref, wk_ref, wv_ref, wo_ref, xbuf, qbuf, kbuf, vbuf, q2, acc, lpart, sbuf, rbuf):
    place = Place(n_ctx)
    rows, width = x_ref.shape
    block_len = rows // 2
    channels = wq_ref.shape[1]
    tiles = channels // 128
    group = 2 * place.across
    plane = group * rows
    gather = Pieces(place, xall_ref, gsems, cut)
    own = load_rows(x_ref, xall_ref.at[place.ctx], lsems.at[0])
    own.start()
    weights = [load_rows(src, dst, psems.at[i]) for i, (src, dst) in enumerate(
        ((wq_hbm, wq_ref), (wk_hbm, wk_ref), (wv_hbm, wv_ref), (wo_hbm, wo_ref)))]
    for copy in weights:
        copy.start()
    place.barrier()
    own.wait()
    gather.each("step_z", 0)
    for copy in weights:
        copy.wait()

    xv = x_ref[...]
    kraw_ref[...] = dot32(xv, wk_ref[...])
    qraw_ref[...] = dot32(xv, wq_ref[...])
    for t in range(tiles):
        cols = slice(t * 128, (t + 1) * 128)
        raw = qraw_ref[:, cols]
        q2[t] = stack_heads((raw * head_rms(raw) * qs_ref[:, cols]).astype(BF))
    acc[...] = jnp.zeros_like(acc)
    lpart[...] = jnp.zeros_like(lpart)

    def plane_of(s, k):
        return place.z - s * k

    def hbm(ref, zp):
        return ref.at[pl.ds(zp * group, group)]

    def x_load(s, k):
        side = 0 if s > 0 else 1
        return load_rows(hbm(xall_ref, plane_of(s, k)), xbuf.at[side], lsems.at[1 + side])

    def stores(s, k):
        side = 0 if s > 0 else 1
        zp = plane_of(s, k)
        return [load_rows(buf.at[side], hbm(ref, zp), wsems.at[side, i])
                for i, (buf, ref) in enumerate(((qbuf, qall_ref), (kbuf, kall_ref), (vbuf, vall_ref)))]

    def project(s, k):
        side = 0 if s > 0 else 1
        x_load(s, k).wait()

        @pl.loop(0, group // TOGETHER)
        def _(r):
            some = pl.ds(r * TOGETHER, TOGETHER)
            xr = xbuf[side, some].reshape(TOGETHER * rows, width)
            for w_ref, buf in ((wq_ref, qbuf), (wk_ref, kbuf)):
                raw = dot32(xr, w_ref[...])
                for t in range(tiles):
                    cols = slice(t * 128, (t + 1) * 128)
                    part = raw[:, cols]
                    normed = (part * head_rms(part) * qs_ref[:, cols]).astype(BF)
                    buf[side, some, :, cols] = normed.reshape(TOGETHER, rows, 128)
            vbuf[side, some] = dot32(xr, wv_ref[...]).astype(BF).reshape(TOGETHER, rows, channels)

        for copy in stores(s, k):
            copy.start()

    def attend(s, k):
        side = 0 if s > 0 else 1
        zp = plane_of(s, k)
        qi = lax.broadcasted_iota(jnp.int32, (2 * rows, 1), 0)
        qi = jnp.where(qi >= rows, qi - rows, qi)
        qpos = position_of(place.ctx, qi, block_len, n_ctx)
        ki = lax.broadcasted_iota(jnp.int32, (1, plane), 1)
        kpos = position_of(zp * group + lax.div(ki, rows), lax.rem(ki, rows), block_len, n_ctx)
        allowed = kpos <= qpos

        @pl.loop(0, tiles)
        def _(t):
            cols = pl.ds(pl.multiple_of(t * 128, 128), 128)
            kt = kbuf[side, :, :, cols].reshape(plane, 128)
            vt = vbuf[side, :, :, cols].reshape(plane, 128)
            score = dot_nt(q2[t], kt)
            e = jnp.where(allowed, jnp.exp2(score * (LOG2E / math.sqrt(HD))), 0.0)
            total = e[:, :128]
            for j in range(1, plane // 128):
                total = total + e[:, j * 128:(j + 1) * 128]
            lpart[t] += total
            acc[t] += dot32(e.astype(BF), vt)

        for copy in stores(s, k):
            copy.wait()

    def both(k, fn):
        for s in (1, -1):
            pl.when(gather.parts[0].exists(s, k))(functools.partial(fn, s, k))

    gather.each("step_z", 1)

    @pl.loop(1, place.line + 2)
    def _(t):
        gather.each("step_x", t - 1)
        gather.each("step_y", t - 1)
        both(t - 2, attend)
        gather.each("step_yx", t - 1)
        gather.each("step_c", t - 1)
        both(t - 1, lambda s, k: x_load(s, k).start())
        gather.each("step_z", t + 1)
        both(t - 1, project)

    for t in range(tiles):
        mass = jnp.sum(lpart[t], axis=1, keepdims=True)
        o_ref[:, t * 128:(t + 1) * 128] = join_heads(acc[t] / mass)
        lse_ref[t] = jnp.broadcast_to(jnp.log(mass) * LOG2E, (2 * rows, 128))

    exchange(place, lambda cols: dot32(o_ref[...].astype(BF), wo_ref[:, cols]), ha_ref, sbuf, rbuf, esems)
    ha = ha_ref[...]
    xf = x_ref[...].astype(F32)
    w = xf + step_ref[...] * (ha * inv_rms(ha) - xf)
    h1_ref[...] = w * inv_rms(w)
    gather.finish()


def exchange(place, term, sum_ref, sbuf, rbuf, esems, between=None):
    width = sum_ref.shape[1]

    def copy(n):
        return pltpu.make_async_remote_copy(
            src_ref=sbuf.at[n], dst_ref=rbuf.at[n], send_sem=esems.at[0, n], recv_sem=esems.at[1, n],
            device_id=place.partner(), device_id_type=MESH)

    count = width // EXCHANGE
    for n in range(count):
        sbuf[n] = term(slice(n * EXCHANGE, (n + 1) * EXCHANGE)).astype(BF)
        copy(n).start()
    if between is not None:
        between()
    for n in range(count):
        copy(n).wait()
        sum_ref[:, n * EXCHANGE:(n + 1) * EXCHANGE] = sbuf[n].astype(F32) + rbuf[n].astype(F32)


def vmem_spec():
    return pl.BlockSpec(memory_space=pltpu.VMEM)


def in_hbm(v):
    return pltpu.with_memory_space_constraint(v, pltpu.HBM)


def hbm_spec():
    return pl.BlockSpec(memory_space=pltpu.HBM)


def any_spec():
    return pl.BlockSpec(memory_space=pl.ANY)


def forward_attention(x, w_query, w_key, w_value, qk_scale, w_out, step, n_ctx, collective_id, cut):
    rows, width = x.shape
    channels = w_query.shape[1]
    tiles = channels // 128
    line, across = layout_of(n_ctx)
    group = 2 * across
    count = width // EXCHANGE
    shape = jax.ShapeDtypeStruct
    return pl.pallas_call(
        functools.partial(fwd_kernel, n_ctx, cut),
        out_shape=(pltpu.HBM((n_ctx, rows, width), BF),) + (pltpu.HBM((n_ctx, rows, channels), BF),) * 3
        + (shape((rows, channels), F32),) * 3 + (shape((tiles, 2 * rows, 128), F32),) + (shape((rows, width), F32),) * 2,
        in_specs=[vmem_spec()] * 3 + [hbm_spec()] * 4,
        out_specs=(hbm_spec(),) * 4 + (vmem_spec(),) * 6,
        scratch_shapes=[
            gather_sems(n_ctx, cut), pltpu.SemaphoreType.DMA((3,)), pltpu.SemaphoreType.DMA((2, 3)),
            pltpu.SemaphoreType.DMA((2, count)), pltpu.SemaphoreType.DMA((4,)),
            pltpu.VMEM((width, channels), BF), pltpu.VMEM((width, channels), BF), pltpu.VMEM((width, channels), BF),
            pltpu.VMEM((channels, width), BF),
            pltpu.VMEM((2, group, rows, width), BF),
            pltpu.VMEM((2, group, rows, channels), BF), pltpu.VMEM((2, group, rows, channels), BF),
            pltpu.VMEM((2, group, rows, channels), BF),
            pltpu.VMEM((tiles, 2 * rows, 128), BF), pltpu.VMEM((tiles, 2 * rows, 128), F32),
            pltpu.VMEM((tiles, 2 * rows, 128), F32),
            pltpu.VMEM((count, rows, EXCHANGE), BF), pltpu.VMEM((count, rows, EXCHANGE), BF)],
        compiler_params=pltpu.CompilerParams(collective_id=collective_id, has_side_effects=True,
                                             vmem_limit_bytes=32 << 20),
        cost_estimate=pl.CostEstimate(flops=12 * 10 ** 9, bytes_accessed=40 * 10 ** 6, transcendentals=3 * 10 ** 6),
        name="forward_attention",
    )(x, qk_scale, step, *(in_hbm(w) for w in (w_query, w_key, w_value, w_out)))


HIDDEN_CUT = 256


def mid_kernel(n_ctx, cut, h1_ref, ha_ref, x_ref, cot_ref, fs_ref, as_ref, us_ref, gs_ref, wu_ref, wg_ref, wd_ref,
               hball_ref, dmball_ref, out_ref, dab_ref, dxr_ref, gfs_ref, gas_ref,
               hsems, msems, lsems, wsems, e1sems, e2sems, wu, wg, wd, hbv, dmv, u_buf, g_buf, low_a, low_b, total,
               s1, r1, s2, r2):
    place = Place(n_ctx)
    rows, width = h1_ref.shape
    hidden = us_ref.shape[1]
    cuts = hidden // HIDDEN_CUT
    h_gather = Pieces(place, hball_ref, hsems, cut)
    m_gather = Pieces(place, dmball_ref, msems, cut)

    def part(n):
        return slice(n * HIDDEN_CUT, (n + 1) * HIDDEN_CUT)

    loads = [[load_rows(wu_ref.at[:, part(n)], wu.at[:, part(n)], wsems.at[0, n]),
              load_rows(wg_ref.at[:, part(n)], wg.at[:, part(n)], wsems.at[1, n])] for n in range(cuts)]
    down = [load_rows(wd_ref.at[part(n)], wd.at[part(n)], wsems.at[2, n]) for n in range(cuts)]
    for pair in loads:
        for copy in pair:
            copy.start()
    for copy in down:
        copy.start()
    hbv[...] = h1_ref[...].astype(BF)
    own = load_rows(hbv, hball_ref.at[place.ctx], lsems.at[0])
    own.start()
    place.barrier()
    own.wait()
    h_gather.each("step_z", 0)

    hb = hbv[...]
    for n in range(cuts):
        for copy in loads[n]:
            copy.wait()
        u = dot32(hb, wu[:, part(n)])
        g = dot32(hb, wg[:, part(n)])
        u_buf[:, part(n)] = u
        g_buf[:, part(n)] = g
        c = g * gs_ref[:, part(n)]
        low_a[:, part(n)] = (u * us_ref[:, part(n)] * (c * lax.logistic(c))).astype(BF)
        if n == cuts - 3:
            h_gather.each("step_z", 1)
    for copy in down:
        copy.wait()

    def serve_first():
        h_gather.each("step_x", 0)
        h_gather.each("step_z", 2)

    exchange(place, lambda cols: dot32(low_a[...], wd[:, cols]), total, s1, r1, e1sems, serve_first)
    h1 = h1_ref[...]
    fs = fs_ref[...]
    hm = total[...]
    m_inv = inv_rms(hm)
    step = hm * m_inv - h1
    z = h1 + fs * step
    z_inv = inv_rms(z)
    out_ref[...] = (z * z_inv).astype(BF)
    dz = rms_back(z, z_inv, cot_ref[...].astype(F32))
    gfs_ref[...] = jnp.sum(dz * step, axis=0, keepdims=True)
    dxr_ref[...] = (1.0 - fs) * dz
    dmv[...] = rms_back(hm, m_inv, fs * dz).astype(BF)
    own = load_rows(dmv, dmball_ref.at[place.ctx], lsems.at[1])
    own.start()
    own.wait()
    m_gather.each("step_z", 0)
    h_gather.each("step_z", 3)
    h_gather.each("step_x", 1)
    h_gather.each("step_y", 1)
    h_gather.each("step_yx", 0)

    dm = dmv[...]
    for n in range(cuts):
        dgated = dot_nt(dm, wd[part(n), :])
        u, g = u_buf[:, part(n)], g_buf[:, part(n)]
        us, gs = us_ref[:, part(n)], gs_ref[:, part(n)]
        c = g * gs
        s = lax.logistic(c)
        low_a[:, part(n)] = (dgated * (c * s) * us).astype(BF)
        low_b[:, part(n)] = (dgated * (u * us) * (s * (1.0 + c * (1.0 - s))) * gs).astype(BF)
        if n == cuts // 2:
            h_gather.each("step_x", 2)
            h_gather.each("step_y", 2)
            h_gather.each("step_yx", 1)
            h_gather.each("step_c", 0)

    m_gather.each("step_z", 1)

    def serve_second():
        h_gather.each("step_x", 3)
        h_gather.each("step_y", 3)
        m_gather.each("step_x", 0)
        h_gather.each("step_yx", 2)
        m_gather.each("step_z", 2)

    exchange(place, lambda cols: dot_nt(low_a[...], wu[cols, :]) + dot_nt(low_b[...], wg[cols, :]), total, s2, r2,
             e2sems, serve_second)
    m_gather.each("step_z", 3)
    m_gather.each("step_x", 1)
    m_gather.each("step_y", 1)
    m_gather.each("step_yx", 0)
    dh1 = dxr_ref[...] + total[...]
    xf = x_ref[...].astype(F32)
    step_size = as_ref[...]
    ha = ha_ref[...]
    a_inv = inv_rms(ha)
    step = ha * a_inv - xf
    w = xf + step_size * step
    dw = rms_back(w, inv_rms(w), dh1)
    gas_ref[...] = jnp.sum(dw * step, axis=0, keepdims=True)
    dxr_ref[...] = (1.0 - step_size) * dw
    dab_ref[...] = rms_back(ha, a_inv, step_size * dw).astype(BF)

    @pl.loop(4, place.line)
    def _(k):
        for name in ("step_z", "step_x", "step_y"):
            h_gather.each(name, k)
        m_gather.each("step_z", k)

    @pl.loop(2, place.line + 1)
    def _(k):
        m_gather.each("step_x", k)
        m_gather.each("step_y", k)
        m_gather.each("step_yx", k - 1)

        @pl.when(k > 2)
        def _():
            h_gather.each("step_yx", k)
        h_gather.each("step_c", k - 1)
        m_gather.each("step_c", k - 2)

    m_gather.each("step_c", place.line - 1)
    h_gather.finish()
    m_gather.finish()


def feed_forward(hidden_one, branch_attn, x, cotangent, ff_step, attn_step, up_scale, gate_scale, w_up, w_gate, w_down,
                 n_ctx, collective_id, cut):
    rows, width = x.shape
    hidden = w_up.shape[1]
    cuts = hidden // HIDDEN_CUT
    count = width // EXCHANGE
    shape = jax.ShapeDtypeStruct
    dma = pltpu.SemaphoreType.DMA
    V = pltpu.VMEM
    box = V((count, rows, EXCHANGE), BF)
    return pl.pallas_call(
        functools.partial(mid_kernel, n_ctx, cut),
        out_shape=(pltpu.HBM((n_ctx, rows, width), BF), pltpu.HBM((n_ctx, rows, width), BF), shape((rows, width), BF),
                   shape((rows, width), BF), shape((rows, width), F32), shape((1, width), F32), shape((1, width), F32)),
        in_specs=[vmem_spec()] * 8 + [hbm_spec()] * 3,
        out_specs=(hbm_spec(),) * 2 + (vmem_spec(),) * 5,
        scratch_shapes=[
            gather_sems(n_ctx, cut), gather_sems(n_ctx, cut), dma((2,)), dma((3, cuts)), dma((2, count)), dma((2, count)),
            V((width, hidden), BF), V((width, hidden), BF), V((hidden, width), BF), V((rows, width), BF),
            V((rows, width), BF), V((rows, hidden), F32), V((rows, hidden), F32), V((rows, hidden), BF),
            V((rows, hidden), BF), V((rows, width), F32), box, box, box, box],
        compiler_params=pltpu.CompilerParams(collective_id=collective_id, has_side_effects=True,
                                             vmem_limit_bytes=30 << 20),
        cost_estimate=pl.CostEstimate(flops=5 * 10 ** 9, bytes_accessed=30 * 10 ** 6, transcendentals=10 ** 6),
        name="feed_forward",
    )(hidden_one, branch_attn, x, cotangent, ff_step, attn_step, up_scale, gate_scale, in_hbm(w_up), in_hbm(w_gate), in_hbm(w_down))


BLOCK = 4
STATS = 128


def split_parts(v, count):
    parts = []
    rest = v
    for _ in range(count):
        part = rest.astype(BF)
        parts.append(part)
        rest = rest - part.astype(F32)
    return parts


def transposed(src, dst, dtype):
    for n in range(src.shape[1] // 128):
        dst[n * 128:(n + 1) * 128, :] = src[:, n * 128:(n + 1) * 128].T.astype(dtype)


class UnitScatter:
    def __init__(self, place, source, target, send_sems, recv_sems, senders, per_sender, per_owner):
        self.p, self.source, self.target = place, source, target
        self.send_sems, self.recv_sems = send_sems, recv_sems
        self.senders, self.per_sender, self.per_owner = senders, per_sender, per_owner

    def rows(self, unit):
        return pl.ds(pl.multiple_of(unit * 8, 8), 8)

    def copy(self, unit, slot, owner):
        return pltpu.make_async_remote_copy(
            src_ref=self.source.at[self.rows(unit)], dst_ref=self.target.at[self.rows(slot)],
            send_sem=self.send_sems.at[unit], recv_sem=self.recv_sems.at[slot],
            device_id=(owner, self.p.wa), device_id_type=MESH)

    def local(self, unit, slot):
        return pltpu.make_async_copy(self.source.at[self.rows(unit)], self.target.at[self.rows(slot)],
                                     self.recv_sems.at[slot])

    def outgoing(self, remote, near):
        p = self.p

        @pl.when(p.ctx < self.senders)
        def _():
            @pl.loop(0, self.per_sender)
            def _(unit):
                place_of = p.ctx * self.per_sender + unit
                owner, slot = lax.div(place_of, self.per_owner), lax.rem(place_of, self.per_owner)

                @pl.when(owner != p.ctx)
                def _():
                    remote(self.copy(unit, slot, owner))

                if near is not None:
                    @pl.when(owner == p.ctx)
                    def _():
                        near(self.local(unit, slot))

    def start(self):
        self.outgoing(lambda c: c.start(), lambda c: c.start())

    def wait(self):
        p = self.p

        @pl.loop(0, self.per_owner)
        def _(slot):
            place_of = p.ctx * self.per_owner + slot
            sender, unit = lax.div(place_of, self.per_sender), lax.rem(place_of, self.per_sender)

            @pl.when(sender != p.ctx)
            def _():
                self.copy(unit, slot, p.ctx).wait_recv()

            @pl.when(sender == p.ctx)
            def _():
                self.local(unit, slot).wait()

    def sent(self):
        self.outgoing(lambda c: c.wait_send(), None)


class Scatter:
    def __init__(self, place, source, target, sems, count, senders):
        self.p, self.source, self.target, self.sems = place, source, target, sems
        self.count, self.senders = count, senders

    def copy(self, dest, sender):
        return pltpu.make_async_remote_copy(
            src_ref=self.source(dest), dst_ref=self.target(sender),
            send_sem=self.sems.at[0, dest], recv_sem=self.sems.at[1, sender],
            device_id=(dest, self.p.wa), device_id_type=MESH)

    def each(self, fn):
        p = self.p

        @pl.loop(1, p.n_ctx)
        def _(shift):
            fn(lax.rem(p.ctx + shift, p.n_ctx))

    def start(self):
        p = self.p

        @pl.when(p.ctx < self.senders)
        def _():
            def go(dest):
                @pl.when(dest < self.count)
                def _():
                    self.copy(dest, p.ctx).start()
            self.each(go)

            @pl.when(p.ctx < self.count)
            def _():
                self.local().start()

    def local(self):
        return pltpu.make_async_copy(self.source(self.p.ctx), self.target(self.p.ctx), self.sems.at[1, self.p.ctx])

    def wait(self):
        p = self.p

        @pl.when(p.ctx < self.count)
        def _():
            def got(sender):
                @pl.when(sender < self.senders)
                def _():
                    self.copy(p.ctx, sender).wait_recv()
            self.each(got)

            @pl.when(p.ctx < self.senders)
            def _():
                self.local().wait()

    def sent(self):
        p = self.p

        @pl.when(p.ctx < self.senders)
        def _():
            def left(dest):
                @pl.when(dest < self.count)
                def _():
                    self.copy(dest, p.ctx).wait_send()
            self.each(left)


def bwd_kernel(n_ctx, cut, aligned, out_aligned, *refs):
    (dab_ref, gfs_ref, gas_ref, qraw_ref, kraw_ref, lse_ref, o_ref, dxr_ref, qs_ref, us_ref, gs_ref,
     wo_ref, wq_ref, wk_ref, wv_ref, xall_ref, qall_ref, kall_ref, vall_ref, hball_ref, dmball_ref, wu_ref, wg_ref, wd_ref,
     dx_ref, got_q, gout_ref, got_u, gdown_ref, got_s, gus_ref, ggs_ref,
     daball_ref, statall_ref, turned, turned_qkv, gocc,
     asems, ssts, lsems, csems, esems, usems, tsems, osems, rsems, vsems, ssems, xsems, nsems,
     hbbuf, dmbuf, dabbuf, stbuf, qbuf, kvbuf, dobuf, rowstats, stats, delta, q2, k2, v2, do2, dq2, dk2, dv2,
     wuw, wgw, wdw, gu, gg, gd, colu, colg, comb, small, small_row, dqkv, got_t, got_o, obs, accq, sbuf, rbuf) = refs
    place = Place(n_ctx)
    rows, width = dxr_ref.shape
    block_len = rows // 2
    channels = qraw_ref.shape[1]
    tiles = channels // 128
    hidden = us_ref.shape[1]
    mine = hidden // n_ctx
    group = 2 * place.across
    subs = group // BLOCK
    many = BLOCK * rows
    window = gu.shape[0]
    scale = 1.0 / math.sqrt(HD)
    a_gather = Pieces(place, daball_ref, asems, cut)
    s_gather = Pieces(place, statall_ref, ssts, ((rows, rows, rows),))
    start = jnp.minimum(lax.div(place.ctx * mine, 128) * 128, hidden - window)
    start = pl.multiple_of(start, 128)
    offset = pl.multiple_of(place.ctx * mine - start, 8)
    win = pl.ds(start, window)
    own = [load_rows(dab_ref, daball_ref.at[place.ctx], lsems.at[0]),
           load_rows(wu_ref.at[:, win], wuw, lsems.at[2]), load_rows(wg_ref.at[:, win], wgw, lsems.at[3]),
           load_rows(wd_ref.at[win, :], wdw, lsems.at[4])]
    for copy in own:
        copy.start()
    for t in range(tiles):
        obs[t] = o_ref[:, t * 128:(t + 1) * 128].astype(BF)
    place.barrier_all()
    own[0].wait()
    a_gather.each("step_z", 0)
    d_out = dot_nt(dab_ref[...], wo_ref[...]).astype(BF)
    lane = lax.broadcasted_iota(jnp.int32, (rows, 128), 1)
    packed = jnp.zeros((rows, 128), F32)
    for t in range(tiles):
        cols = slice(t * 128, (t + 1) * 128)
        do2[t] = stack_heads(d_out[:, cols])
        both_heads = stack_heads(d_out[:, cols].astype(F32) * o_ref[:, cols])
        delta[t] = jnp.broadcast_to(jnp.sum(both_heads, axis=1, keepdims=True), (2 * rows, 128))
        for h in range(2):
            part_rows = slice(h * rows, (h + 1) * rows)
            values = split_parts(lse_ref[t, part_rows], 3) + split_parts(delta[t, part_rows], 2)
            for i, value in enumerate(values):
                packed = jnp.where(lane == i * 2 * tiles + 2 * t + h, value.astype(F32), packed)
    stats[...] = packed.astype(BF)
    own_stats = load_rows(stats, statall_ref.at[place.ctx], lsems.at[0])
    own_stats.start()
    own_stats.wait()
    s_gather.each("step_z", 0)
    o_scatter = Scatter(place, lambda dest: obs.at[dest], lambda sender: got_o.at[sender], osems, tiles, n_ctx)
    o_scatter.start()

    for t in range(tiles):
        cols = slice(t * 128, (t + 1) * 128)
        for raw_ref, dest in ((qraw_ref, q2), (kraw_ref, k2)):
            raw = raw_ref[:, cols]
            dest[t] = stack_heads((raw * head_rms(raw) * qs_ref[:, cols]).astype(BF))
    dq2[...] = jnp.zeros_like(dq2)
    dk2[...] = jnp.zeros_like(dk2)
    dv2[...] = jnp.zeros_like(dv2)
    gu[...] = jnp.zeros_like(gu)
    gg[...] = jnp.zeros_like(gg)
    gd[...] = jnp.zeros_like(gd)
    colu[...] = jnp.zeros_like(colu)
    colg[...] = jnp.zeros_like(colg)
    gocc[...] = jnp.zeros_like(gocc)

    def row_positions(shape, axis, first):
        i = lax.broadcasted_iota(jnp.int32, shape, axis)
        return position_of(first + lax.div(i, rows), lax.rem(i, rows), block_len, n_ctx)

    def own_positions(shape, axis):
        i = lax.broadcasted_iota(jnp.int32, shape, axis)
        return position_of(place.ctx, lax.rem(i, rows), block_len, n_ctx)

    total_blocks = n_ctx // BLOCK

    def serve(name, k):
        a_gather.each(name, k)
        s_gather.each(name, k)

    def kv_loads(b):
        side = lax.rem(b, 2)
        return [load_rows(ref.at[pl.ds(b * BLOCK, BLOCK)], kvbuf.at[side, i], csems.at[side, i])
                for i, ref in enumerate((kall_ref, vall_ref))]

    def wide(v):
        return jnp.concatenate([v] * (many // 128), axis=1)

    for copy in kv_loads(0):
        copy.start()

    @pl.loop(0, total_blocks)
    def _(b):
        side = lax.rem(b, 2)

        @pl.when(b + 1 < total_blocks)
        def _():
            for copy in kv_loads(b + 1):
                copy.start()

        for copy in kv_loads(b):
            copy.wait()
        allowed = row_positions((1, many), 1, b * BLOCK) <= own_positions((2 * rows, 1), 0)

        @pl.loop(0, tiles)
        def _(t):
            cols = pl.ds(pl.multiple_of(t * 128, 128), 128)
            kt = kvbuf[side, 0, :, :, cols].reshape(many, 128)
            vt = kvbuf[side, 1, :, :, cols].reshape(many, 128)
            score = dot_nt(q2[t], kt)
            p = jnp.where(allowed, jnp.exp2(score * (LOG2E * scale) - wide(lse_ref[t])), 0.0)
            dp = dot_nt(do2[t], vt)
            ds = (p * (dp - wide(delta[t])) * scale).astype(BF)
            dq2[t] += dot32(ds, kt)

        @pl.when(b == total_blocks // 4)
        def _():
            serve("step_z", 1)

        @pl.when(b == total_blocks - 1)
        def _():
            serve("step_z", 2)
            serve("step_x", 0)

    own_v = load_rows(vall_ref.at[place.ctx], dobuf.at[0], lsems.at[0])
    own_v.start()
    own_v.wait()
    for t in range(tiles):
        v2[t] = stack_heads(dobuf[0, :, t * 128:(t + 1) * 128])
    for copy in own[1:]:
        copy.wait()

    def block_of(s, k, sub):
        return ((place.z - s * k) * subs + sub) * BLOCK

    def a_loads(side, first):
        return [load_rows(ref.at[pl.ds(first, BLOCK)], buf.at[side], rsems.at[side, i])
                for i, (ref, buf) in enumerate(((daball_ref, dabbuf), (qall_ref, qbuf), (statall_ref, stbuf)))]

    def m_loads(b):
        side = lax.rem(b, 2)
        return [load_rows(dmball_ref.at[pl.ds(b * BLOCK, BLOCK)], dmbuf.at[side], xsems.at[side, 0]),
                load_rows(hball_ref.at[pl.ds(b * BLOCK, BLOCK)], hbbuf.at[side], xsems.at[side, 1])]

    def keys_part(side, first):
        for copy in a_loads(side, first):
            copy.wait()
        dab = dabbuf[side].reshape(many, width)
        dobuf[...] = dot_nt(dab, wo_ref[...]).astype(BF).reshape(BLOCK, rows, channels)
        for j in range(BLOCK):
            rowstats[:, j * rows:(j + 1) * rows] = stbuf[side, j].astype(F32).T

        @pl.when(place.ctx < tiles)
        def _():
            gocc[...] += dot_tn(got_o[pl.ds(first, BLOCK)].reshape(many, 128), dab)

        allowed = own_positions((2 * rows, 1), 0) <= row_positions((1, many), 1, first)
        heads = 2 * tiles

        @pl.loop(0, tiles)
        def _(t):
            cols = pl.ds(pl.multiple_of(t * 128, 128), 128)
            qt = qbuf[side, :, :, cols].reshape(many, 128)
            dot_ = dobuf[:, :, cols].reshape(many, 128)

            def both_rows(parts, at):
                def one(h):
                    row = rowstats[pl.ds(at * heads + h, 1), :]
                    for i in range(1, parts):
                        row = row + rowstats[pl.ds((at + i) * heads + h, 1), :]
                    return jnp.broadcast_to(row, (rows, many))
                return jnp.concatenate([one(2 * t), one(2 * t + 1)], axis=0)

            score = dot_nt(k2[t], qt)
            p = jnp.where(allowed, jnp.exp2(score * (LOG2E * scale) - both_rows(3, 0)), 0.0)
            dp = dot_nt(v2[t], dot_)
            ds = (p * (dp - both_rows(2, 3)) * scale).astype(BF)
            dv2[t] += dot32(p.astype(BF), dot_)
            dk2[t] += dot32(ds, qt)

    def hidden_part(side):
        hb = hbbuf[side].reshape(many, width)
        dm = dmbuf[side].reshape(many, width)
        us, gs = us_ref[:, win], gs_ref[:, win]
        u = dot32(hb, wuw[...])
        g = dot32(hb, wgw[...])
        dgated = dot_nt(dm, wdw[...])
        a, c = u * us, g * gs
        s = lax.logistic(c)
        cs = c * s
        r = s * (1.0 + c * (1.0 - s))
        da = dgated * cs
        dc = dgated * a * r
        colu[...] += jnp.sum((da * u).reshape(many // 8, 8, window), axis=0)
        colg[...] += jnp.sum((dc * g).reshape(many // 8, 8, window), axis=0)
        gu[...] += dot_tn((da * us).astype(BF), hb)
        gg[...] += dot_tn((dc * gs).astype(BF), hb)
        gd[...] += dot_tn((a * cs).astype(BF), dm)

    def hidden_all():
        for copy in m_loads(0):
            copy.start()

        @pl.loop(0, total_blocks)
        def _(b):
            @pl.when(b + 1 < total_blocks)
            def _():
                for copy in m_loads(b + 1):
                    copy.start()

            for copy in m_loads(b):
                copy.wait()
            hidden_part(lax.rem(b, 2))

            serve("step_z", b + 3)
            serve("step_x", b + 1)
            serve("step_y", b + 1)
            serve("step_yx", b)
            serve("step_c", b - 1)

    def both(k, fn):
        for s in (1, -1):
            @pl.when(a_gather.parts[0].exists(s, k))
            def _():
                @pl.loop(0, subs)
                def _(sub):
                    fn(0 if s > 0 else 1, block_of(s, k, sub))

    def begin(loads):
        for copy in loads:
            copy.start()

    def keys_full(side, first):
        begin(a_loads(side, first))
        keys_part(side, first)

    hidden_all()

    gdown_ref[...] = gd[pl.ds(offset, mine), :]
    comb[0:mine] = gu[pl.ds(offset, mine), :]
    comb[mine:2 * mine] = gg[pl.ds(offset, mine), :]
    comb[2 * mine:] = jnp.zeros((comb.shape[0] - 2 * mine, width), F32)
    transposed(comb, turned, BF)
    part = width // n_ctx

    def row_block(ref, size):
        return lambda dest: ref.at[pl.ds(pl.multiple_of(dest * size, 8), size)]

    if aligned:
        u_scatter = Scatter(place, row_block(turned, part), lambda sender: got_u.at[sender], usems, n_ctx, n_ctx)
        u_scatter.start()
    shift = lax.rem(window - offset, window)
    gus_ref[...] = pltpu.roll(jnp.broadcast_to(jnp.sum(colu[...], axis=0, keepdims=True), (8, window)), shift, 1)
    ggs_ref[...] = pltpu.roll(jnp.broadcast_to(jnp.sum(colg[...], axis=0, keepdims=True), (8, window)), shift, 1)

    o_scatter.wait()

    @pl.loop(0, place.line)
    def _(k):
        serve("step_c", total_blocks - 1 + k)
        if subs == 1:
            both(k, lambda side, first: begin(a_loads(side, first)))
            both(k, keys_part)
        else:
            both(k, keys_full)

    if out_aligned:
        g_scatter = UnitScatter(place, gocc, gout_ref, ssems.at[0], ssems.at[1], tiles, 16, channels // n_ctx // 8)
        g_scatter.start()

    for t in range(tiles):
        cols = slice(t * 128, (t + 1) * 128)
        scales = qs_ref[:, cols]
        grad_scale = jnp.zeros((1, 128), F32)
        for n, (raw_ref, grads) in enumerate(((qraw_ref, dq2), (kraw_ref, dk2))):
            raw = raw_ref[:, cols]
            inv = head_rms(raw)
            normed = raw * inv
            grad = join_heads(grads[t])
            grad_scale = grad_scale + jnp.sum(grad * normed, axis=0, keepdims=True)
            e = grad * scales
            dqkv[n * tiles + t] = ((e - normed * pair_mean(normed * e)) * inv).astype(BF)
        small_row[:, cols] = grad_scale
        dqkv[2 * tiles + t] = join_heads(dv2[t]).astype(BF)
    t_scatter = Scatter(place, lambda dest: dqkv.at[dest], lambda sender: got_t.at[sender], tsems, 3 * tiles, n_ctx)
    t_scatter.start()
    head_part = channels // n_ctx
    for i in range(n_ctx):
        small[i, 0:1, 0:part] = gfs_ref[:, i * part:(i + 1) * part]
        small[i, 1:2, 0:part] = gas_ref[:, i * part:(i + 1) * part]
        small[i, 2:3, 0:head_part] = small_row[:, i * head_part:(i + 1) * head_part]
    n_scatter = Scatter(place, lambda dest: small.at[dest], lambda sender: got_s.at[sender], nsems, n_ctx, n_ctx)
    n_scatter.start()

    def input_terms(cols):
        total = None
        for n, w_ref in enumerate((wq_ref, wk_ref, wv_ref)):
            grad = jnp.concatenate([dqkv[n * tiles + t] for t in range(tiles)], axis=1)
            term = dot_nt(grad, w_ref[cols, :])
            total = term if total is None else total + term
        return total

    pl.when(place.ctx < 3 * tiles)(load_rows(xall_ref.at[pl.ds(0, BLOCK)], hbbuf.at[0], xsems.at[0, 0]).start)
    exchange(place, input_terms, dx_ref, sbuf, rbuf, esems)
    dx_ref[...] += dxr_ref[...]

    t_scatter.wait()

    @pl.when(place.ctx < 3 * tiles)
    def _():
        accq[...] = jnp.zeros_like(accq)

        def x_load(b):
            side = lax.rem(b, 2)
            return load_rows(xall_ref.at[pl.ds(b * BLOCK, BLOCK)], hbbuf.at[side], xsems.at[side, 0])

        @pl.loop(0, total_blocks)
        def _(b):
            @pl.when(b + 1 < total_blocks)
            def _():
                x_load(b + 1).start()

            x_load(b).wait()
            accq[...] += dot_tn(got_t[pl.ds(b * BLOCK, BLOCK)].reshape(many, 128),
                                hbbuf[lax.rem(b, 2)].reshape(many, width))

        transposed(accq, turned_qkv, BF)

    if aligned:
        q_scatter = Scatter(place, row_block(turned_qkv, part), lambda sender: got_q.at[sender], vsems, n_ctx, 3 * tiles)
        q_scatter.start()
        u_scatter.wait()
        q_scatter.wait()
        u_scatter.sent()
        q_scatter.sent()
    if out_aligned:
        g_scatter.wait()
        g_scatter.sent()
    a_gather.finish()
    s_gather.finish()
    o_scatter.sent()
    t_scatter.sent()
    n_scatter.wait()
    n_scatter.sent()


def backward_attention(dab, grad_ff_step, grad_attn_step, q_raw, k_raw, lse, attended, dxr, qk_scale, up_scale, gate_scale,
                       w_out, w_query, w_key, w_value, x_all, q_all, k_all, v_all, hb_all, dmb_all, w_up, w_gate, w_down,
                       n_ctx, collective_id, cut):
    rows, width = dxr.shape
    channels = q_raw.shape[1]
    tiles = channels // 128
    hidden = up_scale.shape[1]
    mine = hidden // n_ctx
    part = width // n_ctx
    aligned = part % 16 == 0
    out_rows = channels // n_ctx
    out_aligned = out_rows % 8 == 0
    window = 256
    pair = -(-2 * mine // 128) * 128
    count = width // EXCHANGE
    many = BLOCK * rows
    n_blocks = n_ctx
    shape = jax.ShapeDtypeStruct
    dma = pltpu.SemaphoreType.DMA
    V = pltpu.VMEM
    stack = lambda dtype: V((tiles, 2 * rows, 128), dtype)
    outs = (
        shape((rows, width), F32),
        shape((3 * tiles, part, 128), BF), shape((out_rows, width), F32), shape((n_ctx, part, pair), BF),
        shape((mine, width), F32), shape((n_ctx, 8, 128), F32), shape((8, window), F32), shape((8, window), F32),
        shape((n_ctx, rows, width), BF), shape((n_ctx, rows, STATS), BF),
        shape((width, pair), BF), shape((width, 128), BF), shape((128, width), F32))
    return pl.pallas_call(
        functools.partial(bwd_kernel, n_ctx, cut, aligned, out_aligned),
        out_shape=outs,
        in_specs=[vmem_spec()] * 15 + [any_spec()] * 9,
        out_specs=(vmem_spec(),) * 8 + (hbm_spec(),) * 2 + (vmem_spec(),) * 3,
        scratch_shapes=[
            gather_sems(n_ctx, cut), gather_sems(n_ctx, ((rows, rows, rows),)), dma((5,)), dma((2, 2)), dma((2, count)),
            dma((2, n_ctx)), dma((2, n_ctx)), dma((2, n_ctx)), dma((2, 3)), dma((2, n_ctx)), dma((2, 16)), dma((2, 2)), dma((2, n_ctx)),
            V((2, BLOCK, rows, width), BF), V((2, BLOCK, rows, width), BF), V((2, BLOCK, rows, width), BF), V((2, BLOCK, rows, STATS), BF),
            V((2, BLOCK, rows, channels), BF), V((2, 2, BLOCK, rows, channels), BF), V((BLOCK, rows, channels), BF),
            V((STATS, many), F32), V((rows, STATS), BF), stack(F32), stack(BF), stack(BF), stack(BF), stack(BF), stack(F32), stack(F32), stack(F32),
            V((width, window), BF), V((width, window), BF), V((window, width), BF),
            V((window, width), F32), V((window, width), F32), V((window, width), F32),
            V((8, window), F32), V((8, window), F32), V((pair, width), F32), V((n_ctx, 8, 128), F32), V((1, channels), F32),
            V((3 * tiles, rows, 128), BF), V((n_ctx, rows, 128), BF), V((n_ctx, rows, 128), BF), V((tiles, rows, 128), BF),
            V((128, width), F32),
            V((count, rows, EXCHANGE), BF), V((count, rows, EXCHANGE), BF)],
        compiler_params=pltpu.CompilerParams(collective_id=collective_id, has_side_effects=True,
                                             vmem_limit_bytes=40 << 20),
        cost_estimate=pl.CostEstimate(flops=20 * 10 ** 9, bytes_accessed=60 * 10 ** 6, transcendentals=6 * 10 ** 6),
        name="backward_attention",
    )(dab, grad_ff_step, grad_attn_step, q_raw, k_raw, lse, attended, dxr, qk_scale, up_scale, gate_scale,
      w_out, w_query, w_key, w_value, x_all, q_all, k_all, v_all, hb_all, dmb_all, w_up, w_gate, w_down)


def last_kernel(result_ref, dx_ref, gotq_ref, gout_ref, gotu_ref, gdown_ref, gots_ref, gus_ref, ggs_ref,
                o_result, o_dx, o_gq, o_gk, o_gv, o_gout, o_gup, o_ggate, o_gdown, o_gqs, o_gus, o_ggs, o_gas, o_gfs):
    o_result[...] = result_ref[...]
    o_dx[...] = dx_ref[...]
    o_gout[...] = gout_ref[...]
    o_gdown[...] = gdown_ref[...]
    mine = o_gus.shape[1]
    tiles = o_gq.shape[1] // 128
    for j in range(gotu_ref.shape[0]):
        o_gup[:, j * mine:(j + 1) * mine] = gotu_ref[j, :, 0:mine].astype(F32)
        o_ggate[:, j * mine:(j + 1) * mine] = gotu_ref[j, :, mine:2 * mine].astype(F32)
    for n, ref in enumerate((o_gq, o_gk, o_gv)):
        for t in range(tiles):
            ref[:, t * 128:(t + 1) * 128] = gotq_ref[n * tiles + t].astype(F32)
    total = jnp.sum(gots_ref[...], axis=0)
    for row, ref in enumerate((o_gfs, o_gas, o_gqs)):
        ref[...] = total[row:row + 1, 0:ref.shape[1]]
    o_gus[...] = gus_ref[0:1, 0:mine]
    o_ggs[...] = ggs_ref[0:1, 0:mine]


def last_step(parts, n_ctx, channels, hidden):
    width = parts[1].shape[1]
    part, mine = width // n_ctx, hidden // n_ctx
    shape = jax.ShapeDtypeStruct
    outs = [shape(parts[0].shape, BF), shape(parts[1].shape, F32)] + [shape((part, channels), F32)] * 3
    outs += [shape(parts[3].shape, F32)] + [shape((part, hidden), F32)] * 2 + [shape((mine, width), F32)]
    outs += [shape((1, channels // n_ctx), F32)] + [shape((1, mine), F32)] * 2 + [shape((1, part), F32)] * 2
    return pl.pallas_call(
        last_kernel, out_shape=tuple(outs), in_specs=[vmem_spec()] * len(parts), out_specs=(vmem_spec(),) * len(outs),
        compiler_params=pltpu.CompilerParams(vmem_limit_bytes=32 << 20), name="last_step")(*parts)


CUT = ((64, 48, 32), (64, 48, 48))


def shards(layer_input, w_query, w_key, w_value, w_out, w_up, w_gate, w_down, qk_scale, up_scale,
           gate_scale, attention_step, feedforward_step, cotangent):
    n_ctx = lax.axis_size("ctx")
    ctx = lax.axis_index("ctx")
    rows = 2 * layer_input.shape[2]
    width = layer_input.shape[3]
    channels = w_query.shape[1]
    hidden = w_up.shape[1]
    tiles = channels // 128
    x = layer_input.reshape(rows, width)
    flat = lambda v: v.reshape(1, -1)
    x_all, q_all, k_all, v_all, q_raw, k_raw, attended, lse, hidden_one, branch_attn = forward_attention(
        x, w_query, w_key, w_value, flat(qk_scale), w_out, flat(attention_step), n_ctx, 0, CUT)
    hb_all, dmb_all, result, dab, input_res, grad_ff_step, grad_attn_step = feed_forward(
        hidden_one, branch_attn, x, cotangent.reshape(rows, width), flat(feedforward_step), flat(attention_step),
        flat(up_scale), flat(gate_scale), w_up, w_gate, w_down, n_ctx, 1, CUT)
    (input_grad, got_q, grad_out, got_u, grad_down, got_s, gus, ggs,
     _, _, turned, turned_qkv, gocc) = backward_attention(
        dab, grad_ff_step, grad_attn_step, q_raw, k_raw, lse, attended, input_res, flat(qk_scale), flat(up_scale),
        flat(gate_scale), w_out, w_query, w_key, w_value, x_all, q_all, k_all, v_all, hb_all, dmb_all,
        w_up, w_gate, w_down, n_ctx, 2, CUT)
    part = width // n_ctx
    if part % 16:
        turned, turned_qkv = lax.optimization_barrier((turned, turned_qkv))
        got_u = lax.all_to_all(turned, "ctx", 0, 0, tiled=True).reshape(n_ctx, part, -1)
        got_q = lax.all_to_all(turned_qkv, "ctx", 0, 0, tiled=True).reshape(n_ctx, part, 128)[:3 * tiles]
    if (channels // n_ctx) % 8:
        gocc = lax.optimization_barrier(gocc)
        whole = jnp.zeros((n_ctx, 128, width), F32)
        whole = lax.dynamic_update_slice_in_dim(whole, gocc[None], ctx, 0)[:tiles]
        grad_out = lax.psum_scatter(whole.reshape(channels, width), "ctx", scatter_dimension=0, tiled=True)
    outs = last_step((result, input_grad, got_q, grad_out, got_u, grad_down, got_s, gus, ggs), n_ctx, channels, hidden)
    tokens = tuple(v.reshape(layer_input.shape) for v in outs[:2])
    return tokens + tuple(outs[2:9]) + tuple(v.reshape(-1) for v in outs[9:])


def solution(mesh):
    placed = (
        P("ctx", None, None, None),
        P(None, "wa"),
        P(None, "wa"),
        P(None, "wa"),
        P("wa", None),
        P(None, "wa"),
        P(None, "wa"),
        P("wa", None),
        P("wa"),
        P("wa"),
        P("wa"),
        P(),
        P(),
        P("ctx", None, None, None),
    )
    return jax.shard_map(
        shards,
        mesh=mesh,
        in_specs=placed,
        out_specs=(
            P("ctx", None, None, None),
            P("ctx", None, None, None),
            P("ctx", "wa"),
            P("ctx", "wa"),
            P("ctx", "wa"),
            P(("wa", "ctx"), None),
            P("ctx", "wa"),
            P("ctx", "wa"),
            P(("wa", "ctx"), None),
            P(("wa", "ctx")),
            P(("wa", "ctx")),
            P(("wa", "ctx")),
            P("ctx"),
            P("ctx"),
        ),
        check_vma=False,
    )
```

```python
import functools
from functools import partial
import math

import jax
import jax.numpy as jnp
from jax import lax
from jax.experimental import pallas as pl
from jax.experimental.pallas import tpu as pltpu
from jax.sharding import PartitionSpec as P

HD = 64
MESH = pl.DeviceIdType.MESH


def layout_of(n_ctx):
    chips = n_ctx // 2
    across = 2 if chips <= 8 else 4
    return chips // across, across


class Place:
    def __init__(self, n_ctx):
        self.n_ctx = n_ctx
        self.line, self.across = layout_of(n_ctx)
        self.ctx = lax.axis_index("ctx")
        self.wa = lax.axis_index("wa")
        self.core = lax.rem(self.ctx, 2)
        chip = lax.div(self.ctx, 2)
        self.x = lax.rem(chip, self.across)
        self.z = lax.div(chip, self.across)

    def index(self, z, x, core):
        return (z * self.across + x) * 2 + core

    def at(self, z, x, core):
        return (self.index(z, x, core), self.wa)

    def sibling(self):
        return self.at(self.z, self.x, 1 - self.core)

    def partner(self):
        return (self.ctx, 1 - self.wa)

    def inside(self, z):
        return (z >= 0) & (z < self.line)

    def column(self, shift):
        return lax.rem(self.x + shift, self.across)

    def barrier(self):
        sem = pltpu.get_barrier_semaphore()

        def signal(device):
            pl.semaphore_signal(sem, inc=1, device_id=device, device_id_type=MESH)

        signal(self.sibling())
        signal(self.partner())
        for shift in range(1, self.across):
            signal(self.at(self.z, self.column(shift), self.core))
        count = jnp.int32(self.across + 1)
        for step in (-1, 1):
            near = self.inside(self.z + step)
            pl.when(near)(functools.partial(signal, self.at(self.z + step, self.x, self.core)))
            count = count + near.astype(jnp.int32)
        pl.semaphore_wait(sem, count)

    def barrier_all(self):
        sem = pltpu.get_barrier_semaphore()
        pl.semaphore_signal(sem, inc=1, device_id=self.partner(), device_id_type=MESH)

        @pl.loop(1, self.n_ctx)
        def _(shift):
            other = lax.rem(self.ctx + shift, self.n_ctx)
            pl.semaphore_signal(sem, inc=1, device_id=(other, self.wa), device_id_type=MESH)

        pl.semaphore_wait(sem, self.n_ctx)


class Gather:
    def __init__(self, place, out, sems, base, first, rows, z_rows, x_rows):
        self.p = place
        self.out = out
        self.sems = sems
        self.base = base
        self.first, self.rows = first, rows
        self.z_rows, self.x_rows = z_rows, x_rows
        self.slots = 2 * place.line

    @staticmethod
    def sem_count(n_ctx):
        line, across = layout_of(n_ctx)
        return 2 * line * 3 * across

    def sem(self, kind, s, k, shift=0):
        kinds = self.p.across - 1
        order = {"z": 0, "y": 1, "c": 2, "x": 3, "yx": 3 + kinds, "cx": 3 + 2 * kinds}[kind]
        return self.base + (order + shift) * self.slots + (0 if s > 0 else self.p.line) + k

    def copy(self, sem, block, start, size, device):
        view = self.out.at[block, pl.ds(pl.multiple_of(self.first + start, 16), size)]
        return pltpu.make_async_remote_copy(
            src_ref=view, dst_ref=view, send_sem=self.sems.at[0, sem], recv_sem=self.sems.at[1, sem],
            device_id=device, device_id_type=MESH)

    def exists(self, s, k):
        ok = self.p.inside(self.p.z - s * k) & (k >= 0) & (k < self.p.line)
        return ok if s > 0 else ok & (k > 0)

    def d_z(self, s, k, block, device):
        return self.copy(self.sem("z", s, k), block, self.p.wa * (self.rows - self.z_rows), self.z_rows, device)

    def d_x(self, s, k, shift, block, device):
        return self.copy(self.sem("x", s, k, shift - 1), block, self.p.wa * (self.rows - self.x_rows), self.x_rows, device)

    def d_y(self, kind, s, k, shift, block, size, sending):
        side = self.p.wa if sending else 1 - self.p.wa
        return self.copy(self.sem(kind, s, k, shift), block, side * size, self.rows - size, self.p.partner())

    def d_c(self, kind, s, k, shift, block):
        return self.copy(self.sem(kind, s, k, shift), block, 0, self.rows, self.p.sibling())

    def ok_forward(self, s, k):
        p = self.p
        return p.inside(p.z - s * k) & p.inside(p.z + s) & (k >= 0) & (k + 1 < p.line)

    def step_z(self, k):
        p = self.p
        me = (p.ctx, p.wa)
        for s in (1, -1):
            block = p.index(p.z - s * k, p.x, p.core)

            @pl.when(self.exists(s, k) & (k > 0))
            def _():
                self.d_z(s, k, block, me).wait_recv()

            @pl.when(self.ok_forward(s, k))
            def _():
                self.d_z(s, k + 1, block, p.at(p.z + s, p.x, p.core)).start()

            @pl.when(self.exists(s, k))
            def _():
                for shift in range(1, p.across):
                    self.d_x(s, k, shift, block, p.at(p.z, p.column(shift), p.core)).start()
                if s > 0:
                    @pl.when(k == 0)
                    def _():
                        self.d_c("c", s, k, 0, block).start()

                if self.z_rows < self.rows:
                    @pl.when(k > 0)
                    def _():
                        self.d_y("y", s, k, 0, block, self.z_rows, True).start()

    def step_y(self, k):
        p = self.p
        for s in (1, -1):
            @pl.when(self.exists(s, k) & (k > 0))
            def _():
                block = p.index(p.z - s * k, p.x, p.core)
                if self.z_rows < self.rows:
                    self.d_y("y", s, k, 0, block, self.z_rows, False).wait_recv()
                self.d_c("c", s, k, 0, block).start()

    def step_x(self, k):
        p = self.p
        for s in (1, -1):
            @pl.when(self.exists(s, k))
            def _():
                for shift in range(1, p.across):
                    block = p.index(p.z - s * k, p.column(p.across - shift), p.core)
                    self.d_x(s, k, shift, block, (p.ctx, p.wa)).wait_recv()
                    if self.x_rows < self.rows:
                        self.d_y("yx", s, k, shift - 1, block, self.x_rows, True).start()

    def step_yx(self, k):
        p = self.p
        for s in (1, -1):
            @pl.when(self.exists(s, k))
            def _():
                for shift in range(1, p.across):
                    block = p.index(p.z - s * k, p.column(p.across - shift), p.core)
                    if self.x_rows < self.rows:
                        self.d_y("yx", s, k, shift - 1, block, self.x_rows, False).wait_recv()
                    self.d_c("cx", s, k, shift - 1, block).start()

    def step_c(self, k):
        p = self.p
        for s in (1, -1):
            @pl.when(self.exists(s, k))
            def _():
                self.d_c("c", s, k, 0, p.index(p.z - s * k, p.x, 1 - p.core)).wait_recv()
                for shift in range(1, p.across):
                    block = p.index(p.z - s * k, p.column(p.across - shift), 1 - p.core)
                    self.d_c("cx", s, k, shift - 1, block).wait_recv()

    def finish(self):
        p = self.p

        @pl.loop(0, p.line)
        def _(k):
            for s in (1, -1):
                block = p.index(p.z - s * k, p.x, p.core)

                @pl.when(self.ok_forward(s, k))
                def _():
                    self.d_z(s, k + 1, block, p.at(p.z + s, p.x, p.core)).wait_send()

                @pl.when(self.exists(s, k))
                def _():
                    self.d_c("c", s, k, 0, block).wait_send()
                    if self.z_rows < self.rows:
                        @pl.when(k > 0)
                        def _():
                            self.d_y("y", s, k, 0, block, self.z_rows, True).wait_send()
                    for shift in range(1, p.across):
                        self.d_x(s, k, shift, block, p.at(p.z, p.column(shift), p.core)).wait_send()
                        other = p.index(p.z - s * k, p.column(p.across - shift), p.core)
                        if self.x_rows < self.rows:
                            self.d_y("yx", s, k, shift - 1, other, self.x_rows, True).wait_send()
                        self.d_c("cx", s, k, shift - 1, other).wait_send()


class Pieces:
    def __init__(self, place, out, sems, cut):
        n = Gather.sem_count(place.n_ctx)
        self.p = place
        self.parts = []
        first = 0
        for number, (rows, z_rows, x_rows) in enumerate(cut):
            self.parts.append(Gather(place, out, sems, number * n, first, rows, z_rows, x_rows))
            first += rows

    def each(self, name, k):
        for part in self.parts:
            getattr(part, name)(k)

    def step(self, t):
        self.each("step_z", t)
        for part in self.parts:
            part.step_x(t - 1)
            part.step_y(t - 1)
        self.each("step_yx", t - 2)
        self.each("step_c", t - 3)

    def step_count(self):
        return self.p.line + 3

    def finish(self):
        for part in self.parts:
            part.finish()


def gather_sems(n_ctx, cut):
    return pltpu.SemaphoreType.DMA((2, len(cut) * Gather.sem_count(n_ctx)))


NORM_EPS = 1e-06
BF = jnp.bfloat16
F32 = jnp.float32


def dot32(a, b):
    return jnp.dot(a, b, preferred_element_type=F32)


def dot_tn(a, b):
    return lax.dot_general(a, b, (((0,), (0,)), ((), ())), preferred_element_type=F32)


def dot_nt(a, b):
    return lax.dot_general(a, b, (((1,), (1,)), ((), ())), preferred_element_type=F32)


def row_mean(v):
    return jnp.mean(v, axis=-1, keepdims=True)


def inv_rms(v):
    return lax.rsqrt(row_mean(v * v) + NORM_EPS)


def rms_back(v, inv, grad):
    n = v * inv
    return (grad - n * row_mean(n * grad)) * inv


def pair_mean(v):
    row = lax.broadcasted_iota(jnp.int32, (128, 128), 0)
    col = lax.broadcasted_iota(jnp.int32, (128, 128), 1)
    ones = jnp.where((row < HD) == (col < HD), 1.0 / HD, 0.0).astype(BF)
    high = v.astype(BF)
    lowp = (v - high.astype(F32)).astype(BF)
    return dot32(high, ones) + dot32(lowp, ones)


def head_rms(v):
    return lax.rsqrt(pair_mean(v * v) + NORM_EPS)


def position_of(shard, index, block_len, n_ctx):
    late = index >= block_len
    block = jnp.where(late, 2 * n_ctx - 1 - shard, shard)
    return block * block_len + jnp.where(late, index - block_len, index)


def stack_heads(v):
    first = lax.broadcasted_iota(jnp.int32, v.shape, 1) < HD
    zero = jnp.zeros_like(v)
    return jnp.concatenate([jnp.where(first, v, zero), jnp.where(first, zero, v)], axis=0)


def join_heads(v):
    rows = v.shape[0] // 2
    first = lax.broadcasted_iota(jnp.int32, (rows, 128), 1) < HD
    return jnp.where(first, v[:rows], v[rows:])


def load_rows(src, dst, sem):
    return pltpu.make_async_copy(src, dst, sem)


LOG2E = 1.4426950408889634
EXCHANGE = 256
TOGETHER = 4


def fwd_kernel(n_ctx, cut, x_ref, qs_ref, step_ref, wq_hbm, wk_hbm, wv_hbm, wo_hbm,
               xall_ref, qall_ref, kall_ref, vall_ref, qraw_ref, kraw_ref, o_ref, lse_ref, h1_ref, ha_ref,
               gsems, lsems, wsems, esems, psems, wq_ref, wk_ref, wv_ref, wo_ref, xbuf, qbuf, kbuf, vbuf, q2, acc, lpart, sbuf, rbuf):
    place = Place(n_ctx)
    rows, width = x_ref.shape
    block_len = rows // 2
    channels = wq_ref.shape[1]
    tiles = channels // 128
    group = 2 * place.across
    plane = group * rows
    gather = Pieces(place, xall_ref, gsems, cut)
    own = load_rows(x_ref, xall_ref.at[place.ctx], lsems.at[0])
    own.start()
    weights = [load_rows(src, dst, psems.at[i]) for i, (src, dst) in enumerate(
        ((wq_hbm, wq_ref), (wk_hbm, wk_ref), (wv_hbm, wv_ref), (wo_hbm, wo_ref)))]
    for copy in weights:
        copy.start()
    place.barrier()
    own.wait()
    gather.each("step_z", 0)
    for copy in weights:
        copy.wait()

    xv = x_ref[...]
    kraw_ref[...] = dot32(xv, wk_ref[...])
    qraw_ref[...] = dot32(xv, wq_ref[...])
    for t in range(tiles):
        cols = slice(t * 128, (t + 1) * 128)
        raw = qraw_ref[:, cols]
        q2[t] = stack_heads((raw * head_rms(raw) * qs_ref[:, cols]).astype(BF))
    acc[...] = jnp.zeros_like(acc)
    lpart[...] = jnp.zeros_like(lpart)

    def plane_of(s, k):
        return place.z - s * k

    def hbm(ref, zp):
        return ref.at[pl.ds(zp * group, group)]

    def x_load(s, k):
        side = 0 if s > 0 else 1
        return load_rows(hbm(xall_ref, plane_of(s, k)), xbuf.at[side], lsems.at[1 + side])

    def stores(s, k):
        side = 0 if s > 0 else 1
        zp = plane_of(s, k)
        return [load_rows(buf.at[side], hbm(ref, zp), wsems.at[side, i])
                for i, (buf, ref) in enumerate(((qbuf, qall_ref), (kbuf, kall_ref), (vbuf, vall_ref)))]

    def project(s, k):
        side = 0 if s > 0 else 1
        x_load(s, k).wait()

        @pl.loop(0, group // TOGETHER)
        def _(r):
            some = pl.ds(r * TOGETHER, TOGETHER)
            xr = xbuf[side, some].reshape(TOGETHER * rows, width)
            for w_ref, buf in ((wq_ref, qbuf), (wk_ref, kbuf)):
                raw = dot32(xr, w_ref[...])
                for t in range(tiles):
                    cols = slice(t * 128, (t + 1) * 128)
                    part = raw[:, cols]
                    normed = (part * head_rms(part) * qs_ref[:, cols]).astype(BF)
                    buf[side, some, :, cols] = normed.reshape(TOGETHER, rows, 128)
            vbuf[side, some] = dot32(xr, wv_ref[...]).astype(BF).reshape(TOGETHER, rows, channels)

        for copy in stores(s, k):
            copy.start()

    def attend(s, k):
        side = 0 if s > 0 else 1
        zp = plane_of(s, k)
        qi = lax.broadcasted_iota(jnp.int32, (2 * rows, 1), 0)
        qi = jnp.where(qi >= rows, qi - rows, qi)
        qpos = position_of(place.ctx, qi, block_len, n_ctx)
        ki = lax.broadcasted_iota(jnp.int32, (1, plane), 1)
        kpos = position_of(zp * group + lax.div(ki, rows), lax.rem(ki, rows), block_len, n_ctx)
        allowed = kpos <= qpos

        @pl.loop(0, tiles)
        def _(t):
            cols = pl.ds(pl.multiple_of(t * 128, 128), 128)
            kt = kbuf[side, :, :, cols].reshape(plane, 128)
            vt = vbuf[side, :, :, cols].reshape(plane, 128)
            score = dot_nt(q2[t], kt)
            e = jnp.where(allowed, jnp.exp2(score * (LOG2E / math.sqrt(HD))), 0.0)
            total = e[:, :128]
            for j in range(1, plane // 128):
                total = total + e[:, j * 128:(j + 1) * 128]
            lpart[t] += total
            acc[t] += dot32(e.astype(BF), vt)

        for copy in stores(s, k):
            copy.wait()

    def both(k, fn):
        for s in (1, -1):
            pl.when(gather.parts[0].exists(s, k))(functools.partial(fn, s, k))

    gather.each("step_z", 1)

    @pl.loop(1, place.line + 2)
    def _(t):
        gather.each("step_x", t - 1)
        gather.each("step_y", t - 1)
        both(t - 2, attend)
        gather.each("step_yx", t - 1)
        gather.each("step_c", t - 1)
        both(t - 1, lambda s, k: x_load(s, k).start())
        gather.each("step_z", t + 1)
        both(t - 1, project)

    for t in range(tiles):
        mass = jnp.sum(lpart[t], axis=1, keepdims=True)
        o_ref[:, t * 128:(t + 1) * 128] = join_heads(acc[t] / mass)
        lse_ref[t] = jnp.broadcast_to(jnp.log(mass) * LOG2E, (2 * rows, 128))

    exchange(place, lambda cols: dot32(o_ref[...].astype(BF), wo_ref[:, cols]), ha_ref, sbuf, rbuf, esems)
    ha = ha_ref[...]
    xf = x_ref[...].astype(F32)
    w = xf + step_ref[...] * (ha * inv_rms(ha) - xf)
    h1_ref[...] = w * inv_rms(w)
    gather.finish()


def exchange(place, term, sum_ref, sbuf, rbuf, esems, between=None):
    width = sum_ref.shape[1]

    def copy(n):
        return pltpu.make_async_remote_copy(
            src_ref=sbuf.at[n], dst_ref=rbuf.at[n], send_sem=esems.at[0, n], recv_sem=esems.at[1, n],
            device_id=place.partner(), device_id_type=MESH)

    count = width // EXCHANGE
    for n in range(count):
        sbuf[n] = term(slice(n * EXCHANGE, (n + 1) * EXCHANGE)).astype(BF)
        copy(n).start()
    if between is not None:
        between()
    for n in range(count):
        copy(n).wait()
        sum_ref[:, n * EXCHANGE:(n + 1) * EXCHANGE] = sbuf[n].astype(F32) + rbuf[n].astype(F32)


def vmem_spec():
    return pl.BlockSpec(memory_space=pltpu.VMEM)


def in_hbm(v):
    return pltpu.with_memory_space_constraint(v, pltpu.HBM)


def hbm_spec():
    return pl.BlockSpec(memory_space=pltpu.HBM)


def any_spec():
    return pl.BlockSpec(memory_space=pl.ANY)


def forward_attention(x, w_query, w_key, w_value, qk_scale, w_out, step, n_ctx, collective_id, cut):
    rows, width = x.shape
    channels = w_query.shape[1]
    tiles = channels // 128
    line, across = layout_of(n_ctx)
    group = 2 * across
    count = width // EXCHANGE
    shape = jax.ShapeDtypeStruct
    return pl.pallas_call(
        functools.partial(fwd_kernel, n_ctx, cut),
        out_shape=(pltpu.HBM((n_ctx, rows, width), BF),) + (pltpu.HBM((n_ctx, rows, channels), BF),) * 3
        + (shape((rows, channels), F32),) * 3 + (shape((tiles, 2 * rows, 128), F32),) + (shape((rows, width), F32),) * 2,
        in_specs=[vmem_spec()] * 3 + [hbm_spec()] * 4,
        out_specs=(hbm_spec(),) * 4 + (vmem_spec(),) * 6,
        scratch_shapes=[
            gather_sems(n_ctx, cut), pltpu.SemaphoreType.DMA((3,)), pltpu.SemaphoreType.DMA((2, 3)),
            pltpu.SemaphoreType.DMA((2, count)), pltpu.SemaphoreType.DMA((4,)),
            pltpu.VMEM((width, channels), BF), pltpu.VMEM((width, channels), BF), pltpu.VMEM((width, channels), BF),
            pltpu.VMEM((channels, width), BF),
            pltpu.VMEM((2, group, rows, width), BF),
            pltpu.VMEM((2, group, rows, channels), BF), pltpu.VMEM((2, group, rows, channels), BF),
            pltpu.VMEM((2, group, rows, channels), BF),
            pltpu.VMEM((tiles, 2 * rows, 128), BF), pltpu.VMEM((tiles, 2 * rows, 128), F32),
            pltpu.VMEM((tiles, 2 * rows, 128), F32),
            pltpu.VMEM((count, rows, EXCHANGE), BF), pltpu.VMEM((count, rows, EXCHANGE), BF)],
        compiler_params=pltpu.CompilerParams(collective_id=collective_id, has_side_effects=True,
                                             vmem_limit_bytes=32 << 20),
        cost_estimate=pl.CostEstimate(flops=12 * 10 ** 9, bytes_accessed=40 * 10 ** 6, transcendentals=3 * 10 ** 6),
        name="forward_attention",
    )(x, qk_scale, step, *(in_hbm(w) for w in (w_query, w_key, w_value, w_out)))


HIDDEN_CUT = 256


def mid_kernel(n_ctx, cut, h1_ref, ha_ref, x_ref, cot_ref, fs_ref, as_ref, us_ref, gs_ref, wu_ref, wg_ref, wd_ref,
               hball_ref, dmball_ref, out_ref, dab_ref, dxr_ref, gfs_ref, gas_ref,
               hsems, msems, lsems, wsems, e1sems, e2sems, wu, wg, wd, hbv, dmv, u_buf, g_buf, low_a, low_b, total,
               s1, r1, s2, r2):
    place = Place(n_ctx)
    rows, width = h1_ref.shape
    hidden = us_ref.shape[1]
    cuts = hidden // HIDDEN_CUT
    h_gather = Pieces(place, hball_ref, hsems, cut)
    m_gather = Pieces(place, dmball_ref, msems, cut)

    def part(n):
        return slice(n * HIDDEN_CUT, (n + 1) * HIDDEN_CUT)

    loads = [[load_rows(wu_ref.at[:, part(n)], wu.at[:, part(n)], wsems.at[0, n]),
              load_rows(wg_ref.at[:, part(n)], wg.at[:, part(n)], wsems.at[1, n])] for n in range(cuts)]
    down = [load_rows(wd_ref.at[part(n)], wd.at[part(n)], wsems.at[2, n]) for n in range(cuts)]
    for pair in loads:
        for copy in pair:
            copy.start()
    for copy in down:
        copy.start()
    hbv[...] = h1_ref[...].astype(BF)
    own = load_rows(hbv, hball_ref.at[place.ctx], lsems.at[0])
    own.start()
    place.barrier()
    own.wait()
    h_gather.each("step_z", 0)

    hb = hbv[...]
    for n in range(cuts):
        for copy in loads[n]:
            copy.wait()
        u = dot32(hb, wu[:, part(n)])
        g = dot32(hb, wg[:, part(n)])
        u_buf[:, part(n)] = u
        g_buf[:, part(n)] = g
        c = g * gs_ref[:, part(n)]
        low_a[:, part(n)] = (u * us_ref[:, part(n)] * (c * lax.logistic(c))).astype(BF)
        if n == cuts - 3:
            h_gather.each("step_z", 1)
    for copy in down:
        copy.wait()

    def serve_first():
        h_gather.each("step_x", 0)
        h_gather.each("step_z", 2)

    exchange(place, lambda cols: dot32(low_a[...], wd[:, cols]), total, s1, r1, e1sems, serve_first)
    h1 = h1_ref[...]
    fs = fs_ref[...]
    hm = total[...]
    m_inv = inv_rms(hm)
    step = hm * m_inv - h1
    z = h1 + fs * step
    z_inv = inv_rms(z)
    out_ref[...] = (z * z_inv).astype(BF)
    dz = rms_back(z, z_inv, cot_ref[...].astype(F32))
    gfs_ref[...] = jnp.sum(dz * step, axis=0, keepdims=True)
    dxr_ref[...] = (1.0 - fs) * dz
    dmv[...] = rms_back(hm, m_inv, fs * dz).astype(BF)
    own = load_rows(dmv, dmball_ref.at[place.ctx], lsems.at[1])
    own.start()
    own.wait()
    m_gather.each("step_z", 0)
    h_gather.each("step_z", 3)
    h_gather.each("step_x", 1)
    h_gather.each("step_y", 1)
    h_gather.each("step_yx", 0)

    dm = dmv[...]
    for n in range(cuts):
        dgated = dot_nt(dm, wd[part(n), :])
        u, g = u_buf[:, part(n)], g_buf[:, part(n)]
        us, gs = us_ref[:, part(n)], gs_ref[:, part(n)]
        c = g * gs
        s = lax.logistic(c)
        low_a[:, part(n)] = (dgated * (c * s) * us).astype(BF)
        low_b[:, part(n)] = (dgated * (u * us) * (s * (1.0 + c * (1.0 - s))) * gs).astype(BF)
        if n == cuts // 2:
            h_gather.each("step_x", 2)
            h_gather.each("step_y", 2)
            h_gather.each("step_yx", 1)
            h_gather.each("step_c", 0)

    m_gather.each("step_z", 1)

    def serve_second():
        h_gather.each("step_x", 3)
        h_gather.each("step_y", 3)
        m_gather.each("step_x", 0)
        h_gather.each("step_yx", 2)
        m_gather.each("step_z", 2)

    exchange(place, lambda cols: dot_nt(low_a[...], wu[cols, :]) + dot_nt(low_b[...], wg[cols, :]), total, s2, r2,
             e2sems, serve_second)
    m_gather.each("step_z", 3)
    m_gather.each("step_x", 1)
    m_gather.each("step_y", 1)
    m_gather.each("step_yx", 0)
    dh1 = dxr_ref[...] + total[...]
    xf = x_ref[...].astype(F32)
    step_size = as_ref[...]
    ha = ha_ref[...]
    a_inv = inv_rms(ha)
    step = ha * a_inv - xf
    w = xf + step_size * step
    dw = rms_back(w, inv_rms(w), dh1)
    gas_ref[...] = jnp.sum(dw * step, axis=0, keepdims=True)
    dxr_ref[...] = (1.0 - step_size) * dw
    dab_ref[...] = rms_back(ha, a_inv, step_size * dw).astype(BF)

    @pl.loop(4, place.line)
    def _(k):
        for name in ("step_z", "step_x", "step_y"):
            h_gather.each(name, k)
        m_gather.each("step_z", k)

    @pl.loop(2, place.line + 1)
    def _(k):
        m_gather.each("step_x", k)
        m_gather.each("step_y", k)
        m_gather.each("step_yx", k - 1)

        @pl.when(k > 2)
        def _():
            h_gather.each("step_yx", k)
        h_gather.each("step_c", k - 1)
        m_gather.each("step_c", k - 2)

    m_gather.each("step_c", place.line - 1)
    h_gather.finish()
    m_gather.finish()


def feed_forward(hidden_one, branch_attn, x, cotangent, ff_step, attn_step, up_scale, gate_scale, w_up, w_gate, w_down,
                 n_ctx, collective_id, cut):
    rows, width = x.shape
    hidden = w_up.shape[1]
    cuts = hidden // HIDDEN_CUT
    count = width // EXCHANGE
    shape = jax.ShapeDtypeStruct
    dma = pltpu.SemaphoreType.DMA
    V = pltpu.VMEM
    box = V((count, rows, EXCHANGE), BF)
    return pl.pallas_call(
        functools.partial(mid_kernel, n_ctx, cut),
        out_shape=(pltpu.HBM((n_ctx, rows, width), BF), pltpu.HBM((n_ctx, rows, width), BF), shape((rows, width), BF),
                   shape((rows, width), BF), shape((rows, width), F32), shape((1, width), F32), shape((1, width), F32)),
        in_specs=[vmem_spec()] * 8 + [hbm_spec()] * 3,
        out_specs=(hbm_spec(),) * 2 + (vmem_spec(),) * 5,
        scratch_shapes=[
            gather_sems(n_ctx, cut), gather_sems(n_ctx, cut), dma((2,)), dma((3, cuts)), dma((2, count)), dma((2, count)),
            V((width, hidden), BF), V((width, hidden), BF), V((hidden, width), BF), V((rows, width), BF),
            V((rows, width), BF), V((rows, hidden), F32), V((rows, hidden), F32), V((rows, hidden), BF),
            V((rows, hidden), BF), V((rows, width), F32), box, box, box, box],
        compiler_params=pltpu.CompilerParams(collective_id=collective_id, has_side_effects=True,
                                             vmem_limit_bytes=30 << 20),
        cost_estimate=pl.CostEstimate(flops=5 * 10 ** 9, bytes_accessed=30 * 10 ** 6, transcendentals=10 ** 6),
        name="feed_forward",
    )(hidden_one, branch_attn, x, cotangent, ff_step, attn_step, up_scale, gate_scale, in_hbm(w_up), in_hbm(w_gate), in_hbm(w_down))


BLOCK = 4
STATS = 128


def split_parts(v, count):
    parts = []
    rest = v
    for _ in range(count):
        part = rest.astype(BF)
        parts.append(part)
        rest = rest - part.astype(F32)
    return parts


def transposed(src, dst, dtype):
    for n in range(src.shape[1] // 128):
        dst[n * 128:(n + 1) * 128, :] = src[:, n * 128:(n + 1) * 128].T.astype(dtype)


class Among:
    def __init__(self, count, stride=1, first=0):
        self.count, self.stride, self.first = count, stride, first

    def device(self, number):
        return number * self.stride + self.first

    def number(self, device):
        return lax.div(device - self.first, self.stride)

    def has(self, device):
        away = device - self.first
        return (away >= 0) & (lax.rem(away, self.stride) == 0) & (away < self.count * self.stride)


class UnitScatter:
    def __init__(self, place, source, target, send_sems, recv_sems, senders, per_sender, per_owner):
        self.p, self.source, self.target = place, source, target
        self.send_sems, self.recv_sems = send_sems, recv_sems
        self.senders, self.per_sender, self.per_owner = senders, per_sender, per_owner

    def rows(self, unit):
        return pl.ds(pl.multiple_of(unit * 8, 8), 8)

    def copy(self, unit, slot, owner):
        return pltpu.make_async_remote_copy(
            src_ref=self.source.at[self.rows(unit)], dst_ref=self.target.at[self.rows(slot)],
            send_sem=self.send_sems.at[unit], recv_sem=self.recv_sems.at[slot],
            device_id=(owner, self.p.wa), device_id_type=MESH)

    def local(self, unit, slot):
        return pltpu.make_async_copy(self.source.at[self.rows(unit)], self.target.at[self.rows(slot)],
                                     self.recv_sems.at[slot])

    def outgoing(self, remote, near):
        p = self.p

        @pl.when(self.senders.has(p.ctx))
        def _():
            @pl.loop(0, self.per_sender)
            def _(unit):
                place_of = self.senders.number(p.ctx) * self.per_sender + unit
                owner, slot = lax.div(place_of, self.per_owner), lax.rem(place_of, self.per_owner)

                @pl.when(owner != p.ctx)
                def _():
                    remote(self.copy(unit, slot, owner))

                if near is not None:
                    @pl.when(owner == p.ctx)
                    def _():
                        near(self.local(unit, slot))

    def start(self):
        self.outgoing(lambda c: c.start(), lambda c: c.start())

    def wait(self):
        p = self.p

        @pl.loop(0, self.per_owner)
        def _(slot):
            place_of = p.ctx * self.per_owner + slot
            number, unit = lax.div(place_of, self.per_sender), lax.rem(place_of, self.per_sender)
            sender = self.senders.device(number)

            @pl.when(sender != p.ctx)
            def _():
                self.copy(unit, slot, p.ctx).wait_recv()

            @pl.when(sender == p.ctx)
            def _():
                self.local(unit, slot).wait()

    def sent(self):
        self.outgoing(lambda c: c.wait_send(), None)


class Scatter:
    def __init__(self, place, source, target, sems, receivers, senders):
        self.p, self.source, self.target, self.sems = place, source, target, sems
        self.receivers, self.senders = receivers, senders

    def copy(self, dest, sender):
        number = self.receivers.number(dest)
        return pltpu.make_async_remote_copy(
            src_ref=self.source(number), dst_ref=self.target(sender),
            send_sem=self.sems.at[0, number], recv_sem=self.sems.at[1, sender],
            device_id=(dest, self.p.wa), device_id_type=MESH)

    def each(self, fn):
        p = self.p

        @pl.loop(1, p.n_ctx)
        def _(shift):
            fn(lax.rem(p.ctx + shift, p.n_ctx))

    def start(self):
        p = self.p

        @pl.when(self.senders.has(p.ctx))
        def _():
            def go(dest):
                @pl.when(self.receivers.has(dest))
                def _():
                    self.copy(dest, p.ctx).start()
            self.each(go)

            @pl.when(self.receivers.has(p.ctx))
            def _():
                self.local().start()

    def local(self):
        source = self.source(self.receivers.number(self.p.ctx))
        return pltpu.make_async_copy(source, self.target(self.p.ctx), self.sems.at[1, self.p.ctx])

    def wait(self):
        p = self.p

        @pl.when(self.receivers.has(p.ctx))
        def _():
            def got(sender):
                @pl.when(self.senders.has(sender))
                def _():
                    self.copy(p.ctx, sender).wait_recv()
            self.each(got)

            @pl.when(self.senders.has(p.ctx))
            def _():
                self.local().wait()

    def sent(self):
        p = self.p

        @pl.when(self.senders.has(p.ctx))
        def _():
            def left(dest):
                @pl.when(self.receivers.has(dest))
                def _():
                    self.copy(dest, p.ctx).wait_send()
            self.each(left)


def out_devices(n_ctx, tiles):
    stride = n_ctx // tiles
    return Among(tiles, stride, stride // 2)


def bwd_kernel(n_ctx, cut, aligned, out_aligned, *refs):
    (dab_ref, gfs_ref, gas_ref, qraw_ref, kraw_ref, lse_ref, o_ref, dxr_ref, qs_ref, us_ref, gs_ref,
     wo_ref, wq_ref, wk_ref, wv_ref, xall_ref, qall_ref, kall_ref, vall_ref, hball_ref, dmball_ref, wu_ref, wg_ref, wd_ref,
     dx_ref, got_q, gout_ref, got_u, gdown_ref, got_s, gus_ref, ggs_ref,
     daball_ref, statall_ref, turned, turned_qkv, gocc,
     asems, ssts, lsems, csems, esems, usems, tsems, osems, rsems, vsems, ssems, xsems, nsems, fsems,
     hbbuf, dmbuf, dabbuf, stbuf, qbuf, kvbuf, dobuf, rowstats, stats, delta, q2, k2, v2, do2, dq2, dk2, dv2,
     wuw, wgw, wdw, gu, gg, gd, colu, colg, comb, small, small_row, dqkv, got_t, got_o, obs, accq, sbuf, rbuf) = refs
    place = Place(n_ctx)
    rows, width = dxr_ref.shape
    block_len = rows // 2
    channels = qraw_ref.shape[1]
    tiles = channels // 128
    hidden = us_ref.shape[1]
    mine = hidden // n_ctx
    group = 2 * place.across
    subs = group // BLOCK
    many = BLOCK * rows
    window = gu.shape[0]
    scale = 1.0 / math.sqrt(HD)
    a_gather = Pieces(place, daball_ref, asems, cut)
    s_gather = Pieces(place, statall_ref, ssts, ((rows, rows, rows),))
    start = jnp.minimum(lax.div(place.ctx * mine, 128) * 128, hidden - window)
    start = pl.multiple_of(start, 128)
    offset = pl.multiple_of(place.ctx * mine - start, 8)
    win = pl.ds(start, window)
    own = [load_rows(dab_ref, daball_ref.at[place.ctx], lsems.at[0]),
           load_rows(wu_ref.at[:, win], wuw, lsems.at[2]), load_rows(wg_ref.at[:, win], wgw, lsems.at[3]),
           load_rows(wd_ref.at[win, :], wdw, lsems.at[4])]
    for copy in own:
        copy.start()
    for t in range(tiles):
        obs[t] = o_ref[:, t * 128:(t + 1) * 128].astype(BF)
    place.barrier_all()
    own[0].wait()
    a_gather.each("step_z", 0)
    d_out = dot_nt(dab_ref[...], wo_ref[...]).astype(BF)
    lane = lax.broadcasted_iota(jnp.int32, (rows, 128), 1)
    packed = jnp.zeros((rows, 128), F32)
    for t in range(tiles):
        cols = slice(t * 128, (t + 1) * 128)
        do2[t] = stack_heads(d_out[:, cols])
        both_heads = stack_heads(d_out[:, cols].astype(F32) * o_ref[:, cols])
        delta[t] = jnp.broadcast_to(jnp.sum(both_heads, axis=1, keepdims=True), (2 * rows, 128))
        for h in range(2):
            part_rows = slice(h * rows, (h + 1) * rows)
            values = split_parts(lse_ref[t, part_rows], 3) + split_parts(delta[t, part_rows], 2)
            for i, value in enumerate(values):
                packed = jnp.where(lane == i * 2 * tiles + 2 * t + h, value.astype(F32), packed)
    stats[...] = packed.astype(BF)
    own_stats = load_rows(stats, statall_ref.at[place.ctx], lsems.at[0])
    own_stats.start()
    own_stats.wait()
    s_gather.each("step_z", 0)
    everyone = Among(n_ctx)
    owners = out_devices(n_ctx, tiles)
    o_scatter = Scatter(place, lambda dest: obs.at[dest], lambda sender: got_o.at[sender], osems, owners, everyone)
    o_scatter.start()

    for t in range(tiles):
        cols = slice(t * 128, (t + 1) * 128)
        for raw_ref, dest in ((qraw_ref, q2), (kraw_ref, k2)):
            raw = raw_ref[:, cols]
            dest[t] = stack_heads((raw * head_rms(raw) * qs_ref[:, cols]).astype(BF))
    dq2[...] = jnp.zeros_like(dq2)
    dk2[...] = jnp.zeros_like(dk2)
    dv2[...] = jnp.zeros_like(dv2)
    gu[...] = jnp.zeros_like(gu)
    gg[...] = jnp.zeros_like(gg)
    gd[...] = jnp.zeros_like(gd)
    colu[...] = jnp.zeros_like(colu)
    colg[...] = jnp.zeros_like(colg)
    gocc[...] = jnp.zeros_like(gocc)

    def row_positions(shape, axis, first):
        i = lax.broadcasted_iota(jnp.int32, shape, axis)
        return position_of(first + lax.div(i, rows), lax.rem(i, rows), block_len, n_ctx)

    def own_positions(shape, axis):
        i = lax.broadcasted_iota(jnp.int32, shape, axis)
        return position_of(place.ctx, lax.rem(i, rows), block_len, n_ctx)

    total_blocks = n_ctx // BLOCK

    def serve(name, k):
        a_gather.each(name, k)
        s_gather.each(name, k)

    def kv_loads(b):
        side = lax.rem(b, 2)
        return [load_rows(ref.at[pl.ds(b * BLOCK, BLOCK)], kvbuf.at[side, i], csems.at[side, i])
                for i, ref in enumerate((kall_ref, vall_ref))]

    def wide(v):
        return jnp.concatenate([v] * (many // 128), axis=1)

    for copy in kv_loads(0):
        copy.start()

    @pl.loop(0, total_blocks)
    def _(b):
        side = lax.rem(b, 2)

        @pl.when(b + 1 < total_blocks)
        def _():
            for copy in kv_loads(b + 1):
                copy.start()

        for copy in kv_loads(b):
            copy.wait()
        allowed = row_positions((1, many), 1, b * BLOCK) <= own_positions((2 * rows, 1), 0)

        @pl.loop(0, tiles)
        def _(t):
            cols = pl.ds(pl.multiple_of(t * 128, 128), 128)
            kt = kvbuf[side, 0, :, :, cols].reshape(many, 128)
            vt = kvbuf[side, 1, :, :, cols].reshape(many, 128)
            score = dot_nt(q2[t], kt)
            p = jnp.where(allowed, jnp.exp2(score * (LOG2E * scale) - wide(lse_ref[t])), 0.0)
            dp = dot_nt(do2[t], vt)
            ds = (p * (dp - wide(delta[t])) * scale).astype(BF)
            dq2[t] += dot32(ds, kt)

        @pl.when(b == total_blocks // 4)
        def _():
            serve("step_z", 1)

        @pl.when(b == total_blocks - 1)
        def _():
            serve("step_z", 2)
            serve("step_x", 0)

    def head_back(raw_ref, grads, base, first):
        for t in range(tiles):
            cols = slice(t * 128, (t + 1) * 128)
            raw = raw_ref[:, cols]
            inv = head_rms(raw)
            normed = raw * inv
            grad = join_heads(grads[t])
            grad_scale = jnp.sum(grad * normed, axis=0, keepdims=True)
            small_row[:, cols] = grad_scale if first else small_row[:, cols] + grad_scale
            e = grad * qs_ref[:, cols]
            dqkv[base + t] = ((e - normed * pair_mean(normed * e)) * inv).astype(BF)

    head_back(qraw_ref, dq2, 0, True)
    f_scatter = Scatter(place, lambda dest: dqkv.at[dest], lambda sender: got_t.at[sender], fsems, Among(tiles), everyone)
    f_scatter.start()
    own_v = load_rows(vall_ref.at[place.ctx], dobuf.at[0], lsems.at[0])
    own_v.start()
    own_v.wait()
    for t in range(tiles):
        v2[t] = stack_heads(dobuf[0, :, t * 128:(t + 1) * 128])
    for copy in own[1:]:
        copy.wait()

    def block_of(s, k, sub):
        return ((place.z - s * k) * subs + sub) * BLOCK

    def a_loads(side, first):
        return [load_rows(ref.at[pl.ds(first, BLOCK)], buf.at[side], rsems.at[side, i])
                for i, (ref, buf) in enumerate(((daball_ref, dabbuf), (qall_ref, qbuf), (statall_ref, stbuf)))]

    def m_loads(b):
        side = lax.rem(b, 2)
        return [load_rows(dmball_ref.at[pl.ds(b * BLOCK, BLOCK)], dmbuf.at[side], xsems.at[side, 0]),
                load_rows(hball_ref.at[pl.ds(b * BLOCK, BLOCK)], hbbuf.at[side], xsems.at[side, 1])]

    def keys_part(side, first):
        for copy in a_loads(side, first):
            copy.wait()
        dab = dabbuf[side].reshape(many, width)
        dobuf[...] = dot_nt(dab, wo_ref[...]).astype(BF).reshape(BLOCK, rows, channels)
        for j in range(BLOCK):
            rowstats[:, j * rows:(j + 1) * rows] = stbuf[side, j].astype(F32).T

        @pl.when(owners.has(place.ctx))
        def _():
            gocc[...] += dot_tn(got_o[pl.ds(first, BLOCK)].reshape(many, 128), dab)

        allowed = own_positions((2 * rows, 1), 0) <= row_positions((1, many), 1, first)
        heads = 2 * tiles

        @pl.loop(0, tiles)
        def _(t):
            cols = pl.ds(pl.multiple_of(t * 128, 128), 128)
            qt = qbuf[side, :, :, cols].reshape(many, 128)
            dot_ = dobuf[:, :, cols].reshape(many, 128)

            def both_rows(parts, at):
                def one(h):
                    row = rowstats[pl.ds(at * heads + h, 1), :]
                    for i in range(1, parts):
                        row = row + rowstats[pl.ds((at + i) * heads + h, 1), :]
                    return jnp.broadcast_to(row, (rows, many))
                return jnp.concatenate([one(2 * t), one(2 * t + 1)], axis=0)

            score = dot_nt(k2[t], qt)
            p = jnp.where(allowed, jnp.exp2(score * (LOG2E * scale) - both_rows(3, 0)), 0.0)
            dp = dot_nt(v2[t], dot_)
            ds = (p * (dp - both_rows(2, 3)) * scale).astype(BF)
            dv2[t] += dot32(p.astype(BF), dot_)
            dk2[t] += dot32(ds, qt)

    def hidden_part(side):
        hb = hbbuf[side].reshape(many, width)
        dm = dmbuf[side].reshape(many, width)
        us, gs = us_ref[:, win], gs_ref[:, win]
        u = dot32(hb, wuw[...])
        g = dot32(hb, wgw[...])
        dgated = dot_nt(dm, wdw[...])
        a, c = u * us, g * gs
        s = lax.logistic(c)
        cs = c * s
        r = s * (1.0 + c * (1.0 - s))
        da = dgated * cs
        dc = dgated * a * r
        colu[...] += jnp.sum((da * u).reshape(many // 8, 8, window), axis=0)
        colg[...] += jnp.sum((dc * g).reshape(many // 8, 8, window), axis=0)
        gu[...] += dot_tn((da * us).astype(BF), hb)
        gg[...] += dot_tn((dc * gs).astype(BF), hb)
        gd[...] += dot_tn((a * cs).astype(BF), dm)

    def hidden_all():
        for copy in m_loads(0):
            copy.start()

        @pl.loop(0, total_blocks)
        def _(b):
            @pl.when(b + 1 < total_blocks)
            def _():
                for copy in m_loads(b + 1):
                    copy.start()

            for copy in m_loads(b):
                copy.wait()
            hidden_part(lax.rem(b, 2))

            serve("step_z", b + 3)
            serve("step_x", b + 1)
            serve("step_y", b + 1)
            serve("step_yx", b)
            serve("step_c", b - 1)

    def both(k, fn):
        for s in (1, -1):
            @pl.when(a_gather.parts[0].exists(s, k))
            def _():
                @pl.loop(0, subs)
                def _(sub):
                    fn(0 if s > 0 else 1, block_of(s, k, sub))

    def begin(loads):
        for copy in loads:
            copy.start()

    def keys_full(side, first):
        begin(a_loads(side, first))
        keys_part(side, first)

    hidden_all()

    gdown_ref[...] = gd[pl.ds(offset, mine), :]
    comb[0:mine] = gu[pl.ds(offset, mine), :]
    comb[mine:2 * mine] = gg[pl.ds(offset, mine), :]
    comb[2 * mine:] = jnp.zeros((comb.shape[0] - 2 * mine, width), F32)
    transposed(comb, turned, BF)
    part = width // n_ctx

    def row_block(ref, size):
        return lambda dest: ref.at[pl.ds(pl.multiple_of(dest * size, 8), size)]

    if aligned:
        u_scatter = Scatter(place, row_block(turned, part), lambda sender: got_u.at[sender], usems, everyone, everyone)
        u_scatter.start()
    shift = lax.rem(window - offset, window)
    gus_ref[...] = pltpu.roll(jnp.broadcast_to(jnp.sum(colu[...], axis=0, keepdims=True), (8, window)), shift, 1)
    ggs_ref[...] = pltpu.roll(jnp.broadcast_to(jnp.sum(colg[...], axis=0, keepdims=True), (8, window)), shift, 1)

    o_scatter.wait()

    @pl.loop(0, place.line)
    def _(k):
        serve("step_c", total_blocks - 1 + k)
        if subs == 1:
            both(k, lambda side, first: begin(a_loads(side, first)))
            both(k, keys_part)
        else:
            both(k, keys_full)

    if out_aligned:
        g_scatter = UnitScatter(place, gocc, gout_ref, ssems.at[0], ssems.at[1], owners, 16, channels // n_ctx // 8)
        g_scatter.start()

    head_back(kraw_ref, dk2, tiles, False)
    for t in range(tiles):
        dqkv[2 * tiles + t] = join_heads(dv2[t]).astype(BF)
    t_scatter = Scatter(place, lambda dest: dqkv.at[dest + tiles], lambda sender: got_t.at[sender], tsems,
                        Among(2 * tiles, 1, tiles), everyone)
    t_scatter.start()
    head_part = channels // n_ctx
    for i in range(n_ctx):
        small[i, 0:1, 0:part] = gfs_ref[:, i * part:(i + 1) * part]
        small[i, 1:2, 0:part] = gas_ref[:, i * part:(i + 1) * part]
        small[i, 2:3, 0:head_part] = small_row[:, i * head_part:(i + 1) * head_part]
    n_scatter = Scatter(place, lambda dest: small.at[dest], lambda sender: got_s.at[sender], nsems, everyone, everyone)
    n_scatter.start()

    def input_terms(cols):
        total = None
        for n, w_ref in enumerate((wq_ref, wk_ref, wv_ref)):
            grad = jnp.concatenate([dqkv[n * tiles + t] for t in range(tiles)], axis=1)
            term = dot_nt(grad, w_ref[cols, :])
            total = term if total is None else total + term
        return total

    pl.when(place.ctx < 3 * tiles)(load_rows(xall_ref.at[pl.ds(0, BLOCK)], hbbuf.at[0], xsems.at[0, 0]).start)
    exchange(place, input_terms, dx_ref, sbuf, rbuf, esems)
    dx_ref[...] += dxr_ref[...]

    f_scatter.wait()
    t_scatter.wait()

    @pl.when(place.ctx < 3 * tiles)
    def _():
        accq[...] = jnp.zeros_like(accq)

        def x_load(b):
            side = lax.rem(b, 2)
            return load_rows(xall_ref.at[pl.ds(b * BLOCK, BLOCK)], hbbuf.at[side], xsems.at[side, 0])

        @pl.loop(0, total_blocks)
        def _(b):
            @pl.when(b + 1 < total_blocks)
            def _():
                x_load(b + 1).start()

            x_load(b).wait()
            accq[...] += dot_tn(got_t[pl.ds(b * BLOCK, BLOCK)].reshape(many, 128),
                                hbbuf[lax.rem(b, 2)].reshape(many, width))

        transposed(accq, turned_qkv, BF)

    if aligned:
        q_scatter = Scatter(place, row_block(turned_qkv, part), lambda sender: got_q.at[sender], vsems, everyone, Among(3 * tiles))
        q_scatter.start()
        u_scatter.wait()
        q_scatter.wait()
        u_scatter.sent()
        q_scatter.sent()
    if out_aligned:
        g_scatter.wait()
        g_scatter.sent()
    a_gather.finish()
    s_gather.finish()
    o_scatter.sent()
    f_scatter.sent()
    t_scatter.sent()
    n_scatter.wait()
    n_scatter.sent()


def backward_attention(dab, grad_ff_step, grad_attn_step, q_raw, k_raw, lse, attended, dxr, qk_scale, up_scale, gate_scale,
                       w_out, w_query, w_key, w_value, x_all, q_all, k_all, v_all, hb_all, dmb_all, w_up, w_gate, w_down,
                       n_ctx, collective_id, cut):
    rows, width = dxr.shape
    channels = q_raw.shape[1]
    tiles = channels // 128
    hidden = up_scale.shape[1]
    mine = hidden // n_ctx
    part = width // n_ctx
    aligned = part % 16 == 0
    out_rows = channels // n_ctx
    out_aligned = out_rows % 8 == 0
    window = 256
    pair = -(-2 * mine // 128) * 128
    count = width // EXCHANGE
    many = BLOCK * rows
    n_blocks = n_ctx
    shape = jax.ShapeDtypeStruct
    dma = pltpu.SemaphoreType.DMA
    V = pltpu.VMEM
    stack = lambda dtype: V((tiles, 2 * rows, 128), dtype)
    outs = (
        shape((rows, width), F32),
        shape((3 * tiles, part, 128), BF), shape((out_rows, width), F32), shape((n_ctx, part, pair), BF),
        shape((mine, width), F32), shape((n_ctx, 8, 128), F32), shape((8, window), F32), shape((8, window), F32),
        shape((n_ctx, rows, width), BF), shape((n_ctx, rows, STATS), BF),
        shape((width, pair), BF), shape((width, 128), BF), shape((128, width), F32))
    return pl.pallas_call(
        functools.partial(bwd_kernel, n_ctx, cut, aligned, out_aligned),
        out_shape=outs,
        in_specs=[vmem_spec()] * 15 + [any_spec()] * 9,
        out_specs=(vmem_spec(),) * 8 + (hbm_spec(),) * 2 + (vmem_spec(),) * 3,
        scratch_shapes=[
            gather_sems(n_ctx, cut), gather_sems(n_ctx, ((rows, rows, rows),)), dma((5,)), dma((2, 2)), dma((2, count)),
            dma((2, n_ctx)), dma((2, n_ctx)), dma((2, n_ctx)), dma((2, 3)), dma((2, n_ctx)), dma((2, 16)), dma((2, 2)), dma((2, n_ctx)), dma((2, n_ctx)),
            V((2, BLOCK, rows, width), BF), V((2, BLOCK, rows, width), BF), V((2, BLOCK, rows, width), BF), V((2, BLOCK, rows, STATS), BF),
            V((2, BLOCK, rows, channels), BF), V((2, 2, BLOCK, rows, channels), BF), V((BLOCK, rows, channels), BF),
            V((STATS, many), F32), V((rows, STATS), BF), stack(F32), stack(BF), stack(BF), stack(BF), stack(BF), stack(F32), stack(F32), stack(F32),
            V((width, window), BF), V((width, window), BF), V((window, width), BF),
            V((window, width), F32), V((window, width), F32), V((window, width), F32),
            V((8, window), F32), V((8, window), F32), V((pair, width), F32), V((n_ctx, 8, 128), F32), V((1, channels), F32),
            V((3 * tiles, rows, 128), BF), V((n_ctx, rows, 128), BF), V((n_ctx, rows, 128), BF), V((tiles, rows, 128), BF),
            V((128, width), F32),
            V((count, rows, EXCHANGE), BF), V((count, rows, EXCHANGE), BF)],
        compiler_params=pltpu.CompilerParams(collective_id=collective_id, has_side_effects=True,
                                             vmem_limit_bytes=40 << 20),
        cost_estimate=pl.CostEstimate(flops=20 * 10 ** 9, bytes_accessed=60 * 10 ** 6, transcendentals=6 * 10 ** 6),
        name="backward_attention",
    )(dab, grad_ff_step, grad_attn_step, q_raw, k_raw, lse, attended, dxr, qk_scale, up_scale, gate_scale,
      w_out, w_query, w_key, w_value, x_all, q_all, k_all, v_all, hb_all, dmb_all, w_up, w_gate, w_down)


def last_kernel(result_ref, dx_ref, gotq_ref, gout_ref, gotu_ref, gdown_ref, gots_ref, gus_ref, ggs_ref,
                o_result, o_dx, o_gq, o_gk, o_gv, o_gout, o_gup, o_ggate, o_gdown, o_gqs, o_gus, o_ggs, o_gas, o_gfs):
    o_result[...] = result_ref[...]
    o_dx[...] = dx_ref[...]
    o_gout[...] = gout_ref[...]
    o_gdown[...] = gdown_ref[...]
    mine = o_gus.shape[1]
    tiles = o_gq.shape[1] // 128
    for j in range(gotu_ref.shape[0]):
        o_gup[:, j * mine:(j + 1) * mine] = gotu_ref[j, :, 0:mine].astype(F32)
        o_ggate[:, j * mine:(j + 1) * mine] = gotu_ref[j, :, mine:2 * mine].astype(F32)
    for n, ref in enumerate((o_gq, o_gk, o_gv)):
        for t in range(tiles):
            ref[:, t * 128:(t + 1) * 128] = gotq_ref[n * tiles + t].astype(F32)
    total = jnp.sum(gots_ref[...], axis=0)
    for row, ref in enumerate((o_gfs, o_gas, o_gqs)):
        ref[...] = total[row:row + 1, 0:ref.shape[1]]
    o_gus[...] = gus_ref[0:1, 0:mine]
    o_ggs[...] = ggs_ref[0:1, 0:mine]


def last_step(parts, n_ctx, channels, hidden):
    width = parts[1].shape[1]
    part, mine = width // n_ctx, hidden // n_ctx
    shape = jax.ShapeDtypeStruct
    outs = [shape(parts[0].shape, BF), shape(parts[1].shape, F32)] + [shape((part, channels), F32)] * 3
    outs += [shape(parts[3].shape, F32)] + [shape((part, hidden), F32)] * 2 + [shape((mine, width), F32)]
    outs += [shape((1, channels // n_ctx), F32)] + [shape((1, mine), F32)] * 2 + [shape((1, part), F32)] * 2
    return pl.pallas_call(
        last_kernel, out_shape=tuple(outs), in_specs=[vmem_spec()] * len(parts), out_specs=(vmem_spec(),) * len(outs),
        compiler_params=pltpu.CompilerParams(vmem_limit_bytes=32 << 20), name="last_step")(*parts)


CUT = ((64, 48, 32), (64, 48, 48))


def shards(layer_input, w_query, w_key, w_value, w_out, w_up, w_gate, w_down, qk_scale, up_scale,
           gate_scale, attention_step, feedforward_step, cotangent):
    n_ctx = lax.axis_size("ctx")
    ctx = lax.axis_index("ctx")
    rows = 2 * layer_input.shape[2]
    width = layer_input.shape[3]
    channels = w_query.shape[1]
    hidden = w_up.shape[1]
    tiles = channels // 128
    x = layer_input.reshape(rows, width)
    flat = lambda v: v.reshape(1, -1)
    x_all, q_all, k_all, v_all, q_raw, k_raw, attended, lse, hidden_one, branch_attn = forward_attention(
        x, w_query, w_key, w_value, flat(qk_scale), w_out, flat(attention_step), n_ctx, 0, CUT)
    hb_all, dmb_all, result, dab, input_res, grad_ff_step, grad_attn_step = feed_forward(
        hidden_one, branch_attn, x, cotangent.reshape(rows, width), flat(feedforward_step), flat(attention_step),
        flat(up_scale), flat(gate_scale), w_up, w_gate, w_down, n_ctx, 1, CUT)
    (input_grad, got_q, grad_out, got_u, grad_down, got_s, gus, ggs,
     _, _, turned, turned_qkv, gocc) = backward_attention(
        dab, grad_ff_step, grad_attn_step, q_raw, k_raw, lse, attended, input_res, flat(qk_scale), flat(up_scale),
        flat(gate_scale), w_out, w_query, w_key, w_value, x_all, q_all, k_all, v_all, hb_all, dmb_all,
        w_up, w_gate, w_down, n_ctx, 2, CUT)
    part = width // n_ctx
    if part % 16:
        turned, turned_qkv = lax.optimization_barrier((turned, turned_qkv))
        got_u = lax.all_to_all(turned, "ctx", 0, 0, tiled=True).reshape(n_ctx, part, -1)
        got_q = lax.all_to_all(turned_qkv, "ctx", 0, 0, tiled=True).reshape(n_ctx, part, 128)[:3 * tiles]
    if (channels // n_ctx) % 8:
        gocc = lax.optimization_barrier(gocc)
        whole = jnp.zeros((n_ctx, 128, width), F32)
        whole = lax.dynamic_update_slice_in_dim(whole, gocc[None], ctx, 0)[n_ctx // tiles // 2::n_ctx // tiles][:tiles]
        grad_out = lax.psum_scatter(whole.reshape(channels, width), "ctx", scatter_dimension=0, tiled=True)
    outs = last_step((result, input_grad, got_q, grad_out, got_u, grad_down, got_s, gus, ggs), n_ctx, channels, hidden)
    tokens = tuple(v.reshape(layer_input.shape) for v in outs[:2])
    return tokens + tuple(outs[2:9]) + tuple(v.reshape(-1) for v in outs[9:])


def solution(mesh):
    placed = (
        P("ctx", None, None, None),
        P(None, "wa"),
        P(None, "wa"),
        P(None, "wa"),
        P("wa", None),
        P(None, "wa"),
        P(None, "wa"),
        P("wa", None),
        P("wa"),
        P("wa"),
        P("wa"),
        P(),
        P(),
        P("ctx", None, None, None),
    )
    return jax.shard_map(
        shards,
        mesh=mesh,
        in_specs=placed,
        out_specs=(
            P("ctx", None, None, None),
            P("ctx", None, None, None),
            P("ctx", "wa"),
            P("ctx", "wa"),
            P("ctx", "wa"),
            P(("wa", "ctx"), None),
            P("ctx", "wa"),
            P("ctx", "wa"),
            P(("wa", "ctx"), None),
            P(("wa", "ctx")),
            P(("wa", "ctx")),
            P(("wa", "ctx")),
            P("ctx"),
            P("ctx"),
        ),
        check_vma=False,
    )
```

```python
import functools
from functools import partial
import math

import jax
import jax.numpy as jnp
from jax import lax
from jax.experimental import pallas as pl
from jax.experimental.pallas import tpu as pltpu
from jax.sharding import PartitionSpec as P

HD = 64
MESH = pl.DeviceIdType.MESH


def layout_of(n_ctx):
    chips = n_ctx // 2
    across = 2 if chips <= 8 else 4
    return chips // across, across


class Place:
    def __init__(self, n_ctx):
        self.n_ctx = n_ctx
        self.line, self.across = layout_of(n_ctx)
        self.ctx = lax.axis_index("ctx")
        self.wa = lax.axis_index("wa")
        self.core = lax.rem(self.ctx, 2)
        chip = lax.div(self.ctx, 2)
        self.x = lax.rem(chip, self.across)
        self.z = lax.div(chip, self.across)

    def index(self, z, x, core):
        return (z * self.across + x) * 2 + core

    def at(self, z, x, core):
        return (self.index(z, x, core), self.wa)

    def sibling(self):
        return self.at(self.z, self.x, 1 - self.core)

    def partner(self):
        return (self.ctx, 1 - self.wa)

    def inside(self, z):
        return (z >= 0) & (z < self.line)

    def column(self, shift):
        return lax.rem(self.x + shift, self.across)

    def barrier(self):
        sem = pltpu.get_barrier_semaphore()

        def signal(device):
            pl.semaphore_signal(sem, inc=1, device_id=device, device_id_type=MESH)

        signal(self.sibling())
        signal(self.partner())
        for shift in range(1, self.across):
            signal(self.at(self.z, self.column(shift), self.core))
        count = jnp.int32(self.across + 1)
        for step in (-1, 1):
            near = self.inside(self.z + step)
            pl.when(near)(functools.partial(signal, self.at(self.z + step, self.x, self.core)))
            count = count + near.astype(jnp.int32)
        pl.semaphore_wait(sem, count)

    def barrier_all(self):
        sem = pltpu.get_barrier_semaphore()
        pl.semaphore_signal(sem, inc=1, device_id=self.partner(), device_id_type=MESH)

        @pl.loop(1, self.n_ctx)
        def _(shift):
            other = lax.rem(self.ctx + shift, self.n_ctx)
            pl.semaphore_signal(sem, inc=1, device_id=(other, self.wa), device_id_type=MESH)

        pl.semaphore_wait(sem, self.n_ctx)


class Gather:
    def __init__(self, place, out, sems, base, first, rows, z_rows, x_rows):
        self.p = place
        self.out = out
        self.sems = sems
        self.base = base
        self.first, self.rows = first, rows
        self.z_rows, self.x_rows = z_rows, x_rows
        self.slots = 2 * place.line

    @staticmethod
    def sem_count(n_ctx):
        line, across = layout_of(n_ctx)
        return 2 * line * 3 * across

    def sem(self, kind, s, k, shift=0):
        kinds = self.p.across - 1
        order = {"z": 0, "y": 1, "c": 2, "x": 3, "yx": 3 + kinds, "cx": 3 + 2 * kinds}[kind]
        return self.base + (order + shift) * self.slots + (0 if s > 0 else self.p.line) + k

    def copy(self, sem, block, start, size, device):
        view = self.out.at[block, pl.ds(pl.multiple_of(self.first + start, 16), size)]
        return pltpu.make_async_remote_copy(
            src_ref=view, dst_ref=view, send_sem=self.sems.at[0, sem], recv_sem=self.sems.at[1, sem],
            device_id=device, device_id_type=MESH)

    def exists(self, s, k):
        ok = self.p.inside(self.p.z - s * k) & (k >= 0) & (k < self.p.line)
        return ok if s > 0 else ok & (k > 0)

    def d_z(self, s, k, block, device):
        return self.copy(self.sem("z", s, k), block, self.p.wa * (self.rows - self.z_rows), self.z_rows, device)

    def d_x(self, s, k, shift, block, device):
        return self.copy(self.sem("x", s, k, shift - 1), block, self.p.wa * (self.rows - self.x_rows), self.x_rows, device)

    def d_y(self, kind, s, k, shift, block, size, sending):
        side = self.p.wa if sending else 1 - self.p.wa
        return self.copy(self.sem(kind, s, k, shift), block, side * size, self.rows - size, self.p.partner())

    def d_c(self, kind, s, k, shift, block):
        return self.copy(self.sem(kind, s, k, shift), block, 0, self.rows, self.p.sibling())

    def ok_forward(self, s, k):
        p = self.p
        return p.inside(p.z - s * k) & p.inside(p.z + s) & (k >= 0) & (k + 1 < p.line)

    def step_z(self, k):
        p = self.p
        me = (p.ctx, p.wa)
        for s in (1, -1):
            block = p.index(p.z - s * k, p.x, p.core)

            @pl.when(self.exists(s, k) & (k > 0))
            def _():
                self.d_z(s, k, block, me).wait_recv()

            @pl.when(self.ok_forward(s, k))
            def _():
                self.d_z(s, k + 1, block, p.at(p.z + s, p.x, p.core)).start()

            @pl.when(self.exists(s, k))
            def _():
                for shift in range(1, p.across):
                    self.d_x(s, k, shift, block, p.at(p.z, p.column(shift), p.core)).start()
                if s > 0:
                    @pl.when(k == 0)
                    def _():
                        self.d_c("c", s, k, 0, block).start()

                if self.z_rows < self.rows:
                    @pl.when(k > 0)
                    def _():
                        self.d_y("y", s, k, 0, block, self.z_rows, True).start()

    def step_y(self, k):
        p = self.p
        for s in (1, -1):
            @pl.when(self.exists(s, k) & (k > 0))
            def _():
                block = p.index(p.z - s * k, p.x, p.core)
                if self.z_rows < self.rows:
                    self.d_y("y", s, k, 0, block, self.z_rows, False).wait_recv()
                self.d_c("c", s, k, 0, block).start()

    def step_x(self, k):
        p = self.p
        for s in (1, -1):
            @pl.when(self.exists(s, k))
            def _():
                for shift in range(1, p.across):
                    block = p.index(p.z - s * k, p.column(p.across - shift), p.core)
                    self.d_x(s, k, shift, block, (p.ctx, p.wa)).wait_recv()
                    if self.x_rows < self.rows:
                        self.d_y("yx", s, k, shift - 1, block, self.x_rows, True).start()

    def step_yx(self, k):
        p = self.p
        for s in (1, -1):
            @pl.when(self.exists(s, k))
            def _():
                for shift in range(1, p.across):
                    block = p.index(p.z - s * k, p.column(p.across - shift), p.core)
                    if self.x_rows < self.rows:
                        self.d_y("yx", s, k, shift - 1, block, self.x_rows, False).wait_recv()
                    self.d_c("cx", s, k, shift - 1, block).start()

    def step_c(self, k):
        p = self.p
        for s in (1, -1):
            @pl.when(self.exists(s, k))
            def _():
                self.d_c("c", s, k, 0, p.index(p.z - s * k, p.x, 1 - p.core)).wait_recv()
                for shift in range(1, p.across):
                    block = p.index(p.z - s * k, p.column(p.across - shift), 1 - p.core)
                    self.d_c("cx", s, k, shift - 1, block).wait_recv()

    def finish(self):
        p = self.p

        @pl.loop(0, p.line)
        def _(k):
            for s in (1, -1):
                block = p.index(p.z - s * k, p.x, p.core)

                @pl.when(self.ok_forward(s, k))
                def _():
                    self.d_z(s, k + 1, block, p.at(p.z + s, p.x, p.core)).wait_send()

                @pl.when(self.exists(s, k))
                def _():
                    self.d_c("c", s, k, 0, block).wait_send()
                    if self.z_rows < self.rows:
                        @pl.when(k > 0)
                        def _():
                            self.d_y("y", s, k, 0, block, self.z_rows, True).wait_send()
                    for shift in range(1, p.across):
                        self.d_x(s, k, shift, block, p.at(p.z, p.column(shift), p.core)).wait_send()
                        other = p.index(p.z - s * k, p.column(p.across - shift), p.core)
                        if self.x_rows < self.rows:
                            self.d_y("yx", s, k, shift - 1, other, self.x_rows, True).wait_send()
                        self.d_c("cx", s, k, shift - 1, other).wait_send()


class Pieces:
    def __init__(self, place, out, sems, cut):
        n = Gather.sem_count(place.n_ctx)
        self.p = place
        self.parts = []
        first = 0
        for number, (rows, z_rows, x_rows) in enumerate(cut):
            self.parts.append(Gather(place, out, sems, number * n, first, rows, z_rows, x_rows))
            first += rows

    def each(self, name, k):
        for part in self.parts:
            getattr(part, name)(k)

    def step(self, t):
        self.each("step_z", t)
        for part in self.parts:
            part.step_x(t - 1)
            part.step_y(t - 1)
        self.each("step_yx", t - 2)
        self.each("step_c", t - 3)

    def step_count(self):
        return self.p.line + 3

    def finish(self):
        for part in self.parts:
            part.finish()


def gather_sems(n_ctx, cut):
    return pltpu.SemaphoreType.DMA((2, len(cut) * Gather.sem_count(n_ctx)))


NORM_EPS = 1e-06
BF = jnp.bfloat16
F32 = jnp.float32


def dot32(a, b):
    return jnp.dot(a, b, preferred_element_type=F32)


def dot_tn(a, b):
    return lax.dot_general(a, b, (((0,), (0,)), ((), ())), preferred_element_type=F32)


def dot_nt(a, b):
    return lax.dot_general(a, b, (((1,), (1,)), ((), ())), preferred_element_type=F32)


def row_mean(v):
    return jnp.mean(v, axis=-1, keepdims=True)


def inv_rms(v):
    return lax.rsqrt(row_mean(v * v) + NORM_EPS)


def rms_back(v, inv, grad):
    n = v * inv
    return (grad - n * row_mean(n * grad)) * inv


def pair_mean(v):
    row = lax.broadcasted_iota(jnp.int32, (128, 128), 0)
    col = lax.broadcasted_iota(jnp.int32, (128, 128), 1)
    ones = jnp.where((row < HD) == (col < HD), 1.0 / HD, 0.0).astype(BF)
    high = v.astype(BF)
    lowp = (v - high.astype(F32)).astype(BF)
    return dot32(high, ones) + dot32(lowp, ones)


def head_rms(v):
    return lax.rsqrt(pair_mean(v * v) + NORM_EPS)


def position_of(shard, index, block_len, n_ctx):
    late = index >= block_len
    block = jnp.where(late, 2 * n_ctx - 1 - shard, shard)
    return block * block_len + jnp.where(late, index - block_len, index)


def stack_heads(v):
    first = lax.broadcasted_iota(jnp.int32, v.shape, 1) < HD
    zero = jnp.zeros_like(v)
    return jnp.concatenate([jnp.where(first, v, zero), jnp.where(first, zero, v)], axis=0)


def join_heads(v):
    rows = v.shape[0] // 2
    first = lax.broadcasted_iota(jnp.int32, (rows, 128), 1) < HD
    return jnp.where(first, v[:rows], v[rows:])


def load_rows(src, dst, sem):
    return pltpu.make_async_copy(src, dst, sem)


LOG2E = 1.4426950408889634
EXCHANGE = 256
TOGETHER = 4


def fwd_kernel(n_ctx, cut, x_ref, qs_ref, step_ref, wq_hbm, wk_hbm, wv_hbm, wo_hbm,
               xall_ref, qall_ref, kall_ref, vall_ref, qraw_ref, kraw_ref, o_ref, lse_ref, h1_ref, ha_ref,
               gsems, lsems, wsems, esems, psems, wq_ref, wk_ref, wv_ref, wo_ref, xbuf, qbuf, kbuf, vbuf, q2, acc, lpart, sbuf, rbuf):
    place = Place(n_ctx)
    rows, width = x_ref.shape
    block_len = rows // 2
    channels = wq_ref.shape[1]
    tiles = channels // 128
    group = 2 * place.across
    plane = group * rows
    gather = Pieces(place, xall_ref, gsems, cut)
    own = load_rows(x_ref, xall_ref.at[place.ctx], lsems.at[0])
    own.start()
    weights = [load_rows(src, dst, psems.at[i]) for i, (src, dst) in enumerate(
        ((wq_hbm, wq_ref), (wk_hbm, wk_ref), (wv_hbm, wv_ref), (wo_hbm, wo_ref)))]
    for copy in weights:
        copy.start()
    place.barrier()
    own.wait()
    gather.each("step_z", 0)
    for copy in weights:
        copy.wait()

    xv = x_ref[...]
    kraw_ref[...] = dot32(xv, wk_ref[...])
    qraw_ref[...] = dot32(xv, wq_ref[...])
    for t in range(tiles):
        cols = slice(t * 128, (t + 1) * 128)
        raw = qraw_ref[:, cols]
        q2[t] = stack_heads((raw * head_rms(raw) * qs_ref[:, cols]).astype(BF))
    acc[...] = jnp.zeros_like(acc)
    lpart[...] = jnp.zeros_like(lpart)

    def plane_of(s, k):
        return place.z - s * k

    def hbm(ref, zp):
        return ref.at[pl.ds(zp * group, group)]

    def x_load(s, k):
        side = 0 if s > 0 else 1
        return load_rows(hbm(xall_ref, plane_of(s, k)), xbuf.at[side], lsems.at[1 + side])

    def stores(s, k):
        side = 0 if s > 0 else 1
        zp = plane_of(s, k)
        return [load_rows(buf.at[side], hbm(ref, zp), wsems.at[side, i])
                for i, (buf, ref) in enumerate(((qbuf, qall_ref), (kbuf, kall_ref), (vbuf, vall_ref)))]

    def project(s, k):
        side = 0 if s > 0 else 1
        x_load(s, k).wait()

        @pl.loop(0, group // TOGETHER)
        def _(r):
            some = pl.ds(r * TOGETHER, TOGETHER)
            xr = xbuf[side, some].reshape(TOGETHER * rows, width)
            for w_ref, buf in ((wq_ref, qbuf), (wk_ref, kbuf)):
                raw = dot32(xr, w_ref[...])
                for t in range(tiles):
                    cols = slice(t * 128, (t + 1) * 128)
                    part = raw[:, cols]
                    normed = (part * head_rms(part) * qs_ref[:, cols]).astype(BF)
                    buf[side, some, :, cols] = normed.reshape(TOGETHER, rows, 128)
            vbuf[side, some] = dot32(xr, wv_ref[...]).astype(BF).reshape(TOGETHER, rows, channels)

        for copy in stores(s, k):
            copy.start()

    def attend(s, k):
        side = 0 if s > 0 else 1
        zp = plane_of(s, k)
        qi = lax.broadcasted_iota(jnp.int32, (2 * rows, 1), 0)
        qi = jnp.where(qi >= rows, qi - rows, qi)
        qpos = position_of(place.ctx, qi, block_len, n_ctx)
        ki = lax.broadcasted_iota(jnp.int32, (1, plane), 1)
        kpos = position_of(zp * group + lax.div(ki, rows), lax.rem(ki, rows), block_len, n_ctx)
        allowed = kpos <= qpos

        @pl.loop(0, tiles)
        def _(t):
            cols = pl.ds(pl.multiple_of(t * 128, 128), 128)
            kt = kbuf[side, :, :, cols].reshape(plane, 128)
            vt = vbuf[side, :, :, cols].reshape(plane, 128)
            score = dot_nt(q2[t], kt)
            e = jnp.where(allowed, jnp.exp2(score * (LOG2E / math.sqrt(HD))), 0.0)
            total = e[:, :128]
            for j in range(1, plane // 128):
                total = total + e[:, j * 128:(j + 1) * 128]
            lpart[t] += total
            acc[t] += dot32(e.astype(BF), vt)

        for copy in stores(s, k):
            copy.wait()

    def both(k, fn):
        for s in (1, -1):
            pl.when(gather.parts[0].exists(s, k))(functools.partial(fn, s, k))

    gather.each("step_z", 1)

    @pl.loop(1, place.line + 2)
    def _(t):
        gather.each("step_x", t - 1)
        gather.each("step_y", t - 1)
        both(t - 2, attend)
        gather.each("step_yx", t - 1)
        gather.each("step_c", t - 1)
        both(t - 1, lambda s, k: x_load(s, k).start())
        gather.each("step_z", t + 1)
        both(t - 1, project)

    for t in range(tiles):
        mass = jnp.sum(lpart[t], axis=1, keepdims=True)
        o_ref[:, t * 128:(t + 1) * 128] = join_heads(acc[t] / mass)
        lse_ref[t] = jnp.broadcast_to(jnp.log(mass) * LOG2E, (2 * rows, 128))

    exchange(place, lambda cols: dot32(o_ref[...].astype(BF), wo_ref[:, cols]), ha_ref, sbuf, rbuf, esems)
    ha = ha_ref[...]
    xf = x_ref[...].astype(F32)
    w = xf + step_ref[...] * (ha * inv_rms(ha) - xf)
    h1_ref[...] = w * inv_rms(w)
    gather.finish()


def exchange(place, term, sum_ref, sbuf, rbuf, esems, between=None):
    width = sum_ref.shape[1]

    def copy(n):
        return pltpu.make_async_remote_copy(
            src_ref=sbuf.at[n], dst_ref=rbuf.at[n], send_sem=esems.at[0, n], recv_sem=esems.at[1, n],
            device_id=place.partner(), device_id_type=MESH)

    count = width // EXCHANGE
    for n in range(count):
        sbuf[n] = term(slice(n * EXCHANGE, (n + 1) * EXCHANGE)).astype(BF)
        copy(n).start()
    if between is not None:
        between()
    for n in range(count):
        copy(n).wait()
        sum_ref[:, n * EXCHANGE:(n + 1) * EXCHANGE] = sbuf[n].astype(F32) + rbuf[n].astype(F32)


def vmem_spec():
    return pl.BlockSpec(memory_space=pltpu.VMEM)


def in_hbm(v):
    return pltpu.with_memory_space_constraint(v, pltpu.HBM)


def hbm_spec():
    return pl.BlockSpec(memory_space=pltpu.HBM)


def any_spec():
    return pl.BlockSpec(memory_space=pl.ANY)


def forward_attention(x, w_query, w_key, w_value, qk_scale, w_out, step, n_ctx, collective_id, cut):
    rows, width = x.shape
    channels = w_query.shape[1]
    tiles = channels // 128
    line, across = layout_of(n_ctx)
    group = 2 * across
    count = width // EXCHANGE
    shape = jax.ShapeDtypeStruct
    return pl.pallas_call(
        functools.partial(fwd_kernel, n_ctx, cut),
        out_shape=(pltpu.HBM((n_ctx, rows, width), BF),) + (pltpu.HBM((n_ctx, rows, channels), BF),) * 3
        + (shape((rows, channels), F32),) * 3 + (shape((tiles, 2 * rows, 128), F32),) + (shape((rows, width), F32),) * 2,
        in_specs=[vmem_spec()] * 3 + [hbm_spec()] * 4,
        out_specs=(hbm_spec(),) * 4 + (vmem_spec(),) * 6,
        scratch_shapes=[
            gather_sems(n_ctx, cut), pltpu.SemaphoreType.DMA((3,)), pltpu.SemaphoreType.DMA((2, 3)),
            pltpu.SemaphoreType.DMA((2, count)), pltpu.SemaphoreType.DMA((4,)),
            pltpu.VMEM((width, channels), BF), pltpu.VMEM((width, channels), BF), pltpu.VMEM((width, channels), BF),
            pltpu.VMEM((channels, width), BF),
            pltpu.VMEM((2, group, rows, width), BF),
            pltpu.VMEM((2, group, rows, channels), BF), pltpu.VMEM((2, group, rows, channels), BF),
            pltpu.VMEM((2, group, rows, channels), BF),
            pltpu.VMEM((tiles, 2 * rows, 128), BF), pltpu.VMEM((tiles, 2 * rows, 128), F32),
            pltpu.VMEM((tiles, 2 * rows, 128), F32),
            pltpu.VMEM((count, rows, EXCHANGE), BF), pltpu.VMEM((count, rows, EXCHANGE), BF)],
        compiler_params=pltpu.CompilerParams(collective_id=collective_id, has_side_effects=True,
                                             vmem_limit_bytes=32 << 20),
        cost_estimate=pl.CostEstimate(flops=12 * 10 ** 9, bytes_accessed=40 * 10 ** 6, transcendentals=3 * 10 ** 6),
        name="forward_attention",
    )(x, qk_scale, step, *(in_hbm(w) for w in (w_query, w_key, w_value, w_out)))


HIDDEN_CUT = 256


def mid_kernel(n_ctx, cut, h1_ref, ha_ref, x_ref, cot_ref, fs_ref, as_ref, us_ref, gs_ref, wu_ref, wg_ref, wd_ref,
               hball_ref, dmball_ref, out_ref, dab_ref, dxr_ref, gfs_ref, gas_ref,
               hsems, msems, lsems, wsems, e1sems, e2sems, wu, wg, wd, hbv, dmv, u_buf, g_buf, low_a, low_b, total,
               s1, r1, s2, r2):
    place = Place(n_ctx)
    rows, width = h1_ref.shape
    hidden = us_ref.shape[1]
    cuts = hidden // HIDDEN_CUT
    h_gather = Pieces(place, hball_ref, hsems, cut)
    m_gather = Pieces(place, dmball_ref, msems, cut)

    def part(n):
        return slice(n * HIDDEN_CUT, (n + 1) * HIDDEN_CUT)

    loads = [[load_rows(wu_ref.at[:, part(n)], wu.at[:, part(n)], wsems.at[0, n]),
              load_rows(wg_ref.at[:, part(n)], wg.at[:, part(n)], wsems.at[1, n])] for n in range(cuts)]
    down = [load_rows(wd_ref.at[part(n)], wd.at[part(n)], wsems.at[2, n]) for n in range(cuts)]
    for pair in loads:
        for copy in pair:
            copy.start()
    for copy in down:
        copy.start()
    hbv[...] = h1_ref[...].astype(BF)
    own = load_rows(hbv, hball_ref.at[place.ctx], lsems.at[0])
    own.start()
    place.barrier()
    own.wait()
    h_gather.each("step_z", 0)

    hb = hbv[...]
    for n in range(cuts):
        for copy in loads[n]:
            copy.wait()
        u = dot32(hb, wu[:, part(n)])
        g = dot32(hb, wg[:, part(n)])
        u_buf[:, part(n)] = u
        g_buf[:, part(n)] = g
        c = g * gs_ref[:, part(n)]
        low_a[:, part(n)] = (u * us_ref[:, part(n)] * (c * lax.logistic(c))).astype(BF)
        if n == cuts - 3:
            h_gather.each("step_z", 1)
    for copy in down:
        copy.wait()

    def serve_first():
        h_gather.each("step_x", 0)
        h_gather.each("step_z", 2)

    exchange(place, lambda cols: dot32(low_a[...], wd[:, cols]), total, s1, r1, e1sems, serve_first)
    h1 = h1_ref[...]
    fs = fs_ref[...]
    hm = total[...]
    m_inv = inv_rms(hm)
    step = hm * m_inv - h1
    z = h1 + fs * step
    z_inv = inv_rms(z)
    out_ref[...] = (z * z_inv).astype(BF)
    dz = rms_back(z, z_inv, cot_ref[...].astype(F32))
    gfs_ref[...] = jnp.sum(dz * step, axis=0, keepdims=True)
    dxr_ref[...] = (1.0 - fs) * dz
    dmv[...] = rms_back(hm, m_inv, fs * dz).astype(BF)
    own = load_rows(dmv, dmball_ref.at[place.ctx], lsems.at[1])
    own.start()
    own.wait()
    m_gather.each("step_z", 0)
    h_gather.each("step_z", 3)
    h_gather.each("step_x", 1)
    h_gather.each("step_y", 1)
    h_gather.each("step_yx", 0)

    dm = dmv[...]
    for n in range(cuts):
        dgated = dot_nt(dm, wd[part(n), :])
        u, g = u_buf[:, part(n)], g_buf[:, part(n)]
        us, gs = us_ref[:, part(n)], gs_ref[:, part(n)]
        c = g * gs
        s = lax.logistic(c)
        low_a[:, part(n)] = (dgated * (c * s) * us).astype(BF)
        low_b[:, part(n)] = (dgated * (u * us) * (s * (1.0 + c * (1.0 - s))) * gs).astype(BF)
        if n == cuts // 2:
            h_gather.each("step_x", 2)
            h_gather.each("step_y", 2)
            h_gather.each("step_yx", 1)
            h_gather.each("step_c", 0)

    m_gather.each("step_z", 1)

    def serve_second():
        h_gather.each("step_x", 3)
        h_gather.each("step_y", 3)
        m_gather.each("step_x", 0)
        h_gather.each("step_yx", 2)
        m_gather.each("step_z", 2)

    exchange(place, lambda cols: dot_nt(low_a[...], wu[cols, :]) + dot_nt(low_b[...], wg[cols, :]), total, s2, r2,
             e2sems, serve_second)
    m_gather.each("step_z", 3)
    m_gather.each("step_x", 1)
    m_gather.each("step_y", 1)
    m_gather.each("step_yx", 0)
    dh1 = dxr_ref[...] + total[...]
    xf = x_ref[...].astype(F32)
    step_size = as_ref[...]
    ha = ha_ref[...]
    a_inv = inv_rms(ha)
    step = ha * a_inv - xf
    w = xf + step_size * step
    dw = rms_back(w, inv_rms(w), dh1)
    gas_ref[...] = jnp.sum(dw * step, axis=0, keepdims=True)
    dxr_ref[...] = (1.0 - step_size) * dw
    dab_ref[...] = rms_back(ha, a_inv, step_size * dw).astype(BF)

    @pl.loop(4, place.line)
    def _(k):
        for name in ("step_z", "step_x", "step_y"):
            h_gather.each(name, k)
        m_gather.each("step_z", k)

    @pl.loop(2, place.line + 1)
    def _(k):
        m_gather.each("step_x", k)
        m_gather.each("step_y", k)
        m_gather.each("step_yx", k - 1)

        @pl.when(k > 2)
        def _():
            h_gather.each("step_yx", k)
        h_gather.each("step_c", k - 1)
        m_gather.each("step_c", k - 2)

    m_gather.each("step_c", place.line - 1)
    h_gather.finish()
    m_gather.finish()


def feed_forward(hidden_one, branch_attn, x, cotangent, ff_step, attn_step, up_scale, gate_scale, w_up, w_gate, w_down,
                 n_ctx, collective_id, cut):
    rows, width = x.shape
    hidden = w_up.shape[1]
    cuts = hidden // HIDDEN_CUT
    count = width // EXCHANGE
    shape = jax.ShapeDtypeStruct
    dma = pltpu.SemaphoreType.DMA
    V = pltpu.VMEM
    box = V((count, rows, EXCHANGE), BF)
    return pl.pallas_call(
        functools.partial(mid_kernel, n_ctx, cut),
        out_shape=(pltpu.HBM((n_ctx, rows, width), BF), pltpu.HBM((n_ctx, rows, width), BF), shape((rows, width), BF),
                   shape((rows, width), BF), shape((rows, width), F32), shape((1, width), F32), shape((1, width), F32)),
        in_specs=[vmem_spec()] * 8 + [hbm_spec()] * 3,
        out_specs=(hbm_spec(),) * 2 + (vmem_spec(),) * 5,
        scratch_shapes=[
            gather_sems(n_ctx, cut), gather_sems(n_ctx, cut), dma((2,)), dma((3, cuts)), dma((2, count)), dma((2, count)),
            V((width, hidden), BF), V((width, hidden), BF), V((hidden, width), BF), V((rows, width), BF),
            V((rows, width), BF), V((rows, hidden), F32), V((rows, hidden), F32), V((rows, hidden), BF),
            V((rows, hidden), BF), V((rows, width), F32), box, box, box, box],
        compiler_params=pltpu.CompilerParams(collective_id=collective_id, has_side_effects=True,
                                             vmem_limit_bytes=30 << 20),
        cost_estimate=pl.CostEstimate(flops=5 * 10 ** 9, bytes_accessed=30 * 10 ** 6, transcendentals=10 ** 6),
        name="feed_forward",
    )(hidden_one, branch_attn, x, cotangent, ff_step, attn_step, up_scale, gate_scale, in_hbm(w_up), in_hbm(w_gate), in_hbm(w_down))


BLOCK = 4
STATS = 128


def split_parts(v, count):
    parts = []
    rest = v
    for _ in range(count):
        part = rest.astype(BF)
        parts.append(part)
        rest = rest - part.astype(F32)
    return parts


def transposed(src, dst, dtype):
    for n in range(src.shape[1] // 128):
        dst[n * 128:(n + 1) * 128, :] = src[:, n * 128:(n + 1) * 128].T.astype(dtype)


class Among:
    def __init__(self, count, stride=1, first=0):
        self.count, self.stride, self.first = count, stride, first

    def device(self, number):
        return number * self.stride + self.first

    def number(self, device):
        return lax.div(device - self.first, self.stride)

    def has(self, device):
        away = device - self.first
        return (away >= 0) & (lax.rem(away, self.stride) == 0) & (away < self.count * self.stride)


class UnitScatter:
    def __init__(self, place, source, target, send_sems, recv_sems, senders, per_sender, per_owner):
        self.p, self.source, self.target = place, source, target
        self.send_sems, self.recv_sems = send_sems, recv_sems
        self.senders, self.per_sender, self.per_owner = senders, per_sender, per_owner

    def rows(self, unit):
        return pl.ds(pl.multiple_of(unit * 8, 8), 8)

    def copy(self, unit, slot, owner):
        return pltpu.make_async_remote_copy(
            src_ref=self.source.at[self.rows(unit)], dst_ref=self.target.at[self.rows(slot)],
            send_sem=self.send_sems.at[unit], recv_sem=self.recv_sems.at[slot],
            device_id=(owner, self.p.wa), device_id_type=MESH)

    def local(self, unit, slot):
        return pltpu.make_async_copy(self.source.at[self.rows(unit)], self.target.at[self.rows(slot)],
                                     self.recv_sems.at[slot])

    def outgoing(self, remote, near):
        p = self.p

        @pl.when(self.senders.has(p.ctx))
        def _():
            @pl.loop(0, self.per_sender)
            def _(unit):
                place_of = self.senders.number(p.ctx) * self.per_sender + unit
                owner, slot = lax.div(place_of, self.per_owner), lax.rem(place_of, self.per_owner)

                @pl.when(owner != p.ctx)
                def _():
                    remote(self.copy(unit, slot, owner))

                if near is not None:
                    @pl.when(owner == p.ctx)
                    def _():
                        near(self.local(unit, slot))

    def start(self):
        self.outgoing(lambda c: c.start(), lambda c: c.start())

    def wait(self):
        p = self.p

        @pl.loop(0, self.per_owner)
        def _(slot):
            place_of = p.ctx * self.per_owner + slot
            number, unit = lax.div(place_of, self.per_sender), lax.rem(place_of, self.per_sender)
            sender = self.senders.device(number)

            @pl.when(sender != p.ctx)
            def _():
                self.copy(unit, slot, p.ctx).wait_recv()

            @pl.when(sender == p.ctx)
            def _():
                self.local(unit, slot).wait()

    def sent(self):
        self.outgoing(lambda c: c.wait_send(), None)


class Scatter:
    def __init__(self, place, source, target, sems, receivers, senders):
        self.p, self.source, self.target, self.sems = place, source, target, sems
        self.receivers, self.senders = receivers, senders

    def copy(self, dest, sender):
        number = self.receivers.number(dest)
        return pltpu.make_async_remote_copy(
            src_ref=self.source(number), dst_ref=self.target(sender),
            send_sem=self.sems.at[0, number], recv_sem=self.sems.at[1, sender],
            device_id=(dest, self.p.wa), device_id_type=MESH)

    def each(self, fn):
        p = self.p

        @pl.loop(1, p.n_ctx)
        def _(shift):
            fn(lax.rem(p.ctx + shift, p.n_ctx))

    def start(self):
        p = self.p

        @pl.when(self.senders.has(p.ctx))
        def _():
            def go(dest):
                @pl.when(self.receivers.has(dest))
                def _():
                    self.copy(dest, p.ctx).start()
            self.each(go)

            @pl.when(self.receivers.has(p.ctx))
            def _():
                self.local().start()

    def local(self):
        source = self.source(self.receivers.number(self.p.ctx))
        return pltpu.make_async_copy(source, self.target(self.p.ctx), self.sems.at[1, self.p.ctx])

    def wait(self):
        p = self.p

        @pl.when(self.receivers.has(p.ctx))
        def _():
            def got(sender):
                @pl.when(self.senders.has(sender))
                def _():
                    self.copy(p.ctx, sender).wait_recv()
            self.each(got)

            @pl.when(self.senders.has(p.ctx))
            def _():
                self.local().wait()

    def sent(self):
        p = self.p

        @pl.when(self.senders.has(p.ctx))
        def _():
            def left(dest):
                @pl.when(self.receivers.has(dest))
                def _():
                    self.copy(dest, p.ctx).wait_send()
            self.each(left)


def out_devices(n_ctx, tiles):
    stride = n_ctx // tiles
    return Among(tiles, stride, stride // 2)


def bwd_kernel(n_ctx, cut, aligned, out_aligned, *refs):
    (dab_ref, gfs_ref, gas_ref, qraw_ref, kraw_ref, lse_ref, o_ref, dxr_ref, qs_ref, us_ref, gs_ref,
     wo_ref, wq_ref, wk_ref, wv_ref, xall_ref, qall_ref, kall_ref, vall_ref, hball_ref, dmball_ref, wu_ref, wg_ref, wd_ref,
     dx_ref, got_q, gout_ref, got_u, gdown_ref, got_s, gus_ref, ggs_ref,
     daball_ref, statall_ref, turned, turned_qkv, gocc,
     asems, ssts, lsems, csems, esems, usems, tsems, osems, rsems, vsems, ssems, xsems, nsems, fsems,
     hbbuf, dmbuf, dabbuf, stbuf, qbuf, kvbuf, dobuf, rowstats, stats, delta, q2, k2, v2, do2, dq2, dk2, dv2,
     wuw, wgw, wdw, gu, gg, gd, colu, colg, comb, small, small_row, dqkv, got_t, got_o, obs, accq, sbuf, rbuf) = refs
    place = Place(n_ctx)
    rows, width = dxr_ref.shape
    block_len = rows // 2
    channels = qraw_ref.shape[1]
    tiles = channels // 128
    hidden = us_ref.shape[1]
    mine = hidden // n_ctx
    group = 2 * place.across
    subs = group // BLOCK
    many = BLOCK * rows
    window = gu.shape[0]
    scale = 1.0 / math.sqrt(HD)
    a_gather = Pieces(place, daball_ref, asems, cut)
    s_gather = Pieces(place, statall_ref, ssts, ((rows, rows, rows),))
    start = jnp.minimum(lax.div(place.ctx * mine, 128) * 128, hidden - window)
    start = pl.multiple_of(start, 128)
    offset = pl.multiple_of(place.ctx * mine - start, 8)
    win = pl.ds(start, window)
    own = [load_rows(dab_ref, daball_ref.at[place.ctx], lsems.at[0]),
           load_rows(wu_ref.at[:, win], wuw, lsems.at[2]), load_rows(wg_ref.at[:, win], wgw, lsems.at[3]),
           load_rows(wd_ref.at[win, :], wdw, lsems.at[4])]
    for copy in own:
        copy.start()
    for t in range(tiles):
        obs[t] = o_ref[:, t * 128:(t + 1) * 128].astype(BF)
    place.barrier_all()
    own[0].wait()
    a_gather.each("step_z", 0)
    d_out = dot_nt(dab_ref[...], wo_ref[...]).astype(BF)
    lane = lax.broadcasted_iota(jnp.int32, (rows, 128), 1)
    packed = jnp.zeros((rows, 128), F32)
    for t in range(tiles):
        cols = slice(t * 128, (t + 1) * 128)
        do2[t] = stack_heads(d_out[:, cols])
        both_heads = stack_heads(d_out[:, cols].astype(F32) * o_ref[:, cols])
        delta[t] = jnp.broadcast_to(jnp.sum(both_heads, axis=1, keepdims=True), (2 * rows, 128))
        for h in range(2):
            part_rows = slice(h * rows, (h + 1) * rows)
            values = split_parts(lse_ref[t, part_rows], 3) + split_parts(delta[t, part_rows], 2)
            for i, value in enumerate(values):
                packed = jnp.where(lane == i * 2 * tiles + 2 * t + h, value.astype(F32), packed)
    stats[...] = packed.astype(BF)
    own_stats = load_rows(stats, statall_ref.at[place.ctx], lsems.at[0])
    own_stats.start()
    own_stats.wait()
    s_gather.each("step_z", 0)
    everyone = Among(n_ctx)
    owners = out_devices(n_ctx, tiles)
    o_scatter = Scatter(place, lambda dest: obs.at[dest], lambda sender: got_o.at[sender], osems, owners, everyone)
    o_scatter.start()

    for t in range(tiles):
        cols = slice(t * 128, (t + 1) * 128)
        for raw_ref, dest in ((qraw_ref, q2), (kraw_ref, k2)):
            raw = raw_ref[:, cols]
            dest[t] = stack_heads((raw * head_rms(raw) * qs_ref[:, cols]).astype(BF))
    dq2[...] = jnp.zeros_like(dq2)
    dk2[...] = jnp.zeros_like(dk2)
    dv2[...] = jnp.zeros_like(dv2)
    gu[...] = jnp.zeros_like(gu)
    gg[...] = jnp.zeros_like(gg)
    gd[...] = jnp.zeros_like(gd)
    colu[...] = jnp.zeros_like(colu)
    colg[...] = jnp.zeros_like(colg)
    gocc[...] = jnp.zeros_like(gocc)

    def row_positions(shape, axis, first):
        i = lax.broadcasted_iota(jnp.int32, shape, axis)
        return position_of(first + lax.div(i, rows), lax.rem(i, rows), block_len, n_ctx)

    def own_positions(shape, axis):
        i = lax.broadcasted_iota(jnp.int32, shape, axis)
        return position_of(place.ctx, lax.rem(i, rows), block_len, n_ctx)

    total_blocks = n_ctx // BLOCK

    def serve(name, k):
        a_gather.each(name, k)
        s_gather.each(name, k)

    def kv_loads(b):
        side = lax.rem(b, 2)
        return [load_rows(ref.at[pl.ds(b * BLOCK, BLOCK)], kvbuf.at[side, i], csems.at[side, i])
                for i, ref in enumerate((kall_ref, vall_ref))]

    def wide(v):
        return jnp.concatenate([v] * (many // 128), axis=1)

    for copy in kv_loads(0):
        copy.start()

    @pl.loop(0, total_blocks)
    def _(b):
        side = lax.rem(b, 2)

        @pl.when(b + 1 < total_blocks)
        def _():
            for copy in kv_loads(b + 1):
                copy.start()

        for copy in kv_loads(b):
            copy.wait()
        allowed = row_positions((1, many), 1, b * BLOCK) <= own_positions((2 * rows, 1), 0)

        @pl.loop(0, tiles)
        def _(t):
            cols = pl.ds(pl.multiple_of(t * 128, 128), 128)
            kt = kvbuf[side, 0, :, :, cols].reshape(many, 128)
            vt = kvbuf[side, 1, :, :, cols].reshape(many, 128)
            score = dot_nt(q2[t], kt)
            p = jnp.where(allowed, jnp.exp2(score * (LOG2E * scale) - wide(lse_ref[t])), 0.0)
            dp = dot_nt(do2[t], vt)
            ds = (p * (dp - wide(delta[t])) * scale).astype(BF)
            dq2[t] += dot32(ds, kt)

        @pl.when(b == total_blocks // 4)
        def _():
            serve("step_z", 1)

        @pl.when(b == total_blocks - 1)
        def _():
            serve("step_z", 2)
            serve("step_x", 0)

    def head_back(raw_ref, grads, base, first):
        for t in range(tiles):
            cols = slice(t * 128, (t + 1) * 128)
            raw = raw_ref[:, cols]
            inv = head_rms(raw)
            normed = raw * inv
            grad = join_heads(grads[t])
            grad_scale = jnp.sum(grad * normed, axis=0, keepdims=True)
            small_row[:, cols] = grad_scale if first else small_row[:, cols] + grad_scale
            e = grad * qs_ref[:, cols]
            dqkv[base + t] = ((e - normed * pair_mean(normed * e)) * inv).astype(BF)

    head_back(qraw_ref, dq2, 0, True)
    f_scatter = Scatter(place, lambda dest: dqkv.at[dest], lambda sender: got_t.at[sender], fsems, Among(tiles), everyone)
    f_scatter.start()
    own_v = load_rows(vall_ref.at[place.ctx], dobuf.at[0], lsems.at[0])
    own_v.start()
    own_v.wait()
    for t in range(tiles):
        v2[t] = stack_heads(dobuf[0, :, t * 128:(t + 1) * 128])
    for copy in own[1:]:
        copy.wait()

    def block_of(s, k, sub):
        return ((place.z - s * k) * subs + sub) * BLOCK

    def a_loads(side, first):
        return [load_rows(ref.at[pl.ds(first, BLOCK)], buf.at[side], rsems.at[side, i])
                for i, (ref, buf) in enumerate(((daball_ref, dabbuf), (qall_ref, qbuf), (statall_ref, stbuf)))]

    def m_loads(b):
        side = lax.rem(b, 2)
        return [load_rows(dmball_ref.at[pl.ds(b * BLOCK, BLOCK)], dmbuf.at[side], xsems.at[side, 0]),
                load_rows(hball_ref.at[pl.ds(b * BLOCK, BLOCK)], hbbuf.at[side], xsems.at[side, 1])]

    def keys_part(side, first):
        for copy in a_loads(side, first):
            copy.wait()
        dab = dabbuf[side].reshape(many, width)
        dobuf[...] = dot_nt(dab, wo_ref[...]).astype(BF).reshape(BLOCK, rows, channels)
        for j in range(BLOCK):
            rowstats[:, j * rows:(j + 1) * rows] = stbuf[side, j].astype(F32).T

        @pl.when(owners.has(place.ctx))
        def _():
            gocc[...] += dot_tn(got_o[pl.ds(first, BLOCK)].reshape(many, 128), dab)

        allowed = own_positions((2 * rows, 1), 0) <= row_positions((1, many), 1, first)
        heads = 2 * tiles

        @pl.loop(0, tiles)
        def _(t):
            cols = pl.ds(pl.multiple_of(t * 128, 128), 128)
            qt = qbuf[side, :, :, cols].reshape(many, 128)
            dot_ = dobuf[:, :, cols].reshape(many, 128)

            def both_rows(parts, at):
                def one(h):
                    row = rowstats[pl.ds(at * heads + h, 1), :]
                    for i in range(1, parts):
                        row = row + rowstats[pl.ds((at + i) * heads + h, 1), :]
                    return jnp.broadcast_to(row, (rows, many))
                return jnp.concatenate([one(2 * t), one(2 * t + 1)], axis=0)

            score = dot_nt(k2[t], qt)
            p = jnp.where(allowed, jnp.exp2(score * (LOG2E * scale) - both_rows(3, 0)), 0.0)
            dp = dot_nt(v2[t], dot_)
            ds = (p * (dp - both_rows(2, 3)) * scale).astype(BF)
            dv2[t] += dot32(p.astype(BF), dot_)
            dk2[t] += dot32(ds, qt)

    def hidden_part(side):
        hb = hbbuf[side].reshape(many, width)
        dm = dmbuf[side].reshape(many, width)
        us, gs = us_ref[:, win], gs_ref[:, win]
        u = dot32(hb, wuw[...])
        g = dot32(hb, wgw[...])
        dgated = dot_nt(dm, wdw[...])
        a, c = u * us, g * gs
        s = lax.logistic(c)
        cs = c * s
        r = s * (1.0 + c * (1.0 - s))
        da = dgated * cs
        dc = dgated * a * r
        colu[...] += jnp.sum((da * u).reshape(many // 8, 8, window), axis=0)
        colg[...] += jnp.sum((dc * g).reshape(many // 8, 8, window), axis=0)
        gu[...] += dot_tn((da * us).astype(BF), hb)
        gg[...] += dot_tn((dc * gs).astype(BF), hb)
        gd[...] += dot_tn((a * cs).astype(BF), dm)

    def hidden_all():
        for copy in m_loads(0):
            copy.start()

        @pl.loop(0, total_blocks)
        def _(b):
            @pl.when(b + 1 < total_blocks)
            def _():
                for copy in m_loads(b + 1):
                    copy.start()

            for copy in m_loads(b):
                copy.wait()
            hidden_part(lax.rem(b, 2))

            serve("step_z", b + 3)
            serve("step_x", b + 1)
            serve("step_y", b + 1)
            serve("step_yx", b)
            serve("step_c", b - 1)

    def both(k, fn):
        for s in (1, -1):
            @pl.when(a_gather.parts[0].exists(s, k))
            def _():
                @pl.loop(0, subs)
                def _(sub):
                    fn(0 if s > 0 else 1, block_of(s, k, sub))

    def begin(loads):
        for copy in loads:
            copy.start()

    def keys_full(side, first):
        begin(a_loads(side, first))
        keys_part(side, first)

    hidden_all()

    gdown_ref[...] = gd[pl.ds(offset, mine), :]
    comb[0:mine] = gu[pl.ds(offset, mine), :]
    comb[mine:2 * mine] = gg[pl.ds(offset, mine), :]
    comb[2 * mine:] = jnp.zeros((comb.shape[0] - 2 * mine, width), F32)
    transposed(comb, turned, BF)
    part = width // n_ctx

    def row_block(ref, size):
        return lambda dest: ref.at[pl.ds(pl.multiple_of(dest * size, 8), size)]

    if aligned:
        u_scatter = Scatter(place, row_block(turned, part), lambda sender: got_u.at[sender], usems, everyone, everyone)
        u_scatter.start()
    shift = lax.rem(window - offset, window)
    gus_ref[...] = pltpu.roll(jnp.broadcast_to(jnp.sum(colu[...], axis=0, keepdims=True), (8, window)), shift, 1)
    ggs_ref[...] = pltpu.roll(jnp.broadcast_to(jnp.sum(colg[...], axis=0, keepdims=True), (8, window)), shift, 1)

    o_scatter.wait()

    @pl.loop(0, place.line)
    def _(k):
        serve("step_c", total_blocks - 1 + k)
        if subs == 1:
            both(k, lambda side, first: begin(a_loads(side, first)))
            both(k, keys_part)
        else:
            both(k, keys_full)

    if out_aligned:
        g_scatter = UnitScatter(place, gocc, gout_ref, ssems.at[0], ssems.at[1], owners, 16, channels // n_ctx // 8)
        g_scatter.start()

    head_back(kraw_ref, dk2, tiles, False)
    for t in range(tiles):
        dqkv[2 * tiles + t] = join_heads(dv2[t]).astype(BF)
    t_scatter = Scatter(place, lambda dest: dqkv.at[dest + tiles], lambda sender: got_t.at[sender], tsems,
                        Among(2 * tiles, 1, tiles), everyone)
    t_scatter.start()
    head_part = channels // n_ctx
    for i in range(n_ctx):
        small[i, 0:1, 0:part] = gfs_ref[:, i * part:(i + 1) * part]
        small[i, 1:2, 0:part] = gas_ref[:, i * part:(i + 1) * part]
        small[i, 2:3, 0:head_part] = small_row[:, i * head_part:(i + 1) * head_part]
    n_scatter = Scatter(place, lambda dest: small.at[dest], lambda sender: got_s.at[sender], nsems, everyone, everyone)
    n_scatter.start()

    def input_terms(cols):
        total = None
        for n, w_ref in enumerate((wq_ref, wk_ref, wv_ref)):
            grad = jnp.concatenate([dqkv[n * tiles + t] for t in range(tiles)], axis=1)
            term = dot_nt(grad, w_ref[cols, :])
            total = term if total is None else total + term
        return total

    pl.when(place.ctx < 3 * tiles)(load_rows(xall_ref.at[pl.ds(0, BLOCK)], hbbuf.at[0], xsems.at[0, 0]).start)
    exchange(place, input_terms, dx_ref, sbuf, rbuf, esems)
    dx_ref[...] += dxr_ref[...]

    f_scatter.wait()
    t_scatter.wait()

    @pl.when(place.ctx < 3 * tiles)
    def _():
        accq[...] = jnp.zeros_like(accq)

        def x_load(b):
            side = lax.rem(b, 2)
            return load_rows(xall_ref.at[pl.ds(b * BLOCK, BLOCK)], hbbuf.at[side], xsems.at[side, 0])

        @pl.loop(0, total_blocks)
        def _(b):
            @pl.when(b + 1 < total_blocks)
            def _():
                x_load(b + 1).start()

            x_load(b).wait()
            accq[...] += dot_tn(got_t[pl.ds(b * BLOCK, BLOCK)].reshape(many, 128),
                                hbbuf[lax.rem(b, 2)].reshape(many, width))

        transposed(accq, turned_qkv, BF)

    if aligned:
        q_scatter = Scatter(place, row_block(turned_qkv, part), lambda sender: got_q.at[sender], vsems, everyone, Among(3 * tiles))
        q_scatter.start()
        u_scatter.wait()
        q_scatter.wait()
        u_scatter.sent()
        q_scatter.sent()
    if out_aligned:
        g_scatter.wait()
        g_scatter.sent()
    a_gather.finish()
    s_gather.finish()
    o_scatter.sent()
    f_scatter.sent()
    t_scatter.sent()
    n_scatter.wait()
    n_scatter.sent()


def backward_attention(dab, grad_ff_step, grad_attn_step, q_raw, k_raw, lse, attended, dxr, qk_scale, up_scale, gate_scale,
                       w_out, w_query, w_key, w_value, x_all, q_all, k_all, v_all, hb_all, dmb_all, w_up, w_gate, w_down,
                       n_ctx, collective_id, cut):
    rows, width = dxr.shape
    channels = q_raw.shape[1]
    tiles = channels // 128
    hidden = up_scale.shape[1]
    mine = hidden // n_ctx
    part = width // n_ctx
    aligned = part % 16 == 0
    out_rows = channels // n_ctx
    out_aligned = out_rows % 8 == 0
    window = 256
    pair = -(-2 * mine // 128) * 128
    count = width // EXCHANGE
    many = BLOCK * rows
    n_blocks = n_ctx
    shape = jax.ShapeDtypeStruct
    dma = pltpu.SemaphoreType.DMA
    V = pltpu.VMEM
    stack = lambda dtype: V((tiles, 2 * rows, 128), dtype)
    outs = (
        shape((rows, width), F32),
        shape((3 * tiles, part, 128), BF), shape((out_rows, width), F32), shape((n_ctx, part, pair), BF),
        shape((mine, width), F32), shape((n_ctx, 8, 128), F32), shape((8, window), F32), shape((8, window), F32),
        shape((n_ctx, rows, width), BF), shape((n_ctx, rows, STATS), BF),
        shape((width, pair), BF), shape((width, 128), BF), shape((128, width), F32))
    return pl.pallas_call(
        functools.partial(bwd_kernel, n_ctx, cut, aligned, out_aligned),
        out_shape=outs,
        in_specs=[vmem_spec()] * 15 + [any_spec()] * 9,
        out_specs=(vmem_spec(),) * 8 + (hbm_spec(),) * 2 + (vmem_spec(),) * 3,
        scratch_shapes=[
            gather_sems(n_ctx, cut), gather_sems(n_ctx, ((rows, rows, rows),)), dma((5,)), dma((2, 2)), dma((2, count)),
            dma((2, n_ctx)), dma((2, n_ctx)), dma((2, n_ctx)), dma((2, 3)), dma((2, n_ctx)), dma((2, 16)), dma((2, 2)), dma((2, n_ctx)), dma((2, n_ctx)),
            V((2, BLOCK, rows, width), BF), V((2, BLOCK, rows, width), BF), V((2, BLOCK, rows, width), BF), V((2, BLOCK, rows, STATS), BF),
            V((2, BLOCK, rows, channels), BF), V((2, 2, BLOCK, rows, channels), BF), V((BLOCK, rows, channels), BF),
            V((STATS, many), F32), V((rows, STATS), BF), stack(F32), stack(BF), stack(BF), stack(BF), stack(BF), stack(F32), stack(F32), stack(F32),
            V((width, window), BF), V((width, window), BF), V((window, width), BF),
            V((window, width), F32), V((window, width), F32), V((window, width), F32),
            V((8, window), F32), V((8, window), F32), V((pair, width), F32), V((n_ctx, 8, 128), F32), V((1, channels), F32),
            V((3 * tiles, rows, 128), BF), V((n_ctx, rows, 128), BF), V((n_ctx, rows, 128), BF), V((tiles, rows, 128), BF),
            V((128, width), F32),
            V((count, rows, EXCHANGE), BF), V((count, rows, EXCHANGE), BF)],
        compiler_params=pltpu.CompilerParams(collective_id=collective_id, has_side_effects=True,
                                             vmem_limit_bytes=40 << 20),
        cost_estimate=pl.CostEstimate(flops=20 * 10 ** 9, bytes_accessed=60 * 10 ** 6, transcendentals=6 * 10 ** 6),
        name="backward_attention",
    )(dab, grad_ff_step, grad_attn_step, q_raw, k_raw, lse, attended, dxr, qk_scale, up_scale, gate_scale,
      w_out, w_query, w_key, w_value, x_all, q_all, k_all, v_all, hb_all, dmb_all, w_up, w_gate, w_down)


def last_kernel(result_ref, dx_ref, gotq_ref, gout_ref, gotu_ref, gdown_ref, gots_ref, gus_ref, ggs_ref,
                o_result, o_dx, o_gq, o_gk, o_gv, o_gout, o_gup, o_ggate, o_gdown, o_gqs, o_gus, o_ggs, o_gas, o_gfs):
    o_result[...] = result_ref[...]
    o_dx[...] = dx_ref[...]
    o_gout[...] = gout_ref[...]
    o_gdown[...] = gdown_ref[...]
    mine = o_gus.shape[1]
    tiles = o_gq.shape[1] // 128
    for j in range(gotu_ref.shape[0]):
        o_gup[:, j * mine:(j + 1) * mine] = gotu_ref[j, :, 0:mine].astype(F32)
        o_ggate[:, j * mine:(j + 1) * mine] = gotu_ref[j, :, mine:2 * mine].astype(F32)
    for n, ref in enumerate((o_gq, o_gk, o_gv)):
        for t in range(tiles):
            ref[:, t * 128:(t + 1) * 128] = gotq_ref[n * tiles + t].astype(F32)
    total = jnp.sum(gots_ref[...], axis=0)
    for row, ref in enumerate((o_gfs, o_gas, o_gqs)):
        ref[...] = total[row:row + 1, 0:ref.shape[1]]
    o_gus[...] = gus_ref[0:1, 0:mine]
    o_ggs[...] = ggs_ref[0:1, 0:mine]


def last_step(parts, n_ctx, channels, hidden):
    width = parts[1].shape[1]
    part, mine = width // n_ctx, hidden // n_ctx
    shape = jax.ShapeDtypeStruct
    outs = [shape(parts[0].shape, BF), shape(parts[1].shape, F32)] + [shape((part, channels), F32)] * 3
    outs += [shape(parts[3].shape, F32)] + [shape((part, hidden), F32)] * 2 + [shape((mine, width), F32)]
    outs += [shape((1, channels // n_ctx), F32)] + [shape((1, mine), F32)] * 2 + [shape((1, part), F32)] * 2
    return pl.pallas_call(
        last_kernel, out_shape=tuple(outs), in_specs=[vmem_spec()] * len(parts), out_specs=(vmem_spec(),) * len(outs),
        compiler_params=pltpu.CompilerParams(vmem_limit_bytes=32 << 20), name="last_step")(*parts)


CUT = ((64, 48, 48), (64, 48, 48))


def shards(layer_input, w_query, w_key, w_value, w_out, w_up, w_gate, w_down, qk_scale, up_scale,
           gate_scale, attention_step, feedforward_step, cotangent):
    n_ctx = lax.axis_size("ctx")
    ctx = lax.axis_index("ctx")
    rows = 2 * layer_input.shape[2]
    width = layer_input.shape[3]
    channels = w_query.shape[1]
    hidden = w_up.shape[1]
    tiles = channels // 128
    x = layer_input.reshape(rows, width)
    flat = lambda v: v.reshape(1, -1)
    x_all, q_all, k_all, v_all, q_raw, k_raw, attended, lse, hidden_one, branch_attn = forward_attention(
        x, w_query, w_key, w_value, flat(qk_scale), w_out, flat(attention_step), n_ctx, 0, CUT)
    hb_all, dmb_all, result, dab, input_res, grad_ff_step, grad_attn_step = feed_forward(
        hidden_one, branch_attn, x, cotangent.reshape(rows, width), flat(feedforward_step), flat(attention_step),
        flat(up_scale), flat(gate_scale), w_up, w_gate, w_down, n_ctx, 1, CUT)
    (input_grad, got_q, grad_out, got_u, grad_down, got_s, gus, ggs,
     _, _, turned, turned_qkv, gocc) = backward_attention(
        dab, grad_ff_step, grad_attn_step, q_raw, k_raw, lse, attended, input_res, flat(qk_scale), flat(up_scale),
        flat(gate_scale), w_out, w_query, w_key, w_value, x_all, q_all, k_all, v_all, hb_all, dmb_all,
        w_up, w_gate, w_down, n_ctx, 2, CUT)
    part = width // n_ctx
    if part % 16:
        turned, turned_qkv = lax.optimization_barrier((turned, turned_qkv))
        got_u = lax.all_to_all(turned, "ctx", 0, 0, tiled=True).reshape(n_ctx, part, -1)
        got_q = lax.all_to_all(turned_qkv, "ctx", 0, 0, tiled=True).reshape(n_ctx, part, 128)[:3 * tiles]
    if (channels // n_ctx) % 8:
        gocc = lax.optimization_barrier(gocc)
        whole = jnp.zeros((n_ctx, 128, width), F32)
        whole = lax.dynamic_update_slice_in_dim(whole, gocc[None], ctx, 0)[n_ctx // tiles // 2::n_ctx // tiles][:tiles]
        grad_out = lax.psum_scatter(whole.reshape(channels, width), "ctx", scatter_dimension=0, tiled=True)
    outs = last_step((result, input_grad, got_q, grad_out, got_u, grad_down, got_s, gus, ggs), n_ctx, channels, hidden)
    tokens = tuple(v.reshape(layer_input.shape) for v in outs[:2])
    return tokens + tuple(outs[2:9]) + tuple(v.reshape(-1) for v in outs[9:])


def solution(mesh):
    placed = (
        P("ctx", None, None, None),
        P(None, "wa"),
        P(None, "wa"),
        P(None, "wa"),
        P("wa", None),
        P(None, "wa"),
        P(None, "wa"),
        P("wa", None),
        P("wa"),
        P("wa"),
        P("wa"),
        P(),
        P(),
        P("ctx", None, None, None),
    )
    return jax.shard_map(
        shards,
        mesh=mesh,
        in_specs=placed,
        out_specs=(
            P("ctx", None, None, None),
            P("ctx", None, None, None),
            P("ctx", "wa"),
            P("ctx", "wa"),
            P("ctx", "wa"),
            P(("wa", "ctx"), None),
            P("ctx", "wa"),
            P("ctx", "wa"),
            P(("wa", "ctx"), None),
            P(("wa", "ctx")),
            P(("wa", "ctx")),
            P(("wa", "ctx")),
            P("ctx"),
            P("ctx"),
        ),
        check_vma=False,
    )
```

```python
import functools
from functools import partial
import math

import jax
import jax.numpy as jnp
from jax import lax
from jax.experimental import pallas as pl
from jax.experimental.pallas import tpu as pltpu
from jax.sharding import PartitionSpec as P

HD = 64
MESH = pl.DeviceIdType.MESH


def layout_of(n_ctx):
    chips = n_ctx // 2
    across = 2 if chips <= 8 else 4
    return chips // across, across


class Place:
    def __init__(self, n_ctx):
        self.n_ctx = n_ctx
        self.line, self.across = layout_of(n_ctx)
        self.ctx = lax.axis_index("ctx")
        self.wa = lax.axis_index("wa")
        self.core = lax.rem(self.ctx, 2)
        chip = lax.div(self.ctx, 2)
        self.x = lax.rem(chip, self.across)
        self.z = lax.div(chip, self.across)

    def index(self, z, x, core):
        return (z * self.across + x) * 2 + core

    def at(self, z, x, core):
        return (self.index(z, x, core), self.wa)

    def sibling(self):
        return self.at(self.z, self.x, 1 - self.core)

    def partner(self):
        return (self.ctx, 1 - self.wa)

    def inside(self, z):
        return (z >= 0) & (z < self.line)

    def column(self, shift):
        return lax.rem(self.x + shift, self.across)

    def barrier(self):
        sem = pltpu.get_barrier_semaphore()

        def signal(device):
            pl.semaphore_signal(sem, inc=1, device_id=device, device_id_type=MESH)

        signal(self.sibling())
        signal(self.partner())
        for shift in range(1, self.across):
            signal(self.at(self.z, self.column(shift), self.core))
        count = jnp.int32(self.across + 1)
        for step in (-1, 1):
            near = self.inside(self.z + step)
            pl.when(near)(functools.partial(signal, self.at(self.z + step, self.x, self.core)))
            count = count + near.astype(jnp.int32)
        pl.semaphore_wait(sem, count)

    def barrier_all(self):
        sem = pltpu.get_barrier_semaphore()
        pl.semaphore_signal(sem, inc=1, device_id=self.partner(), device_id_type=MESH)

        @pl.loop(1, self.n_ctx)
        def _(shift):
            other = lax.rem(self.ctx + shift, self.n_ctx)
            pl.semaphore_signal(sem, inc=1, device_id=(other, self.wa), device_id_type=MESH)

        pl.semaphore_wait(sem, self.n_ctx)


class Gather:
    def __init__(self, place, out, sems, base, first, rows, z_rows, x_rows):
        self.p = place
        self.out = out
        self.sems = sems
        self.base = base
        self.first, self.rows = first, rows
        self.z_rows, self.x_rows = z_rows, x_rows
        self.slots = 2 * place.line

    @staticmethod
    def sem_count(n_ctx):
        line, across = layout_of(n_ctx)
        return 2 * line * 3 * across

    def sem(self, kind, s, k, shift=0):
        kinds = self.p.across - 1
        order = {"z": 0, "y": 1, "c": 2, "x": 3, "yx": 3 + kinds, "cx": 3 + 2 * kinds}[kind]
        return self.base + (order + shift) * self.slots + (0 if s > 0 else self.p.line) + k

    def copy(self, sem, block, start, size, device):
        view = self.out.at[block, pl.ds(pl.multiple_of(self.first + start, 16), size)]
        return pltpu.make_async_remote_copy(
            src_ref=view, dst_ref=view, send_sem=self.sems.at[0, sem], recv_sem=self.sems.at[1, sem],
            device_id=device, device_id_type=MESH)

    def exists(self, s, k):
        ok = self.p.inside(self.p.z - s * k) & (k >= 0) & (k < self.p.line)
        return ok if s > 0 else ok & (k > 0)

    def d_z(self, s, k, block, device):
        return self.copy(self.sem("z", s, k), block, self.p.wa * (self.rows - self.z_rows), self.z_rows, device)

    def d_x(self, s, k, shift, block, device):
        return self.copy(self.sem("x", s, k, shift - 1), block, self.p.wa * (self.rows - self.x_rows), self.x_rows, device)

    def d_y(self, kind, s, k, shift, block, size, sending):
        side = self.p.wa if sending else 1 - self.p.wa
        return self.copy(self.sem(kind, s, k, shift), block, side * size, self.rows - size, self.p.partner())

    def d_c(self, kind, s, k, shift, block):
        return self.copy(self.sem(kind, s, k, shift), block, 0, self.rows, self.p.sibling())

    def ok_forward(self, s, k):
        p = self.p
        return p.inside(p.z - s * k) & p.inside(p.z + s) & (k >= 0) & (k + 1 < p.line)

    def step_z(self, k):
        p = self.p
        me = (p.ctx, p.wa)
        for s in (1, -1):
            block = p.index(p.z - s * k, p.x, p.core)

            @pl.when(self.exists(s, k) & (k > 0))
            def _():
                self.d_z(s, k, block, me).wait_recv()

            @pl.when(self.ok_forward(s, k))
            def _():
                self.d_z(s, k + 1, block, p.at(p.z + s, p.x, p.core)).start()

            @pl.when(self.exists(s, k))
            def _():
                for shift in range(1, p.across):
                    self.d_x(s, k, shift, block, p.at(p.z, p.column(shift), p.core)).start()
                if s > 0:
                    @pl.when(k == 0)
                    def _():
                        self.d_c("c", s, k, 0, block).start()

                if self.z_rows < self.rows:
                    @pl.when(k > 0)
                    def _():
                        self.d_y("y", s, k, 0, block, self.z_rows, True).start()

    def step_y(self, k):
        p = self.p
        for s in (1, -1):
            @pl.when(self.exists(s, k) & (k > 0))
            def _():
                block = p.index(p.z - s * k, p.x, p.core)
                if self.z_rows < self.rows:
                    self.d_y("y", s, k, 0, block, self.z_rows, False).wait_recv()
                self.d_c("c", s, k, 0, block).start()

    def step_x(self, k):
        p = self.p
        for s in (1, -1):
            @pl.when(self.exists(s, k))
            def _():
                for shift in range(1, p.across):
                    block = p.index(p.z - s * k, p.column(p.across - shift), p.core)
                    self.d_x(s, k, shift, block, (p.ctx, p.wa)).wait_recv()
                    if self.x_rows < self.rows:
                        self.d_y("yx", s, k, shift - 1, block, self.x_rows, True).start()

    def step_yx(self, k):
        p = self.p
        for s in (1, -1):
            @pl.when(self.exists(s, k))
            def _():
                for shift in range(1, p.across):
                    block = p.index(p.z - s * k, p.column(p.across - shift), p.core)
                    if self.x_rows < self.rows:
                        self.d_y("yx", s, k, shift - 1, block, self.x_rows, False).wait_recv()
                    self.d_c("cx", s, k, shift - 1, block).start()

    def step_c(self, k):
        p = self.p
        for s in (1, -1):
            @pl.when(self.exists(s, k))
            def _():
                self.d_c("c", s, k, 0, p.index(p.z - s * k, p.x, 1 - p.core)).wait_recv()
                for shift in range(1, p.across):
                    block = p.index(p.z - s * k, p.column(p.across - shift), 1 - p.core)
                    self.d_c("cx", s, k, shift - 1, block).wait_recv()

    def finish(self):
        p = self.p

        @pl.loop(0, p.line)
        def _(k):
            for s in (1, -1):
                block = p.index(p.z - s * k, p.x, p.core)

                @pl.when(self.ok_forward(s, k))
                def _():
                    self.d_z(s, k + 1, block, p.at(p.z + s, p.x, p.core)).wait_send()

                @pl.when(self.exists(s, k))
                def _():
                    self.d_c("c", s, k, 0, block).wait_send()
                    if self.z_rows < self.rows:
                        @pl.when(k > 0)
                        def _():
                            self.d_y("y", s, k, 0, block, self.z_rows, True).wait_send()
                    for shift in range(1, p.across):
                        self.d_x(s, k, shift, block, p.at(p.z, p.column(shift), p.core)).wait_send()
                        other = p.index(p.z - s * k, p.column(p.across - shift), p.core)
                        if self.x_rows < self.rows:
                            self.d_y("yx", s, k, shift - 1, other, self.x_rows, True).wait_send()
                        self.d_c("cx", s, k, shift - 1, other).wait_send()


class Pieces:
    def __init__(self, place, out, sems, cut):
        n = Gather.sem_count(place.n_ctx)
        self.p = place
        self.parts = []
        first = 0
        for number, (rows, z_rows, x_rows) in enumerate(cut):
            self.parts.append(Gather(place, out, sems, number * n, first, rows, z_rows, x_rows))
            first += rows

    def each(self, name, k):
        for part in self.parts:
            getattr(part, name)(k)

    def step(self, t):
        self.each("step_z", t)
        for part in self.parts:
            part.step_x(t - 1)
            part.step_y(t - 1)
        self.each("step_yx", t - 2)
        self.each("step_c", t - 3)

    def step_count(self):
        return self.p.line + 3

    def finish(self):
        for part in self.parts:
            part.finish()


def gather_sems(n_ctx, cut):
    return pltpu.SemaphoreType.DMA((2, len(cut) * Gather.sem_count(n_ctx)))


NORM_EPS = 1e-06
BF = jnp.bfloat16
F32 = jnp.float32


def dot32(a, b):
    return jnp.dot(a, b, preferred_element_type=F32)


def dot_tn(a, b):
    return lax.dot_general(a, b, (((0,), (0,)), ((), ())), preferred_element_type=F32)


def dot_nt(a, b):
    return lax.dot_general(a, b, (((1,), (1,)), ((), ())), preferred_element_type=F32)


def row_mean(v):
    return jnp.mean(v, axis=-1, keepdims=True)


def inv_rms(v):
    return lax.rsqrt(row_mean(v * v) + NORM_EPS)


def rms_back(v, inv, grad):
    n = v * inv
    return (grad - n * row_mean(n * grad)) * inv


def pair_mean(v):
    row = lax.broadcasted_iota(jnp.int32, (128, 128), 0)
    col = lax.broadcasted_iota(jnp.int32, (128, 128), 1)
    ones = jnp.where((row < HD) == (col < HD), 1.0 / HD, 0.0).astype(BF)
    high = v.astype(BF)
    lowp = (v - high.astype(F32)).astype(BF)
    return dot32(high, ones) + dot32(lowp, ones)


def head_rms(v):
    return lax.rsqrt(pair_mean(v * v) + NORM_EPS)


def position_of(shard, index, block_len, n_ctx):
    late = index >= block_len
    block = jnp.where(late, 2 * n_ctx - 1 - shard, shard)
    return block * block_len + jnp.where(late, index - block_len, index)


def stack_heads(v):
    first = lax.broadcasted_iota(jnp.int32, v.shape, 1) < HD
    zero = jnp.zeros_like(v)
    return jnp.concatenate([jnp.where(first, v, zero), jnp.where(first, zero, v)], axis=0)


def join_heads(v):
    rows = v.shape[0] // 2
    first = lax.broadcasted_iota(jnp.int32, (rows, 128), 1) < HD
    return jnp.where(first, v[:rows], v[rows:])


def load_rows(src, dst, sem):
    return pltpu.make_async_copy(src, dst, sem)


LOG2E = 1.4426950408889634
EXCHANGE = 256
TOGETHER = 4


def fwd_kernel(n_ctx, cut, x_ref, qs_ref, step_ref, wq_hbm, wk_hbm, wv_hbm, wo_hbm,
               xall_ref, qall_ref, kall_ref, vall_ref, qraw_ref, kraw_ref, o_ref, lse_ref, h1_ref, ha_ref,
               gsems, lsems, wsems, esems, psems, wq_ref, wk_ref, wv_ref, wo_ref, xbuf, qbuf, kbuf, vbuf, q2, acc, lpart, sbuf, rbuf):
    place = Place(n_ctx)
    rows, width = x_ref.shape
    block_len = rows // 2
    channels = wq_ref.shape[1]
    tiles = channels // 128
    group = 2 * place.across
    plane = group * rows
    gather = Pieces(place, xall_ref, gsems, cut)
    own = load_rows(x_ref, xall_ref.at[place.ctx], lsems.at[0])
    own.start()
    weights = [load_rows(src, dst, psems.at[i]) for i, (src, dst) in enumerate(
        ((wq_hbm, wq_ref), (wk_hbm, wk_ref), (wv_hbm, wv_ref), (wo_hbm, wo_ref)))]
    for copy in weights:
        copy.start()
    place.barrier()
    own.wait()
    gather.each("step_z", 0)
    for copy in weights:
        copy.wait()

    xv = x_ref[...]
    kraw_ref[...] = dot32(xv, wk_ref[...])
    qraw_ref[...] = dot32(xv, wq_ref[...])
    for t in range(tiles):
        cols = slice(t * 128, (t + 1) * 128)
        raw = qraw_ref[:, cols]
        q2[t] = stack_heads((raw * head_rms(raw) * qs_ref[:, cols]).astype(BF))
    acc[...] = jnp.zeros_like(acc)
    lpart[...] = jnp.zeros_like(lpart)

    def plane_of(s, k):
        return place.z - s * k

    def hbm(ref, zp):
        return ref.at[pl.ds(zp * group, group)]

    def x_load(s, k):
        side = 0 if s > 0 else 1
        return load_rows(hbm(xall_ref, plane_of(s, k)), xbuf.at[side], lsems.at[1 + side])

    def stores(s, k):
        side = 0 if s > 0 else 1
        zp = plane_of(s, k)
        return [load_rows(buf.at[side], hbm(ref, zp), wsems.at[side, i])
                for i, (buf, ref) in enumerate(((qbuf, qall_ref), (kbuf, kall_ref), (vbuf, vall_ref)))]

    def project(s, k):
        side = 0 if s > 0 else 1
        x_load(s, k).wait()

        @pl.loop(0, group // TOGETHER)
        def _(r):
            some = pl.ds(r * TOGETHER, TOGETHER)
            xr = xbuf[side, some].reshape(TOGETHER * rows, width)
            for w_ref, buf in ((wq_ref, qbuf), (wk_ref, kbuf)):
                raw = dot32(xr, w_ref[...])
                for t in range(tiles):
                    cols = slice(t * 128, (t + 1) * 128)
                    part = raw[:, cols]
                    normed = (part * head_rms(part) * qs_ref[:, cols]).astype(BF)
                    buf[side, some, :, cols] = normed.reshape(TOGETHER, rows, 128)
            vbuf[side, some] = dot32(xr, wv_ref[...]).astype(BF).reshape(TOGETHER, rows, channels)

        for copy in stores(s, k):
            copy.start()

    def attend(s, k):
        side = 0 if s > 0 else 1
        zp = plane_of(s, k)
        qi = lax.broadcasted_iota(jnp.int32, (2 * rows, 1), 0)
        qi = jnp.where(qi >= rows, qi - rows, qi)
        qpos = position_of(place.ctx, qi, block_len, n_ctx)
        ki = lax.broadcasted_iota(jnp.int32, (1, plane), 1)
        kpos = position_of(zp * group + lax.div(ki, rows), lax.rem(ki, rows), block_len, n_ctx)
        allowed = kpos <= qpos

        @pl.loop(0, tiles)
        def _(t):
            cols = pl.ds(pl.multiple_of(t * 128, 128), 128)
            kt = kbuf[side, :, :, cols].reshape(plane, 128)
            vt = vbuf[side, :, :, cols].reshape(plane, 128)
            score = dot_nt(q2[t], kt)
            e = jnp.where(allowed, jnp.exp2(score * (LOG2E / math.sqrt(HD))), 0.0)
            total = e[:, :128]
            for j in range(1, plane // 128):
                total = total + e[:, j * 128:(j + 1) * 128]
            lpart[t] += total
            acc[t] += dot32(e.astype(BF), vt)

        for copy in stores(s, k):
            copy.wait()

    def both(k, fn):
        for s in (1, -1):
            pl.when(gather.parts[0].exists(s, k))(functools.partial(fn, s, k))

    gather.each("step_z", 1)

    @pl.loop(1, place.line + 2)
    def _(t):
        gather.each("step_x", t - 1)
        gather.each("step_y", t - 1)
        both(t - 2, attend)
        gather.each("step_yx", t - 1)
        gather.each("step_c", t - 1)
        both(t - 1, lambda s, k: x_load(s, k).start())
        gather.each("step_z", t + 1)
        both(t - 1, project)

    for t in range(tiles):
        mass = jnp.sum(lpart[t], axis=1, keepdims=True)
        o_ref[:, t * 128:(t + 1) * 128] = join_heads(acc[t] / mass)
        lse_ref[t] = jnp.broadcast_to(jnp.log(mass) * LOG2E, (2 * rows, 128))

    exchange(place, lambda cols: dot32(o_ref[...].astype(BF), wo_ref[:, cols]), ha_ref, sbuf, rbuf, esems)
    ha = ha_ref[...]
    xf = x_ref[...].astype(F32)
    w = xf + step_ref[...] * (ha * inv_rms(ha) - xf)
    h1_ref[...] = w * inv_rms(w)
    gather.finish()


def exchange(place, term, sum_ref, sbuf, rbuf, esems, between=None):
    width = sum_ref.shape[1]

    def copy(n):
        return pltpu.make_async_remote_copy(
            src_ref=sbuf.at[n], dst_ref=rbuf.at[n], send_sem=esems.at[0, n], recv_sem=esems.at[1, n],
            device_id=place.partner(), device_id_type=MESH)

    count = width // EXCHANGE
    for n in range(count):
        sbuf[n] = term(slice(n * EXCHANGE, (n + 1) * EXCHANGE)).astype(BF)
        copy(n).start()
    if between is not None:
        between()
    for n in range(count):
        copy(n).wait()
        sum_ref[:, n * EXCHANGE:(n + 1) * EXCHANGE] = sbuf[n].astype(F32) + rbuf[n].astype(F32)


def vmem_spec():
    return pl.BlockSpec(memory_space=pltpu.VMEM)


def in_hbm(v):
    return pltpu.with_memory_space_constraint(v, pltpu.HBM)


def hbm_spec():
    return pl.BlockSpec(memory_space=pltpu.HBM)


def any_spec():
    return pl.BlockSpec(memory_space=pl.ANY)


def forward_attention(x, w_query, w_key, w_value, qk_scale, w_out, step, n_ctx, collective_id, cut):
    rows, width = x.shape
    channels = w_query.shape[1]
    tiles = channels // 128
    line, across = layout_of(n_ctx)
    group = 2 * across
    count = width // EXCHANGE
    shape = jax.ShapeDtypeStruct
    return pl.pallas_call(
        functools.partial(fwd_kernel, n_ctx, cut),
        out_shape=(pltpu.HBM((n_ctx, rows, width), BF),) + (pltpu.HBM((n_ctx, rows, channels), BF),) * 3
        + (shape((rows, channels), F32),) * 3 + (shape((tiles, 2 * rows, 128), F32),) + (shape((rows, width), F32),) * 2,
        in_specs=[vmem_spec()] * 3 + [hbm_spec()] * 4,
        out_specs=(hbm_spec(),) * 4 + (vmem_spec(),) * 6,
        scratch_shapes=[
            gather_sems(n_ctx, cut), pltpu.SemaphoreType.DMA((3,)), pltpu.SemaphoreType.DMA((2, 3)),
            pltpu.SemaphoreType.DMA((2, count)), pltpu.SemaphoreType.DMA((4,)),
            pltpu.VMEM((width, channels), BF), pltpu.VMEM((width, channels), BF), pltpu.VMEM((width, channels), BF),
            pltpu.VMEM((channels, width), BF),
            pltpu.VMEM((2, group, rows, width), BF),
            pltpu.VMEM((2, group, rows, channels), BF), pltpu.VMEM((2, group, rows, channels), BF),
            pltpu.VMEM((2, group, rows, channels), BF),
            pltpu.VMEM((tiles, 2 * rows, 128), BF), pltpu.VMEM((tiles, 2 * rows, 128), F32),
            pltpu.VMEM((tiles, 2 * rows, 128), F32),
            pltpu.VMEM((count, rows, EXCHANGE), BF), pltpu.VMEM((count, rows, EXCHANGE), BF)],
        compiler_params=pltpu.CompilerParams(collective_id=collective_id, has_side_effects=True,
                                             vmem_limit_bytes=32 << 20),
        cost_estimate=pl.CostEstimate(flops=12 * 10 ** 9, bytes_accessed=40 * 10 ** 6, transcendentals=3 * 10 ** 6),
        name="forward_attention",
    )(x, qk_scale, step, *(in_hbm(w) for w in (w_query, w_key, w_value, w_out)))


HIDDEN_CUT = 256


def mid_kernel(n_ctx, cut, h1_ref, ha_ref, x_ref, cot_ref, fs_ref, as_ref, us_ref, gs_ref, wu_ref, wg_ref, wd_ref,
               hball_ref, dmball_ref, out_ref, dab_ref, dxr_ref, gfs_ref, gas_ref,
               hsems, msems, lsems, wsems, e1sems, e2sems, wu, wg, wd, hbv, dmv, u_buf, g_buf, low_a, low_b, total,
               s1, r1, s2, r2):
    place = Place(n_ctx)
    rows, width = h1_ref.shape
    hidden = us_ref.shape[1]
    cuts = hidden // HIDDEN_CUT
    h_gather = Pieces(place, hball_ref, hsems, cut)
    m_gather = Pieces(place, dmball_ref, msems, cut)

    def part(n):
        return slice(n * HIDDEN_CUT, (n + 1) * HIDDEN_CUT)

    loads = [[load_rows(wu_ref.at[:, part(n)], wu.at[:, part(n)], wsems.at[0, n]),
              load_rows(wg_ref.at[:, part(n)], wg.at[:, part(n)], wsems.at[1, n])] for n in range(cuts)]
    down = [load_rows(wd_ref.at[part(n)], wd.at[part(n)], wsems.at[2, n]) for n in range(cuts)]
    for pair in loads:
        for copy in pair:
            copy.start()
    for copy in down:
        copy.start()
    hbv[...] = h1_ref[...].astype(BF)
    own = load_rows(hbv, hball_ref.at[place.ctx], lsems.at[0])
    own.start()
    place.barrier()
    own.wait()
    h_gather.each("step_z", 0)

    hb = hbv[...]
    for n in range(cuts):
        for copy in loads[n]:
            copy.wait()
        u = dot32(hb, wu[:, part(n)])
        g = dot32(hb, wg[:, part(n)])
        u_buf[:, part(n)] = u
        g_buf[:, part(n)] = g
        c = g * gs_ref[:, part(n)]
        low_a[:, part(n)] = (u * us_ref[:, part(n)] * (c * lax.logistic(c))).astype(BF)
        if n == cuts - 3:
            h_gather.each("step_z", 1)
    for copy in down:
        copy.wait()

    def serve_first():
        h_gather.each("step_x", 0)
        h_gather.each("step_z", 2)

    exchange(place, lambda cols: dot32(low_a[...], wd[:, cols]), total, s1, r1, e1sems, serve_first)
    h1 = h1_ref[...]
    fs = fs_ref[...]
    hm = total[...]
    m_inv = inv_rms(hm)
    step = hm * m_inv - h1
    z = h1 + fs * step
    z_inv = inv_rms(z)
    out_ref[...] = (z * z_inv).astype(BF)
    dz = rms_back(z, z_inv, cot_ref[...].astype(F32))
    gfs_ref[...] = jnp.sum(dz * step, axis=0, keepdims=True)
    dxr_ref[...] = (1.0 - fs) * dz
    dmv[...] = rms_back(hm, m_inv, fs * dz).astype(BF)
    own = load_rows(dmv, dmball_ref.at[place.ctx], lsems.at[1])
    own.start()
    own.wait()
    m_gather.each("step_z", 0)
    h_gather.each("step_z", 3)
    h_gather.each("step_x", 1)
    h_gather.each("step_y", 1)
    h_gather.each("step_yx", 0)

    dm = dmv[...]
    for n in range(cuts):
        dgated = dot_nt(dm, wd[part(n), :])
        u, g = u_buf[:, part(n)], g_buf[:, part(n)]
        us, gs = us_ref[:, part(n)], gs_ref[:, part(n)]
        c = g * gs
        s = lax.logistic(c)
        low_a[:, part(n)] = (dgated * (c * s) * us).astype(BF)
        low_b[:, part(n)] = (dgated * (u * us) * (s * (1.0 + c * (1.0 - s))) * gs).astype(BF)
        if n == cuts // 2:
            h_gather.each("step_x", 2)
            h_gather.each("step_y", 2)
            h_gather.each("step_yx", 1)
            h_gather.each("step_c", 0)

    m_gather.each("step_z", 1)

    def serve_second():
        h_gather.each("step_x", 3)
        h_gather.each("step_y", 3)
        m_gather.each("step_x", 0)
        h_gather.each("step_yx", 2)
        m_gather.each("step_z", 2)

    exchange(place, lambda cols: dot_nt(low_a[...], wu[cols, :]) + dot_nt(low_b[...], wg[cols, :]), total, s2, r2,
             e2sems, serve_second)
    m_gather.each("step_z", 3)
    m_gather.each("step_x", 1)
    m_gather.each("step_y", 1)
    m_gather.each("step_yx", 0)
    dh1 = dxr_ref[...] + total[...]
    xf = x_ref[...].astype(F32)
    step_size = as_ref[...]
    ha = ha_ref[...]
    a_inv = inv_rms(ha)
    step = ha * a_inv - xf
    w = xf + step_size * step
    dw = rms_back(w, inv_rms(w), dh1)
    gas_ref[...] = jnp.sum(dw * step, axis=0, keepdims=True)
    dxr_ref[...] = (1.0 - step_size) * dw
    dab_ref[...] = rms_back(ha, a_inv, step_size * dw).astype(BF)

    @pl.loop(4, place.line)
    def _(k):
        for name in ("step_z", "step_x", "step_y"):
            h_gather.each(name, k)
        m_gather.each("step_z", k)

    @pl.loop(2, place.line + 1)
    def _(k):
        m_gather.each("step_x", k)
        m_gather.each("step_y", k)
        m_gather.each("step_yx", k - 1)

        @pl.when(k > 2)
        def _():
            h_gather.each("step_yx", k)
        h_gather.each("step_c", k - 1)
        m_gather.each("step_c", k - 2)

    m_gather.each("step_c", place.line - 1)
    h_gather.finish()
    m_gather.finish()


def feed_forward(hidden_one, branch_attn, x, cotangent, ff_step, attn_step, up_scale, gate_scale, w_up, w_gate, w_down,
                 n_ctx, collective_id, cut):
    rows, width = x.shape
    hidden = w_up.shape[1]
    cuts = hidden // HIDDEN_CUT
    count = width // EXCHANGE
    shape = jax.ShapeDtypeStruct
    dma = pltpu.SemaphoreType.DMA
    V = pltpu.VMEM
    box = V((count, rows, EXCHANGE), BF)
    return pl.pallas_call(
        functools.partial(mid_kernel, n_ctx, cut),
        out_shape=(pltpu.HBM((n_ctx, rows, width), BF), pltpu.HBM((n_ctx, rows, width), BF), shape((rows, width), BF),
                   shape((rows, width), BF), shape((rows, width), F32), shape((1, width), F32), shape((1, width), F32)),
        in_specs=[vmem_spec()] * 8 + [hbm_spec()] * 3,
        out_specs=(hbm_spec(),) * 2 + (vmem_spec(),) * 5,
        scratch_shapes=[
            gather_sems(n_ctx, cut), gather_sems(n_ctx, cut), dma((2,)), dma((3, cuts)), dma((2, count)), dma((2, count)),
            V((width, hidden), BF), V((width, hidden), BF), V((hidden, width), BF), V((rows, width), BF),
            V((rows, width), BF), V((rows, hidden), F32), V((rows, hidden), F32), V((rows, hidden), BF),
            V((rows, hidden), BF), V((rows, width), F32), box, box, box, box],
        compiler_params=pltpu.CompilerParams(collective_id=collective_id, has_side_effects=True,
                                             vmem_limit_bytes=30 << 20),
        cost_estimate=pl.CostEstimate(flops=5 * 10 ** 9, bytes_accessed=30 * 10 ** 6, transcendentals=10 ** 6),
        name="feed_forward",
    )(hidden_one, branch_attn, x, cotangent, ff_step, attn_step, up_scale, gate_scale, in_hbm(w_up), in_hbm(w_gate), in_hbm(w_down))


BLOCK = 4
STATS = 128


def split_parts(v, count):
    parts = []
    rest = v
    for _ in range(count):
        part = rest.astype(BF)
        parts.append(part)
        rest = rest - part.astype(F32)
    return parts


def transposed(src, dst, dtype):
    for n in range(src.shape[1] // 128):
        dst[n * 128:(n + 1) * 128, :] = src[:, n * 128:(n + 1) * 128].T.astype(dtype)


class Among:
    def __init__(self, count, stride=1, first=0):
        self.count, self.stride, self.first = count, stride, first

    def device(self, number):
        return number * self.stride + self.first

    def number(self, device):
        return lax.div(device - self.first, self.stride)

    def has(self, device):
        away = device - self.first
        return (away >= 0) & (lax.rem(away, self.stride) == 0) & (away < self.count * self.stride)


class UnitScatter:
    def __init__(self, place, source, target, send_sems, recv_sems, senders, per_sender, per_owner):
        self.p, self.source, self.target = place, source, target
        self.send_sems, self.recv_sems = send_sems, recv_sems
        self.senders, self.per_sender, self.per_owner = senders, per_sender, per_owner

    def rows(self, unit):
        return pl.ds(pl.multiple_of(unit * 8, 8), 8)

    def copy(self, unit, slot, owner):
        return pltpu.make_async_remote_copy(
            src_ref=self.source.at[self.rows(unit)], dst_ref=self.target.at[self.rows(slot)],
            send_sem=self.send_sems.at[unit], recv_sem=self.recv_sems.at[slot],
            device_id=(owner, self.p.wa), device_id_type=MESH)

    def local(self, unit, slot):
        return pltpu.make_async_copy(self.source.at[self.rows(unit)], self.target.at[self.rows(slot)],
                                     self.recv_sems.at[slot])

    def outgoing(self, remote, near):
        p = self.p

        @pl.when(self.senders.has(p.ctx))
        def _():
            @pl.loop(0, self.per_sender)
            def _(unit):
                place_of = self.senders.number(p.ctx) * self.per_sender + unit
                owner, slot = lax.div(place_of, self.per_owner), lax.rem(place_of, self.per_owner)

                @pl.when(owner != p.ctx)
                def _():
                    remote(self.copy(unit, slot, owner))

                if near is not None:
                    @pl.when(owner == p.ctx)
                    def _():
                        near(self.local(unit, slot))

    def start(self):
        self.outgoing(lambda c: c.start(), lambda c: c.start())

    def wait(self):
        p = self.p

        @pl.loop(0, self.per_owner)
        def _(slot):
            place_of = p.ctx * self.per_owner + slot
            number, unit = lax.div(place_of, self.per_sender), lax.rem(place_of, self.per_sender)
            sender = self.senders.device(number)

            @pl.when(sender != p.ctx)
            def _():
                self.copy(unit, slot, p.ctx).wait_recv()

            @pl.when(sender == p.ctx)
            def _():
                self.local(unit, slot).wait()

    def sent(self):
        self.outgoing(lambda c: c.wait_send(), None)


class Scatter:
    def __init__(self, place, source, target, sems, receivers, senders):
        self.p, self.source, self.target, self.sems = place, source, target, sems
        self.receivers, self.senders = receivers, senders

    def copy(self, dest, sender):
        number = self.receivers.number(dest)
        return pltpu.make_async_remote_copy(
            src_ref=self.source(number), dst_ref=self.target(sender),
            send_sem=self.sems.at[0, number], recv_sem=self.sems.at[1, sender],
            device_id=(dest, self.p.wa), device_id_type=MESH)

    def each(self, fn):
        p = self.p

        @pl.loop(1, p.n_ctx)
        def _(shift):
            fn(lax.rem(p.ctx + shift, p.n_ctx))

    def start(self):
        p = self.p

        @pl.when(self.senders.has(p.ctx))
        def _():
            def go(dest):
                @pl.when(self.receivers.has(dest))
                def _():
                    self.copy(dest, p.ctx).start()
            self.each(go)

            @pl.when(self.receivers.has(p.ctx))
            def _():
                self.local().start()

    def local(self):
        source = self.source(self.receivers.number(self.p.ctx))
        return pltpu.make_async_copy(source, self.target(self.p.ctx), self.sems.at[1, self.p.ctx])

    def wait(self):
        p = self.p

        @pl.when(self.receivers.has(p.ctx))
        def _():
            def got(sender):
                @pl.when(self.senders.has(sender))
                def _():
                    self.copy(p.ctx, sender).wait_recv()
            self.each(got)

            @pl.when(self.senders.has(p.ctx))
            def _():
                self.local().wait()

    def sent(self):
        p = self.p

        @pl.when(self.senders.has(p.ctx))
        def _():
            def left(dest):
                @pl.when(self.receivers.has(dest))
                def _():
                    self.copy(dest, p.ctx).wait_send()
            self.each(left)


def out_devices(n_ctx, tiles):
    stride = n_ctx // tiles
    return Among(tiles, stride, stride // 2)


def bwd_kernel(n_ctx, cut, aligned, out_aligned, *refs):
    (dab_ref, gfs_ref, gas_ref, qraw_ref, kraw_ref, lse_ref, o_ref, dxr_ref, qs_ref, us_ref, gs_ref,
     wo_ref, wq_ref, wk_ref, wv_ref, xall_ref, qall_ref, kall_ref, vall_ref, hball_ref, dmball_ref, wu_ref, wg_ref, wd_ref,
     dx_ref, got_q, gout_ref, got_u, gdown_ref, got_s, gus_ref, ggs_ref,
     daball_ref, statall_ref, turned, turned_qkv, gocc,
     asems, ssts, lsems, csems, esems, usems, tsems, osems, rsems, vsems, ssems, xsems, nsems, fsems,
     hbbuf, dmbuf, dabbuf, stbuf, qbuf, kvbuf, dobuf, rowstats, stats, delta, q2, k2, v2, do2, dq2, dk2, dv2,
     wuw, wgw, wdw, gu, gg, gd, colu, colg, comb, small, small_row, dqkv, got_t, got_o, obs, accq, sbuf, rbuf) = refs
    place = Place(n_ctx)
    rows, width = dxr_ref.shape
    block_len = rows // 2
    channels = qraw_ref.shape[1]
    tiles = channels // 128
    hidden = us_ref.shape[1]
    mine = hidden // n_ctx
    group = 2 * place.across
    subs = group // BLOCK
    many = BLOCK * rows
    window = gu.shape[0]
    scale = 1.0 / math.sqrt(HD)
    a_gather = Pieces(place, daball_ref, asems, cut)
    s_gather = Pieces(place, statall_ref, ssts, ((rows, rows, rows),))
    start = jnp.minimum(lax.div(place.ctx * mine, 128) * 128, hidden - window)
    start = pl.multiple_of(start, 128)
    offset = pl.multiple_of(place.ctx * mine - start, 8)
    win = pl.ds(start, window)
    own = [load_rows(dab_ref, daball_ref.at[place.ctx], lsems.at[0]),
           load_rows(wu_ref.at[:, win], wuw, lsems.at[2]), load_rows(wg_ref.at[:, win], wgw, lsems.at[3]),
           load_rows(wd_ref.at[win, :], wdw, lsems.at[4])]
    for copy in own:
        copy.start()
    for t in range(tiles):
        obs[t] = o_ref[:, t * 128:(t + 1) * 128].astype(BF)
    place.barrier_all()
    own[0].wait()
    a_gather.each("step_z", 0)
    d_out = dot_nt(dab_ref[...], wo_ref[...]).astype(BF)
    lane = lax.broadcasted_iota(jnp.int32, (rows, 128), 1)
    packed = jnp.zeros((rows, 128), F32)
    for t in range(tiles):
        cols = slice(t * 128, (t + 1) * 128)
        do2[t] = stack_heads(d_out[:, cols])
        both_heads = stack_heads(d_out[:, cols].astype(F32) * o_ref[:, cols])
        delta[t] = jnp.broadcast_to(jnp.sum(both_heads, axis=1, keepdims=True), (2 * rows, 128))
        for h in range(2):
            part_rows = slice(h * rows, (h + 1) * rows)
            values = split_parts(lse_ref[t, part_rows], 3) + split_parts(delta[t, part_rows], 2)
            for i, value in enumerate(values):
                packed = jnp.where(lane == i * 2 * tiles + 2 * t + h, value.astype(F32), packed)
    stats[...] = packed.astype(BF)
    own_stats = load_rows(stats, statall_ref.at[place.ctx], lsems.at[0])
    own_stats.start()
    own_stats.wait()
    s_gather.each("step_z", 0)
    everyone = Among(n_ctx)
    owners = out_devices(n_ctx, tiles)
    o_scatter = Scatter(place, lambda dest: obs.at[dest], lambda sender: got_o.at[sender], osems, owners, everyone)

    for t in range(tiles):
        cols = slice(t * 128, (t + 1) * 128)
        for raw_ref, dest in ((qraw_ref, q2), (kraw_ref, k2)):
            raw = raw_ref[:, cols]
            dest[t] = stack_heads((raw * head_rms(raw) * qs_ref[:, cols]).astype(BF))
    dq2[...] = jnp.zeros_like(dq2)
    dk2[...] = jnp.zeros_like(dk2)
    dv2[...] = jnp.zeros_like(dv2)
    gu[...] = jnp.zeros_like(gu)
    gg[...] = jnp.zeros_like(gg)
    gd[...] = jnp.zeros_like(gd)
    colu[...] = jnp.zeros_like(colu)
    colg[...] = jnp.zeros_like(colg)
    gocc[...] = jnp.zeros_like(gocc)

    def row_positions(shape, axis, first):
        i = lax.broadcasted_iota(jnp.int32, shape, axis)
        return position_of(first + lax.div(i, rows), lax.rem(i, rows), block_len, n_ctx)

    def own_positions(shape, axis):
        i = lax.broadcasted_iota(jnp.int32, shape, axis)
        return position_of(place.ctx, lax.rem(i, rows), block_len, n_ctx)

    total_blocks = n_ctx // BLOCK

    def serve(name, k):
        a_gather.each(name, k)
        s_gather.each(name, k)

    def kv_loads(b):
        side = lax.rem(b, 2)
        return [load_rows(ref.at[pl.ds(b * BLOCK, BLOCK)], kvbuf.at[side, i], csems.at[side, i])
                for i, ref in enumerate((kall_ref, vall_ref))]

    def wide(v):
        return jnp.concatenate([v] * (many // 128), axis=1)

    for copy in kv_loads(0):
        copy.start()

    @pl.loop(0, total_blocks)
    def _(b):
        side = lax.rem(b, 2)

        @pl.when(b + 1 < total_blocks)
        def _():
            for copy in kv_loads(b + 1):
                copy.start()

        for copy in kv_loads(b):
            copy.wait()
        allowed = row_positions((1, many), 1, b * BLOCK) <= own_positions((2 * rows, 1), 0)

        @pl.loop(0, tiles)
        def _(t):
            cols = pl.ds(pl.multiple_of(t * 128, 128), 128)
            kt = kvbuf[side, 0, :, :, cols].reshape(many, 128)
            vt = kvbuf[side, 1, :, :, cols].reshape(many, 128)
            score = dot_nt(q2[t], kt)
            p = jnp.where(allowed, jnp.exp2(score * (LOG2E * scale) - wide(lse_ref[t])), 0.0)
            dp = dot_nt(do2[t], vt)
            ds = (p * (dp - wide(delta[t])) * scale).astype(BF)
            dq2[t] += dot32(ds, kt)

        @pl.when(b == total_blocks // 4)
        def _():
            serve("step_z", 1)

        @pl.when(b == total_blocks - 1)
        def _():
            serve("step_z", 2)
            serve("step_x", 0)

    def head_back(raw_ref, grads, base, first):
        for t in range(tiles):
            cols = slice(t * 128, (t + 1) * 128)
            raw = raw_ref[:, cols]
            inv = head_rms(raw)
            normed = raw * inv
            grad = join_heads(grads[t])
            grad_scale = jnp.sum(grad * normed, axis=0, keepdims=True)
            small_row[:, cols] = grad_scale if first else small_row[:, cols] + grad_scale
            e = grad * qs_ref[:, cols]
            dqkv[base + t] = ((e - normed * pair_mean(normed * e)) * inv).astype(BF)

    head_back(qraw_ref, dq2, 0, True)
    f_scatter = Scatter(place, lambda dest: dqkv.at[dest], lambda sender: got_t.at[sender], fsems, Among(tiles), everyone)
    f_scatter.start()
    o_scatter.start()
    own_v = load_rows(vall_ref.at[place.ctx], dobuf.at[0], lsems.at[0])
    own_v.start()
    own_v.wait()
    for t in range(tiles):
        v2[t] = stack_heads(dobuf[0, :, t * 128:(t + 1) * 128])
    for copy in own[1:]:
        copy.wait()

    def block_of(s, k, sub):
        return ((place.z - s * k) * subs + sub) * BLOCK

    def a_loads(side, first):
        return [load_rows(ref.at[pl.ds(first, BLOCK)], buf.at[side], rsems.at[side, i])
                for i, (ref, buf) in enumerate(((daball_ref, dabbuf), (qall_ref, qbuf), (statall_ref, stbuf)))]

    def m_loads(b):
        side = lax.rem(b, 2)
        return [load_rows(dmball_ref.at[pl.ds(b * BLOCK, BLOCK)], dmbuf.at[side], xsems.at[side, 0]),
                load_rows(hball_ref.at[pl.ds(b * BLOCK, BLOCK)], hbbuf.at[side], xsems.at[side, 1])]

    def keys_part(side, first):
        for copy in a_loads(side, first):
            copy.wait()
        dab = dabbuf[side].reshape(many, width)
        dobuf[...] = dot_nt(dab, wo_ref[...]).astype(BF).reshape(BLOCK, rows, channels)
        for j in range(BLOCK):
            rowstats[:, j * rows:(j + 1) * rows] = stbuf[side, j].astype(F32).T

        @pl.when(owners.has(place.ctx))
        def _():
            gocc[...] += dot_tn(got_o[pl.ds(first, BLOCK)].reshape(many, 128), dab)

        allowed = own_positions((2 * rows, 1), 0) <= row_positions((1, many), 1, first)
        heads = 2 * tiles

        @pl.loop(0, tiles)
        def _(t):
            cols = pl.ds(pl.multiple_of(t * 128, 128), 128)
            qt = qbuf[side, :, :, cols].reshape(many, 128)
            dot_ = dobuf[:, :, cols].reshape(many, 128)

            def both_rows(parts, at):
                def one(h):
                    row = rowstats[pl.ds(at * heads + h, 1), :]
                    for i in range(1, parts):
                        row = row + rowstats[pl.ds((at + i) * heads + h, 1), :]
                    return jnp.broadcast_to(row, (rows, many))
                return jnp.concatenate([one(2 * t), one(2 * t + 1)], axis=0)

            score = dot_nt(k2[t], qt)
            p = jnp.where(allowed, jnp.exp2(score * (LOG2E * scale) - both_rows(3, 0)), 0.0)
            dp = dot_nt(v2[t], dot_)
            ds = (p * (dp - both_rows(2, 3)) * scale).astype(BF)
            dv2[t] += dot32(p.astype(BF), dot_)
            dk2[t] += dot32(ds, qt)

    def hidden_part(side):
        hb = hbbuf[side].reshape(many, width)
        dm = dmbuf[side].reshape(many, width)
        us, gs = us_ref[:, win], gs_ref[:, win]
        u = dot32(hb, wuw[...])
        g = dot32(hb, wgw[...])
        dgated = dot_nt(dm, wdw[...])
        a, c = u * us, g * gs
        s = lax.logistic(c)
        cs = c * s
        r = s * (1.0 + c * (1.0 - s))
        da = dgated * cs
        dc = dgated * a * r
        colu[...] += jnp.sum((da * u).reshape(many // 8, 8, window), axis=0)
        colg[...] += jnp.sum((dc * g).reshape(many // 8, 8, window), axis=0)
        gu[...] += dot_tn((da * us).astype(BF), hb)
        gg[...] += dot_tn((dc * gs).astype(BF), hb)
        gd[...] += dot_tn((a * cs).astype(BF), dm)

    def hidden_all():
        for copy in m_loads(0):
            copy.start()

        @pl.loop(0, total_blocks)
        def _(b):
            @pl.when(b + 1 < total_blocks)
            def _():
                for copy in m_loads(b + 1):
                    copy.start()

            for copy in m_loads(b):
                copy.wait()
            hidden_part(lax.rem(b, 2))

            serve("step_z", b + 3)
            serve("step_x", b + 1)
            serve("step_y", b + 1)
            serve("step_yx", b)
            serve("step_c", b - 1)

    def both(k, fn):
        for s in (1, -1):
            @pl.when(a_gather.parts[0].exists(s, k))
            def _():
                @pl.loop(0, subs)
                def _(sub):
                    fn(0 if s > 0 else 1, block_of(s, k, sub))

    def begin(loads):
        for copy in loads:
            copy.start()

    def keys_full(side, first):
        begin(a_loads(side, first))
        keys_part(side, first)

    hidden_all()

    gdown_ref[...] = gd[pl.ds(offset, mine), :]
    comb[0:mine] = gu[pl.ds(offset, mine), :]
    comb[mine:2 * mine] = gg[pl.ds(offset, mine), :]
    comb[2 * mine:] = jnp.zeros((comb.shape[0] - 2 * mine, width), F32)
    transposed(comb, turned, BF)
    part = width // n_ctx

    def row_block(ref, size):
        return lambda dest: ref.at[pl.ds(pl.multiple_of(dest * size, 8), size)]

    if aligned:
        u_scatter = Scatter(place, row_block(turned, part), lambda sender: got_u.at[sender], usems, everyone, everyone)
        u_scatter.start()
    shift = lax.rem(window - offset, window)
    gus_ref[...] = pltpu.roll(jnp.broadcast_to(jnp.sum(colu[...], axis=0, keepdims=True), (8, window)), shift, 1)
    ggs_ref[...] = pltpu.roll(jnp.broadcast_to(jnp.sum(colg[...], axis=0, keepdims=True), (8, window)), shift, 1)

    o_scatter.wait()

    @pl.loop(0, place.line)
    def _(k):
        serve("step_c", total_blocks - 1 + k)
        if subs == 1:
            both(k, lambda side, first: begin(a_loads(side, first)))
            both(k, keys_part)
        else:
            both(k, keys_full)

    if out_aligned:
        g_scatter = UnitScatter(place, gocc, gout_ref, ssems.at[0], ssems.at[1], owners, 16, channels // n_ctx // 8)
        g_scatter.start()

    head_back(kraw_ref, dk2, tiles, False)
    for t in range(tiles):
        dqkv[2 * tiles + t] = join_heads(dv2[t]).astype(BF)
    t_scatter = Scatter(place, lambda dest: dqkv.at[dest + tiles], lambda sender: got_t.at[sender], tsems,
                        Among(2 * tiles, 1, tiles), everyone)
    t_scatter.start()
    head_part = channels // n_ctx
    for i in range(n_ctx):
        small[i, 0:1, 0:part] = gfs_ref[:, i * part:(i + 1) * part]
        small[i, 1:2, 0:part] = gas_ref[:, i * part:(i + 1) * part]
        small[i, 2:3, 0:head_part] = small_row[:, i * head_part:(i + 1) * head_part]
    n_scatter = Scatter(place, lambda dest: small.at[dest], lambda sender: got_s.at[sender], nsems, everyone, everyone)
    n_scatter.start()

    def input_terms(cols):
        total = None
        for n, w_ref in enumerate((wq_ref, wk_ref, wv_ref)):
            grad = jnp.concatenate([dqkv[n * tiles + t] for t in range(tiles)], axis=1)
            term = dot_nt(grad, w_ref[cols, :])
            total = term if total is None else total + term
        return total

    pl.when(place.ctx < 3 * tiles)(load_rows(xall_ref.at[pl.ds(0, BLOCK)], hbbuf.at[0], xsems.at[0, 0]).start)
    exchange(place, input_terms, dx_ref, sbuf, rbuf, esems)
    dx_ref[...] += dxr_ref[...]

    f_scatter.wait()
    t_scatter.wait()

    @pl.when(place.ctx < 3 * tiles)
    def _():
        accq[...] = jnp.zeros_like(accq)

        def x_load(b):
            side = lax.rem(b, 2)
            return load_rows(xall_ref.at[pl.ds(b * BLOCK, BLOCK)], hbbuf.at[side], xsems.at[side, 0])

        @pl.loop(0, total_blocks)
        def _(b):
            @pl.when(b + 1 < total_blocks)
            def _():
                x_load(b + 1).start()

            x_load(b).wait()
            accq[...] += dot_tn(got_t[pl.ds(b * BLOCK, BLOCK)].reshape(many, 128),
                                hbbuf[lax.rem(b, 2)].reshape(many, width))

        transposed(accq, turned_qkv, BF)

    if aligned:
        q_scatter = Scatter(place, row_block(turned_qkv, part), lambda sender: got_q.at[sender], vsems, everyone, Among(3 * tiles))
        q_scatter.start()
        u_scatter.wait()
        q_scatter.wait()
        u_scatter.sent()
        q_scatter.sent()
    if out_aligned:
        g_scatter.wait()
        g_scatter.sent()
    a_gather.finish()
    s_gather.finish()
    o_scatter.sent()
    f_scatter.sent()
    t_scatter.sent()
    n_scatter.wait()
    n_scatter.sent()


def backward_attention(dab, grad_ff_step, grad_attn_step, q_raw, k_raw, lse, attended, dxr, qk_scale, up_scale, gate_scale,
                       w_out, w_query, w_key, w_value, x_all, q_all, k_all, v_all, hb_all, dmb_all, w_up, w_gate, w_down,
                       n_ctx, collective_id, cut):
    rows, width = dxr.shape
    channels = q_raw.shape[1]
    tiles = channels // 128
    hidden = up_scale.shape[1]
    mine = hidden // n_ctx
    part = width // n_ctx
    aligned = part % 16 == 0
    out_rows = channels // n_ctx
    out_aligned = out_rows % 8 == 0
    window = 256
    pair = -(-2 * mine // 128) * 128
    count = width // EXCHANGE
    many = BLOCK * rows
    n_blocks = n_ctx
    shape = jax.ShapeDtypeStruct
    dma = pltpu.SemaphoreType.DMA
    V = pltpu.VMEM
    stack = lambda dtype: V((tiles, 2 * rows, 128), dtype)
    outs = (
        shape((rows, width), F32),
        shape((3 * tiles, part, 128), BF), shape((out_rows, width), F32), shape((n_ctx, part, pair), BF),
        shape((mine, width), F32), shape((n_ctx, 8, 128), F32), shape((8, window), F32), shape((8, window), F32),
        shape((n_ctx, rows, width), BF), shape((n_ctx, rows, STATS), BF),
        shape((width, pair), BF), shape((width, 128), BF), shape((128, width), F32))
    return pl.pallas_call(
        functools.partial(bwd_kernel, n_ctx, cut, aligned, out_aligned),
        out_shape=outs,
        in_specs=[vmem_spec()] * 15 + [any_spec()] * 9,
        out_specs=(vmem_spec(),) * 8 + (hbm_spec(),) * 2 + (vmem_spec(),) * 3,
        scratch_shapes=[
            gather_sems(n_ctx, cut), gather_sems(n_ctx, ((rows, rows, rows),)), dma((5,)), dma((2, 2)), dma((2, count)),
            dma((2, n_ctx)), dma((2, n_ctx)), dma((2, n_ctx)), dma((2, 3)), dma((2, n_ctx)), dma((2, 16)), dma((2, 2)), dma((2, n_ctx)), dma((2, n_ctx)),
            V((2, BLOCK, rows, width), BF), V((2, BLOCK, rows, width), BF), V((2, BLOCK, rows, width), BF), V((2, BLOCK, rows, STATS), BF),
            V((2, BLOCK, rows, channels), BF), V((2, 2, BLOCK, rows, channels), BF), V((BLOCK, rows, channels), BF),
            V((STATS, many), F32), V((rows, STATS), BF), stack(F32), stack(BF), stack(BF), stack(BF), stack(BF), stack(F32), stack(F32), stack(F32),
            V((width, window), BF), V((width, window), BF), V((window, width), BF),
            V((window, width), F32), V((window, width), F32), V((window, width), F32),
            V((8, window), F32), V((8, window), F32), V((pair, width), F32), V((n_ctx, 8, 128), F32), V((1, channels), F32),
            V((3 * tiles, rows, 128), BF), V((n_ctx, rows, 128), BF), V((n_ctx, rows, 128), BF), V((tiles, rows, 128), BF),
            V((128, width), F32),
            V((count, rows, EXCHANGE), BF), V((count, rows, EXCHANGE), BF)],
        compiler_params=pltpu.CompilerParams(collective_id=collective_id, has_side_effects=True,
                                             vmem_limit_bytes=40 << 20),
        cost_estimate=pl.CostEstimate(flops=20 * 10 ** 9, bytes_accessed=60 * 10 ** 6, transcendentals=6 * 10 ** 6),
        name="backward_attention",
    )(dab, grad_ff_step, grad_attn_step, q_raw, k_raw, lse, attended, dxr, qk_scale, up_scale, gate_scale,
      w_out, w_query, w_key, w_value, x_all, q_all, k_all, v_all, hb_all, dmb_all, w_up, w_gate, w_down)


def last_kernel(result_ref, dx_ref, gotq_ref, gout_ref, gotu_ref, gdown_ref, gots_ref, gus_ref, ggs_ref,
                o_result, o_dx, o_gq, o_gk, o_gv, o_gout, o_gup, o_ggate, o_gdown, o_gqs, o_gus, o_ggs, o_gas, o_gfs):
    o_result[...] = result_ref[...]
    o_dx[...] = dx_ref[...]
    o_gout[...] = gout_ref[...]
    o_gdown[...] = gdown_ref[...]
    mine = o_gus.shape[1]
    tiles = o_gq.shape[1] // 128
    for j in range(gotu_ref.shape[0]):
        o_gup[:, j * mine:(j + 1) * mine] = gotu_ref[j, :, 0:mine].astype(F32)
        o_ggate[:, j * mine:(j + 1) * mine] = gotu_ref[j, :, mine:2 * mine].astype(F32)
    for n, ref in enumerate((o_gq, o_gk, o_gv)):
        for t in range(tiles):
            ref[:, t * 128:(t + 1) * 128] = gotq_ref[n * tiles + t].astype(F32)
    total = jnp.sum(gots_ref[...], axis=0)
    for row, ref in enumerate((o_gfs, o_gas, o_gqs)):
        ref[...] = total[row:row + 1, 0:ref.shape[1]]
    o_gus[...] = gus_ref[0:1, 0:mine]
    o_ggs[...] = ggs_ref[0:1, 0:mine]


def last_step(parts, n_ctx, channels, hidden):
    width = parts[1].shape[1]
    part, mine = width // n_ctx, hidden // n_ctx
    shape = jax.ShapeDtypeStruct
    outs = [shape(parts[0].shape, BF), shape(parts[1].shape, F32)] + [shape((part, channels), F32)] * 3
    outs += [shape(parts[3].shape, F32)] + [shape((part, hidden), F32)] * 2 + [shape((mine, width), F32)]
    outs += [shape((1, channels // n_ctx), F32)] + [shape((1, mine), F32)] * 2 + [shape((1, part), F32)] * 2
    return pl.pallas_call(
        last_kernel, out_shape=tuple(outs), in_specs=[vmem_spec()] * len(parts), out_specs=(vmem_spec(),) * len(outs),
        compiler_params=pltpu.CompilerParams(vmem_limit_bytes=32 << 20), name="last_step")(*parts)


CUT = ((64, 48, 48), (64, 48, 48))
BACK_CUT = ((32, 32, 32), (96, 64, 64))


def shards(layer_input, w_query, w_key, w_value, w_out, w_up, w_gate, w_down, qk_scale, up_scale,
           gate_scale, attention_step, feedforward_step, cotangent):
    n_ctx = lax.axis_size("ctx")
    ctx = lax.axis_index("ctx")
    rows = 2 * layer_input.shape[2]
    width = layer_input.shape[3]
    channels = w_query.shape[1]
    hidden = w_up.shape[1]
    tiles = channels // 128
    x = layer_input.reshape(rows, width)
    flat = lambda v: v.reshape(1, -1)
    x_all, q_all, k_all, v_all, q_raw, k_raw, attended, lse, hidden_one, branch_attn = forward_attention(
        x, w_query, w_key, w_value, flat(qk_scale), w_out, flat(attention_step), n_ctx, 0, CUT)
    hb_all, dmb_all, result, dab, input_res, grad_ff_step, grad_attn_step = feed_forward(
        hidden_one, branch_attn, x, cotangent.reshape(rows, width), flat(feedforward_step), flat(attention_step),
        flat(up_scale), flat(gate_scale), w_up, w_gate, w_down, n_ctx, 1, CUT)
    (input_grad, got_q, grad_out, got_u, grad_down, got_s, gus, ggs,
     _, _, turned, turned_qkv, gocc) = backward_attention(
        dab, grad_ff_step, grad_attn_step, q_raw, k_raw, lse, attended, input_res, flat(qk_scale), flat(up_scale),
        flat(gate_scale), w_out, w_query, w_key, w_value, x_all, q_all, k_all, v_all, hb_all, dmb_all,
        w_up, w_gate, w_down, n_ctx, 2, BACK_CUT)
    part = width // n_ctx
    if part % 16:
        turned, turned_qkv = lax.optimization_barrier((turned, turned_qkv))
        got_u = lax.all_to_all(turned, "ctx", 0, 0, tiled=True).reshape(n_ctx, part, -1)
        got_q = lax.all_to_all(turned_qkv, "ctx", 0, 0, tiled=True).reshape(n_ctx, part, 128)[:3 * tiles]
    if (channels // n_ctx) % 8:
        gocc = lax.optimization_barrier(gocc)
        whole = jnp.zeros((n_ctx, 128, width), F32)
        whole = lax.dynamic_update_slice_in_dim(whole, gocc[None], ctx, 0)[n_ctx // tiles // 2::n_ctx // tiles][:tiles]
        grad_out = lax.psum_scatter(whole.reshape(channels, width), "ctx", scatter_dimension=0, tiled=True)
    outs = last_step((result, input_grad, got_q, grad_out, got_u, grad_down, got_s, gus, ggs), n_ctx, channels, hidden)
    tokens = tuple(v.reshape(layer_input.shape) for v in outs[:2])
    return tokens + tuple(outs[2:9]) + tuple(v.reshape(-1) for v in outs[9:])


def solution(mesh):
    placed = (
        P("ctx", None, None, None),
        P(None, "wa"),
        P(None, "wa"),
        P(None, "wa"),
        P("wa", None),
        P(None, "wa"),
        P(None, "wa"),
        P("wa", None),
        P("wa"),
        P("wa"),
        P("wa"),
        P(),
        P(),
        P("ctx", None, None, None),
    )
    return jax.shard_map(
        shards,
        mesh=mesh,
        in_specs=placed,
        out_specs=(
            P("ctx", None, None, None),
            P("ctx", None, None, None),
            P("ctx", "wa"),
            P("ctx", "wa"),
            P("ctx", "wa"),
            P(("wa", "ctx"), None),
            P("ctx", "wa"),
            P("ctx", "wa"),
            P(("wa", "ctx"), None),
            P(("wa", "ctx")),
            P(("wa", "ctx")),
            P(("wa", "ctx")),
            P("ctx"),
            P("ctx"),
        ),
        check_vma=False,
    )
```
